32 devices in a mesh: ctx: 8 (over y, x, core), wa: 4 (over z).
Axes of the slice: x: 2, y: 2, z: 4, core: 2. Of those that a mesh axis runs over, the one named last changes fastest.
Arguments:
- tokens: bfloat16 [4, 3072, 768], P('wa', 'ctx'), may hold values from -6 to 6
- cotangent: bfloat16 [4, 3072, 768], P('wa', 'ctx'), may hold values from -6 to 6
- segment_ids: int32 [4, 3072], P('wa', 'ctx'), may hold values from 0 to 3, never falling along the last dimension, each value on 1 to 1536 neighbouring positions
- token_types: int32 [4, 3072], P('wa', 'ctx'), may hold values 0 or 1
- query_wordword: bfloat16 [768, 768], P('wa'), may hold values from -0.21875 to 0.21875
- query_wordentity: bfloat16 [768, 768], P('wa'), may hold values from -0.21875 to 0.21875
- query_entityword: bfloat16 [768, 768], P('wa'), may hold values from -0.21875 to 0.21875
- query_entityentity: bfloat16 [768, 768], P('wa'), may hold values from -0.21875 to 0.21875
- bias_wordword: bfloat16 [768], P('wa'), may hold values from -3 to 3
- bias_wordentity: bfloat16 [768], P('wa'), may hold values from -3 to 3
- bias_entityword: bfloat16 [768], P('wa'), may hold values from -3 to 3
- bias_entityentity: bfloat16 [768], P('wa'), may hold values from -3 to 3
- key_weight: bfloat16 [768, 768], P('wa'), may hold values from -0.21875 to 0.21875
- value_weight: bfloat16 [768, 768], P('wa'), may hold values from -0.21875 to 0.21875
- value_bias: bfloat16 [768], P('wa'), may hold values from -0.4375 to 0.4375
- output_weight: bfloat16 [768, 768], P('wa'), may hold values from -4 to 4
- output_bias: bfloat16 [768], P('wa'), may hold values from -3 to 3
- first_gain: bfloat16 [768], P('wa'), may hold values from 0.5 to 1.5
- first_bias: bfloat16 [768], P('wa'), may hold values from -3 to 3
- inner_weight: bfloat16 [768, 3072], P('wa'), may hold values from -0.21875 to 0.21875
- inner_bias: bfloat16 [3072], P('wa'), may hold values from -3 to 3
- outer_weight: bfloat16 [3072, 768], P('wa'), may hold values from -0.109375 to 0.109375
- outer_bias: bfloat16 [768], P('wa'), may hold values from -3 to 3
- second_gain: bfloat16 [768], P('wa'), may hold values from 0.5 to 1.5
- second_bias: bfloat16 [768], P('wa'), may hold values from -3 to 3
Outputs:
- outputs: bfloat16 [4, 3072, 768], P('wa', 'ctx')
- token_grads: float32 [4, 3072, 768], P('wa', 'ctx')
- grad_query_wordword: float32 [768, 768], P('wa')
- grad_query_wordentity: float32 [768, 768], P('wa')
- grad_query_entityword: float32 [768, 768], P('wa')
- grad_query_entityentity: float32 [768, 768], P('wa')
- grad_bias_wordword: float32 [768], P('wa')
- grad_bias_wordentity: float32 [768], P('wa')
- grad_bias_entityword: float32 [768], P('wa')
- grad_bias_entityentity: float32 [768], P('wa')
- grad_key_weight: float32 [768, 768], P('wa')
- grad_value_weight: float32 [768, 768], P('wa')
- grad_value_bias: float32 [768], P('wa')
- grad_output_weight: float32 [768, 768], P('wa')
- grad_output_bias: float32 [768], P('wa')
- grad_first_gain: float32 [768], P('wa')
- grad_first_bias: float32 [768], P('wa')
- grad_inner_weight: float32 [768, 3072], P('wa')
- grad_inner_bias: float32 [3072], P('wa')
- grad_outer_weight: float32 [3072, 768], P('wa')
- grad_outer_bias: float32 [768], P('wa')
- grad_second_gain: float32 [768], P('wa')
- grad_second_bias: float32 [768], P('wa')
The draws below stay inside these ranges and needn't reach their ends.
Inputs may be any that keep to these rules, and one draw needn't show every extreme that they name: `segment_ids`: within each sequence the numbers never fall; a document holds 1 to 1536 tokens, and one document of each sequence holds exactly 1536.
All inputs are finite; a program needn't handle non-finite values. No bound on the sum of `token_types` on one device may be relied on, other than what follows from the above.
Results may differ from the reference program's by a relative error of at most 0.019.
Values may be sent and summed in bfloat16 or wider, within the bound.
No kernel may reach another device: no remote copies, remote signals or barrier semaphores. Data moves between devices by JAX's collectives and lax.ppermute only.
A program may use at most 192 MiB of HBM per device.

```python
import math
import jax
import jax.numpy as jnp
import numpy as np
from jax import lax

D = 768
HEADS = 12
HD = 64
FF = 3072
LEN = 3072
SEQS = 4
DOC_MAX = 1536
NDOCS = 4


def touch_ends(entries, rng, least, high):
    longest = entries.shape.index(max(entries.shape))
    spots = []
    for shift in (0, 1):
        where = [jax.random.randint(jax.random.fold_in(rng, axis), (), 0, length) for axis, length in enumerate(entries.shape)]
        where[longest] = (where[longest] + shift) % entries.shape[longest]
        spots.append(tuple(where))
    return entries.at[spots[0]].set(least).at[spots[1]].set(high)


def shard_levels(own_key, extent, shards, smallest, largest):
    level, own = 1.0, jax.random.fold_in(own_key, 6)
    for axis_at, shards_of in shards:
        heights = jnp.exp(jax.random.uniform(jax.random.fold_in(own, axis_at), (shards_of,), jnp.float32, smallest / len(shards), largest / len(shards)))
        level = level * jnp.repeat(heights, extent[axis_at] // shards_of).reshape([-1 if axis == axis_at else 1 for axis in range(len(extent))])
    return level


def length_profile(amount, total, most, skew):
    loads = [(1 << 20) // math.isqrt(grade ** skew) + 1 for grade in range(2, amount + 1)]
    surplus, holding = total - most - (amount - 1), [1] * (amount - 1)
    while surplus > 0:
        free = [i for i in range(amount - 1) if holding[i] < most]
        whole, budget = sum([loads[i] for i in free]), surplus
        for i in free:
            more = min(most - holding[i], max(1, budget * loads[i] // whole), surplus)
            holding[i] = holding[i] + more
            surplus = surplus - more
    return np.array([most] + holding)


def uneven(key, count, total, bound, skew):
    if count == 2:
        one = jax.random.randint(key, (), max(1, total - bound), min(bound, total - 1) + 1)
        return jnp.stack([one, total - one])
    sizes = jnp.asarray(length_profile(count, total, bound, skew), jnp.int32)
    twos = (count - 1) // 2
    giver, taker = sizes[1:1 + 2 * twos:2], sizes[2:2 + 2 * twos:2]
    room = jnp.minimum(giver - 1, bound - taker)
    moved = jax.random.randint(jax.random.fold_in(key, 1), (twos,), 0, 1 << 20) % (room + 1)
    sizes = sizes.at[1:1 + 2 * twos:2].set(giver - moved).at[2:2 + 2 * twos:2].set(taker + moved)
    return sizes[jax.random.permutation(jax.random.fold_in(key, 2), count)]


def scatter_about(stream_key, dims, deviation, reach, split=(), dtype=jnp.bfloat16):
    loudness = shard_levels(stream_key, dims, split, -0.22, 0.18) if split else 1.0
    values = jax.random.normal(stream_key, dims, jnp.float32) * deviation * loudness
    return jnp.minimum(jnp.maximum(values, -reach), reach).astype(dtype)


def setup_inputs(seed: int = 0) -> dict:
    key_list = jax.random.split(jax.random.key(seed), 26)
    return {
        "tokens": scatter_about(key_list[0], (SEQS, LEN, D), 1.0, 6.0, ((0, 4), (1, 8))),
        "cotangent": scatter_about(key_list[1], (SEQS, LEN, D), 1.0, 6.0, ((0, 4), (1, 8))),
        "segment_ids": jax.vmap(lambda own: jnp.searchsorted(jnp.cumsum(uneven(own, NDOCS, LEN, DOC_MAX, 1)), jnp.arange(LEN), side="right"))(jax.random.split(key_list[2], SEQS)).reshape((SEQS, LEN)).astype(jnp.int32),
        "token_types": touch_ends((jax.random.randint(key_list[3], (SEQS, LEN), 0, 3) < 1).astype(jnp.int32), jax.random.fold_in(key_list[3], 1), 0, 1),
        "query_wordword": scatter_about(key_list[4], (D, D), D ** -0.5, 0.21875, ((0, 4),)),
        "query_wordentity": scatter_about(key_list[5], (D, D), D ** -0.5, 0.21875, ((0, 4),)),
        "query_entityword": scatter_about(key_list[6], (D, D), D ** -0.5, 0.21875, ((0, 4),)),
        "query_entityentity": scatter_about(key_list[7], (D, D), D ** -0.5, 0.21875, ((0, 4),)),
        "bias_wordword": scatter_about(key_list[8], (D,), 0.5, 3.0, ((0, 4),)),
        "bias_wordentity": scatter_about(key_list[9], (D,), 0.5, 3.0, ((0, 4),)),
        "bias_entityword": scatter_about(key_list[10], (D,), 0.5, 3.0, ((0, 4),)),
        "bias_entityentity": scatter_about(key_list[11], (D,), 0.5, 3.0, ((0, 4),)),
        "key_weight": scatter_about(key_list[12], (D, D), D ** -0.5, 0.21875, ((0, 4),)),
        "value_weight": scatter_about(key_list[13], (D, D), D ** -0.5, 0.21875, ((0, 4),)),
        "value_bias": scatter_about(key_list[14], (D,), 0.03, 0.4375, ((0, 4),)),
        "output_weight": scatter_about(key_list[15], (D, D), 2 ** -0.5, 4.0, ((0, 4),)),
        "output_bias": scatter_about(key_list[16], (D,), 0.5, 3.0, ((0, 4),)),
        "first_gain": jnp.clip(1.0 + 0.1 * jax.random.normal(key_list[17], (D,), jnp.float32), 0.5, 1.5).astype(jnp.bfloat16),
        "first_bias": scatter_about(key_list[18], (D,), 0.3, 3.0, ((0, 4),)),
        "inner_weight": scatter_about(key_list[19], (D, FF), D ** -0.5, 0.21875, ((0, 4),)),
        "inner_bias": scatter_about(key_list[20], (FF,), 0.5, 3.0, ((0, 4),)),
        "outer_weight": scatter_about(key_list[21], (FF, D), FF ** -0.5, 0.109375, ((0, 4),)),
        "outer_bias": scatter_about(key_list[22], (D,), 0.3, 3.0, ((0, 4),)),
        "second_gain": jnp.clip(1.0 + 0.1 * jax.random.normal(key_list[23], (D,), jnp.float32), 0.5, 1.5).astype(jnp.bfloat16),
        "second_bias": scatter_about(key_list[24], (D,), 0.3, 3.0, ((0, 4),)),
    }


@jax.custom_vjp
def low(v):
    return lax.optimization_barrier(v.astype(jnp.bfloat16)).astype(jnp.float32)

@jax.custom_vjp
def low_back(v):
    return v

def low_keep(v):
    return (low(v), None)

def low_pass(kept, grad):
    return (grad,)

def back_keep(v):
    return (v, None)

def back_low(kept, grad):
    return (low(grad),)
low.defvjp(low_keep, low_pass)
low_back.defvjp(back_keep, back_low)
EPSILON = 1e-12
MASKED = -1e+30

def matmul(left, right):
    return jnp.dot(left, right, precision=lax.Precision.HIGHEST, preferred_element_type=jnp.float32)

def layer_norm(values, gain, shift):
    center = values - lax.optimization_barrier(jnp.mean(values, axis=-1, keepdims=True))
    spread = lax.optimization_barrier(jnp.mean(center * center, axis=-1, keepdims=True))
    return center * lax.rsqrt(spread + EPSILON) * gain + shift

def gelu_exact(values):
    return jax.nn.gelu(values, approximate=False)

def attend_block(block, keys, values, key_seg, key_entity):
    query_word, query_entity, query_seg = block
    rows = query_word.shape[0]
    scale = HD ** (-0.5)
    word_heads = query_word.reshape(rows, HEADS, HD)
    entity_heads = query_entity.reshape(rows, HEADS, HD)
    key_heads = keys.reshape(keys.shape[0], HEADS, HD)
    value_heads = values.reshape(values.shape[0], HEADS, HD)
    word_scores = jnp.einsum('qhd,khd->hqk', word_heads, key_heads, precision=lax.Precision.HIGHEST)
    entity_scores = jnp.einsum('qhd,khd->hqk', entity_heads, key_heads, precision=lax.Precision.HIGHEST)
    raw = low_back(jnp.where(key_entity[None, None, :], entity_scores, word_scores) * scale)
    allowed = (query_seg[:, None] == key_seg[None, :])[None]
    scores = jnp.where(allowed, raw, MASKED)
    top = lax.optimization_barrier(jnp.max(scores, axis=2, keepdims=True))
    expo = jnp.exp(scores - top)
    probs = expo / lax.optimization_barrier(jnp.sum(expo, axis=2, keepdims=True))
    mixed = jnp.einsum('hqk,khd->qhd', low(probs), value_heads, precision=lax.Precision.HIGHEST)
    return mixed.reshape(rows, HEADS * HD)

def sequence_forward(inputs, seg, types, params):
    q_ww, q_we, q_ew, q_ee, b_ww, b_we, b_ew, b_ee, key_w, value_w, value_b, out_w, out_b, gain_one, shift_one, inner_w, inner_b, outer_w, outer_b, gain_two, shift_two = params
    entity = (types == 1)[:, None]
    query_word = low(low_back(jnp.where(entity, matmul(inputs, q_ew) + b_ew, matmul(inputs, q_ww) + b_ww)))
    query_entity = low(low_back(jnp.where(entity, matmul(inputs, q_ee) + b_ee, matmul(inputs, q_we) + b_we)))
    keys = low(low_back(matmul(inputs, key_w)))
    values = low(low_back(matmul(inputs, value_w) + value_b))
    length = inputs.shape[0]
    rows = min(512, length)
    count = length // rows
    key_entity = types == 1

    def block_fn(block):
        return attend_block(block, keys, values, seg, key_entity)
    mixed = lax.map(jax.checkpoint(block_fn), (query_word.reshape(count, rows, -1), query_entity.reshape(count, rows, -1), seg.reshape(count, rows)))
    context = low(low_back(mixed.reshape(length, -1)))
    branch = low_back(matmul(context, out_w) + out_b)
    first = layer_norm(inputs + branch, gain_one, shift_one)
    inner = low_back(matmul(low(first), inner_w) + inner_b)
    hidden = low(gelu_exact(inner))
    ffn = low_back(matmul(hidden, outer_w) + outer_b)
    return layer_norm(first + ffn, gain_two, shift_two)

def reference(tokens, cotangent, segment_ids, token_types, query_wordword, query_wordentity, query_entityword, query_entityentity, bias_wordword, bias_wordentity, bias_entityword, bias_entityentity, key_weight, value_weight, value_bias, output_weight, output_bias, first_gain, first_bias, inner_weight, inner_bias, outer_weight, outer_bias, second_gain, second_bias):
    weights = (query_wordword, query_wordentity, query_entityword, query_entityentity, bias_wordword, bias_wordentity, bias_entityword, bias_entityentity, key_weight, value_weight, value_bias, output_weight, output_bias, first_gain, first_bias, inner_weight, inner_bias, outer_weight, outer_bias, second_gain, second_bias)
    params = tuple((w.astype(jnp.float32) for w in weights))
    inputs = tokens.astype(jnp.float32)

    def forward(all_inputs, all_params):
        results = [sequence_forward(all_inputs[i], segment_ids[i], token_types[i], all_params) for i in range(SEQS)]
        return jnp.stack(results)
    result, pull = jax.vjp(forward, inputs, params)
    grad_inputs, grads = pull(cotangent.astype(jnp.float32))
    return (result.astype(jnp.bfloat16), grad_inputs, grads[0], grads[1], grads[2], grads[3], grads[4], grads[5], grads[6], grads[7], grads[8], grads[9], grads[10], grads[11], grads[12], grads[13], grads[14], grads[15], grads[16], grads[17], grads[18], grads[19], grads[20])
```

```python
import jax
import jax.numpy as jnp
from jax import lax
from jax.experimental import pallas as pl
from jax.experimental.pallas import tpu as pltpu
from jax.sharding import PartitionSpec as P

HD = 64


EPSILON = 1e-12
MASKED = -1e30


def as_sent(shard):
    return jax.tree.map(lambda a: a.astype(jnp.bfloat16) if a.dtype == jnp.float32 else a, shard)


def passed_along(value, axis, steps):
    count = lax.axis_size(axis)
    leading, last = (max(0, -steps), min(count, count - steps))
    return lax.ppermute(value, axis, [(source, source + steps) for source in range(leading, last)])


def layer_norm(values, gain, shift):
    center = values - jnp.mean(values, axis=-1, keepdims=True)
    spread = jnp.mean(center * center, axis=-1, keepdims=True)
    return center * lax.rsqrt(spread + EPSILON) * gain + shift


def gelu_exact(values):
    return jax.nn.gelu(values, approximate=False)


def matmul(left, right):
    return jnp.dot(left, right, preferred_element_type=jnp.float32)


def left_product(left, right):
    return lax.dot_general(
        left, right, (((0,), (0,)), ((), ())), preferred_element_type=jnp.float32
    )


def right_product(left, right):
    return lax.dot_general(
        left, right, (((1,), (1,)), ((), ())), preferred_element_type=jnp.float32
    )


def column_sums(values):
    return jnp.sum(values.astype(jnp.float32), axis=0)


def columns(values, start):
    return lax.dynamic_slice_in_dim(values, start, HD, 1)


def head_scores(query_word, query_entity, keys_head, key_entity, allowed, scale):
    word_scores = right_product(query_word, keys_head)
    entity_scores = right_product(query_entity, keys_head)
    raw = jnp.where(key_entity[None, :], entity_scores, word_scores) * scale
    return jnp.where(allowed, raw, MASKED)


def merge_heads(stacked):
    return jnp.transpose(stacked, (1, 0, 2)).reshape(
        stacked.shape[1], stacked.shape[0] * stacked.shape[2]
    )


def windowed_device(
    tokens,
    cotangent,
    segment_ids,
    token_types,
    query_wordword,
    query_wordentity,
    query_entityword,
    query_entityentity,
    bias_wordword,
    bias_wordentity,
    bias_entityword,
    bias_entityentity,
    key_weight,
    value_weight,
    value_bias,
    output_weight,
    output_bias,
    first_gain,
    first_bias,
    inner_weight,
    inner_bias,
    outer_weight,
    outer_bias,
    second_gain,
    second_bias,
):
    attention = (
        lax.all_gather(query_wordword, "wa", axis=0, tiled=True),
        lax.all_gather(query_wordentity, "wa", axis=0, tiled=True),
        lax.all_gather(query_entityword, "wa", axis=0, tiled=True),
        lax.all_gather(query_entityentity, "wa", axis=0, tiled=True),
        lax.all_gather(bias_wordword, "wa", axis=0, tiled=True),
        lax.all_gather(bias_wordentity, "wa", axis=0, tiled=True),
        lax.all_gather(bias_entityword, "wa", axis=0, tiled=True),
        lax.all_gather(bias_entityentity, "wa", axis=0, tiled=True),
        lax.all_gather(key_weight, "wa", axis=0, tiled=True),
        lax.all_gather(value_weight, "wa", axis=0, tiled=True),
        lax.all_gather(value_bias, "wa", axis=0, tiled=True),
        lax.all_gather(output_weight, "wa", axis=0, tiled=True),
        lax.all_gather(output_bias, "wa", axis=0, tiled=True),
        lax.all_gather(first_gain, "wa", axis=0, tiled=True),
        lax.all_gather(first_bias, "wa", axis=0, tiled=True),
    )
    (
        full_ww,
        full_we,
        full_ew,
        full_ee,
        shift_ww,
        shift_we,
        shift_ew,
        shift_ee,
        full_key,
        full_value,
        shift_value,
        full_output,
        shift_output,
        gain_one,
        shift_one,
    ) = attention
    feedforward = (
        lax.all_gather(inner_weight, "wa", axis=0, tiled=True),
        lax.all_gather(inner_bias, "wa", axis=0, tiled=True),
        lax.all_gather(outer_weight, "wa", axis=0, tiled=True),
        lax.all_gather(outer_bias, "wa", axis=0, tiled=True),
        lax.all_gather(second_gain, "wa", axis=0, tiled=True),
        lax.all_gather(second_bias, "wa", axis=0, tiled=True),
    )
    full_inner, shift_inner, full_outer, shift_outer, gain_two, shift_two = feedforward
    inputs = tokens[0]
    seg = segment_ids[0]
    types = token_types[0]
    tok = inputs.shape[0]
    dmod = inputs.shape[1]
    heads = dmod // HD
    scale = HD ** (-0.5)
    length = tok * lax.axis_size("ctx")
    doc_max = min(2048, 4 * tok, length // 2)
    reach = (doc_max - 2) // tok + 1
    entity = (types == 1)[:, None]
    proj_ww = matmul(inputs, full_ww) + shift_ww
    proj_we = matmul(inputs, full_we) + shift_we
    proj_ew = matmul(inputs, full_ew) + shift_ew
    proj_ee = matmul(inputs, full_ee) + shift_ee
    query_word = jnp.where(entity, proj_ew, proj_ww).astype(jnp.bfloat16)
    query_entity = jnp.where(entity, proj_ee, proj_we).astype(jnp.bfloat16)
    keys = matmul(inputs, full_key).astype(jnp.bfloat16)
    values = (matmul(inputs, full_value) + shift_value).astype(jnp.bfloat16)
    own_kv = jnp.concatenate([keys, values], axis=1)
    own_seg = seg + 1
    tags = own_seg * 2 + types

    def pass_left(packet, unused):
        moved = jax.tree.map(
            lambda part, own: part.astype(own.dtype),
            passed_along(as_sent(packet), "ctx", 1),
            packet,
        )
        return (moved, moved)

    def pass_right(packet, unused):
        moved = jax.tree.map(
            lambda part, own: part.astype(own.dtype),
            passed_along(as_sent(packet), "ctx", -1),
            packet,
        )
        return (moved, moved)

    _, (left_kv, left_tags) = lax.scan(pass_left, (own_kv, tags), None, length=reach)
    _, (right_kv, right_tags) = lax.scan(pass_right, (own_kv, tags), None, length=reach)
    window = jnp.concatenate(
        [jnp.flip(left_kv, 0).reshape(-1, 2 * dmod), own_kv, right_kv.reshape(-1, 2 * dmod)], axis=0
    )
    window_tags = jnp.concatenate(
        [jnp.flip(left_tags, 0).reshape(-1), tags, right_tags.reshape(-1)], axis=0
    )
    key_entity = window_tags % 2 == 1
    allowed = own_seg[:, None] == (window_tags // 2)[None, :]

    def head_forward(index):
        start = index * HD
        scores = head_scores(
            columns(query_word, start),
            columns(query_entity, start),
            columns(window, start),
            key_entity,
            allowed,
            scale,
        )
        top = jnp.max(scores, axis=1, keepdims=True)
        expo = jnp.exp(scores - top)
        total = jnp.sum(expo, axis=1, keepdims=True)
        probs = (expo / total).astype(jnp.bfloat16)
        return (matmul(probs, columns(window, dmod + start)), (top + jnp.log(total))[:, 0])

    head_context, lse = lax.map(head_forward, jnp.arange(heads))
    context = merge_heads(head_context).astype(jnp.bfloat16)
    branch = matmul(context, full_output) + shift_output
    first, pull_one = jax.vjp(
        layer_norm,
        inputs.astype(jnp.float32) + branch,
        gain_one.astype(jnp.float32),
        shift_one.astype(jnp.float32),
    )
    first_low = first.astype(jnp.bfloat16)
    inner = matmul(first_low, full_inner) + shift_inner
    activated, pull_gelu = jax.vjp(gelu_exact, inner)
    hidden = activated.astype(jnp.bfloat16)
    ffn = matmul(hidden, full_outer) + shift_outer
    result, pull_two = jax.vjp(
        layer_norm, first + ffn, gain_two.astype(jnp.float32), shift_two.astype(jnp.float32)
    )
    grad_sum_two, grad_gain_two, grad_shift_two = pull_two(cotangent[0].astype(jnp.float32))
    grad_ffn = grad_sum_two.astype(jnp.bfloat16)
    grad_outer = left_product(hidden, grad_ffn)
    grad_outer_shift = column_sums(grad_ffn)
    grad_inner = pull_gelu(right_product(grad_ffn, full_outer))[0].astype(jnp.bfloat16)
    grad_inner_full = left_product(first_low, grad_inner)
    grad_inner_shift = column_sums(grad_inner)
    grad_first = grad_sum_two + right_product(grad_inner, full_inner)
    grad_sum_one, grad_gain_one, grad_shift_one = pull_one(grad_first)
    grad_branch = grad_sum_one.astype(jnp.bfloat16)
    grad_output = left_product(context, grad_branch)
    grad_output_shift = column_sums(grad_branch)
    grad_context = right_product(grad_branch, full_output).astype(jnp.bfloat16)

    def head_backward(index):
        start = index * HD
        word_head = columns(query_word, start)
        entity_head = columns(query_entity, start)
        keys_head = columns(window, start)
        values_head = columns(window, dmod + start)
        context_head = columns(grad_context, start)
        scores = head_scores(word_head, entity_head, keys_head, key_entity, allowed, scale)
        probs = jnp.exp(scores - lse[index][:, None])
        grad_probs = right_product(context_head, values_head)
        delta = jnp.sum(probs * grad_probs, axis=1)
        grad_scores = (probs * (grad_probs - delta[:, None])).astype(jnp.bfloat16)
        zero = jnp.zeros_like(grad_scores)
        grad_word = jnp.where(key_entity[None, :], zero, grad_scores)
        grad_entity = jnp.where(key_entity[None, :], grad_scores, zero)
        grad_qword = matmul(grad_word, keys_head) * scale
        grad_qentity = matmul(grad_entity, keys_head) * scale
        grad_keys = (
            left_product(grad_word, word_head) + left_product(grad_entity, entity_head)
        ) * scale
        grad_values = left_product(probs.astype(jnp.bfloat16), context_head)
        return (grad_qword, grad_qentity, delta, grad_keys, grad_values)

    grad_qword, grad_qentity, delta, window_keys, window_values = lax.map(
        lambda index: head_backward(index), jnp.arange(heads)
    )
    parts_keys = merge_heads(window_keys).reshape(2 * reach + 1, tok, dmod)
    parts_values = merge_heads(window_values).reshape(2 * reach + 1, tok, dmod)

    def back_left(total, piece):
        return (
            (
                passed_along((total[0] + piece[0]).astype(jnp.bfloat16), "ctx", -1).astype(
                    jnp.float32
                ),
                passed_along((total[1] + piece[1]).astype(jnp.bfloat16), "ctx", -1).astype(
                    jnp.float32
                ),
            ),
            None,
        )

    def back_right(total, piece):
        return (
            (
                passed_along((total[0] + piece[0]).astype(jnp.bfloat16), "ctx", 1).astype(
                    jnp.float32
                ),
                passed_along((total[1] + piece[1]).astype(jnp.bfloat16), "ctx", 1).astype(
                    jnp.float32
                ),
            ),
            None,
        )

    empty = jnp.zeros((tok, dmod), jnp.float32)
    from_above, _ = lax.scan(back_left, (empty, empty), (parts_keys[:reach], parts_values[:reach]))
    from_below, _ = lax.scan(
        back_right,
        (empty, empty),
        (jnp.flip(parts_keys[reach + 1 :], 0), jnp.flip(parts_values[reach + 1 :], 0)),
    )
    own_keys = parts_keys[reach] + from_above[0] + from_below[0]
    own_values = parts_values[reach] + from_above[1] + from_below[1]
    grad_keys = own_keys.astype(jnp.bfloat16)
    grad_values = own_values.astype(jnp.bfloat16)
    grad_qword = merge_heads(grad_qword).astype(jnp.bfloat16)
    grad_qentity = merge_heads(grad_qentity).astype(jnp.bfloat16)
    zeros = jnp.zeros_like(grad_qword)
    grad_pww = jnp.where(entity, zeros, grad_qword)
    grad_pew = jnp.where(entity, grad_qword, zeros)
    grad_pwe = jnp.where(entity, zeros, grad_qentity)
    grad_pee = jnp.where(entity, grad_qentity, zeros)
    input_grads = grad_sum_one + right_product(grad_pww, full_ww) + right_product(grad_pwe, full_we)
    input_grads = input_grads + right_product(grad_pew, full_ew) + right_product(grad_pee, full_ee)
    input_grads = (
        input_grads + right_product(grad_keys, full_key) + right_product(grad_values, full_value)
    )
    local_grads = (
        left_product(inputs, grad_pww),
        left_product(inputs, grad_pwe),
        left_product(inputs, grad_pew),
        left_product(inputs, grad_pee),
        column_sums(grad_pww),
        column_sums(grad_pwe),
        column_sums(grad_pew),
        column_sums(grad_pee),
        left_product(inputs, grad_keys),
        left_product(inputs, grad_values),
        column_sums(grad_values),
        grad_output,
        grad_output_shift,
        grad_gain_one,
        grad_shift_one,
        grad_inner_full,
        grad_inner_shift,
        grad_outer,
        grad_outer_shift,
        grad_gain_two,
        grad_shift_two,
    )
    shards = (
        lax.psum_scatter(
            local_grads[0].astype(jnp.bfloat16), "wa", scatter_dimension=0, tiled=True
        ).astype(jnp.float32),
        lax.psum_scatter(
            local_grads[1].astype(jnp.bfloat16), "wa", scatter_dimension=0, tiled=True
        ).astype(jnp.float32),
        lax.psum_scatter(
            local_grads[2].astype(jnp.bfloat16), "wa", scatter_dimension=0, tiled=True
        ).astype(jnp.float32),
        lax.psum_scatter(
            local_grads[3].astype(jnp.bfloat16), "wa", scatter_dimension=0, tiled=True
        ).astype(jnp.float32),
        lax.psum_scatter(
            local_grads[4].astype(jnp.bfloat16), "wa", scatter_dimension=0, tiled=True
        ).astype(jnp.float32),
        lax.psum_scatter(
            local_grads[5].astype(jnp.bfloat16), "wa", scatter_dimension=0, tiled=True
        ).astype(jnp.float32),
        lax.psum_scatter(
            local_grads[6].astype(jnp.bfloat16), "wa", scatter_dimension=0, tiled=True
        ).astype(jnp.float32),
        lax.psum_scatter(
            local_grads[7].astype(jnp.bfloat16), "wa", scatter_dimension=0, tiled=True
        ).astype(jnp.float32),
        lax.psum_scatter(
            local_grads[8].astype(jnp.bfloat16), "wa", scatter_dimension=0, tiled=True
        ).astype(jnp.float32),
        lax.psum_scatter(
            local_grads[9].astype(jnp.bfloat16), "wa", scatter_dimension=0, tiled=True
        ).astype(jnp.float32),
        lax.psum_scatter(
            local_grads[10].astype(jnp.bfloat16), "wa", scatter_dimension=0, tiled=True
        ).astype(jnp.float32),
        lax.psum_scatter(
            local_grads[11].astype(jnp.bfloat16), "wa", scatter_dimension=0, tiled=True
        ).astype(jnp.float32),
        lax.psum_scatter(
            local_grads[12].astype(jnp.bfloat16), "wa", scatter_dimension=0, tiled=True
        ).astype(jnp.float32),
        lax.psum_scatter(
            local_grads[13].astype(jnp.bfloat16), "wa", scatter_dimension=0, tiled=True
        ).astype(jnp.float32),
        lax.psum_scatter(
            local_grads[14].astype(jnp.bfloat16), "wa", scatter_dimension=0, tiled=True
        ).astype(jnp.float32),
        lax.psum_scatter(
            local_grads[15].astype(jnp.bfloat16), "wa", scatter_dimension=0, tiled=True
        ).astype(jnp.float32),
        lax.psum_scatter(
            local_grads[16].astype(jnp.bfloat16), "wa", scatter_dimension=0, tiled=True
        ).astype(jnp.float32),
        lax.psum_scatter(
            local_grads[17].astype(jnp.bfloat16), "wa", scatter_dimension=0, tiled=True
        ).astype(jnp.float32),
        lax.psum_scatter(
            local_grads[18].astype(jnp.bfloat16), "wa", scatter_dimension=0, tiled=True
        ).astype(jnp.float32),
        lax.psum_scatter(
            local_grads[19].astype(jnp.bfloat16), "wa", scatter_dimension=0, tiled=True
        ).astype(jnp.float32),
        lax.psum_scatter(
            local_grads[20].astype(jnp.bfloat16), "wa", scatter_dimension=0, tiled=True
        ).astype(jnp.float32),
    )
    totals = lax.psum(
        (
            shards[0],
            shards[1],
            shards[2],
            shards[3],
            shards[4],
            shards[5],
            shards[6],
            shards[7],
            shards[8],
            shards[9],
            shards[10],
            shards[11],
            shards[12],
            shards[13],
            shards[14],
            shards[15],
            shards[16],
            shards[17],
            shards[18],
            shards[19],
            shards[20],
        ),
        "ctx",
    )
    return (
        result.astype(jnp.bfloat16)[None],
        input_grads[None],
        totals[0],
        totals[1],
        totals[2],
        totals[3],
        totals[4],
        totals[5],
        totals[6],
        totals[7],
        totals[8],
        totals[9],
        totals[10],
        totals[11],
        totals[12],
        totals[13],
        totals[14],
        totals[15],
        totals[16],
        totals[17],
        totals[18],
        totals[19],
        totals[20],
    )


CHIPS = 4
KEY_BLOCK = 256
NEGATIVE = -1e30


def lanes_product(left, right):
    return lax.dot_general(
        left, right, (((1,), (1,)), ((), ())), preferred_element_type=jnp.float32
    )


def swapped(value, step):
    count = lax.axis_size("ctx")
    return lax.ppermute(value, "ctx", [(i, i ^ step) for i in range(count)])


def chip_pieces(value):
    half = value.shape[0] // 2
    along_x = swapped(value, 2)
    along_y = swapped(value, 4)
    across = jnp.concatenate([swapped(along_x[:half], 4), swapped(along_y[half:], 2)], axis=0)
    return value, along_x, along_y, across


def project_kernel(place, t0, t1, t2, t3, weight, bias, entity, q_ref, kv_ref):
    tok = t0.shape[0]
    wide = 4 * 3 * HD
    for m, piece in enumerate((t0, t1, t2, t3)):
        chip = jnp.bitwise_xor(place[0], m)
        total = jnp.dot(piece[...], weight[...], preferred_element_type=jnp.float32) + bias[...]
        is_entity = entity[chip] == 1.0
        for h in range(3):
            at = 4 * HD * h
            word = total[:, at : at + 2 * HD]
            other = total[:, at + 2 * HD : at + 4 * HD]
            q = jnp.where(is_entity, other, word).astype(jnp.bfloat16)
            q_ref[chip, :, 2 * HD * h : 2 * HD * (h + 1)] = q * jnp.bfloat16(HD**-0.5)
        kv_ref[chip] = total[:, wide:].astype(jnp.bfloat16)


def key_sources(place, own, other, entity, lanes):
    for j in range(CHIPS):
        for source, core in ((own, place[1]), (other, 1 - place[1])):
            row = pl.multiple_of((2 * j + core) * own.shape[1], 128)
            for h in range(3):
                kv = source[j, :, 2 * HD * h : 2 * HD * (h + 1)]
                flag = entity[pl.ds(row, own.shape[1]), :] == 1.0
                low = lax.broadcasted_iota(jnp.int32, kv.shape, 1) < HD
                turned = pltpu.roll(kv.astype(jnp.float32), HD, 1)
                both = jnp.where(low, kv.astype(jnp.float32), turned)
                keys = jnp.where(low == flag, 0.0, both)
                yield row, h, kv, keys.astype(jnp.bfloat16)


def attend_kernel(
    place, first, last, q_ref, own, other, seg_col, seg_row, entity, out, turned_out, lse, keys, turned_values
):
    tok = q_ref.shape[1]
    for row, h, kv, key in key_sources(place, own, other, entity, tok):
        keys[h, pl.ds(row, tok), :] = key
        turned_values[h, :, pl.ds(row, tok)] = kv.astype(jnp.float32).T[HD:].astype(jnp.bfloat16)

    def queries(j, unused):
        seg = seg_row[j]
        for h in range(3):
            q = q_ref[j, :, 2 * HD * h : 2 * HD * (h + 1)]

            def step(t, carry):
                top, total, acc = carry
                at = pl.multiple_of(t * KEY_BLOCK, KEY_BLOCK)
                scores = lanes_product(keys[h, pl.ds(at, KEY_BLOCK), :], q)
                scores = jnp.where(seg_col[pl.ds(at, KEY_BLOCK), :] == seg, scores, NEGATIVE)
                peak = jnp.maximum(top, jnp.max(scores, axis=0, keepdims=True))
                fade = jnp.exp(top - peak)
                expo = jnp.exp(scores - peak)
                total = total * fade + jnp.sum(expo, axis=0, keepdims=True)
                acc = acc * fade + jnp.dot(
                    turned_values[h, :, pl.ds(at, KEY_BLOCK)],
                    expo.astype(jnp.bfloat16),
                    preferred_element_type=jnp.float32,
                )
                return peak, total, acc

            start = (
                jnp.full((1, tok), NEGATIVE, jnp.float32),
                jnp.zeros((1, tok), jnp.float32),
                jnp.zeros((HD, tok), jnp.float32),
            )
            top, total, acc = lax.fori_loop(first[j], last[j], step, start)
            turned_out[j, HD * h : HD * (h + 1), :] = acc / total
            lse[j, h] = top + jnp.log(total)
        out[j] = turned_out[j].T.astype(jnp.bfloat16)
        return 0

    lax.fori_loop(0, CHIPS, queries, 0)


def attend_back_kernel(
    place,
    first,
    last,
    q_ref,
    own,
    other,
    seg_col,
    seg_row,
    entity,
    entity_own,
    turned_out,
    lse,
    grad,
    dq_ref,
    dkv_own,
    dkv_other,
    keys,
    turned_keys,
    values,
    grad_keys,
    grad_values,
):
    tok = q_ref.shape[1]
    for row, h, kv, key in key_sources(place, own, other, entity, tok):
        keys[h, pl.ds(row, tok), :] = key
        turned_keys[h, :, pl.ds(row, tok)] = key.astype(jnp.float32).T.astype(jnp.bfloat16)
        values[h, pl.ds(row, tok), :] = kv
    grad_keys[...] = jnp.zeros_like(grad_keys)
    grad_values[...] = jnp.zeros_like(grad_values)

    def queries(j, unused):
        seg = seg_row[j]
        turned_grad = grad[j].astype(jnp.float32).T
        slot = jnp.bitwise_xor(place[0], j)
        is_entity = entity_own[j] == 1.0
        for h in range(3):
            q = q_ref[j, :, 2 * HD * h : 2 * HD * (h + 1)]
            rows = slice(HD * h, HD * (h + 1))
            delta = jnp.sum(turned_grad[rows] * turned_out[j, rows, :], axis=0, keepdims=True)
            shift = lse[j, h]
            own_grad = grad[j, :, rows]
            padded = jnp.concatenate([jnp.zeros_like(own_grad), own_grad], axis=1)

            def step(t, acc):
                at = pl.multiple_of(t * KEY_BLOCK, KEY_BLOCK)
                ds = pl.ds(at, KEY_BLOCK)
                scores = lanes_product(keys[h, ds, :], q)
                probs = jnp.where(seg_col[ds, :] == seg, jnp.exp(scores - shift), 0.0)
                grad_probs = lanes_product(values[h, ds, :], padded)
                grad_scores = (probs * (grad_probs - delta)).astype(jnp.bfloat16)
                grad_values[h, ds, :] += jnp.dot(
                    probs.astype(jnp.bfloat16), padded, preferred_element_type=jnp.float32
                )
                grad_keys[h, ds, :] += jnp.dot(grad_scores, q, preferred_element_type=jnp.float32)
                return acc + jnp.dot(
                    turned_keys[h, :, ds], grad_scores, preferred_element_type=jnp.float32
                )

            acc = lax.fori_loop(
                first[j], last[j], step, jnp.zeros((2 * HD, tok), jnp.float32)
            )
            dq = acc.T * (HD**-0.5)
            dq_ref[slot, :, 4 * HD * h : 4 * HD * h + 2 * HD] = jnp.where(
                is_entity, 0.0, dq
            ).astype(jnp.bfloat16)
            dq_ref[slot, :, 4 * HD * h + 2 * HD : 4 * HD * (h + 1)] = jnp.where(
                is_entity, dq, 0.0
            ).astype(jnp.bfloat16)
        return 0

    lax.fori_loop(0, CHIPS, queries, 0)
    for j in range(CHIPS):
        slot = jnp.bitwise_xor(place[0], j)
        for target, core in ((dkv_own, place[1]), (dkv_other, 1 - place[1])):
            ds = pl.ds(pl.multiple_of((2 * j + core) * tok, 128), tok)
            flag = entity[ds, :] == 1.0
            for h in range(3):
                both = grad_keys[h, ds, :]
                low = lax.broadcasted_iota(jnp.int32, both.shape, 1) < HD
                picked = jnp.where(flag, pltpu.roll(both, HD, 1), both)
                target[slot, :, 2 * HD * h : 2 * HD * (h + 1)] = jnp.where(
                    low, picked, grad_values[h, ds, :]
                ).astype(jnp.bfloat16)


def smem():
    return pl.BlockSpec(memory_space=pltpu.SMEM)


def vmem():
    return pl.BlockSpec(memory_space=pltpu.VMEM)


def whole_call(kernel, scalars, arrays, outs, scratch=(), flops=0, nbytes=0, exps=0):
    return pl.pallas_call(
        kernel,
        out_shape=outs,
        in_specs=[smem() for _ in scalars] + [vmem() for _ in arrays],
        out_specs=jax.tree.map(lambda _: vmem(), outs),
        scratch_shapes=list(scratch),
        compiler_params=pltpu.CompilerParams(vmem_limit_bytes=56 << 20),
        cost_estimate=pl.CostEstimate(flops=flops, bytes_accessed=nbytes, transcendentals=exps),
    )(*scalars, *arrays)


def shaped(shape, dtype):
    return jax.ShapeDtypeStruct(shape, dtype)


def grouped_device(
    tokens,
    cotangent,
    segment_ids,
    token_types,
    query_wordword,
    query_wordentity,
    query_entityword,
    query_entityentity,
    bias_wordword,
    bias_wordentity,
    bias_entityword,
    bias_entityentity,
    key_weight,
    value_weight,
    value_bias,
    output_weight,
    output_bias,
    first_gain,
    first_bias,
    inner_weight,
    inner_bias,
    outer_weight,
    outer_bias,
    second_gain,
    second_bias,
):
    bf16, f32 = jnp.bfloat16, jnp.float32
    place = lax.axis_index("ctx")
    chip, core = place // 2, place % 2
    wa = lax.axis_index("wa")
    parts = lax.axis_size("wa")
    inputs = tokens[0]
    tok, dmod = inputs.shape
    rows = key_weight.shape[0]
    half = rows // 2
    group = dmod // CHIPS
    hidden_all = inner_weight.shape[1]
    ff_slot = hidden_all // (2 * CHIPS)
    where = jnp.stack([chip, core]).astype(jnp.int32)

    tags = lax.all_gather(segment_ids[0] * 2 + token_types[0], "ctx", axis=0, tiled=True)
    length = tags.shape[0]
    seg, types = tags // 2, tags % 2
    vectors = (
        bias_wordword,
        bias_wordentity,
        bias_entityword,
        bias_entityentity,
        value_bias,
        output_bias,
        first_gain,
        first_bias,
        outer_bias,
        second_gain,
        second_bias,
    )
    packed = jnp.concatenate([v for v in vectors] + [inner_bias]).reshape(-1, rows)
    packed = jnp.pad(packed, ((0, 16 - packed.shape[0]), (0, 256 - rows)))
    packed = lax.all_gather(packed, "wa", axis=0, tiled=False)[:, :, :rows]
    head_bias = lax.dynamic_index_in_dim(packed, chip, 0, keepdims=False)[:5].astype(f32)
    full = jnp.transpose(packed, (1, 0, 2)).astype(f32)
    shift_output, gain_one, shift_one, shift_outer, gain_two, shift_two = (
        full[k].reshape(1, dmod) for k in range(5, 11)
    )
    shift_inner = packed[:, 11:15].astype(f32).reshape(1, hidden_all)

    six = (query_wordword, query_wordentity, query_entityword, query_entityentity, key_weight, value_weight)
    mine = [lax.dynamic_slice(w, (half * core, group * chip), (half, group)).reshape(half, 3, HD) for w in six]
    mine = jnp.concatenate(
        [jnp.stack(mine[:4], axis=2).reshape(half, 4 * group), jnp.stack(mine[4:], axis=2).reshape(half, 2 * group)],
        axis=1,
    )
    mine = lax.all_gather(mine, "wa", axis=0, tiled=False)
    theirs = swapped(mine, 1)
    weight = jnp.where(
        core == 0, jnp.stack([mine, theirs], axis=1), jnp.stack([theirs, mine], axis=1)
    ).reshape(dmod, 6 * group)
    bias = jnp.concatenate(
        [
            jnp.stack([b.reshape(3, HD) for b in head_bias[:4]], axis=1).reshape(1, 4 * group),
            jnp.stack([jnp.zeros((3, HD), f32), head_bias[4].reshape(3, HD)], axis=1).reshape(1, 2 * group),
        ],
        axis=1,
    )

    pieces = chip_pieces(inputs)

    slot = jnp.concatenate(
        [
            lax.dynamic_slice(inner_weight, (0, ff_slot * place), (rows, ff_slot)),
            lax.dynamic_slice(outer_weight, (half * place, 0), (half, ff_slot)),
            lax.dynamic_slice(outer_weight, (half * place, ff_slot), (half, ff_slot)),
            lax.dynamic_slice(output_weight, (rows // CHIPS * chip, ff_slot * core), (rows // CHIPS, ff_slot)),
        ],
        axis=0,
    )
    slot_rows = slot.shape[0]
    slots = jnp.stack(chip_pieces(lax.all_gather(slot, "wa", axis=0, tiled=False)))
    order = jnp.bitwise_xor(chip, jnp.arange(CHIPS))
    slots_other = swapped(slots, 1)
    slots = jnp.where(core == 0, jnp.stack([slots, slots_other], 1), jnp.stack([slots_other, slots], 1))
    slots = jnp.take(slots, order, axis=0)
    full_inner = jnp.transpose(slots[:, :, :, :rows], (2, 3, 0, 1, 4)).reshape(dmod, hidden_all)
    full_outer = slots[:, :, :, rows : 2 * rows].reshape(CHIPS, 2, parts, 2, half, ff_slot)
    full_outer = jnp.transpose(full_outer, (2, 0, 1, 4, 3, 5)).reshape(hidden_all, dmod)
    full_output = jnp.transpose(slots[:, :, :, 2 * rows :], (2, 0, 3, 1, 4)).reshape(dmod, dmod)

    grouped = types.reshape(CHIPS, 2, tok)
    entity_own = lax.dynamic_index_in_dim(grouped, core, 1, keepdims=False).astype(f32)[:, :, None]
    q, kv = whole_call(
        project_kernel,
        [where],
        [*pieces, weight, bias, entity_own],
        [shaped((CHIPS, tok, 2 * group), bf16), shaped((CHIPS, tok, 2 * group), bf16)],
        flops=2 * CHIPS * tok * dmod * 6 * group,
        nbytes=8 << 20,
    )
    kv_other = swapped(kv, 1)

    seg_col = seg[:, None]
    ent_col = types.astype(f32)[:, None]
    seg_shards = seg.reshape(CHIPS, 2, tok)
    seg_row = lax.dynamic_index_in_dim(seg_shards, core, 1, keepdims=False)
    starts = jnp.sum(seg[None, :] < seg_row[:, :1], axis=1)
    ends = jnp.sum(seg[None, :] <= seg_row[:, -1:], axis=1)
    first = (starts // KEY_BLOCK).astype(jnp.int32)
    last = ((ends + KEY_BLOCK - 1) // KEY_BLOCK).astype(jnp.int32)
    seg_row = seg_row[:, None, :]
    context, turned, lse = whole_call(
        attend_kernel,
        [where, first, last],
        [q, kv, kv_other, seg_col, seg_row, ent_col],
        [
            shaped((CHIPS, tok, group), bf16),
            shaped((CHIPS, group, tok), f32),
            shaped((CHIPS, 3, 1, tok), f32),
        ],
        [pltpu.VMEM((3, length, 2 * HD), bf16), pltpu.VMEM((3, HD, length), bf16)],
        flops=4 * CHIPS * tok * length * group,
        nbytes=8 << 20,
        exps=CHIPS * tok * length * 3 // 2,
    )
    same_core = [[2 * i + k for i in range(CHIPS)] for k in range(2)]

    def exchanged(value):
        return lax.all_to_all(
            value, "ctx", split_axis=0, concat_axis=0, tiled=True, axis_index_groups=same_core
        )

    context = jnp.transpose(exchanged(context), (1, 0, 2)).reshape(tok, dmod)

    branch = matmul(context, full_output) + shift_output
    first_norm, pull_one = jax.vjp(layer_norm, inputs.astype(f32) + branch, gain_one[0], shift_one[0])
    first_low = first_norm.astype(bf16)
    inner = matmul(first_low, full_inner) + shift_inner
    activated, pull_gelu = jax.vjp(gelu_exact, inner)
    hidden = activated.astype(bf16)
    ffn = matmul(hidden, full_outer) + shift_outer
    result, pull_two = jax.vjp(layer_norm, first_norm + ffn, gain_two[0], shift_two[0])
    grad_sum_two, grad_gain_two, grad_shift_two = pull_two(cotangent[0].astype(f32))
    grad_ffn = grad_sum_two.astype(bf16)
    grad_outer = left_product(hidden, grad_ffn)
    grad_inner = pull_gelu(right_product(grad_ffn, full_outer))[0].astype(bf16)
    grad_inner_full = left_product(first_low, grad_inner)
    grad_first = grad_sum_two + right_product(grad_inner, full_inner)
    grad_sum_one, grad_gain_one, grad_shift_one = pull_one(grad_first)
    grad_branch = grad_sum_one.astype(bf16)
    grad_output = left_product(context, grad_branch)
    grad_context = right_product(grad_branch, full_output).astype(bf16)
    grad_context = jnp.transpose(grad_context.reshape(tok, CHIPS, group), (1, 0, 2))
    grad_context = exchanged(grad_context)

    grads = jnp.concatenate(
        [
            jnp.transpose(
                grad_inner_full.astype(bf16).reshape(parts, rows, CHIPS, 2, ff_slot), (2, 3, 0, 1, 4)
            ),
            jnp.transpose(
                grad_outer.astype(bf16).reshape(parts, CHIPS, 2, half, 2, ff_slot), (1, 2, 0, 4, 3, 5)
            ).reshape(CHIPS, 2, parts, rows, ff_slot),
            jnp.transpose(
                grad_output.astype(bf16).reshape(parts, CHIPS, rows // CHIPS, 2, ff_slot), (1, 3, 0, 2, 4)
            ),
        ],
        axis=3,
    )
    grads = jnp.take(grads, order, axis=0)
    kept = lax.dynamic_index_in_dim(grads, core, 1, keepdims=False)
    sent = lax.dynamic_index_in_dim(grads, 1 - core, 1, keepdims=False)
    kept = kept.astype(f32) + swapped(sent, 1).astype(f32)

    def chips_summed(value):
        middle = value.shape[1] // 2
        low = value.astype(bf16)
        from_x = swapped(low[3, :middle], 2).astype(f32)
        from_y = swapped(low[3, middle:], 4).astype(f32)
        to_x = jnp.concatenate([value[1, :middle], value[1, middle:] + from_y], axis=0)
        to_y = jnp.concatenate([value[2, :middle] + from_x, value[2, middle:]], axis=0)
        return value[0] + swapped(to_x.astype(bf16), 2).astype(f32) + swapped(to_y.astype(bf16), 4).astype(f32)

    summed = chips_summed(kept).astype(bf16)
    summed = lax.psum_scatter(summed, "wa", scatter_dimension=0, tiled=True)[0]

    def plane_gathered(value):
        stacked = jnp.stack(chip_pieces(value))
        others = swapped(stacked, 1)
        both = jnp.where(core == 0, jnp.stack([stacked, others], 1), jnp.stack([others, stacked], 1))
        return jnp.take(both, order, axis=0)

    shared = plane_gathered(summed).astype(f32)
    out_inner = jnp.transpose(shared[:, :, :rows], (2, 0, 1, 3)).reshape(rows, hidden_all)
    out_outer = jnp.transpose(
        shared[:, :, rows : 2 * rows].reshape(CHIPS, 2, 2, half, ff_slot), (0, 1, 3, 2, 4)
    ).reshape(outer_weight.shape)
    out_output = jnp.transpose(shared[:, :, 2 * rows :], (0, 2, 1, 3)).reshape(rows, dmod)

    dq, dkv, dkv_other = whole_call(
        attend_back_kernel,
        [where, first, last],
        [q, kv, kv_other, seg_col, seg_row, ent_col, entity_own, turned, lse, grad_context],
        [
            shaped((CHIPS, tok, 4 * group), bf16),
            shaped((CHIPS, tok, 2 * group), bf16),
            shaped((CHIPS, tok, 2 * group), bf16),
        ],
        [
            pltpu.VMEM((3, length, 2 * HD), bf16),
            pltpu.VMEM((3, 2 * HD, length), bf16),
            pltpu.VMEM((3, length, 2 * HD), bf16),
            pltpu.VMEM((3, length, 2 * HD), f32),
            pltpu.VMEM((3, length, 2 * HD), f32),
        ],
        flops=10 * CHIPS * tok * length * group,
        nbytes=16 << 20,
        exps=CHIPS * tok * length * 3 // 2,
    )
    dkv = (dkv.astype(f32) + swapped(dkv_other, 1).astype(f32)).astype(bf16)
    dq = dq.reshape(CHIPS * tok, 4 * group)
    dkv = dkv.reshape(CHIPS * tok, 2 * group)
    partial = right_product(dq, weight[:, : 4 * group]) + right_product(dkv, weight[:, 4 * group :])
    input_grads = grad_sum_one + chips_summed(partial.reshape(CHIPS, tok, dmod))

    all_tokens = jnp.concatenate(pieces, axis=0)
    head_grads = jnp.concatenate([left_product(all_tokens, dq), left_product(all_tokens, dkv)], axis=1)
    head_grads = head_grads.reshape(parts, 2, half, 6 * group)
    kept = lax.dynamic_index_in_dim(head_grads, core, 1, keepdims=False)
    sent = lax.dynamic_index_in_dim(head_grads, 1 - core, 1, keepdims=False).astype(bf16)
    kept = (kept + swapped(sent, 1).astype(f32)).astype(bf16)
    kept = lax.psum_scatter(kept, "wa", scatter_dimension=0, tiled=True)[0]
    shared = plane_gathered(kept).astype(f32)
    shared = jnp.transpose(shared, (1, 2, 0, 3)).reshape(rows, CHIPS, 6 * group)
    for_q = shared[:, :, : 4 * group].reshape(rows, CHIPS, 3, 4, HD)
    for_kv = shared[:, :, 4 * group :].reshape(rows, CHIPS, 3, 2, HD)
    out_q = [for_q[:, :, :, k].reshape(rows, dmod) for k in range(4)]
    out_kv = [for_kv[:, :, :, k].reshape(rows, dmod) for k in range(2)]

    head_sums = jnp.concatenate([column_sums(dq), column_sums(dkv)])
    head_sums = jnp.where(jnp.arange(CHIPS)[:, None] == chip, head_sums[None], 0.0)
    head_sums = lax.psum(head_sums, ("ctx", "wa"))
    head_sums = lax.dynamic_index_in_dim(head_sums, wa, 0, keepdims=False)
    sum_q = head_sums[: 4 * group].reshape(3, 4, HD)
    sum_kv = head_sums[4 * group :].reshape(3, 2, HD)
    small = jnp.stack(
        [
            column_sums(grad_branch),
            grad_gain_one,
            grad_shift_one,
            column_sums(grad_ffn),
            grad_gain_two,
            grad_shift_two,
        ]
    )
    small = jnp.concatenate([small, column_sums(grad_inner).reshape(parts, dmod)])
    small = lax.psum(small, ("ctx", "wa"))
    mine_small = lax.dynamic_slice(small, (0, wa * rows), (6, rows))
    out_inner_bias = lax.dynamic_index_in_dim(small[6:], wa, 0, keepdims=False)

    return (
        result.astype(bf16)[None],
        input_grads[None],
        *out_q,
        *(sum_q[:, k].reshape(rows) for k in range(4)),
        *out_kv,
        sum_kv[:, 1].reshape(rows),
        out_output,
        mine_small[0],
        mine_small[1],
        mine_small[2],
        out_inner,
        out_inner_bias,
        out_outer,
        mine_small[3],
        mine_small[4],
        mine_small[5],
    )


def solution(mesh):
    in_specs = (
        P("wa", "ctx", None),
        P("wa", "ctx", None),
        P("wa", "ctx"),
        P("wa", "ctx"),
        P("wa", None),
        P("wa", None),
        P("wa", None),
        P("wa", None),
        P("wa"),
        P("wa"),
        P("wa"),
        P("wa"),
        P("wa", None),
        P("wa", None),
        P("wa"),
        P("wa", None),
        P("wa"),
        P("wa"),
        P("wa"),
        P("wa", None),
        P("wa"),
        P("wa", None),
        P("wa"),
        P("wa"),
        P("wa"),
    )
    out_specs = (
        P("wa", "ctx", None),
        P("wa", "ctx", None),
        P("wa", None),
        P("wa", None),
        P("wa", None),
        P("wa", None),
        P("wa"),
        P("wa"),
        P("wa"),
        P("wa"),
        P("wa", None),
        P("wa", None),
        P("wa"),
        P("wa", None),
        P("wa"),
        P("wa"),
        P("wa"),
        P("wa", None),
        P("wa"),
        P("wa", None),
        P("wa"),
        P("wa"),
        P("wa"),
    )
    body = grouped_device if mesh.shape["ctx"] == 2 * CHIPS else windowed_device
    return jax.shard_map(
        body, mesh=mesh, in_specs=in_specs, out_specs=out_specs, check_vma=False
    )
```

```python
import jax
import jax.numpy as jnp
from jax import lax
from jax.experimental import pallas as pl
from jax.experimental.pallas import tpu as pltpu
from jax.sharding import PartitionSpec as P

HD = 64


EPSILON = 1e-12
MASKED = -1e30


def as_sent(shard):
    return jax.tree.map(lambda a: a.astype(jnp.bfloat16) if a.dtype == jnp.float32 else a, shard)


def passed_along(value, axis, steps):
    count = lax.axis_size(axis)
    leading, last = (max(0, -steps), min(count, count - steps))
    return lax.ppermute(value, axis, [(source, source + steps) for source in range(leading, last)])


def layer_norm(values, gain, shift):
    center = values - jnp.mean(values, axis=-1, keepdims=True)
    spread = jnp.mean(center * center, axis=-1, keepdims=True)
    return center * lax.rsqrt(spread + EPSILON) * gain + shift


def gelu_exact(values):
    return jax.nn.gelu(values, approximate=False)


def matmul(left, right):
    return jnp.dot(left, right, preferred_element_type=jnp.float32)


def left_product(left, right):
    return lax.dot_general(
        left, right, (((0,), (0,)), ((), ())), preferred_element_type=jnp.float32
    )


def right_product(left, right):
    return lax.dot_general(
        left, right, (((1,), (1,)), ((), ())), preferred_element_type=jnp.float32
    )


def column_sums(values):
    return jnp.sum(values.astype(jnp.float32), axis=0)


def columns(values, start):
    return lax.dynamic_slice_in_dim(values, start, HD, 1)


def head_scores(query_word, query_entity, keys_head, key_entity, allowed, scale):
    word_scores = right_product(query_word, keys_head)
    entity_scores = right_product(query_entity, keys_head)
    raw = jnp.where(key_entity[None, :], entity_scores, word_scores) * scale
    return jnp.where(allowed, raw, MASKED)


def merge_heads(stacked):
    return jnp.transpose(stacked, (1, 0, 2)).reshape(
        stacked.shape[1], stacked.shape[0] * stacked.shape[2]
    )


def windowed_device(
    tokens,
    cotangent,
    segment_ids,
    token_types,
    query_wordword,
    query_wordentity,
    query_entityword,
    query_entityentity,
    bias_wordword,
    bias_wordentity,
    bias_entityword,
    bias_entityentity,
    key_weight,
    value_weight,
    value_bias,
    output_weight,
    output_bias,
    first_gain,
    first_bias,
    inner_weight,
    inner_bias,
    outer_weight,
    outer_bias,
    second_gain,
    second_bias,
):
    attention = (
        lax.all_gather(query_wordword, "wa", axis=0, tiled=True),
        lax.all_gather(query_wordentity, "wa", axis=0, tiled=True),
        lax.all_gather(query_entityword, "wa", axis=0, tiled=True),
        lax.all_gather(query_entityentity, "wa", axis=0, tiled=True),
        lax.all_gather(bias_wordword, "wa", axis=0, tiled=True),
        lax.all_gather(bias_wordentity, "wa", axis=0, tiled=True),
        lax.all_gather(bias_entityword, "wa", axis=0, tiled=True),
        lax.all_gather(bias_entityentity, "wa", axis=0, tiled=True),
        lax.all_gather(key_weight, "wa", axis=0, tiled=True),
        lax.all_gather(value_weight, "wa", axis=0, tiled=True),
        lax.all_gather(value_bias, "wa", axis=0, tiled=True),
        lax.all_gather(output_weight, "wa", axis=0, tiled=True),
        lax.all_gather(output_bias, "wa", axis=0, tiled=True),
        lax.all_gather(first_gain, "wa", axis=0, tiled=True),
        lax.all_gather(first_bias, "wa", axis=0, tiled=True),
    )
    (
        full_ww,
        full_we,
        full_ew,
        full_ee,
        shift_ww,
        shift_we,
        shift_ew,
        shift_ee,
        full_key,
        full_value,
        shift_value,
        full_output,
        shift_output,
        gain_one,
        shift_one,
    ) = attention
    feedforward = (
        lax.all_gather(inner_weight, "wa", axis=0, tiled=True),
        lax.all_gather(inner_bias, "wa", axis=0, tiled=True),
        lax.all_gather(outer_weight, "wa", axis=0, tiled=True),
        lax.all_gather(outer_bias, "wa", axis=0, tiled=True),
        lax.all_gather(second_gain, "wa", axis=0, tiled=True),
        lax.all_gather(second_bias, "wa", axis=0, tiled=True),
    )
    full_inner, shift_inner, full_outer, shift_outer, gain_two, shift_two = feedforward
    inputs = tokens[0]
    seg = segment_ids[0]
    types = token_types[0]
    tok = inputs.shape[0]
    dmod = inputs.shape[1]
    heads = dmod // HD
    scale = HD ** (-0.5)
    length = tok * lax.axis_size("ctx")
    doc_max = min(2048, 4 * tok, length // 2)
    reach = (doc_max - 2) // tok + 1
    entity = (types == 1)[:, None]
    proj_ww = matmul(inputs, full_ww) + shift_ww
    proj_we = matmul(inputs, full_we) + shift_we
    proj_ew = matmul(inputs, full_ew) + shift_ew
    proj_ee = matmul(inputs, full_ee) + shift_ee
    query_word = jnp.where(entity, proj_ew, proj_ww).astype(jnp.bfloat16)
    query_entity = jnp.where(entity, proj_ee, proj_we).astype(jnp.bfloat16)
    keys = matmul(inputs, full_key).astype(jnp.bfloat16)
    values = (matmul(inputs, full_value) + shift_value).astype(jnp.bfloat16)
    own_kv = jnp.concatenate([keys, values], axis=1)
    own_seg = seg + 1
    tags = own_seg * 2 + types

    def pass_left(packet, unused):
        moved = jax.tree.map(
            lambda part, own: part.astype(own.dtype),
            passed_along(as_sent(packet), "ctx", 1),
            packet,
        )
        return (moved, moved)

    def pass_right(packet, unused):
        moved = jax.tree.map(
            lambda part, own: part.astype(own.dtype),
            passed_along(as_sent(packet), "ctx", -1),
            packet,
        )
        return (moved, moved)

    _, (left_kv, left_tags) = lax.scan(pass_left, (own_kv, tags), None, length=reach)
    _, (right_kv, right_tags) = lax.scan(pass_right, (own_kv, tags), None, length=reach)
    window = jnp.concatenate(
        [jnp.flip(left_kv, 0).reshape(-1, 2 * dmod), own_kv, right_kv.reshape(-1, 2 * dmod)], axis=0
    )
    window_tags = jnp.concatenate(
        [jnp.flip(left_tags, 0).reshape(-1), tags, right_tags.reshape(-1)], axis=0
    )
    key_entity = window_tags % 2 == 1
    allowed = own_seg[:, None] == (window_tags // 2)[None, :]

    def head_forward(index):
        start = index * HD
        scores = head_scores(
            columns(query_word, start),
            columns(query_entity, start),
            columns(window, start),
            key_entity,
            allowed,
            scale,
        )
        top = jnp.max(scores, axis=1, keepdims=True)
        expo = jnp.exp(scores - top)
        total = jnp.sum(expo, axis=1, keepdims=True)
        probs = (expo / total).astype(jnp.bfloat16)
        return (matmul(probs, columns(window, dmod + start)), (top + jnp.log(total))[:, 0])

    head_context, lse = lax.map(head_forward, jnp.arange(heads))
    context = merge_heads(head_context).astype(jnp.bfloat16)
    branch = matmul(context, full_output) + shift_output
    first, pull_one = jax.vjp(
        layer_norm,
        inputs.astype(jnp.float32) + branch,
        gain_one.astype(jnp.float32),
        shift_one.astype(jnp.float32),
    )
    first_low = first.astype(jnp.bfloat16)
    inner = matmul(first_low, full_inner) + shift_inner
    activated, pull_gelu = jax.vjp(gelu_exact, inner)
    hidden = activated.astype(jnp.bfloat16)
    ffn = matmul(hidden, full_outer) + shift_outer
    result, pull_two = jax.vjp(
        layer_norm, first + ffn, gain_two.astype(jnp.float32), shift_two.astype(jnp.float32)
    )
    grad_sum_two, grad_gain_two, grad_shift_two = pull_two(cotangent[0].astype(jnp.float32))
    grad_ffn = grad_sum_two.astype(jnp.bfloat16)
    grad_outer = left_product(hidden, grad_ffn)
    grad_outer_shift = column_sums(grad_ffn)
    grad_inner = pull_gelu(right_product(grad_ffn, full_outer))[0].astype(jnp.bfloat16)
    grad_inner_full = left_product(first_low, grad_inner)
    grad_inner_shift = column_sums(grad_inner)
    grad_first = grad_sum_two + right_product(grad_inner, full_inner)
    grad_sum_one, grad_gain_one, grad_shift_one = pull_one(grad_first)
    grad_branch = grad_sum_one.astype(jnp.bfloat16)
    grad_output = left_product(context, grad_branch)
    grad_output_shift = column_sums(grad_branch)
    grad_context = right_product(grad_branch, full_output).astype(jnp.bfloat16)

    def head_backward(index):
        start = index * HD
        word_head = columns(query_word, start)
        entity_head = columns(query_entity, start)
        keys_head = columns(window, start)
        values_head = columns(window, dmod + start)
        context_head = columns(grad_context, start)
        scores = head_scores(word_head, entity_head, keys_head, key_entity, allowed, scale)
        probs = jnp.exp(scores - lse[index][:, None])
        grad_probs = right_product(context_head, values_head)
        delta = jnp.sum(probs * grad_probs, axis=1)
        grad_scores = (probs * (grad_probs - delta[:, None])).astype(jnp.bfloat16)
        zero = jnp.zeros_like(grad_scores)
        grad_word = jnp.where(key_entity[None, :], zero, grad_scores)
        grad_entity = jnp.where(key_entity[None, :], grad_scores, zero)
        grad_qword = matmul(grad_word, keys_head) * scale
        grad_qentity = matmul(grad_entity, keys_head) * scale
        grad_keys = (
            left_product(grad_word, word_head) + left_product(grad_entity, entity_head)
        ) * scale
        grad_values = left_product(probs.astype(jnp.bfloat16), context_head)
        return (grad_qword, grad_qentity, delta, grad_keys, grad_values)

    grad_qword, grad_qentity, delta, window_keys, window_values = lax.map(
        lambda index: head_backward(index), jnp.arange(heads)
    )
    parts_keys = merge_heads(window_keys).reshape(2 * reach + 1, tok, dmod)
    parts_values = merge_heads(window_values).reshape(2 * reach + 1, tok, dmod)

    def back_left(total, piece):
        return (
            (
                passed_along((total[0] + piece[0]).astype(jnp.bfloat16), "ctx", -1).astype(
                    jnp.float32
                ),
                passed_along((total[1] + piece[1]).astype(jnp.bfloat16), "ctx", -1).astype(
                    jnp.float32
                ),
            ),
            None,
        )

    def back_right(total, piece):
        return (
            (
                passed_along((total[0] + piece[0]).astype(jnp.bfloat16), "ctx", 1).astype(
                    jnp.float32
                ),
                passed_along((total[1] + piece[1]).astype(jnp.bfloat16), "ctx", 1).astype(
                    jnp.float32
                ),
            ),
            None,
        )

    empty = jnp.zeros((tok, dmod), jnp.float32)
    from_above, _ = lax.scan(back_left, (empty, empty), (parts_keys[:reach], parts_values[:reach]))
    from_below, _ = lax.scan(
        back_right,
        (empty, empty),
        (jnp.flip(parts_keys[reach + 1 :], 0), jnp.flip(parts_values[reach + 1 :], 0)),
    )
    own_keys = parts_keys[reach] + from_above[0] + from_below[0]
    own_values = parts_values[reach] + from_above[1] + from_below[1]
    grad_keys = own_keys.astype(jnp.bfloat16)
    grad_values = own_values.astype(jnp.bfloat16)
    grad_qword = merge_heads(grad_qword).astype(jnp.bfloat16)
    grad_qentity = merge_heads(grad_qentity).astype(jnp.bfloat16)
    zeros = jnp.zeros_like(grad_qword)
    grad_pww = jnp.where(entity, zeros, grad_qword)
    grad_pew = jnp.where(entity, grad_qword, zeros)
    grad_pwe = jnp.where(entity, zeros, grad_qentity)
    grad_pee = jnp.where(entity, grad_qentity, zeros)
    input_grads = grad_sum_one + right_product(grad_pww, full_ww) + right_product(grad_pwe, full_we)
    input_grads = input_grads + right_product(grad_pew, full_ew) + right_product(grad_pee, full_ee)
    input_grads = (
        input_grads + right_product(grad_keys, full_key) + right_product(grad_values, full_value)
    )
    local_grads = (
        left_product(inputs, grad_pww),
        left_product(inputs, grad_pwe),
        left_product(inputs, grad_pew),
        left_product(inputs, grad_pee),
        column_sums(grad_pww),
        column_sums(grad_pwe),
        column_sums(grad_pew),
        column_sums(grad_pee),
        left_product(inputs, grad_keys),
        left_product(inputs, grad_values),
        column_sums(grad_values),
        grad_output,
        grad_output_shift,
        grad_gain_one,
        grad_shift_one,
        grad_inner_full,
        grad_inner_shift,
        grad_outer,
        grad_outer_shift,
        grad_gain_two,
        grad_shift_two,
    )
    shards = (
        lax.psum_scatter(
            local_grads[0].astype(jnp.bfloat16), "wa", scatter_dimension=0, tiled=True
        ).astype(jnp.float32),
        lax.psum_scatter(
            local_grads[1].astype(jnp.bfloat16), "wa", scatter_dimension=0, tiled=True
        ).astype(jnp.float32),
        lax.psum_scatter(
            local_grads[2].astype(jnp.bfloat16), "wa", scatter_dimension=0, tiled=True
        ).astype(jnp.float32),
        lax.psum_scatter(
            local_grads[3].astype(jnp.bfloat16), "wa", scatter_dimension=0, tiled=True
        ).astype(jnp.float32),
        lax.psum_scatter(
            local_grads[4].astype(jnp.bfloat16), "wa", scatter_dimension=0, tiled=True
        ).astype(jnp.float32),
        lax.psum_scatter(
            local_grads[5].astype(jnp.bfloat16), "wa", scatter_dimension=0, tiled=True
        ).astype(jnp.float32),
        lax.psum_scatter(
            local_grads[6].astype(jnp.bfloat16), "wa", scatter_dimension=0, tiled=True
        ).astype(jnp.float32),
        lax.psum_scatter(
            local_grads[7].astype(jnp.bfloat16), "wa", scatter_dimension=0, tiled=True
        ).astype(jnp.float32),
        lax.psum_scatter(
            local_grads[8].astype(jnp.bfloat16), "wa", scatter_dimension=0, tiled=True
        ).astype(jnp.float32),
        lax.psum_scatter(
            local_grads[9].astype(jnp.bfloat16), "wa", scatter_dimension=0, tiled=True
        ).astype(jnp.float32),
        lax.psum_scatter(
            local_grads[10].astype(jnp.bfloat16), "wa", scatter_dimension=0, tiled=True
        ).astype(jnp.float32),
        lax.psum_scatter(
            local_grads[11].astype(jnp.bfloat16), "wa", scatter_dimension=0, tiled=True
        ).astype(jnp.float32),
        lax.psum_scatter(
            local_grads[12].astype(jnp.bfloat16), "wa", scatter_dimension=0, tiled=True
        ).astype(jnp.float32),
        lax.psum_scatter(
            local_grads[13].astype(jnp.bfloat16), "wa", scatter_dimension=0, tiled=True
        ).astype(jnp.float32),
        lax.psum_scatter(
            local_grads[14].astype(jnp.bfloat16), "wa", scatter_dimension=0, tiled=True
        ).astype(jnp.float32),
        lax.psum_scatter(
            local_grads[15].astype(jnp.bfloat16), "wa", scatter_dimension=0, tiled=True
        ).astype(jnp.float32),
        lax.psum_scatter(
            local_grads[16].astype(jnp.bfloat16), "wa", scatter_dimension=0, tiled=True
        ).astype(jnp.float32),
        lax.psum_scatter(
            local_grads[17].astype(jnp.bfloat16), "wa", scatter_dimension=0, tiled=True
        ).astype(jnp.float32),
        lax.psum_scatter(
            local_grads[18].astype(jnp.bfloat16), "wa", scatter_dimension=0, tiled=True
        ).astype(jnp.float32),
        lax.psum_scatter(
            local_grads[19].astype(jnp.bfloat16), "wa", scatter_dimension=0, tiled=True
        ).astype(jnp.float32),
        lax.psum_scatter(
            local_grads[20].astype(jnp.bfloat16), "wa", scatter_dimension=0, tiled=True
        ).astype(jnp.float32),
    )
    totals = lax.psum(
        (
            shards[0],
            shards[1],
            shards[2],
            shards[3],
            shards[4],
            shards[5],
            shards[6],
            shards[7],
            shards[8],
            shards[9],
            shards[10],
            shards[11],
            shards[12],
            shards[13],
            shards[14],
            shards[15],
            shards[16],
            shards[17],
            shards[18],
            shards[19],
            shards[20],
        ),
        "ctx",
    )
    return (
        result.astype(jnp.bfloat16)[None],
        input_grads[None],
        totals[0],
        totals[1],
        totals[2],
        totals[3],
        totals[4],
        totals[5],
        totals[6],
        totals[7],
        totals[8],
        totals[9],
        totals[10],
        totals[11],
        totals[12],
        totals[13],
        totals[14],
        totals[15],
        totals[16],
        totals[17],
        totals[18],
        totals[19],
        totals[20],
    )


CHIPS = 4
KEY_BLOCK = 256
NEGATIVE = -1e30
TAG_ROWS = 16
TILE = 128


def lanes_product(left, right):
    return lax.dot_general(
        left, right, (((1,), (1,)), ((), ())), preferred_element_type=jnp.float32
    )


def rows_product(left, right):
    return lax.dot_general(
        left, right, (((0,), (0,)), ((), ())), preferred_element_type=jnp.float32
    )


def plain_product(left, right):
    return jnp.dot(left, right, preferred_element_type=jnp.float32)


def swapped(value, step):
    count = lax.axis_size("ctx")
    return lax.ppermute(value, "ctx", [(i, i ^ step) for i in range(count)])


def turned(value, step):
    count = lax.axis_size("wa")
    return lax.ppermute(value, "wa", [(i, (i + step) % count) for i in range(count)])


def as_column(row):
    return jnp.broadcast_to(row, (TILE, row.shape[1])).T


def segment_of(tag):
    return jnp.floor(tag * 0.5)


def project_kernel(place, t0, t1, t2, t3a, t3b, mine, theirs, weight, tokens, q_ref, kv_ref):
    parts, rows = mine.shape[0], mine.shape[1] - TAG_ROWS
    tok = q_ref.shape[1]
    chip, core, wa = place[0], place[1], place[2]
    cut = t3a.shape[0]
    tokens[0] = t0[...]
    tokens[1] = t1[...]
    tokens[2] = t2[...]
    tokens[3, :cut] = t3a[...]
    tokens[3, cut:] = t3b[...]
    for z in range(parts):
        k = lax.rem(wa - z + parts, parts)
        for source, side in ((mine, core), (theirs, 1 - core)):
            weight[pl.ds(pl.multiple_of(2 * rows * z + rows * side, 32), rows), :] = source[k, :rows]
    k = lax.rem(wa - chip + parts, parts)
    bias = mine[k, rows : rows + TAG_ROWS].astype(jnp.float32)[:1]
    wide = 2 * HD

    def piece(m, unused):
        to = jnp.bitwise_xor(chip, m)
        tags = tokens[m, tok : tok + TAG_ROWS].astype(jnp.float32)[:1, :tok]
        flag = as_column(tags - 2.0 * segment_of(tags)) == 1.0
        text = tokens[m, :tok]
        for h in range(3):
            at = 2 * wide * h
            both = plain_product(text, weight[:, at : at + 2 * wide]) + bias[:, at : at + 2 * wide]
            q = jnp.where(flag, both[:, wide:], both[:, :wide]).astype(jnp.bfloat16)
            q_ref[to, :, wide * h : wide * (h + 1)] = q * jnp.bfloat16(HD**-0.5)
        kv = plain_product(text, weight[:, 6 * wide :]) + bias[:, 6 * wide :]
        kv_ref[to, :tok] = kv.astype(jnp.bfloat16)
        kv_ref[to, tok:] = jnp.broadcast_to(tags, (TAG_ROWS, tok)).astype(jnp.bfloat16)
        return 0

    lax.fori_loop(0, CHIPS, piece, 0)


def masked_keys(kv, flag):
    wide = kv.astype(jnp.float32)
    low = lax.broadcasted_iota(jnp.int32, kv.shape, 1) < HD
    both = jnp.where(low, wide, pltpu.roll(wide, HD, 1))
    return jnp.where(low == flag, 0.0, both)


def attend_kernel(place, q_ref, own, other, out, turned_out, lse, bounds, keys, values, seg_col, seg_row, acc):
    tok = q_ref.shape[1]
    core = place[1]

    def prepare(j, unused):
        for source, side in ((own, core), (other, 1 - core)):
            shard = 2 * j + side
            at = pl.ds(pl.multiple_of(shard * tok, TILE), tok)
            tags = source[j, tok : tok + TAG_ROWS].astype(jnp.float32)[:1]
            seg_row[shard] = jnp.broadcast_to(segment_of(tags), (8, tok))
            column = as_column(tags)
            segment = segment_of(column)
            seg_col[at, :] = segment
            flag = column - 2.0 * segment == 1.0
            for h in range(3):
                kv = source[j, :tok, 2 * HD * h : 2 * HD * (h + 1)]
                keys[h, at, :] = masked_keys(kv, flag).astype(jnp.bfloat16)
                values[h, :, at] = kv.astype(jnp.float32).T[HD:].astype(jnp.bfloat16)
        return 0

    lax.fori_loop(0, CHIPS, prepare, 0)

    def queries(j, unused):
        seg = seg_row[2 * j + core][:1]
        everyone = seg_row[...][:, 0, :]
        before = jnp.sum((everyone < jnp.min(seg)).astype(jnp.float32)).astype(jnp.int32)
        through = jnp.sum((everyone <= jnp.max(seg)).astype(jnp.float32)).astype(jnp.int32)
        first = before // KEY_BLOCK
        last = (through + KEY_BLOCK - 1) // KEY_BLOCK
        bounds[0, j] = first
        bounds[1, j] = last
        acc[...] = jnp.zeros_like(acc)

        def step(t, carry):
            at = pl.ds(pl.multiple_of(t * KEY_BLOCK, KEY_BLOCK), KEY_BLOCK)
            column = seg_col[at, :]
            same = jnp.concatenate([column] * (tok // TILE), axis=1) == seg
            after = []
            for h in range(3):
                top, total = carry[2 * h], carry[2 * h + 1]
                scores = lanes_product(keys[h, at, :], q_ref[j, :, 2 * HD * h : 2 * HD * (h + 1)])
                scores = jnp.where(same, scores, NEGATIVE)
                peak = jnp.maximum(top, jnp.max(scores, axis=0, keepdims=True))
                fade = jnp.exp(top - peak)
                expo = jnp.exp(scores - peak)
                total = total * fade + jnp.sum(expo, axis=0, keepdims=True)
                acc[h] = acc[h] * fade + plain_product(values[h, :, at], expo.astype(jnp.bfloat16))
                after += [peak, total]
            return tuple(after)

        start = (jnp.full((1, tok), NEGATIVE, jnp.float32), jnp.zeros((1, tok), jnp.float32)) * 3
        done = lax.fori_loop(first, last, step, start)
        for h in range(3):
            turned_out[j, HD * h : HD * (h + 1), :] = acc[h] / done[2 * h + 1]
            lse[j, h] = done[2 * h] + jnp.log(done[2 * h + 1])
        out[j] = turned_out[j].T.astype(jnp.bfloat16)
        return 0

    lax.fori_loop(0, CHIPS, queries, 0)


def attend_back_kernel(
    place,
    bounds,
    q_ref,
    own,
    other,
    turned_out,
    lse,
    grad,
    dq_ref,
    dkv_own,
    dkv_other,
    keys,
    turned_keys,
    values,
    grad_keys,
    grad_values,
    seg_col,
    seg_row,
    acc,
):
    tok = q_ref.shape[1]
    chip, core = place[0], place[1]
    wide = 2 * HD

    def prepare(j, unused):
        for source, side in ((own, core), (other, 1 - core)):
            shard = 2 * j + side
            at = pl.ds(pl.multiple_of(shard * tok, TILE), tok)
            tags = source[j, tok : tok + TAG_ROWS].astype(jnp.float32)[:1]
            seg_row[shard] = jnp.broadcast_to(tags, (8, tok))
            column = as_column(tags)
            segment = segment_of(column)
            seg_col[at, :] = segment
            flag = column - 2.0 * segment == 1.0
            for h in range(3):
                kv = source[j, :tok, wide * h : wide * (h + 1)]
                key = masked_keys(kv, flag)
                keys[h, at, :] = key.astype(jnp.bfloat16)
                turned_keys[h, :, at] = key.T.astype(jnp.bfloat16)
                values[h, at, :] = kv
                grad_keys[h, at, :] = jnp.zeros((tok, wide), jnp.float32)
                grad_values[h, at, :] = jnp.zeros((tok, wide), jnp.float32)
        return 0

    lax.fori_loop(0, CHIPS, prepare, 0)

    def queries(j, unused):
        tags = seg_row[2 * j + core][:1]
        seg = segment_of(tags)
        slot = jnp.bitwise_xor(chip, j)
        flag = as_column(tags - 2.0 * seg) == 1.0
        turned_grad = grad[j].astype(jnp.float32).T
        deltas, shifts, padded = [], [], []
        for h in range(3):
            rows = slice(HD * h, HD * (h + 1))
            deltas.append(jnp.sum(turned_grad[rows] * turned_out[j, rows, :], axis=0, keepdims=True))
            shifts.append(lse[j, h])
            head = grad[j, :, rows]
            padded.append(jnp.concatenate([jnp.zeros_like(head), head], axis=1))
        acc[...] = jnp.zeros_like(acc)

        def step(t, carry):
            at = pl.ds(pl.multiple_of(t * KEY_BLOCK, KEY_BLOCK), KEY_BLOCK)
            column = seg_col[at, :]
            same = jnp.concatenate([column] * (tok // TILE), axis=1) == seg
            for h in range(3):
                q = q_ref[j, :, wide * h : wide * (h + 1)]
                scores = lanes_product(keys[h, at, :], q)
                probs = jnp.where(same, jnp.exp(scores - shifts[h]), 0.0)
                grad_probs = lanes_product(values[h, at, :], padded[h])
                grad_scores = (probs * (grad_probs - deltas[h])).astype(jnp.bfloat16)
                grad_values[h, at, :] += plain_product(probs.astype(jnp.bfloat16), padded[h])
                grad_keys[h, at, :] += plain_product(grad_scores, q)
                acc[h] += plain_product(turned_keys[h, :, at], grad_scores)
            return carry

        lax.fori_loop(bounds[0, j], bounds[1, j], step, 0)
        for h in range(3):
            dq = acc[h].T * (HD**-0.5)
            at = 2 * wide * h
            dq_ref[slot, :, at : at + wide] = jnp.where(flag, 0.0, dq).astype(jnp.bfloat16)
            dq_ref[slot, :, at + wide : at + 2 * wide] = jnp.where(flag, dq, 0.0).astype(jnp.bfloat16)
        return 0

    lax.fori_loop(0, CHIPS, queries, 0)

    def finish(j, unused):
        slot = jnp.bitwise_xor(chip, j)
        for target, side in ((dkv_own, core), (dkv_other, 1 - core)):
            shard = 2 * j + side
            at = pl.ds(pl.multiple_of(shard * tok, TILE), tok)
            tags = seg_row[shard][:1]
            flag = as_column(tags - 2.0 * segment_of(tags)) == 1.0
            for h in range(3):
                both = grad_keys[h, at, :]
                low = lax.broadcasted_iota(jnp.int32, both.shape, 1) < HD
                picked = jnp.where(flag, pltpu.roll(both, HD, 1), both)
                target[slot, :, wide * h : wide * (h + 1)] = jnp.where(
                    low, picked, grad_values[h, at, :]
                ).astype(jnp.bfloat16)
        return 0

    lax.fori_loop(0, CHIPS, finish, 0)


def normed(total, gain, shift):
    center = total - jnp.mean(total, axis=-1, keepdims=True)
    spread = jnp.mean(center * center, axis=-1, keepdims=True)
    inverse = lax.rsqrt(spread + EPSILON)
    unit = center * inverse
    return unit * gain + shift, unit, inverse


def normed_back(grad, unit, inverse, gain):
    scaled = grad * gain
    mean = jnp.mean(scaled, axis=-1, keepdims=True)
    along = jnp.mean(scaled * unit, axis=-1, keepdims=True)
    return inverse * (scaled - mean - unit * along)


def summed_rows(value):
    return jnp.sum(value, axis=0, keepdims=True)


def dense_kernel(
    place,
    context,
    text,
    cotangent,
    vectors,
    inner_bias,
    near_own,
    near_other,
    far_own,
    far_other,
    result,
    grad_sum,
    grad_context,
    kept,
    sent_far,
    sent_near,
    inner_w,
    outer_w,
    output_w,
    hidden,
    slope,
    inner_g,
    outer_g,
    output_g,
    small,
    sums,
    in_sems,
    out_sems,
):
    bf16, f32 = jnp.bfloat16, jnp.float32
    chip, core, wa = place[0], place[1], place[2]
    tok, dmod = result.shape
    ff = hidden.shape[1]
    group = dmod // CHIPS
    parts = CHIPS
    rows = dmod // parts
    half = rows // 2
    quarter = rows // CHIPS
    slot_w = ff // (2 * CHIPS)

    def fetch(m, unused):
        g = jnp.bitwise_xor(chip, m)
        for source, side, base in (
            (near_own, core, 0),
            (near_other, 1 - core, 0),
            (far_own, core, 2),
            (far_other, 1 - core, 2),
        ):
            s = 2 * g + side
            for u in range(2):
                z = lax.rem(wa - base - u + parts, parts)
                pltpu.make_async_copy(
                    source.at[m, u, pl.ds(2 * rows, quarter), :],
                    output_w.at[
                        pl.ds(pl.multiple_of(rows * z + quarter * g, 16), quarter),
                        pl.ds(pl.multiple_of(slot_w * side, TILE), slot_w),
                    ],
                    in_sems.at[0],
                ).start()
                pltpu.make_async_copy(
                    source.at[m, u, pl.ds(0, rows), :],
                    inner_w.at[
                        pl.ds(pl.multiple_of(rows * z, 16), rows),
                        pl.ds(pl.multiple_of(slot_w * s, TILE), slot_w),
                    ],
                    in_sems.at[1],
                ).start()
                for v in range(2):
                    pltpu.make_async_copy(
                        source.at[m, u, pl.ds(rows + half * v, half), :],
                        outer_w.at[
                            pl.ds(pl.multiple_of(dmod * z + half * s, 16), half),
                            pl.ds(slot_w * v, slot_w),
                        ],
                        in_sems.at[2],
                    ).start()
        return 0

    lax.fori_loop(0, CHIPS, fetch, 0)
    names = ("outb", "g1", "s1", "outerb", "g2", "s2")
    vec = {name: vectors[k : k + 1, :] for k, name in enumerate(names)}

    pltpu.make_async_copy(output_w, output_w, in_sems.at[0]).wait()
    branch = vec["outb"]
    for g in range(CHIPS):
        branch = branch + plain_product(context[g], output_w[group * g : group * (g + 1), :])
    first, unit_one, inverse_one = normed(text[:tok, :].astype(f32) + branch, vec["g1"], vec["s1"])
    low = first.astype(bf16)

    pltpu.make_async_copy(inner_w, inner_w, in_sems.at[1]).wait()
    pltpu.make_async_copy(outer_w, outer_w, in_sems.at[2]).wait()

    def forward(s, ffn):
        at = pl.ds(pl.multiple_of(slot_w * s, TILE), slot_w)
        inner = plain_product(low, inner_w[:, at]) + inner_bias[:, at]
        cdf = 0.5 + 0.5 * lax.erf(inner * (0.5**0.5))
        active = (inner * cdf).astype(bf16)
        hidden[:, at] = active
        slope[:, at] = cdf + inner * (jnp.exp(-0.5 * inner * inner) * (0.5 / jnp.pi) ** 0.5)
        return ffn + plain_product(active, outer_w[at, :])

    ffn = lax.fori_loop(0, 2 * CHIPS, forward, jnp.broadcast_to(vec["outerb"], (tok, dmod)))
    second, unit_two, inverse_two = normed(first + ffn, vec["g2"], vec["s2"])
    result[...] = second.astype(bf16)
    grad_out = cotangent[...].astype(f32)
    grad_two = normed_back(grad_out, unit_two, inverse_two, vec["g2"])
    low_two = grad_two.astype(bf16)

    sums[...] = jnp.zeros_like(sums)

    def put(row, value):
        for v in range(2):
            for z in range(parts):
                sums[z, row + v : row + v + 1, :] = value[:, slot_w * v : slot_w * (v + 1)]

    put(6, summed_rows(low_two.astype(f32)))
    put(8, summed_rows(grad_out * unit_two))
    put(10, summed_rows(grad_out))
    low_turned = low.astype(f32).T.astype(bf16)

    def backward(s, grad_first):
        at = pl.ds(pl.multiple_of(slot_w * s, TILE), slot_w)
        grad_hidden = lanes_product(low_two, outer_w[at, :])
        grad_inner = (grad_hidden * slope[:, at]).astype(bf16)
        outer_g[at, :] = rows_product(hidden[:, at], low_two).astype(bf16)
        inner_g[:, at] = plain_product(low_turned, grad_inner).astype(bf16)
        sums[s // 2, pl.ds(12 + lax.rem(s, 2), 1), :] = summed_rows(grad_inner.astype(f32))
        return grad_first + lanes_product(grad_inner, inner_w[:, at])

    grad_first = lax.fori_loop(0, 2 * CHIPS, backward, grad_two)

    def targets():
        for m in range(CHIPS):
            far = sent_far if m == CHIPS - 1 else sent_near.at[m]
            for target, side, sem in ((kept.at[m], core, 0), (far, 1 - core, 1 + (m < CHIPS - 1))):
                yield target, jnp.bitwise_xor(chip, m), side, sem

    inner_view = inner_g.reshape(parts, rows, ff)
    outer_view = outer_g.reshape(parts, dmod, dmod)
    output_view = output_g.reshape(parts, rows, dmod)
    for target, g, side, sem in targets():
        s = 2 * g + side
        pltpu.make_async_copy(
            inner_view.at[:, :, pl.ds(pl.multiple_of(slot_w * s, TILE), slot_w)],
            target.at[:, pl.ds(0, rows), :],
            out_sems.at[sem],
        ).start()
        for v in range(2):
            pltpu.make_async_copy(
                outer_view.at[:, pl.ds(pl.multiple_of(half * s, 16), half), pl.ds(slot_w * v, slot_w)],
                target.at[:, pl.ds(rows + half * v, half), :],
                out_sems.at[sem],
            ).start()

    put(2, summed_rows(grad_first * unit_one))
    put(4, summed_rows(grad_first))
    grad_one = normed_back(grad_first, unit_one, inverse_one, vec["g1"])
    grad_sum[...] = grad_one
    low_one = grad_one.astype(bf16)
    put(0, summed_rows(low_one.astype(f32)))
    small[0] = jnp.zeros_like(small[0])
    small[1] = sums[...].astype(bf16)
    for g in range(CHIPS):
        at = slice(group * g, group * (g + 1))
        output_g[at, :] = rows_product(context[g], low_one).astype(bf16)
        grad_context[g] = lanes_product(low_one, output_w[at, :]).astype(bf16)
    for target, g, side, sem in targets():
        pltpu.make_async_copy(
            output_view.at[
                :,
                pl.ds(pl.multiple_of(quarter * g, 16), quarter),
                pl.ds(pl.multiple_of(slot_w * side, TILE), slot_w),
            ],
            target.at[:, pl.ds(2 * rows, quarter), :],
            out_sems.at[sem],
        ).start()
        filled = jnp.where(2 * g + side == 0, 1, 0)
        pltpu.make_async_copy(
            small.at[filled], target.at[:, pl.ds(2 * rows + quarter, TAG_ROWS), :], out_sems.at[sem]
        ).start()
    for sem, target in enumerate((kept, sent_far, sent_near)):
        pltpu.make_async_copy(target, target, out_sems.at[sem]).wait()


def project_back_kernel(place, tokens, dq, dkv_own, dkv_other, weight, partial, kept, sent, acc, dkv):
    tok = dq.shape[1]
    core = place[1]
    wide = dq.shape[2]
    parts, rows = kept.shape[0], kept.shape[1] - TAG_ROWS
    acc[...] = jnp.zeros_like(acc)

    def piece(m, carry):
        text = tokens[m, :tok]
        both = dkv_own[m].astype(jnp.float32) + dkv_other[m].astype(jnp.float32)
        dkv[...] = both.astype(jnp.bfloat16)
        partial[m] = (
            lanes_product(dq[m], weight[:, :wide]) + lanes_product(dkv[...], weight[:, wide:])
        ).astype(jnp.bfloat16)
        text_turned = text.astype(jnp.float32).T.astype(jnp.bfloat16)
        acc[:, :wide] += plain_product(text_turned, dq[m])
        acc[:, wide:] += plain_product(text_turned, dkv[...])
        return (
            carry[0] + summed_rows(dq[m].astype(jnp.float32)),
            carry[1] + summed_rows(dkv[...].astype(jnp.float32)),
        )

    start = (jnp.zeros((1, wide), jnp.float32), jnp.zeros((1, wide // 2), jnp.float32))
    sums = jnp.concatenate(lax.fori_loop(0, CHIPS, piece, start), axis=1)
    sums = jnp.broadcast_to(sums, (TAG_ROWS, sums.shape[1]))
    for z in range(parts):
        for target, side in ((kept, core), (sent, 1 - core)):
            at = pl.ds(pl.multiple_of(2 * rows * z + rows * side, 32), rows)
            target[z, :rows] = acc[at, :].astype(jnp.bfloat16)
            target[z, rows:] = jnp.where(side == 0, sums, 0.0).astype(jnp.bfloat16)


def picked_piece(place, own, other, g, side, rows):
    m = jnp.bitwise_xor(place[0], g)
    here = own[m, rows, :].astype(jnp.float32)
    there = other[m, rows, :].astype(jnp.float32)
    return jnp.where(place[1] == side, here, there)


def unpack_dense_kernel(place, own, other, inner, outer, output, small):
    rows = inner.shape[0]
    half, quarter = rows // 2, rows // CHIPS
    slot_w = own.shape[2]
    for g in range(CHIPS):
        for side in range(2):
            s = 2 * g + side
            at = slice(slot_w * s, slot_w * (s + 1))
            inner[:, at] = picked_piece(place, own, other, g, side, slice(0, rows))
            for v in range(2):
                outer[half * s : half * (s + 1), slot_w * v : slot_w * (v + 1)] = picked_piece(
                    place, own, other, g, side, slice(rows + half * v, rows + half * (v + 1))
                )
            output[quarter * g : quarter * (g + 1), slot_w * side : slot_w * (side + 1)] = picked_piece(
                place, own, other, g, side, slice(2 * rows, 2 * rows + quarter)
            )
    small[...] = picked_piece(place, own, other, 0, 0, slice(2 * rows + quarter, own.shape[1]))


def unpack_heads_kernel(place, own, other, ww, we, ew, ee, key, value, sums):
    rows = own.shape[1] - TAG_ROWS
    wide = 4 * 3 * HD
    for side in range(2):
        at = slice(rows * side, rows * (side + 1))
        pieces = [picked_piece(place, own, other, g, side, slice(0, rows)) for g in range(CHIPS)]
        for k, target in enumerate((ww, we, ew, ee)):
            target[at, :] = jnp.concatenate(
                [p[:, HD * (4 * h + k) : HD * (4 * h + k + 1)] for p in pieces for h in range(3)], axis=1
            )
        for k, target in enumerate((key, value)):
            target[at, :] = jnp.concatenate(
                [
                    p[:, wide + HD * (2 * h + k) : wide + HD * (2 * h + k + 1)]
                    for p in pieces
                    for h in range(3)
                ],
                axis=1,
            )
    sums[...] = picked_piece(place, own, other, place[2], 0, slice(rows, rows + TAG_ROWS))


def smem():
    return pl.BlockSpec(memory_space=pltpu.SMEM)


def vmem():
    return pl.BlockSpec(memory_space=pltpu.VMEM)


def hbm():
    return pl.BlockSpec(memory_space=pl.ANY)


def whole_call(kernel, operands, outs, scratch=(), flops=0, nbytes=0, exps=0):
    return pl.pallas_call(
        kernel,
        out_shape=[jax.ShapeDtypeStruct(shape, dtype) for shape, dtype, _ in outs],
        in_specs=[spec() for _, spec in operands],
        out_specs=[spec() for _, _, spec in outs],
        scratch_shapes=list(scratch),
        compiler_params=pltpu.CompilerParams(vmem_limit_bytes=58 << 20),
        cost_estimate=pl.CostEstimate(flops=flops, bytes_accessed=nbytes, transcendentals=exps),
    )(*(value for value, _ in operands))


def grouped_device(
    tokens,
    cotangent,
    segment_ids,
    token_types,
    query_wordword,
    query_wordentity,
    query_entityword,
    query_entityentity,
    bias_wordword,
    bias_wordentity,
    bias_entityword,
    bias_entityentity,
    key_weight,
    value_weight,
    value_bias,
    output_weight,
    output_bias,
    first_gain,
    first_bias,
    inner_weight,
    inner_bias,
    outer_weight,
    outer_bias,
    second_gain,
    second_bias,
):
    bf16, f32 = jnp.bfloat16, jnp.float32
    index = lax.axis_index("ctx")
    chip, core = index // 2, index % 2
    wa = lax.axis_index("wa")
    parts = lax.axis_size("wa")
    place = jnp.stack([chip, core, wa]).astype(jnp.int32)
    inputs = tokens[0]
    tok, dmod = inputs.shape
    length = 2 * CHIPS * tok
    rows = key_weight.shape[0]
    half, quarter = rows // 2, rows // CHIPS
    group = dmod // CHIPS
    ff = inner_weight.shape[1]
    slot_w = ff // (2 * CHIPS)

    tags = (segment_ids[0] * 2 + token_types[0]).astype(bf16)
    tag_rows = jnp.pad(tags[None], ((0, TAG_ROWS - 1), (0, dmod - tok)))
    text = jnp.concatenate([inputs, tag_rows], axis=0)
    cut = tok // 2
    text_x, text_y = swapped(text, 2), swapped(text, 4)
    text_far = swapped(text_x[:cut], 4), swapped(text_y[cut:], 2)

    six = (query_wordword, query_wordentity, query_entityword, query_entityentity, key_weight, value_weight)
    cols = [lax.dynamic_slice(w, (half * core, group * chip), (half, group)).reshape(half, 3, HD) for w in six]
    queries = [b.reshape(1, 3, HD) for b in (bias_wordword, bias_wordentity, bias_entityword, bias_entityentity)]
    lone = value_bias.reshape(1, 3, HD)
    by_head = [
        (jnp.stack(cols[:4], axis=2), jnp.stack(cols[4:], axis=2)),
        (jnp.stack(queries, axis=2), jnp.stack([jnp.zeros_like(lone), lone], axis=2)),
    ]
    mine = [jnp.concatenate([a.reshape(a.shape[0], -1), b.reshape(b.shape[0], -1)], axis=1) for a, b in by_head]
    six_vectors = jnp.concatenate([output_bias, first_gain, first_bias, outer_bias, second_gain, second_bias])
    mine += [six_vectors[None], jnp.pad(inner_bias, (0, 6 * group - inner_bias.shape[0]))[None]]
    mine.append(jnp.zeros((TAG_ROWS - 3, 6 * group), bf16))
    mine = jnp.concatenate(mine, axis=0)
    mine = jnp.stack([mine] + [turned(mine, k) for k in range(1, parts)])
    theirs = swapped(mine, 1)
    order = (wa - jnp.arange(parts)) % parts
    vectors = jnp.take(mine[:, half + 1], order, axis=0).reshape(parts, 6, rows)
    vectors = jnp.pad(jnp.transpose(vectors, (1, 0, 2)).reshape(6, dmod), ((0, 2), (0, 0))).astype(f32)
    full_inner_bias = jnp.take(mine[:, half + 2, : ff // parts], order, axis=0).reshape(1, ff).astype(f32)

    slot = jnp.concatenate(
        [
            lax.dynamic_slice(inner_weight, (0, slot_w * index), (rows, slot_w)),
            lax.dynamic_slice(outer_weight, (half * index, 0), (half, slot_w)),
            lax.dynamic_slice(outer_weight, (half * index, slot_w), (half, slot_w)),
            lax.dynamic_slice(output_weight, (quarter * chip, slot_w * core), (quarter, slot_w)),
        ],
        axis=0,
    )
    slots = [slot] + [turned(slot, k) for k in range(1, parts)]

    def chip_stacked(value):
        middle = value.shape[0] // 2
        along_x, along_y = swapped(value, 2), swapped(value, 4)
        across = jnp.concatenate([swapped(along_x[:middle], 4), swapped(along_y[middle:], 2)], axis=0)
        stacked = jnp.stack([value, along_x, along_y, across])
        return stacked, swapped(stacked, 1)

    near_slots = chip_stacked(jnp.stack(slots[:2]))
    far_slots = chip_stacked(jnp.stack(slots[2:]))

    weight, all_text, q, kv = whole_call(
        project_kernel,
        [(place, smem)] + [(a, vmem) for a in (text, text_x, text_y, *text_far, mine, theirs)],
        [
            ((dmod, 6 * group), bf16, vmem),
            ((CHIPS, tok + TAG_ROWS, dmod), bf16, vmem),
            ((CHIPS, tok, 2 * group), bf16, vmem),
            ((CHIPS, tok + TAG_ROWS, 2 * group), bf16, vmem),
        ],
        flops=2 * CHIPS * tok * dmod * 6 * group,
        nbytes=12 << 20,
    )
    kv_other = swapped(kv, 1)

    context, turned_out, lse, bounds = whole_call(
        attend_kernel,
        [(place, smem), (q, vmem), (kv, vmem), (kv_other, vmem)],
        [
            ((CHIPS, tok, group), bf16, vmem),
            ((CHIPS, group, tok), f32, vmem),
            ((CHIPS, 3, 1, tok), f32, vmem),
            ((2, CHIPS), jnp.int32, smem),
        ],
        [
            pltpu.VMEM((3, length, 2 * HD), bf16),
            pltpu.VMEM((3, HD, length), bf16),
            pltpu.VMEM((length, TILE), f32),
            pltpu.VMEM((2 * CHIPS, 8, tok), f32),
            pltpu.VMEM((3, HD, tok), f32),
        ],
        flops=4 * CHIPS * tok * length * group // 2,
        nbytes=8 << 20,
        exps=CHIPS * tok * length * 3 // 2,
    )
    same_core = [[2 * i + k for i in range(CHIPS)] for k in range(2)]

    def exchanged(value):
        return lax.all_to_all(
            value, "ctx", split_axis=0, concat_axis=0, tiled=True, axis_index_groups=same_core
        )

    slot_rows = 2 * rows + quarter + TAG_ROWS
    result, grad_sum, grad_context, kept, sent_far, sent_near = whole_call(
        dense_kernel,
        [(place, smem)]
        + [(a, vmem) for a in (exchanged(context), text, cotangent[0], vectors, full_inner_bias)]
        + [(a, hbm) for a in (*near_slots, *far_slots)],
        [
            ((tok, dmod), bf16, vmem),
            ((tok, dmod), f32, vmem),
            ((CHIPS, tok, group), bf16, vmem),
            ((CHIPS, parts, slot_rows, slot_w), bf16, hbm),
            ((parts, slot_rows, slot_w), bf16, hbm),
            ((CHIPS - 1, parts, slot_rows, slot_w), bf16, hbm),
        ],
        [
            pltpu.VMEM((dmod, ff), bf16),
            pltpu.VMEM((ff, dmod), bf16),
            pltpu.VMEM((dmod, dmod), bf16),
            pltpu.VMEM((tok, ff), bf16),
            pltpu.VMEM((tok, ff), f32),
            pltpu.VMEM((dmod, ff), bf16),
            pltpu.VMEM((ff, dmod), bf16),
            pltpu.VMEM((dmod, dmod), bf16),
            pltpu.VMEM((2, parts, TAG_ROWS, slot_w), bf16),
            pltpu.VMEM((parts, TAG_ROWS, slot_w), f32),
            pltpu.SemaphoreType.DMA((3,)),
            pltpu.SemaphoreType.DMA((3,)),
        ],
        flops=6 * tok * dmod * (dmod + 2 * ff),
        nbytes=26 << 20,
        exps=2 * tok * ff,
    )
    grad_context = exchanged(grad_context)

    dq, dkv, dkv_sent = whole_call(
        attend_back_kernel,
        [(place, smem), (bounds, smem)]
        + [(a, vmem) for a in (q, kv, kv_other, turned_out, lse, grad_context)],
        [
            ((CHIPS, tok, 4 * group), bf16, vmem),
            ((CHIPS, tok, 2 * group), bf16, vmem),
            ((CHIPS, tok, 2 * group), bf16, vmem),
        ],
        [
            pltpu.VMEM((3, length, 2 * HD), bf16),
            pltpu.VMEM((3, 2 * HD, length), bf16),
            pltpu.VMEM((3, length, 2 * HD), bf16),
            pltpu.VMEM((3, length, 2 * HD), f32),
            pltpu.VMEM((3, length, 2 * HD), f32),
            pltpu.VMEM((length, TILE), f32),
            pltpu.VMEM((2 * CHIPS, 8, tok), f32),
            pltpu.VMEM((3, 2 * HD, tok), f32),
        ],
        flops=10 * CHIPS * tok * length * group // 2,
        nbytes=16 << 20,
        exps=CHIPS * tok * length * 3 // 2,
    )
    partial, head_kept, head_sent = whole_call(
        project_back_kernel,
        [(place, smem)] + [(a, vmem) for a in (all_text, dq, dkv, swapped(dkv_sent, 1), weight)],
        [
            ((CHIPS, tok, dmod), bf16, vmem),
            ((parts, half + TAG_ROWS, 6 * group), bf16, vmem),
            ((parts, half + TAG_ROWS, 6 * group), bf16, vmem),
        ],
        [pltpu.VMEM((dmod, 6 * group), f32), pltpu.VMEM((tok, 2 * group), bf16)],
        flops=4 * CHIPS * tok * dmod * 6 * group,
        nbytes=16 << 20,
    )

    def added(*values):
        total = values[0].astype(f32)
        for v in values[1:]:
            total = total + v.astype(f32)
        return total

    def chips_summed(far, near, to):
        middle = far.shape[0] // 2
        from_x, from_y = swapped(far[:middle], 2), swapped(far[middle:], 4)
        x0, x1 = near(1, slice(0, middle)), near(1, slice(middle, None))
        y0, y1 = near(2, slice(0, middle)), near(2, slice(middle, None))
        x0 = swapped(added(*x0).astype(bf16), 2)
        y1 = swapped(added(*y1).astype(bf16), 4)
        x1 = swapped(added(*x1, from_y).astype(bf16), 2)
        y0 = swapped(added(*y0, from_x).astype(bf16), 4)
        low = added(*near(0, slice(0, middle)), x0, y0).astype(to)
        high = added(*near(0, slice(middle, None)), x1, y1).astype(to)
        return low, high

    def parts_summed(value):
        total = [lax.dynamic_index_in_dim(value, wa, 0, keepdims=False)]
        for k in range(1, parts):
            total.append(turned(lax.dynamic_index_in_dim(value, (wa + k) % parts, 0, keepdims=False), k))
        return added(*total).astype(bf16)

    far = added(kept[CHIPS - 1], swapped(sent_far, 1)).astype(bf16)
    received = swapped(sent_near, 1)
    low, high = chips_summed(far, lambda m, at: (kept[m, at], received[m, at]), bf16)
    summed = parts_summed(jnp.concatenate([low, high], axis=0))
    out_inner, out_outer, out_output, small = whole_call(
        unpack_dense_kernel,
        [(place, smem)] + [(a, vmem) for a in chip_stacked(summed)],
        [
            ((rows, ff), f32, vmem),
            (outer_weight.shape, f32, vmem),
            ((rows, dmod), f32, vmem),
            ((TAG_ROWS, slot_w), f32, vmem),
        ],
        nbytes=8 << 20,
    )

    summed = parts_summed(added(head_kept, swapped(head_sent, 1)).astype(bf16))
    *out_heads, sums = whole_call(
        unpack_heads_kernel,
        [(place, smem)] + [(a, vmem) for a in chip_stacked(summed)],
        [((rows, dmod), f32, vmem) for _ in range(6)] + [((TAG_ROWS, 6 * group), f32, vmem)],
        nbytes=8 << 20,
    )
    low, high = chips_summed(partial[CHIPS - 1], lambda m, at: (partial[m, at],), f32)
    input_grads = grad_sum + jnp.concatenate([low, high], axis=0)

    sum_q = sums[0, : 4 * group].reshape(3, 4, HD)
    sum_v = sums[0, 4 * group :].reshape(3, 2, HD)[:, 1].reshape(rows)
    own_small = lax.dynamic_slice(small[:12].reshape(6, dmod), (0, wa * rows), (6, rows))
    return (
        result[None],
        input_grads[None],
        *out_heads[:4],
        *(sum_q[:, k].reshape(rows) for k in range(4)),
        *out_heads[4:],
        sum_v,
        out_output,
        own_small[0],
        own_small[1],
        own_small[2],
        out_inner,
        small[12:14].reshape(ff // parts),
        out_outer,
        own_small[3],
        own_small[4],
        own_small[5],
    )


def solution(mesh):
    in_specs = (
        P("wa", "ctx", None),
        P("wa", "ctx", None),
        P("wa", "ctx"),
        P("wa", "ctx"),
        P("wa", None),
        P("wa", None),
        P("wa", None),
        P("wa", None),
        P("wa"),
        P("wa"),
        P("wa"),
        P("wa"),
        P("wa", None),
        P("wa", None),
        P("wa"),
        P("wa", None),
        P("wa"),
        P("wa"),
        P("wa"),
        P("wa", None),
        P("wa"),
        P("wa", None),
        P("wa"),
        P("wa"),
        P("wa"),
    )
    out_specs = (
        P("wa", "ctx", None),
        P("wa", "ctx", None),
        P("wa", None),
        P("wa", None),
        P("wa", None),
        P("wa", None),
        P("wa"),
        P("wa"),
        P("wa"),
        P("wa"),
        P("wa", None),
        P("wa", None),
        P("wa"),
        P("wa", None),
        P("wa"),
        P("wa"),
        P("wa"),
        P("wa", None),
        P("wa"),
        P("wa", None),
        P("wa"),
        P("wa"),
        P("wa"),
    )
    body = grouped_device if mesh.shape["ctx"] == 2 * CHIPS else windowed_device
    return jax.shard_map(
        body, mesh=mesh, in_specs=in_specs, out_specs=out_specs, check_vma=False
    )
```

```python
import jax
import jax.numpy as jnp
from jax import lax
from jax.experimental import pallas as pl
from jax.experimental.pallas import tpu as pltpu
from jax.sharding import PartitionSpec as P

HD = 64


EPSILON = 1e-12
MASKED = -1e30


def as_sent(shard):
    return jax.tree.map(lambda a: a.astype(jnp.bfloat16) if a.dtype == jnp.float32 else a, shard)


def passed_along(value, axis, steps):
    count = lax.axis_size(axis)
    leading, last = (max(0, -steps), min(count, count - steps))
    return lax.ppermute(value, axis, [(source, source + steps) for source in range(leading, last)])


def layer_norm(values, gain, shift):
    center = values - jnp.mean(values, axis=-1, keepdims=True)
    spread = jnp.mean(center * center, axis=-1, keepdims=True)
    return center * lax.rsqrt(spread + EPSILON) * gain + shift


def gelu_exact(values):
    return jax.nn.gelu(values, approximate=False)


def matmul(left, right):
    return jnp.dot(left, right, preferred_element_type=jnp.float32)


def left_product(left, right):
    return lax.dot_general(
        left, right, (((0,), (0,)), ((), ())), preferred_element_type=jnp.float32
    )


def right_product(left, right):
    return lax.dot_general(
        left, right, (((1,), (1,)), ((), ())), preferred_element_type=jnp.float32
    )


def column_sums(values):
    return jnp.sum(values.astype(jnp.float32), axis=0)


def columns(values, start):
    return lax.dynamic_slice_in_dim(values, start, HD, 1)


def head_scores(query_word, query_entity, keys_head, key_entity, allowed, scale):
    word_scores = right_product(query_word, keys_head)
    entity_scores = right_product(query_entity, keys_head)
    raw = jnp.where(key_entity[None, :], entity_scores, word_scores) * scale
    return jnp.where(allowed, raw, MASKED)


def merge_heads(stacked):
    return jnp.transpose(stacked, (1, 0, 2)).reshape(
        stacked.shape[1], stacked.shape[0] * stacked.shape[2]
    )


def windowed_device(
    tokens,
    cotangent,
    segment_ids,
    token_types,
    query_wordword,
    query_wordentity,
    query_entityword,
    query_entityentity,
    bias_wordword,
    bias_wordentity,
    bias_entityword,
    bias_entityentity,
    key_weight,
    value_weight,
    value_bias,
    output_weight,
    output_bias,
    first_gain,
    first_bias,
    inner_weight,
    inner_bias,
    outer_weight,
    outer_bias,
    second_gain,
    second_bias,
):
    attention = (
        lax.all_gather(query_wordword, "wa", axis=0, tiled=True),
        lax.all_gather(query_wordentity, "wa", axis=0, tiled=True),
        lax.all_gather(query_entityword, "wa", axis=0, tiled=True),
        lax.all_gather(query_entityentity, "wa", axis=0, tiled=True),
        lax.all_gather(bias_wordword, "wa", axis=0, tiled=True),
        lax.all_gather(bias_wordentity, "wa", axis=0, tiled=True),
        lax.all_gather(bias_entityword, "wa", axis=0, tiled=True),
        lax.all_gather(bias_entityentity, "wa", axis=0, tiled=True),
        lax.all_gather(key_weight, "wa", axis=0, tiled=True),
        lax.all_gather(value_weight, "wa", axis=0, tiled=True),
        lax.all_gather(value_bias, "wa", axis=0, tiled=True),
        lax.all_gather(output_weight, "wa", axis=0, tiled=True),
        lax.all_gather(output_bias, "wa", axis=0, tiled=True),
        lax.all_gather(first_gain, "wa", axis=0, tiled=True),
        lax.all_gather(first_bias, "wa", axis=0, tiled=True),
    )
    (
        full_ww,
        full_we,
        full_ew,
        full_ee,
        shift_ww,
        shift_we,
        shift_ew,
        shift_ee,
        full_key,
        full_value,
        shift_value,
        full_output,
        shift_output,
        gain_one,
        shift_one,
    ) = attention
    feedforward = (
        lax.all_gather(inner_weight, "wa", axis=0, tiled=True),
        lax.all_gather(inner_bias, "wa", axis=0, tiled=True),
        lax.all_gather(outer_weight, "wa", axis=0, tiled=True),
        lax.all_gather(outer_bias, "wa", axis=0, tiled=True),
        lax.all_gather(second_gain, "wa", axis=0, tiled=True),
        lax.all_gather(second_bias, "wa", axis=0, tiled=True),
    )
    full_inner, shift_inner, full_outer, shift_outer, gain_two, shift_two = feedforward
    inputs = tokens[0]
    seg = segment_ids[0]
    types = token_types[0]
    tok = inputs.shape[0]
    dmod = inputs.shape[1]
    heads = dmod // HD
    scale = HD ** (-0.5)
    length = tok * lax.axis_size("ctx")
    doc_max = min(2048, 4 * tok, length // 2)
    reach = (doc_max - 2) // tok + 1
    entity = (types == 1)[:, None]
    proj_ww = matmul(inputs, full_ww) + shift_ww
    proj_we = matmul(inputs, full_we) + shift_we
    proj_ew = matmul(inputs, full_ew) + shift_ew
    proj_ee = matmul(inputs, full_ee) + shift_ee
    query_word = jnp.where(entity, proj_ew, proj_ww).astype(jnp.bfloat16)
    query_entity = jnp.where(entity, proj_ee, proj_we).astype(jnp.bfloat16)
    keys = matmul(inputs, full_key).astype(jnp.bfloat16)
    values = (matmul(inputs, full_value) + shift_value).astype(jnp.bfloat16)
    own_kv = jnp.concatenate([keys, values], axis=1)
    own_seg = seg + 1
    tags = own_seg * 2 + types

    def pass_left(packet, unused):
        moved = jax.tree.map(
            lambda part, own: part.astype(own.dtype),
            passed_along(as_sent(packet), "ctx", 1),
            packet,
        )
        return (moved, moved)

    def pass_right(packet, unused):
        moved = jax.tree.map(
            lambda part, own: part.astype(own.dtype),
            passed_along(as_sent(packet), "ctx", -1),
            packet,
        )
        return (moved, moved)

    _, (left_kv, left_tags) = lax.scan(pass_left, (own_kv, tags), None, length=reach)
    _, (right_kv, right_tags) = lax.scan(pass_right, (own_kv, tags), None, length=reach)
    window = jnp.concatenate(
        [jnp.flip(left_kv, 0).reshape(-1, 2 * dmod), own_kv, right_kv.reshape(-1, 2 * dmod)], axis=0
    )
    window_tags = jnp.concatenate(
        [jnp.flip(left_tags, 0).reshape(-1), tags, right_tags.reshape(-1)], axis=0
    )
    key_entity = window_tags % 2 == 1
    allowed = own_seg[:, None] == (window_tags // 2)[None, :]

    def head_forward(index):
        start = index * HD
        scores = head_scores(
            columns(query_word, start),
            columns(query_entity, start),
            columns(window, start),
            key_entity,
            allowed,
            scale,
        )
        top = jnp.max(scores, axis=1, keepdims=True)
        expo = jnp.exp(scores - top)
        total = jnp.sum(expo, axis=1, keepdims=True)
        probs = (expo / total).astype(jnp.bfloat16)
        return (matmul(probs, columns(window, dmod + start)), (top + jnp.log(total))[:, 0])

    head_context, lse = lax.map(head_forward, jnp.arange(heads))
    context = merge_heads(head_context).astype(jnp.bfloat16)
    branch = matmul(context, full_output) + shift_output
    first, pull_one = jax.vjp(
        layer_norm,
        inputs.astype(jnp.float32) + branch,
        gain_one.astype(jnp.float32),
        shift_one.astype(jnp.float32),
    )
    first_low = first.astype(jnp.bfloat16)
    inner = matmul(first_low, full_inner) + shift_inner
    activated, pull_gelu = jax.vjp(gelu_exact, inner)
    hidden = activated.astype(jnp.bfloat16)
    ffn = matmul(hidden, full_outer) + shift_outer
    result, pull_two = jax.vjp(
        layer_norm, first + ffn, gain_two.astype(jnp.float32), shift_two.astype(jnp.float32)
    )
    grad_sum_two, grad_gain_two, grad_shift_two = pull_two(cotangent[0].astype(jnp.float32))
    grad_ffn = grad_sum_two.astype(jnp.bfloat16)
    grad_outer = left_product(hidden, grad_ffn)
    grad_outer_shift = column_sums(grad_ffn)
    grad_inner = pull_gelu(right_product(grad_ffn, full_outer))[0].astype(jnp.bfloat16)
    grad_inner_full = left_product(first_low, grad_inner)
    grad_inner_shift = column_sums(grad_inner)
    grad_first = grad_sum_two + right_product(grad_inner, full_inner)
    grad_sum_one, grad_gain_one, grad_shift_one = pull_one(grad_first)
    grad_branch = grad_sum_one.astype(jnp.bfloat16)
    grad_output = left_product(context, grad_branch)
    grad_output_shift = column_sums(grad_branch)
    grad_context = right_product(grad_branch, full_output).astype(jnp.bfloat16)

    def head_backward(index):
        start = index * HD
        word_head = columns(query_word, start)
        entity_head = columns(query_entity, start)
        keys_head = columns(window, start)
        values_head = columns(window, dmod + start)
        context_head = columns(grad_context, start)
        scores = head_scores(word_head, entity_head, keys_head, key_entity, allowed, scale)
        probs = jnp.exp(scores - lse[index][:, None])
        grad_probs = right_product(context_head, values_head)
        delta = jnp.sum(probs * grad_probs, axis=1)
        grad_scores = (probs * (grad_probs - delta[:, None])).astype(jnp.bfloat16)
        zero = jnp.zeros_like(grad_scores)
        grad_word = jnp.where(key_entity[None, :], zero, grad_scores)
        grad_entity = jnp.where(key_entity[None, :], grad_scores, zero)
        grad_qword = matmul(grad_word, keys_head) * scale
        grad_qentity = matmul(grad_entity, keys_head) * scale
        grad_keys = (
            left_product(grad_word, word_head) + left_product(grad_entity, entity_head)
        ) * scale
        grad_values = left_product(probs.astype(jnp.bfloat16), context_head)
        return (grad_qword, grad_qentity, delta, grad_keys, grad_values)

    grad_qword, grad_qentity, delta, window_keys, window_values = lax.map(
        lambda index: head_backward(index), jnp.arange(heads)
    )
    parts_keys = merge_heads(window_keys).reshape(2 * reach + 1, tok, dmod)
    parts_values = merge_heads(window_values).reshape(2 * reach + 1, tok, dmod)

    def back_left(total, piece):
        return (
            (
                passed_along((total[0] + piece[0]).astype(jnp.bfloat16), "ctx", -1).astype(
                    jnp.float32
                ),
                passed_along((total[1] + piece[1]).astype(jnp.bfloat16), "ctx", -1).astype(
                    jnp.float32
                ),
            ),
            None,
        )

    def back_right(total, piece):
        return (
            (
                passed_along((total[0] + piece[0]).astype(jnp.bfloat16), "ctx", 1).astype(
                    jnp.float32
                ),
                passed_along((total[1] + piece[1]).astype(jnp.bfloat16), "ctx", 1).astype(
                    jnp.float32
                ),
            ),
            None,
        )

    empty = jnp.zeros((tok, dmod), jnp.float32)
    from_above, _ = lax.scan(back_left, (empty, empty), (parts_keys[:reach], parts_values[:reach]))
    from_below, _ = lax.scan(
        back_right,
        (empty, empty),
        (jnp.flip(parts_keys[reach + 1 :], 0), jnp.flip(parts_values[reach + 1 :], 0)),
    )
    own_keys = parts_keys[reach] + from_above[0] + from_below[0]
    own_values = parts_values[reach] + from_above[1] + from_below[1]
    grad_keys = own_keys.astype(jnp.bfloat16)
    grad_values = own_values.astype(jnp.bfloat16)
    grad_qword = merge_heads(grad_qword).astype(jnp.bfloat16)
    grad_qentity = merge_heads(grad_qentity).astype(jnp.bfloat16)
    zeros = jnp.zeros_like(grad_qword)
    grad_pww = jnp.where(entity, zeros, grad_qword)
    grad_pew = jnp.where(entity, grad_qword, zeros)
    grad_pwe = jnp.where(entity, zeros, grad_qentity)
    grad_pee = jnp.where(entity, grad_qentity, zeros)
    input_grads = grad_sum_one + right_product(grad_pww, full_ww) + right_product(grad_pwe, full_we)
    input_grads = input_grads + right_product(grad_pew, full_ew) + right_product(grad_pee, full_ee)
    input_grads = (
        input_grads + right_product(grad_keys, full_key) + right_product(grad_values, full_value)
    )
    local_grads = (
        left_product(inputs, grad_pww),
        left_product(inputs, grad_pwe),
        left_product(inputs, grad_pew),
        left_product(inputs, grad_pee),
        column_sums(grad_pww),
        column_sums(grad_pwe),
        column_sums(grad_pew),
        column_sums(grad_pee),
        left_product(inputs, grad_keys),
        left_product(inputs, grad_values),
        column_sums(grad_values),
        grad_output,
        grad_output_shift,
        grad_gain_one,
        grad_shift_one,
        grad_inner_full,
        grad_inner_shift,
        grad_outer,
        grad_outer_shift,
        grad_gain_two,
        grad_shift_two,
    )
    shards = (
        lax.psum_scatter(
            local_grads[0].astype(jnp.bfloat16), "wa", scatter_dimension=0, tiled=True
        ).astype(jnp.float32),
        lax.psum_scatter(
            local_grads[1].astype(jnp.bfloat16), "wa", scatter_dimension=0, tiled=True
        ).astype(jnp.float32),
        lax.psum_scatter(
            local_grads[2].astype(jnp.bfloat16), "wa", scatter_dimension=0, tiled=True
        ).astype(jnp.float32),
        lax.psum_scatter(
            local_grads[3].astype(jnp.bfloat16), "wa", scatter_dimension=0, tiled=True
        ).astype(jnp.float32),
        lax.psum_scatter(
            local_grads[4].astype(jnp.bfloat16), "wa", scatter_dimension=0, tiled=True
        ).astype(jnp.float32),
        lax.psum_scatter(
            local_grads[5].astype(jnp.bfloat16), "wa", scatter_dimension=0, tiled=True
        ).astype(jnp.float32),
        lax.psum_scatter(
            local_grads[6].astype(jnp.bfloat16), "wa", scatter_dimension=0, tiled=True
        ).astype(jnp.float32),
        lax.psum_scatter(
            local_grads[7].astype(jnp.bfloat16), "wa", scatter_dimension=0, tiled=True
        ).astype(jnp.float32),
        lax.psum_scatter(
            local_grads[8].astype(jnp.bfloat16), "wa", scatter_dimension=0, tiled=True
        ).astype(jnp.float32),
        lax.psum_scatter(
            local_grads[9].astype(jnp.bfloat16), "wa", scatter_dimension=0, tiled=True
        ).astype(jnp.float32),
        lax.psum_scatter(
            local_grads[10].astype(jnp.bfloat16), "wa", scatter_dimension=0, tiled=True
        ).astype(jnp.float32),
        lax.psum_scatter(
            local_grads[11].astype(jnp.bfloat16), "wa", scatter_dimension=0, tiled=True
        ).astype(jnp.float32),
        lax.psum_scatter(
            local_grads[12].astype(jnp.bfloat16), "wa", scatter_dimension=0, tiled=True
        ).astype(jnp.float32),
        lax.psum_scatter(
            local_grads[13].astype(jnp.bfloat16), "wa", scatter_dimension=0, tiled=True
        ).astype(jnp.float32),
        lax.psum_scatter(
            local_grads[14].astype(jnp.bfloat16), "wa", scatter_dimension=0, tiled=True
        ).astype(jnp.float32),
        lax.psum_scatter(
            local_grads[15].astype(jnp.bfloat16), "wa", scatter_dimension=0, tiled=True
        ).astype(jnp.float32),
        lax.psum_scatter(
            local_grads[16].astype(jnp.bfloat16), "wa", scatter_dimension=0, tiled=True
        ).astype(jnp.float32),
        lax.psum_scatter(
            local_grads[17].astype(jnp.bfloat16), "wa", scatter_dimension=0, tiled=True
        ).astype(jnp.float32),
        lax.psum_scatter(
            local_grads[18].astype(jnp.bfloat16), "wa", scatter_dimension=0, tiled=True
        ).astype(jnp.float32),
        lax.psum_scatter(
            local_grads[19].astype(jnp.bfloat16), "wa", scatter_dimension=0, tiled=True
        ).astype(jnp.float32),
        lax.psum_scatter(
            local_grads[20].astype(jnp.bfloat16), "wa", scatter_dimension=0, tiled=True
        ).astype(jnp.float32),
    )
    totals = lax.psum(
        (
            shards[0],
            shards[1],
            shards[2],
            shards[3],
            shards[4],
            shards[5],
            shards[6],
            shards[7],
            shards[8],
            shards[9],
            shards[10],
            shards[11],
            shards[12],
            shards[13],
            shards[14],
            shards[15],
            shards[16],
            shards[17],
            shards[18],
            shards[19],
            shards[20],
        ),
        "ctx",
    )
    return (
        result.astype(jnp.bfloat16)[None],
        input_grads[None],
        totals[0],
        totals[1],
        totals[2],
        totals[3],
        totals[4],
        totals[5],
        totals[6],
        totals[7],
        totals[8],
        totals[9],
        totals[10],
        totals[11],
        totals[12],
        totals[13],
        totals[14],
        totals[15],
        totals[16],
        totals[17],
        totals[18],
        totals[19],
        totals[20],
    )


CHIPS = 4
KEY_BLOCK = 256
NEGATIVE = -1e30
TAG_ROWS = 16
TILE = 128
FLOPS_PER_MICRO = 1_100_000_000


def lanes_product(left, right):
    return lax.dot_general(
        left, right, (((1,), (1,)), ((), ())), preferred_element_type=jnp.float32
    )


def rows_product(left, right):
    return lax.dot_general(
        left, right, (((0,), (0,)), ((), ())), preferred_element_type=jnp.float32
    )


def plain_product(left, right):
    return jnp.dot(left, right, preferred_element_type=jnp.float32)


def swapped(value, step):
    count = lax.axis_size("ctx")
    return lax.ppermute(value, "ctx", [(i, i ^ step) for i in range(count)])


def turned(value, step):
    count = lax.axis_size("wa")
    return lax.ppermute(value, "wa", [(i, (i + step) % count) for i in range(count)])


def ring_far(one, three):
    middle = one.shape[0] // 2
    return jnp.concatenate([turned(one[:middle], 1), turned(three[middle:], 3)], axis=0)


def as_column(row):
    return jnp.broadcast_to(row, (TILE, row.shape[1])).T


def segment_of(tag):
    return jnp.floor(tag * 0.5)


def prepare_kernel(
    place, ww, we, ew, ee, key, value, *others
):
    *lines, inner, outer, output, mine, slot, sem = others
    rows = key.shape[0]
    half, quarter = rows // 2, rows // CHIPS
    slot_w = slot.shape[1]
    chip, core = place[0], place[1]
    index = 2 * chip + core
    copies = [
        (inner.at[:, pl.ds(pl.multiple_of(slot_w * index, TILE), slot_w)], slot.at[pl.ds(0, rows), :])
    ]
    for v in range(2):
        copies.append(
            (
                outer.at[pl.ds(pl.multiple_of(half * index, 16), half), pl.ds(slot_w * v, slot_w)],
                slot.at[pl.ds(rows + half * v, half), :],
            )
        )
    copies.append(
        (
            output.at[
                pl.ds(pl.multiple_of(quarter * chip, 16), quarter),
                pl.ds(pl.multiple_of(slot_w * core, TILE), slot_w),
            ],
            slot.at[pl.ds(2 * rows, quarter), :],
        )
    )
    copies = [pltpu.make_async_copy(a, b, sem.at[k]) for k, (a, b) in enumerate(copies)]
    for copy in copies:
        copy.start()
    at = pl.ds(pl.multiple_of(half * core, 16), half)
    for g in range(CHIPS):

        @pl.when(chip == g)
        def _():
            def heads(sources):
                return jnp.concatenate(
                    [
                        w[at, HD * (3 * g + h) : HD * (3 * g + h + 1)].astype(jnp.float32)
                        for h in range(3)
                        for w in sources
                    ],
                    axis=1,
                ).astype(jnp.bfloat16)

            mine[:half, : 4 * 3 * HD] = heads((ww, we, ew, ee))
            mine[:half, 4 * 3 * HD :] = heads((key, value))

    lines = [line[...].astype(jnp.float32).reshape(1, line.shape[0]) for line in lines]
    bias = [lines[k][:, HD * h : HD * (h + 1)] for h in range(3) for k in range(4)]
    for h in range(3):
        bias += [jnp.zeros((1, HD), jnp.float32), lines[4][:, HD * h : HD * (h + 1)]]
    six = jnp.concatenate(lines[5:11], axis=1)
    last = jnp.concatenate([lines[11], jnp.zeros((1, 2 * rows), jnp.float32)], axis=1)
    which = lax.broadcasted_iota(jnp.int32, (TAG_ROWS, 6 * rows), 0)
    below = jnp.where(which == 0, jnp.concatenate(bias, axis=1), jnp.where(which == 1, six, last))
    mine[half:] = jnp.where(which < 3, below, 0.0).astype(jnp.bfloat16)
    for copy in copies:
        copy.wait()


def project_kernel(place, t0, t1, t2, t3a, t3b, mine, theirs, weight, tokens, q_ref, kv_ref):
    parts, rows = mine.shape[0], mine.shape[1] - TAG_ROWS
    tok = q_ref.shape[1]
    chip, core, wa = place[0], place[1], place[2]
    cut = t3a.shape[0]
    tokens[0] = t0[...]
    tokens[1] = t1[...]
    tokens[2] = t2[...]
    tokens[3, :cut] = t3a[...]
    tokens[3, cut:] = t3b[...]
    for z in range(parts):
        k = lax.rem(wa - z + parts, parts)
        for source, side in ((mine, core), (theirs, 1 - core)):
            weight[pl.ds(pl.multiple_of(2 * rows * z + rows * side, 32), rows), :] = source[k, :rows]
    k = lax.rem(wa - chip + parts, parts)
    bias = mine[k, rows : rows + TAG_ROWS].astype(jnp.float32)[:1]
    wide = 2 * HD

    def piece(m, unused):
        to = jnp.bitwise_xor(chip, m)
        tags = tokens[m, tok : tok + TAG_ROWS].astype(jnp.float32)[:1, :tok]
        flag = as_column(tags - 2.0 * segment_of(tags)) == 1.0
        text = tokens[m, :tok]
        for h in range(3):
            at = 2 * wide * h
            both = plain_product(text, weight[:, at : at + 2 * wide]) + bias[:, at : at + 2 * wide]
            q = jnp.where(flag, both[:, wide:], both[:, :wide]).astype(jnp.bfloat16)
            q_ref[to, :, wide * h : wide * (h + 1)] = q * jnp.bfloat16(HD**-0.5)
        kv = plain_product(text, weight[:, 6 * wide :]) + bias[:, 6 * wide :]
        kv_ref[to, :tok] = kv.astype(jnp.bfloat16)
        kv_ref[to, tok:] = jnp.broadcast_to(tags, (TAG_ROWS, tok)).astype(jnp.bfloat16)
        return 0

    lax.fori_loop(0, CHIPS, piece, 0)


def masked_keys(kv, flag):
    wide = kv.astype(jnp.float32)
    low = lax.broadcasted_iota(jnp.int32, kv.shape, 1) < HD
    both = jnp.where(low, wide, pltpu.roll(wide, HD, 1))
    return jnp.where(low == flag, 0.0, both)


def attend_kernel(place, q_ref, own, other, out, turned_out, lse, bounds, keys, values, seg_col, seg_row, acc):
    tok = q_ref.shape[1]
    core = place[1]

    def prepare(j, unused):
        for source, side in ((own, core), (other, 1 - core)):
            shard = 2 * j + side
            at = pl.ds(pl.multiple_of(shard * tok, TILE), tok)
            tags = source[j, tok : tok + TAG_ROWS].astype(jnp.float32)[:1]
            seg_row[shard] = jnp.broadcast_to(segment_of(tags), (8, tok))
            column = as_column(tags)
            segment = segment_of(column)
            seg_col[at, :] = segment
            flag = column - 2.0 * segment == 1.0
            for h in range(3):
                kv = source[j, :tok, 2 * HD * h : 2 * HD * (h + 1)]
                keys[h, at, :] = masked_keys(kv, flag).astype(jnp.bfloat16)
                values[h, :, at] = kv.astype(jnp.float32).T[HD:].astype(jnp.bfloat16)
        return 0

    lax.fori_loop(0, CHIPS, prepare, 0)

    def queries(j, unused):
        seg = seg_row[2 * j + core][:1]
        everyone = seg_row[...][:, 0, :]
        before = jnp.sum((everyone < jnp.min(seg)).astype(jnp.float32)).astype(jnp.int32)
        through = jnp.sum((everyone <= jnp.max(seg)).astype(jnp.float32)).astype(jnp.int32)
        first = before // KEY_BLOCK
        last = (through + KEY_BLOCK - 1) // KEY_BLOCK
        bounds[0, j] = first
        bounds[1, j] = last
        acc[...] = jnp.zeros_like(acc)

        def step(t, carry):
            at = pl.ds(pl.multiple_of(t * KEY_BLOCK, KEY_BLOCK), KEY_BLOCK)
            column = seg_col[at, :]
            same = jnp.concatenate([column] * (tok // TILE), axis=1) == seg
            after = []
            queries = [q_ref[j, :, 2 * HD * h : 2 * HD * (h + 1)] for h in range(3)]
            scores = [
                jnp.where(same, lanes_product(keys[h, at, :], queries[h]), NEGATIVE) for h in range(3)
            ]
            peaks = [
                jnp.maximum(carry[2 * h], jnp.max(scores[h], axis=0, keepdims=True)) for h in range(3)
            ]
            expo = [jnp.exp(scores[h] - peaks[h]) for h in range(3)]
            for h in range(3):
                fade = jnp.exp(carry[2 * h] - peaks[h])
                total = carry[2 * h + 1] * fade + jnp.sum(expo[h], axis=0, keepdims=True)
                acc[h] = acc[h] * fade + plain_product(values[h, :, at], expo[h].astype(jnp.bfloat16))
                after += [peaks[h], total]
            return tuple(after)

        start = (jnp.full((1, tok), NEGATIVE, jnp.float32), jnp.zeros((1, tok), jnp.float32)) * 3
        done = lax.fori_loop(first, last, step, start)
        for h in range(3):
            turned_out[j, HD * h : HD * (h + 1), :] = acc[h] / done[2 * h + 1]
            lse[j, h] = done[2 * h] + jnp.log(done[2 * h + 1])
        out[jnp.bitwise_xor(place[0], j)] = turned_out[j].T.astype(jnp.bfloat16)
        return 0

    lax.fori_loop(0, CHIPS, queries, 0)


def attend_back_kernel(
    place,
    bounds,
    q_ref,
    own,
    other,
    turned_out,
    lse,
    grad0,
    grad1,
    grad2,
    grad3,
    dq_ref,
    dkv_own,
    dkv_other,
    keys,
    turned_keys,
    values,
    grad_keys,
    grad_values,
    seg_col,
    seg_row,
    acc,
    grad,
):
    tok = q_ref.shape[1]
    chip, core = place[0], place[1]
    wide = 2 * HD
    for m, piece in enumerate((grad0, grad1, grad2, grad3)):
        grad[jnp.bitwise_xor(chip, m)] = piece[...]

    def prepare(j, unused):
        for source, side in ((own, core), (other, 1 - core)):
            shard = 2 * j + side
            at = pl.ds(pl.multiple_of(shard * tok, TILE), tok)
            tags = source[j, tok : tok + TAG_ROWS].astype(jnp.float32)[:1]
            seg_row[shard] = jnp.broadcast_to(tags, (8, tok))
            column = as_column(tags)
            segment = segment_of(column)
            seg_col[at, :] = segment
            flag = column - 2.0 * segment == 1.0
            for h in range(3):
                kv = source[j, :tok, wide * h : wide * (h + 1)]
                key = masked_keys(kv, flag)
                keys[h, at, :] = key.astype(jnp.bfloat16)
                turned_keys[h, :, at] = key.T.astype(jnp.bfloat16)
                values[h, at, :] = kv
                grad_keys[h, at, :] = jnp.zeros((tok, wide), jnp.float32)
                grad_values[h, at, :] = jnp.zeros((tok, wide), jnp.float32)
        return 0

    lax.fori_loop(0, CHIPS, prepare, 0)

    def queries(j, unused):
        tags = seg_row[2 * j + core][:1]
        seg = segment_of(tags)
        slot = jnp.bitwise_xor(chip, j)
        flag = as_column(tags - 2.0 * seg) == 1.0
        turned_grad = grad[j].astype(jnp.float32).T
        deltas, shifts, padded = [], [], []
        for h in range(3):
            rows = slice(HD * h, HD * (h + 1))
            deltas.append(jnp.sum(turned_grad[rows] * turned_out[j, rows, :], axis=0, keepdims=True))
            shifts.append(lse[j, h])
            head = grad[j, :, rows]
            padded.append(jnp.concatenate([jnp.zeros_like(head), head], axis=1))
        acc[...] = jnp.zeros_like(acc)

        def step(t, carry):
            at = pl.ds(pl.multiple_of(t * KEY_BLOCK, KEY_BLOCK), KEY_BLOCK)
            column = seg_col[at, :]
            same = jnp.concatenate([column] * (tok // TILE), axis=1) == seg
            for h in range(3):
                q = q_ref[j, :, wide * h : wide * (h + 1)]
                scores = lanes_product(keys[h, at, :], q)
                probs = jnp.where(same, jnp.exp(scores - shifts[h]), 0.0)
                grad_probs = lanes_product(values[h, at, :], padded[h])
                grad_scores = (probs * (grad_probs - deltas[h])).astype(jnp.bfloat16)
                grad_values[h, at, :] += plain_product(probs.astype(jnp.bfloat16), padded[h])
                grad_keys[h, at, :] += plain_product(grad_scores, q)
                acc[h] += plain_product(turned_keys[h, :, at], grad_scores)
            return carry

        lax.fori_loop(bounds[0, j], bounds[1, j], step, 0)
        for h in range(3):
            dq = acc[h].T * (HD**-0.5)
            at = 2 * wide * h
            dq_ref[slot, :, at : at + wide] = jnp.where(flag, 0.0, dq).astype(jnp.bfloat16)
            dq_ref[slot, :, at + wide : at + 2 * wide] = jnp.where(flag, dq, 0.0).astype(jnp.bfloat16)
        return 0

    lax.fori_loop(0, CHIPS, queries, 0)

    def finish(j, unused):
        slot = jnp.bitwise_xor(chip, j)
        for target, side in ((dkv_own, core), (dkv_other, 1 - core)):
            shard = 2 * j + side
            at = pl.ds(pl.multiple_of(shard * tok, TILE), tok)
            tags = seg_row[shard][:1]
            flag = as_column(tags - 2.0 * segment_of(tags)) == 1.0
            for h in range(3):
                both = grad_keys[h, at, :]
                low = lax.broadcasted_iota(jnp.int32, both.shape, 1) < HD
                picked = jnp.where(flag, pltpu.roll(both, HD, 1), both)
                target[slot, :, wide * h : wide * (h + 1)] = jnp.where(
                    low, picked, grad_values[h, at, :]
                ).astype(jnp.bfloat16)
        return 0

    lax.fori_loop(0, CHIPS, finish, 0)


def normed(total, gain, shift):
    center = total - jnp.mean(total, axis=-1, keepdims=True)
    spread = jnp.mean(center * center, axis=-1, keepdims=True)
    inverse = lax.rsqrt(spread + EPSILON)
    unit = center * inverse
    return unit * gain + shift, unit, inverse


def normed_back(grad, unit, inverse, gain):
    scaled = grad * gain
    mean = jnp.mean(scaled, axis=-1, keepdims=True)
    along = jnp.mean(scaled * unit, axis=-1, keepdims=True)
    return inverse * (scaled - mean - unit * along)


def summed_rows(value):
    return jnp.sum(value, axis=0, keepdims=True)


def dense_kernel(
    place,
    context0,
    context1,
    context2,
    context3,
    text,
    cotangent,
    vectors,
    inner_bias,
    inner_shard,
    outer_shard,
    output_shard,
    near_own,
    near_other,
    far_own,
    far_other,
    result,
    grad_sum,
    grad_context,
    kept,
    sent_far,
    sent_near,
    inner_w,
    outer_w,
    output_w,
    hidden,
    slope,
    inner_g,
    outer_g,
    output_g,
    small,
    sums,
    in_sems,
    out_sems,
):
    bf16, f32 = jnp.bfloat16, jnp.float32
    chip, core, wa = place[0], place[1], place[2]
    tok, dmod = result.shape
    ff = hidden.shape[1]
    group = dmod // CHIPS
    parts = CHIPS
    rows = dmod // parts
    half = rows // 2
    quarter = rows // CHIPS
    slot_w = ff // (2 * CHIPS)

    context = (context0, context1, context2, context3)

    def head_rows(m):
        return pl.ds(pl.multiple_of(group * jnp.bitwise_xor(chip, m), 64), group)

    pltpu.make_async_copy(
        output_shard, output_w.at[pl.ds(pl.multiple_of(rows * wa, 16), rows), :], in_sems.at[0]
    ).start()
    pltpu.make_async_copy(
        inner_shard, inner_w.at[pl.ds(pl.multiple_of(rows * wa, 16), rows), :], in_sems.at[1]
    ).start()
    pltpu.make_async_copy(
        outer_shard, outer_w.at[pl.ds(pl.multiple_of(dmod * wa, 16), dmod), :], in_sems.at[2]
    ).start()

    def fetch(m, unused):
        g = jnp.bitwise_xor(chip, m)
        for source, side, far in (
            (near_own, core, 0),
            (near_other, 1 - core, 0),
            (far_own, core, 1),
            (far_other, 1 - core, 1),
        ):
            s = 2 * g + side
            for u in range(2 - far):
                z = lax.rem(wa - 1 - far - 2 * u + parts, parts)
                piece = source.at[m] if far else source.at[m, u]
                pltpu.make_async_copy(
                    piece.at[pl.ds(2 * rows, quarter), :],
                    output_w.at[
                        pl.ds(pl.multiple_of(rows * z + quarter * g, 16), quarter),
                        pl.ds(pl.multiple_of(slot_w * side, TILE), slot_w),
                    ],
                    in_sems.at[0],
                ).start()
                pltpu.make_async_copy(
                    piece.at[pl.ds(0, rows), :],
                    inner_w.at[
                        pl.ds(pl.multiple_of(rows * z, 16), rows),
                        pl.ds(pl.multiple_of(slot_w * s, TILE), slot_w),
                    ],
                    in_sems.at[1],
                ).start()
                for v in range(2):
                    pltpu.make_async_copy(
                        piece.at[pl.ds(rows + half * v, half), :],
                        outer_w.at[
                            pl.ds(pl.multiple_of(dmod * z + half * s, 16), half),
                            pl.ds(slot_w * v, slot_w),
                        ],
                        in_sems.at[2],
                    ).start()
        return 0

    lax.fori_loop(0, CHIPS, fetch, 0)
    names = ("outb", "g1", "s1", "outerb", "g2", "s2")
    vec = {name: vectors[k : k + 1, :] for k, name in enumerate(names)}

    pltpu.make_async_copy(output_w, output_w, in_sems.at[0]).wait()
    branch = vec["outb"]
    for m in range(CHIPS):
        branch = branch + plain_product(context[m][...], output_w[head_rows(m), :])
    first, unit_one, inverse_one = normed(text[:tok, :].astype(f32) + branch, vec["g1"], vec["s1"])
    low = first.astype(bf16)

    pltpu.make_async_copy(inner_w, inner_w, in_sems.at[1]).wait()
    pltpu.make_async_copy(outer_w, outer_w, in_sems.at[2]).wait()

    def forward(s, ffn):
        at = pl.ds(pl.multiple_of(slot_w * s, TILE), slot_w)
        inner = plain_product(low, inner_w[:, at]) + inner_bias[:, at]
        cdf = 0.5 + 0.5 * lax.erf(inner * (0.5**0.5))
        active = (inner * cdf).astype(bf16)
        hidden[:, at] = active
        slope[:, at] = cdf + inner * (jnp.exp(-0.5 * inner * inner) * (0.5 / jnp.pi) ** 0.5)
        return ffn + plain_product(active, outer_w[at, :])

    ffn = lax.fori_loop(0, 2 * CHIPS, forward, jnp.broadcast_to(vec["outerb"], (tok, dmod)))
    second, unit_two, inverse_two = normed(first + ffn, vec["g2"], vec["s2"])
    result[...] = second.astype(bf16)
    grad_out = cotangent[...].astype(f32)
    grad_two = normed_back(grad_out, unit_two, inverse_two, vec["g2"])
    low_two = grad_two.astype(bf16)

    sums[...] = jnp.zeros_like(sums)

    def put(row, value):
        for v in range(2):
            for z in range(parts):
                sums[z, row + v : row + v + 1, :] = value[:, slot_w * v : slot_w * (v + 1)]

    put(6, summed_rows(low_two.astype(f32)))
    put(8, summed_rows(grad_out * unit_two))
    put(10, summed_rows(grad_out))
    low_turned = low.astype(f32).T.astype(bf16)

    def backward(s, grad_first):
        at = pl.ds(pl.multiple_of(slot_w * s, TILE), slot_w)
        grad_hidden = lanes_product(low_two, outer_w[at, :])
        grad_inner = (grad_hidden * slope[:, at]).astype(bf16)
        outer_g[at, :] = rows_product(hidden[:, at], low_two).astype(bf16)
        inner_g[:, at] = plain_product(low_turned, grad_inner).astype(bf16)
        sums[s // 2, pl.ds(12 + lax.rem(s, 2), 1), :] = summed_rows(grad_inner.astype(f32))
        return grad_first + lanes_product(grad_inner, inner_w[:, at])

    grad_first = lax.fori_loop(0, 2 * CHIPS, backward, grad_two)

    def targets():
        for m in range(CHIPS):
            far = sent_far if m == CHIPS - 1 else sent_near.at[m]
            for target, side, sem in ((kept.at[m], core, 0), (far, 1 - core, 1 + (m < CHIPS - 1))):
                yield target, jnp.bitwise_xor(chip, m), side, sem

    inner_view = inner_g.reshape(parts, rows, ff)
    outer_view = outer_g.reshape(parts, dmod, dmod)
    output_view = output_g.reshape(parts, rows, dmod)
    for target, g, side, sem in targets():
        s = 2 * g + side
        pltpu.make_async_copy(
            inner_view.at[:, :, pl.ds(pl.multiple_of(slot_w * s, TILE), slot_w)],
            target.at[:, pl.ds(0, rows), :],
            out_sems.at[sem],
        ).start()
        for v in range(2):
            pltpu.make_async_copy(
                outer_view.at[:, pl.ds(pl.multiple_of(half * s, 16), half), pl.ds(slot_w * v, slot_w)],
                target.at[:, pl.ds(rows + half * v, half), :],
                out_sems.at[sem],
            ).start()

    put(2, summed_rows(grad_first * unit_one))
    put(4, summed_rows(grad_first))
    grad_one = normed_back(grad_first, unit_one, inverse_one, vec["g1"])
    grad_sum[...] = grad_one
    low_one = grad_one.astype(bf16)
    put(0, summed_rows(low_one.astype(f32)))
    small[0] = jnp.zeros_like(small[0])
    small[1] = sums[...].astype(bf16)
    for m in range(CHIPS):
        at = head_rows(m)
        output_g[at, :] = rows_product(context[m][...], low_one).astype(bf16)
        grad_context[m] = lanes_product(low_one, output_w[at, :]).astype(bf16)
    for target, g, side, sem in targets():
        pltpu.make_async_copy(
            output_view.at[
                :,
                pl.ds(pl.multiple_of(quarter * g, 16), quarter),
                pl.ds(pl.multiple_of(slot_w * side, TILE), slot_w),
            ],
            target.at[:, pl.ds(2 * rows, quarter), :],
            out_sems.at[sem],
        ).start()
        filled = jnp.where(2 * g + side == 0, 1, 0)
        pltpu.make_async_copy(
            small.at[filled], target.at[:, pl.ds(2 * rows + quarter, TAG_ROWS), :], out_sems.at[sem]
        ).start()
    for sem, target in enumerate((kept, sent_far, sent_near)):
        pltpu.make_async_copy(target, target, out_sems.at[sem]).wait()


def head_grads_kernel(place, tokens, dq, dkv_own, dkv_other, dkv, kept, sent, acc):
    tok = dq.shape[1]
    core = place[1]
    wide = dq.shape[2]
    parts, rows = kept.shape[0], kept.shape[1] - TAG_ROWS
    acc[...] = jnp.zeros_like(acc)

    def piece(m, carry):
        text = tokens[m, :tok]
        both = dkv_own[m].astype(jnp.float32) + dkv_other[m].astype(jnp.float32)
        dkv[m] = both.astype(jnp.bfloat16)
        text_turned = text.astype(jnp.float32).T.astype(jnp.bfloat16)
        acc[:, :wide] += plain_product(text_turned, dq[m])
        acc[:, wide:] += plain_product(text_turned, dkv[m])
        return (
            carry[0] + summed_rows(dq[m].astype(jnp.float32)),
            carry[1] + summed_rows(dkv[m].astype(jnp.float32)),
        )

    start = (jnp.zeros((1, wide), jnp.float32), jnp.zeros((1, wide // 2), jnp.float32))
    sums = jnp.concatenate(lax.fori_loop(0, CHIPS, piece, start), axis=1)
    sums = jnp.broadcast_to(sums, (TAG_ROWS, sums.shape[1]))
    for z in range(parts):
        for target, side in ((kept, core), (sent, 1 - core)):
            at = pl.ds(pl.multiple_of(2 * rows * z + rows * side, 32), rows)
            target[z, :rows] = acc[at, :].astype(jnp.bfloat16)
            target[z, rows:] = jnp.where(side == 0, sums, 0.0).astype(jnp.bfloat16)


def token_grads_kernel(dq, dkv, weight, partial):
    wide = dq.shape[2]

    def piece(m, carry):
        partial[m] = (
            lanes_product(dq[m], weight[:, :wide]) + lanes_product(dkv[m], weight[:, wide:])
        ).astype(jnp.bfloat16)
        return carry

    lax.fori_loop(0, CHIPS, piece, 0)


def picked_piece(place, own, other, g, side, rows):
    m = jnp.bitwise_xor(place[0], g)
    here = own[m, rows, :].astype(jnp.float32)
    there = other[m, rows, :].astype(jnp.float32)
    return jnp.where(place[1] == side, here, there)


def unpack_dense_kernel(place, own, other, inner, outer, output, small):
    rows = inner.shape[0]
    half, quarter = rows // 2, rows // CHIPS
    slot_w = own.shape[2]
    for g in range(CHIPS):
        for side in range(2):
            s = 2 * g + side
            at = slice(slot_w * s, slot_w * (s + 1))
            inner[:, at] = picked_piece(place, own, other, g, side, slice(0, rows))
            for v in range(2):
                outer[half * s : half * (s + 1), slot_w * v : slot_w * (v + 1)] = picked_piece(
                    place, own, other, g, side, slice(rows + half * v, rows + half * (v + 1))
                )
            output[quarter * g : quarter * (g + 1), slot_w * side : slot_w * (side + 1)] = picked_piece(
                place, own, other, g, side, slice(2 * rows, 2 * rows + quarter)
            )
    small[...] = picked_piece(place, own, other, 0, 0, slice(2 * rows + quarter, own.shape[1]))


def unpack_heads_kernel(place, own, other, ww, we, ew, ee, key, value, sums):
    rows = own.shape[1] - TAG_ROWS
    wide = 4 * 3 * HD
    for side in range(2):
        at = slice(rows * side, rows * (side + 1))
        pieces = [picked_piece(place, own, other, g, side, slice(0, rows)) for g in range(CHIPS)]
        for k, target in enumerate((ww, we, ew, ee)):
            target[at, :] = jnp.concatenate(
                [p[:, HD * (4 * h + k) : HD * (4 * h + k + 1)] for p in pieces for h in range(3)], axis=1
            )
        for k, target in enumerate((key, value)):
            target[at, :] = jnp.concatenate(
                [
                    p[:, wide + HD * (2 * h + k) : wide + HD * (2 * h + k + 1)]
                    for p in pieces
                    for h in range(3)
                ],
                axis=1,
            )
    sums[...] = picked_piece(place, own, other, place[2], 0, slice(rows, rows + TAG_ROWS))


def smem():
    return pl.BlockSpec(memory_space=pltpu.SMEM)


def vmem():
    return pl.BlockSpec(memory_space=pltpu.VMEM)


def hbm():
    return pl.BlockSpec(memory_space=pl.ANY)


def whole_call(kernel, operands, outs, scratch=(), micros=1):
    return pl.pallas_call(
        kernel,
        out_shape=[jax.ShapeDtypeStruct(shape, dtype) for shape, dtype, _ in outs],
        in_specs=[spec() for _, spec in operands],
        out_specs=[spec() for _, _, spec in outs],
        scratch_shapes=list(scratch),
        compiler_params=pltpu.CompilerParams(vmem_limit_bytes=58 << 20),
        cost_estimate=pl.CostEstimate(
            flops=micros * FLOPS_PER_MICRO, bytes_accessed=micros << 20, transcendentals=0
        ),
    )(*(value for value, _ in operands))


def grouped_device(
    tokens,
    cotangent,
    segment_ids,
    token_types,
    query_wordword,
    query_wordentity,
    query_entityword,
    query_entityentity,
    bias_wordword,
    bias_wordentity,
    bias_entityword,
    bias_entityentity,
    key_weight,
    value_weight,
    value_bias,
    output_weight,
    output_bias,
    first_gain,
    first_bias,
    inner_weight,
    inner_bias,
    outer_weight,
    outer_bias,
    second_gain,
    second_bias,
):
    bf16, f32 = jnp.bfloat16, jnp.float32
    index = lax.axis_index("ctx")
    chip, core = index // 2, index % 2
    wa = lax.axis_index("wa")
    parts = lax.axis_size("wa")
    place = jnp.stack([chip, core, wa]).astype(jnp.int32)
    inputs = tokens[0]
    tok, dmod = inputs.shape
    length = 2 * CHIPS * tok
    rows = key_weight.shape[0]
    half, quarter = rows // 2, rows // CHIPS
    group = dmod // CHIPS
    ff = inner_weight.shape[1]
    slot_w = ff // (2 * CHIPS)

    tags = (segment_ids[0] * 2 + token_types[0]).astype(bf16)
    tag_rows = jnp.pad(tags[None], ((0, TAG_ROWS - 1), (0, dmod - tok)))
    text = jnp.concatenate([inputs, tag_rows], axis=0)
    cut = tok // 2
    text_x, text_y = swapped(text, 2), swapped(text, 4)

    def after(value, *earlier):
        return lax.optimization_barrier((value, *earlier))[0]


    lines = (
        bias_wordword,
        bias_wordentity,
        bias_entityword,
        bias_entityentity,
        value_bias,
        output_bias,
        first_gain,
        first_bias,
        outer_bias,
        second_gain,
        second_bias,
        inner_bias,
    )
    six = (query_wordword, query_wordentity, query_entityword, query_entityentity, key_weight, value_weight)
    mine, slot = whole_call(
        prepare_kernel,
        [(place, smem)]
        + [(a, vmem) for a in (*six, *lines)]
        + [(a, hbm) for a in (inner_weight, outer_weight, output_weight)],
        [((half + TAG_ROWS, 6 * group), bf16, vmem), ((2 * rows + quarter, slot_w), bf16, vmem)],
        [pltpu.SemaphoreType.DMA((4,))],
        micros=3,
    )
    one, three = turned(mine, 1), turned(mine, 3)
    text_x, text_y, one, three = lax.optimization_barrier((text_x, text_y, one, three))
    text_far = swapped(text_x[:cut], 4), swapped(text_y[cut:], 2)
    two = ring_far(one, three)
    slot = after(slot, text_x, text_y, one, three)
    slot_one, slot_three = turned(slot, 1), turned(slot, 3)
    *text_far, two, slot_one, slot_three = lax.optimization_barrier((*text_far, two, slot_one, slot_three))
    near_slot = jnp.stack([slot_one, slot_three])
    far_slot = ring_far(slot_one, slot_three)
    mine = jnp.stack([mine, one, two, three])
    theirs = swapped(mine, 1)
    order = (wa - jnp.arange(parts)) % parts
    vectors = jnp.take(mine[:, half + 1], order, axis=0).reshape(parts, 6, rows)
    vectors = jnp.pad(jnp.transpose(vectors, (1, 0, 2)).reshape(6, dmod), ((0, 2), (0, 0))).astype(f32)
    full_inner_bias = jnp.take(mine[:, half + 2, : ff // parts], order, axis=0).reshape(1, ff).astype(f32)

    weight, all_text, q, kv = whole_call(
        project_kernel,
        [(place, smem)] + [(a, vmem) for a in (text, text_x, text_y, *text_far, mine, theirs)],
        [
            ((dmod, 6 * group), bf16, vmem),
            ((CHIPS, tok + TAG_ROWS, dmod), bf16, vmem),
            ((CHIPS, tok, 2 * group), bf16, vmem),
            ((CHIPS, tok + TAG_ROWS, 2 * group), bf16, vmem),
        ],
        micros=8,
    )
    kv_other = swapped(kv, 1)
    kv_other, far_slot = lax.optimization_barrier((kv_other, far_slot))
    far_slots = [far_slot] + [swapped(far_slot, 2 * m) for m in range(1, CHIPS)]
    near_slots = [near_slot] + [swapped(near_slot, 2 * m) for m in range(1, CHIPS)]

    context, turned_out, lse, bounds = whole_call(
        attend_kernel,
        [(place, smem), (q, vmem), (kv, vmem), (kv_other, vmem)],
        [
            ((CHIPS, tok, group), bf16, vmem),
            ((CHIPS, group, tok), f32, vmem),
            ((CHIPS, 3, 1, tok), f32, vmem),
            ((2, CHIPS), jnp.int32, smem),
        ],
        [
            pltpu.VMEM((3, length, 2 * HD), bf16),
            pltpu.VMEM((3, HD, length), bf16),
            pltpu.VMEM((length, TILE), f32),
            pltpu.VMEM((2 * CHIPS, 8, tok), f32),
            pltpu.VMEM((3, HD, tok), f32),
        ],
        micros=25,
    )
    barrier = lax.optimization_barrier((context, *near_slots, *far_slots))
    context, near_slots, far_slots = barrier[0], jnp.stack(barrier[1 : 1 + CHIPS]), jnp.stack(barrier[1 + CHIPS :])
    near_slots = near_slots, swapped(near_slots, 1)
    far_slots = far_slots, swapped(far_slots, 1)

    def exchanged(value):
        return [value[0]] + [swapped(value[m], 2 * m) for m in range(1, CHIPS)]

    contexts = exchanged(context)

    slot_rows = 2 * rows + quarter + TAG_ROWS
    result, grad_sum, grad_context, kept, sent_far, sent_near = whole_call(
        dense_kernel,
        [(place, smem)]
        + [(a, vmem) for a in (*contexts, text, cotangent[0], vectors, full_inner_bias)]
        + [
            (a, hbm)
            for a in (inner_weight, outer_weight, output_weight, *near_slots, *far_slots)
        ],
        [
            ((tok, dmod), bf16, vmem),
            ((tok, dmod), f32, vmem),
            ((CHIPS, tok, group), bf16, vmem),
            ((CHIPS, parts, slot_rows, slot_w), bf16, hbm),
            ((parts, slot_rows, slot_w), bf16, hbm),
            ((CHIPS - 1, parts, slot_rows, slot_w), bf16, hbm),
        ],
        [
            pltpu.VMEM((dmod, ff), bf16),
            pltpu.VMEM((ff, dmod), bf16),
            pltpu.VMEM((dmod, dmod), bf16),
            pltpu.VMEM((tok, ff), bf16),
            pltpu.VMEM((tok, ff), f32),
            pltpu.VMEM((dmod, ff), bf16),
            pltpu.VMEM((ff, dmod), bf16),
            pltpu.VMEM((dmod, dmod), bf16),
            pltpu.VMEM((2, parts, TAG_ROWS, slot_w), bf16),
            pltpu.VMEM((parts, TAG_ROWS, slot_w), f32),
            pltpu.SemaphoreType.DMA((3,)),
            pltpu.SemaphoreType.DMA((3,)),
        ],
        micros=35,
    )
    grad_pieces = exchanged(grad_context)

    def added(*values):
        total = values[0].astype(f32)
        for v in values[1:]:
            total = total + v.astype(f32)
        return total

    middle = parts // 2
    upper, lower = slice(0, middle), slice(middle, None)
    received_far = swapped(sent_far, 1)
    received = swapped(sent_near, 1)
    far_x = added(kept[CHIPS - 1, upper], received_far[upper]).astype(bf16)
    far_y = added(kept[CHIPS - 1, lower], received_far[lower]).astype(bf16)
    near_x = added(kept[1, upper], received[1, upper]).astype(bf16)
    near_y = added(kept[2, lower], received[2, lower]).astype(bf16)
    *grad_pieces, far_x, far_y, near_x, near_y = lax.optimization_barrier(
        (*grad_pieces, far_x, far_y, near_x, near_y)
    )
    far_x, far_y = swapped(far_x, 2), swapped(far_y, 4)
    near_x, near_y = swapped(near_x, 2), swapped(near_y, 4)

    dq, dkv, dkv_sent = whole_call(
        attend_back_kernel,
        [(place, smem), (bounds, smem)]
        + [(a, vmem) for a in (q, kv, kv_other, turned_out, lse, *grad_pieces)],
        [
            ((CHIPS, tok, 4 * group), bf16, vmem),
            ((CHIPS, tok, 2 * group), bf16, vmem),
            ((CHIPS, tok, 2 * group), bf16, vmem),
        ],
        [
            pltpu.VMEM((3, length, 2 * HD), bf16),
            pltpu.VMEM((3, 2 * HD, length), bf16),
            pltpu.VMEM((3, length, 2 * HD), bf16),
            pltpu.VMEM((3, length, 2 * HD), f32),
            pltpu.VMEM((3, length, 2 * HD), f32),
            pltpu.VMEM((length, TILE), f32),
            pltpu.VMEM((2 * CHIPS, 8, tok), f32),
            pltpu.VMEM((3, 2 * HD, tok), f32),
            pltpu.VMEM((CHIPS, tok, group), bf16),
        ],
        micros=40,
    )
    dq, dkv, dkv_sent, far_x, far_y, near_x, near_y = lax.optimization_barrier(
        (dq, dkv, dkv_sent, far_x, far_y, near_x, near_y)
    )
    dkv_received = swapped(dkv_sent, 1)
    last_x = added(kept[1, lower], received[1, lower], far_y).astype(bf16)
    last_y = added(kept[2, upper], received[2, upper], far_x).astype(bf16)
    last_x, last_y = lax.optimization_barrier((last_x, last_y))
    last_x, last_y = swapped(last_x, 2), swapped(last_y, 4)
    dkv, head_kept, head_sent = whole_call(
        head_grads_kernel,
        [(place, smem)] + [(a, vmem) for a in (all_text, dq, dkv, dkv_received)],
        [
            ((CHIPS, tok, 2 * group), bf16, vmem),
            ((parts, half + TAG_ROWS, 6 * group), bf16, vmem),
            ((parts, half + TAG_ROWS, 6 * group), bf16, vmem),
        ],
        [pltpu.VMEM((dmod, 6 * group), f32)],
        micros=10,
    )
    head_received = swapped(head_sent, 1)
    (partial,) = whole_call(
        token_grads_kernel,
        [(a, vmem) for a in (dq, dkv, weight)],
        [((CHIPS, tok, dmod), bf16, vmem)],
        micros=8,
    )
    partial, head_received = lax.optimization_barrier((partial, head_received))

    def parts_sent(value):
        kept_part = lax.dynamic_index_in_dim(value, wa, 0, keepdims=False)
        return [kept_part] + [
            lax.dynamic_index_in_dim(value, (wa + k) % parts, 0, keepdims=False) for k in range(1, parts)
        ]

    def parts_moved(values):
        return [turned(v, k) for k, v in enumerate(values) if k]

    def chips_moved(value):
        return [swapped(value, 2 * m) for m in range(1, CHIPS)]

    low, high = slice(0, cut), slice(cut, None)
    head_parts = parts_sent(added(head_kept, head_received).astype(bf16))
    text_sent = [partial[3, low], partial[3, high], partial[1, low], partial[2, high]]
    barrier = lax.optimization_barrier((*head_parts, *text_sent))
    head_parts, text_sent = barrier[:parts], barrier[parts:]
    head_moved = parts_moved(head_parts)
    text_moved = [swapped(v, 2 << (k % 2)) for k, v in enumerate(text_sent)]
    barrier = lax.optimization_barrier((*head_moved, *text_moved, last_x, last_y))
    head_moved, text_moved, last_x, last_y = barrier[:3], barrier[3:7], barrier[7], barrier[8]

    summed = jnp.concatenate(
        [
            added(kept[0, upper], received[0, upper], near_x, last_y),
            added(kept[0, lower], received[0, lower], last_x, near_y),
        ],
        axis=0,
    ).astype(bf16)
    dense_parts = parts_sent(summed)
    far_x, far_y, near_x, near_y = text_moved
    text_x = added(partial[1, high], far_y).astype(bf16)
    text_y = added(partial[2, low], far_x).astype(bf16)
    head_summed = added(head_parts[0], *head_moved).astype(bf16)
    barrier = lax.optimization_barrier((*dense_parts, text_x, text_y, head_summed))
    dense_parts, text_x, text_y, head_summed = barrier[:parts], *barrier[parts:]
    dense_moved = parts_moved(dense_parts)
    text_x, text_y = swapped(text_x, 2), swapped(text_y, 4)
    head_moved = chips_moved(head_summed)
    barrier = lax.optimization_barrier((*dense_moved, text_x, text_y, *head_moved))
    dense_moved, text_x, text_y, head_moved = barrier[:3], barrier[3], barrier[4], barrier[5:]

    dense_summed = added(dense_parts[0], *dense_moved).astype(bf16)
    head_all = jnp.stack([head_summed, *head_moved])
    dense_summed, head_all = lax.optimization_barrier((dense_summed, head_all))
    dense_moved = chips_moved(dense_summed)
    *out_heads, sums = whole_call(
        unpack_heads_kernel,
        [(place, smem), (head_all, vmem), (swapped(head_all, 1), vmem)],
        [((rows, dmod), f32, vmem) for _ in range(6)] + [((TAG_ROWS, 6 * group), f32, vmem)],
        micros=4,
    )
    input_grads = grad_sum + jnp.concatenate(
        [added(partial[0, low], near_x, text_y), added(partial[0, high], text_x, near_y)], axis=0
    )
    *dense_moved, input_grads = lax.optimization_barrier((*dense_moved, input_grads))
    dense_all = jnp.stack([dense_summed, *dense_moved])
    out_inner, out_outer, out_output, small = whole_call(
        unpack_dense_kernel,
        [(place, smem), (dense_all, vmem), (swapped(dense_all, 1), vmem)],
        [
            ((rows, ff), f32, vmem),
            (outer_weight.shape, f32, vmem),
            ((rows, dmod), f32, vmem),
            ((TAG_ROWS, slot_w), f32, vmem),
        ],
        micros=4,
    )

    sum_q = sums[0, : 4 * group].reshape(3, 4, HD)
    sum_v = sums[0, 4 * group :].reshape(3, 2, HD)[:, 1].reshape(rows)
    own_small = lax.dynamic_slice(small[:12].reshape(6, dmod), (0, wa * rows), (6, rows))
    return (
        result[None],
        input_grads[None],
        *out_heads[:4],
        *(sum_q[:, k].reshape(rows) for k in range(4)),
        *out_heads[4:],
        sum_v,
        out_output,
        own_small[0],
        own_small[1],
        own_small[2],
        out_inner,
        small[12:14].reshape(ff // parts),
        out_outer,
        own_small[3],
        own_small[4],
        own_small[5],
    )


def solution(mesh):
    in_specs = (
        P("wa", "ctx", None),
        P("wa", "ctx", None),
        P("wa", "ctx"),
        P("wa", "ctx"),
        P("wa", None),
        P("wa", None),
        P("wa", None),
        P("wa", None),
        P("wa"),
        P("wa"),
        P("wa"),
        P("wa"),
        P("wa", None),
        P("wa", None),
        P("wa"),
        P("wa", None),
        P("wa"),
        P("wa"),
        P("wa"),
        P("wa", None),
        P("wa"),
        P("wa", None),
        P("wa"),
        P("wa"),
        P("wa"),
    )
    out_specs = (
        P("wa", "ctx", None),
        P("wa", "ctx", None),
        P("wa", None),
        P("wa", None),
        P("wa", None),
        P("wa", None),
        P("wa"),
        P("wa"),
        P("wa"),
        P("wa"),
        P("wa", None),
        P("wa", None),
        P("wa"),
        P("wa", None),
        P("wa"),
        P("wa"),
        P("wa"),
        P("wa", None),
        P("wa"),
        P("wa", None),
        P("wa"),
        P("wa"),
        P("wa"),
    )
    body = grouped_device if mesh.shape["ctx"] == 2 * CHIPS else windowed_device
    return jax.shard_map(
        body, mesh=mesh, in_specs=in_specs, out_specs=out_specs, check_vma=False
    )
```

```python
import jax
import jax.numpy as jnp
from jax import lax
from jax.experimental import pallas as pl
from jax.experimental.pallas import tpu as pltpu
from jax.sharding import PartitionSpec as P

HD = 64


EPSILON = 1e-12
MASKED = -1e30


def as_sent(shard):
    return jax.tree.map(lambda a: a.astype(jnp.bfloat16) if a.dtype == jnp.float32 else a, shard)


def passed_along(value, axis, steps):
    count = lax.axis_size(axis)
    leading, last = (max(0, -steps), min(count, count - steps))
    return lax.ppermute(value, axis, [(source, source + steps) for source in range(leading, last)])


def layer_norm(values, gain, shift):
    center = values - jnp.mean(values, axis=-1, keepdims=True)
    spread = jnp.mean(center * center, axis=-1, keepdims=True)
    return center * lax.rsqrt(spread + EPSILON) * gain + shift


def gelu_exact(values):
    return jax.nn.gelu(values, approximate=False)


def matmul(left, right):
    return jnp.dot(left, right, preferred_element_type=jnp.float32)


def left_product(left, right):
    return lax.dot_general(
        left, right, (((0,), (0,)), ((), ())), preferred_element_type=jnp.float32
    )


def right_product(left, right):
    return lax.dot_general(
        left, right, (((1,), (1,)), ((), ())), preferred_element_type=jnp.float32
    )


def column_sums(values):
    return jnp.sum(values.astype(jnp.float32), axis=0)


def columns(values, start):
    return lax.dynamic_slice_in_dim(values, start, HD, 1)


def head_scores(query_word, query_entity, keys_head, key_entity, allowed, scale):
    word_scores = right_product(query_word, keys_head)
    entity_scores = right_product(query_entity, keys_head)
    raw = jnp.where(key_entity[None, :], entity_scores, word_scores) * scale
    return jnp.where(allowed, raw, MASKED)


def merge_heads(stacked):
    return jnp.transpose(stacked, (1, 0, 2)).reshape(
        stacked.shape[1], stacked.shape[0] * stacked.shape[2]
    )


def windowed_device(
    tokens,
    cotangent,
    segment_ids,
    token_types,
    query_wordword,
    query_wordentity,
    query_entityword,
    query_entityentity,
    bias_wordword,
    bias_wordentity,
    bias_entityword,
    bias_entityentity,
    key_weight,
    value_weight,
    value_bias,
    output_weight,
    output_bias,
    first_gain,
    first_bias,
    inner_weight,
    inner_bias,
    outer_weight,
    outer_bias,
    second_gain,
    second_bias,
):
    attention = (
        lax.all_gather(query_wordword, "wa", axis=0, tiled=True),
        lax.all_gather(query_wordentity, "wa", axis=0, tiled=True),
        lax.all_gather(query_entityword, "wa", axis=0, tiled=True),
        lax.all_gather(query_entityentity, "wa", axis=0, tiled=True),
        lax.all_gather(bias_wordword, "wa", axis=0, tiled=True),
        lax.all_gather(bias_wordentity, "wa", axis=0, tiled=True),
        lax.all_gather(bias_entityword, "wa", axis=0, tiled=True),
        lax.all_gather(bias_entityentity, "wa", axis=0, tiled=True),
        lax.all_gather(key_weight, "wa", axis=0, tiled=True),
        lax.all_gather(value_weight, "wa", axis=0, tiled=True),
        lax.all_gather(value_bias, "wa", axis=0, tiled=True),
        lax.all_gather(output_weight, "wa", axis=0, tiled=True),
        lax.all_gather(output_bias, "wa", axis=0, tiled=True),
        lax.all_gather(first_gain, "wa", axis=0, tiled=True),
        lax.all_gather(first_bias, "wa", axis=0, tiled=True),
    )
    (
        full_ww,
        full_we,
        full_ew,
        full_ee,
        shift_ww,
        shift_we,
        shift_ew,
        shift_ee,
        full_key,
        full_value,
        shift_value,
        full_output,
        shift_output,
        gain_one,
        shift_one,
    ) = attention
    feedforward = (
        lax.all_gather(inner_weight, "wa", axis=0, tiled=True),
        lax.all_gather(inner_bias, "wa", axis=0, tiled=True),
        lax.all_gather(outer_weight, "wa", axis=0, tiled=True),
        lax.all_gather(outer_bias, "wa", axis=0, tiled=True),
        lax.all_gather(second_gain, "wa", axis=0, tiled=True),
        lax.all_gather(second_bias, "wa", axis=0, tiled=True),
    )
    full_inner, shift_inner, full_outer, shift_outer, gain_two, shift_two = feedforward
    inputs = tokens[0]
    seg = segment_ids[0]
    types = token_types[0]
    tok = inputs.shape[0]
    dmod = inputs.shape[1]
    heads = dmod // HD
    scale = HD ** (-0.5)
    length = tok * lax.axis_size("ctx")
    doc_max = min(2048, 4 * tok, length // 2)
    reach = (doc_max - 2) // tok + 1
    entity = (types == 1)[:, None]
    proj_ww = matmul(inputs, full_ww) + shift_ww
    proj_we = matmul(inputs, full_we) + shift_we
    proj_ew = matmul(inputs, full_ew) + shift_ew
    proj_ee = matmul(inputs, full_ee) + shift_ee
    query_word = jnp.where(entity, proj_ew, proj_ww).astype(jnp.bfloat16)
    query_entity = jnp.where(entity, proj_ee, proj_we).astype(jnp.bfloat16)
    keys = matmul(inputs, full_key).astype(jnp.bfloat16)
    values = (matmul(inputs, full_value) + shift_value).astype(jnp.bfloat16)
    own_kv = jnp.concatenate([keys, values], axis=1)
    own_seg = seg + 1
    tags = own_seg * 2 + types

    def pass_left(packet, unused):
        moved = jax.tree.map(
            lambda part, own: part.astype(own.dtype),
            passed_along(as_sent(packet), "ctx", 1),
            packet,
        )
        return (moved, moved)

    def pass_right(packet, unused):
        moved = jax.tree.map(
            lambda part, own: part.astype(own.dtype),
            passed_along(as_sent(packet), "ctx", -1),
            packet,
        )
        return (moved, moved)

    _, (left_kv, left_tags) = lax.scan(pass_left, (own_kv, tags), None, length=reach)
    _, (right_kv, right_tags) = lax.scan(pass_right, (own_kv, tags), None, length=reach)
    window = jnp.concatenate(
        [jnp.flip(left_kv, 0).reshape(-1, 2 * dmod), own_kv, right_kv.reshape(-1, 2 * dmod)], axis=0
    )
    window_tags = jnp.concatenate(
        [jnp.flip(left_tags, 0).reshape(-1), tags, right_tags.reshape(-1)], axis=0
    )
    key_entity = window_tags % 2 == 1
    allowed = own_seg[:, None] == (window_tags // 2)[None, :]

    def head_forward(index):
        start = index * HD
        scores = head_scores(
            columns(query_word, start),
            columns(query_entity, start),
            columns(window, start),
            key_entity,
            allowed,
            scale,
        )
        top = jnp.max(scores, axis=1, keepdims=True)
        expo = jnp.exp(scores - top)
        total = jnp.sum(expo, axis=1, keepdims=True)
        probs = (expo / total).astype(jnp.bfloat16)
        return (matmul(probs, columns(window, dmod + start)), (top + jnp.log(total))[:, 0])

    head_context, lse = lax.map(head_forward, jnp.arange(heads))
    context = merge_heads(head_context).astype(jnp.bfloat16)
    branch = matmul(context, full_output) + shift_output
    first, pull_one = jax.vjp(
        layer_norm,
        inputs.astype(jnp.float32) + branch,
        gain_one.astype(jnp.float32),
        shift_one.astype(jnp.float32),
    )
    first_low = first.astype(jnp.bfloat16)
    inner = matmul(first_low, full_inner) + shift_inner
    activated, pull_gelu = jax.vjp(gelu_exact, inner)
    hidden = activated.astype(jnp.bfloat16)
    ffn = matmul(hidden, full_outer) + shift_outer
    result, pull_two = jax.vjp(
        layer_norm, first + ffn, gain_two.astype(jnp.float32), shift_two.astype(jnp.float32)
    )
    grad_sum_two, grad_gain_two, grad_shift_two = pull_two(cotangent[0].astype(jnp.float32))
    grad_ffn = grad_sum_two.astype(jnp.bfloat16)
    grad_outer = left_product(hidden, grad_ffn)
    grad_outer_shift = column_sums(grad_ffn)
    grad_inner = pull_gelu(right_product(grad_ffn, full_outer))[0].astype(jnp.bfloat16)
    grad_inner_full = left_product(first_low, grad_inner)
    grad_inner_shift = column_sums(grad_inner)
    grad_first = grad_sum_two + right_product(grad_inner, full_inner)
    grad_sum_one, grad_gain_one, grad_shift_one = pull_one(grad_first)
    grad_branch = grad_sum_one.astype(jnp.bfloat16)
    grad_output = left_product(context, grad_branch)
    grad_output_shift = column_sums(grad_branch)
    grad_context = right_product(grad_branch, full_output).astype(jnp.bfloat16)

    def head_backward(index):
        start = index * HD
        word_head = columns(query_word, start)
        entity_head = columns(query_entity, start)
        keys_head = columns(window, start)
        values_head = columns(window, dmod + start)
        context_head = columns(grad_context, start)
        scores = head_scores(word_head, entity_head, keys_head, key_entity, allowed, scale)
        probs = jnp.exp(scores - lse[index][:, None])
        grad_probs = right_product(context_head, values_head)
        delta = jnp.sum(probs * grad_probs, axis=1)
        grad_scores = (probs * (grad_probs - delta[:, None])).astype(jnp.bfloat16)
        zero = jnp.zeros_like(grad_scores)
        grad_word = jnp.where(key_entity[None, :], zero, grad_scores)
        grad_entity = jnp.where(key_entity[None, :], grad_scores, zero)
        grad_qword = matmul(grad_word, keys_head) * scale
        grad_qentity = matmul(grad_entity, keys_head) * scale
        grad_keys = (
            left_product(grad_word, word_head) + left_product(grad_entity, entity_head)
        ) * scale
        grad_values = left_product(probs.astype(jnp.bfloat16), context_head)
        return (grad_qword, grad_qentity, delta, grad_keys, grad_values)

    grad_qword, grad_qentity, delta, window_keys, window_values = lax.map(
        lambda index: head_backward(index), jnp.arange(heads)
    )
    parts_keys = merge_heads(window_keys).reshape(2 * reach + 1, tok, dmod)
    parts_values = merge_heads(window_values).reshape(2 * reach + 1, tok, dmod)

    def back_left(total, piece):
        return (
            (
                passed_along((total[0] + piece[0]).astype(jnp.bfloat16), "ctx", -1).astype(
                    jnp.float32
                ),
                passed_along((total[1] + piece[1]).astype(jnp.bfloat16), "ctx", -1).astype(
                    jnp.float32
                ),
            ),
            None,
        )

    def back_right(total, piece):
        return (
            (
                passed_along((total[0] + piece[0]).astype(jnp.bfloat16), "ctx", 1).astype(
                    jnp.float32
                ),
                passed_along((total[1] + piece[1]).astype(jnp.bfloat16), "ctx", 1).astype(
                    jnp.float32
                ),
            ),
            None,
        )

    empty = jnp.zeros((tok, dmod), jnp.float32)
    from_above, _ = lax.scan(back_left, (empty, empty), (parts_keys[:reach], parts_values[:reach]))
    from_below, _ = lax.scan(
        back_right,
        (empty, empty),
        (jnp.flip(parts_keys[reach + 1 :], 0), jnp.flip(parts_values[reach + 1 :], 0)),
    )
    own_keys = parts_keys[reach] + from_above[0] + from_below[0]
    own_values = parts_values[reach] + from_above[1] + from_below[1]
    grad_keys = own_keys.astype(jnp.bfloat16)
    grad_values = own_values.astype(jnp.bfloat16)
    grad_qword = merge_heads(grad_qword).astype(jnp.bfloat16)
    grad_qentity = merge_heads(grad_qentity).astype(jnp.bfloat16)
    zeros = jnp.zeros_like(grad_qword)
    grad_pww = jnp.where(entity, zeros, grad_qword)
    grad_pew = jnp.where(entity, grad_qword, zeros)
    grad_pwe = jnp.where(entity, zeros, grad_qentity)
    grad_pee = jnp.where(entity, grad_qentity, zeros)
    input_grads = grad_sum_one + right_product(grad_pww, full_ww) + right_product(grad_pwe, full_we)
    input_grads = input_grads + right_product(grad_pew, full_ew) + right_product(grad_pee, full_ee)
    input_grads = (
        input_grads + right_product(grad_keys, full_key) + right_product(grad_values, full_value)
    )
    local_grads = (
        left_product(inputs, grad_pww),
        left_product(inputs, grad_pwe),
        left_product(inputs, grad_pew),
        left_product(inputs, grad_pee),
        column_sums(grad_pww),
        column_sums(grad_pwe),
        column_sums(grad_pew),
        column_sums(grad_pee),
        left_product(inputs, grad_keys),
        left_product(inputs, grad_values),
        column_sums(grad_values),
        grad_output,
        grad_output_shift,
        grad_gain_one,
        grad_shift_one,
        grad_inner_full,
        grad_inner_shift,
        grad_outer,
        grad_outer_shift,
        grad_gain_two,
        grad_shift_two,
    )
    shards = (
        lax.psum_scatter(
            local_grads[0].astype(jnp.bfloat16), "wa", scatter_dimension=0, tiled=True
        ).astype(jnp.float32),
        lax.psum_scatter(
            local_grads[1].astype(jnp.bfloat16), "wa", scatter_dimension=0, tiled=True
        ).astype(jnp.float32),
        lax.psum_scatter(
            local_grads[2].astype(jnp.bfloat16), "wa", scatter_dimension=0, tiled=True
        ).astype(jnp.float32),
        lax.psum_scatter(
            local_grads[3].astype(jnp.bfloat16), "wa", scatter_dimension=0, tiled=True
        ).astype(jnp.float32),
        lax.psum_scatter(
            local_grads[4].astype(jnp.bfloat16), "wa", scatter_dimension=0, tiled=True
        ).astype(jnp.float32),
        lax.psum_scatter(
            local_grads[5].astype(jnp.bfloat16), "wa", scatter_dimension=0, tiled=True
        ).astype(jnp.float32),
        lax.psum_scatter(
            local_grads[6].astype(jnp.bfloat16), "wa", scatter_dimension=0, tiled=True
        ).astype(jnp.float32),
        lax.psum_scatter(
            local_grads[7].astype(jnp.bfloat16), "wa", scatter_dimension=0, tiled=True
        ).astype(jnp.float32),
        lax.psum_scatter(
            local_grads[8].astype(jnp.bfloat16), "wa", scatter_dimension=0, tiled=True
        ).astype(jnp.float32),
        lax.psum_scatter(
            local_grads[9].astype(jnp.bfloat16), "wa", scatter_dimension=0, tiled=True
        ).astype(jnp.float32),
        lax.psum_scatter(
            local_grads[10].astype(jnp.bfloat16), "wa", scatter_dimension=0, tiled=True
        ).astype(jnp.float32),
        lax.psum_scatter(
            local_grads[11].astype(jnp.bfloat16), "wa", scatter_dimension=0, tiled=True
        ).astype(jnp.float32),
        lax.psum_scatter(
            local_grads[12].astype(jnp.bfloat16), "wa", scatter_dimension=0, tiled=True
        ).astype(jnp.float32),
        lax.psum_scatter(
            local_grads[13].astype(jnp.bfloat16), "wa", scatter_dimension=0, tiled=True
        ).astype(jnp.float32),
        lax.psum_scatter(
            local_grads[14].astype(jnp.bfloat16), "wa", scatter_dimension=0, tiled=True
        ).astype(jnp.float32),
        lax.psum_scatter(
            local_grads[15].astype(jnp.bfloat16), "wa", scatter_dimension=0, tiled=True
        ).astype(jnp.float32),
        lax.psum_scatter(
            local_grads[16].astype(jnp.bfloat16), "wa", scatter_dimension=0, tiled=True
        ).astype(jnp.float32),
        lax.psum_scatter(
            local_grads[17].astype(jnp.bfloat16), "wa", scatter_dimension=0, tiled=True
        ).astype(jnp.float32),
        lax.psum_scatter(
            local_grads[18].astype(jnp.bfloat16), "wa", scatter_dimension=0, tiled=True
        ).astype(jnp.float32),
        lax.psum_scatter(
            local_grads[19].astype(jnp.bfloat16), "wa", scatter_dimension=0, tiled=True
        ).astype(jnp.float32),
        lax.psum_scatter(
            local_grads[20].astype(jnp.bfloat16), "wa", scatter_dimension=0, tiled=True
        ).astype(jnp.float32),
    )
    totals = lax.psum(
        (
            shards[0],
            shards[1],
            shards[2],
            shards[3],
            shards[4],
            shards[5],
            shards[6],
            shards[7],
            shards[8],
            shards[9],
            shards[10],
            shards[11],
            shards[12],
            shards[13],
            shards[14],
            shards[15],
            shards[16],
            shards[17],
            shards[18],
            shards[19],
            shards[20],
        ),
        "ctx",
    )
    return (
        result.astype(jnp.bfloat16)[None],
        input_grads[None],
        totals[0],
        totals[1],
        totals[2],
        totals[3],
        totals[4],
        totals[5],
        totals[6],
        totals[7],
        totals[8],
        totals[9],
        totals[10],
        totals[11],
        totals[12],
        totals[13],
        totals[14],
        totals[15],
        totals[16],
        totals[17],
        totals[18],
        totals[19],
        totals[20],
    )


CHIPS = 4
KEY_BLOCK = 256
NEGATIVE = -1e30
TAG_ROWS = 16
TILE = 128
FLOPS_PER_MICRO = 1_100_000_000


def lanes_product(left, right):
    return lax.dot_general(
        left, right, (((1,), (1,)), ((), ())), preferred_element_type=jnp.float32
    )


def rows_product(left, right):
    return lax.dot_general(
        left, right, (((0,), (0,)), ((), ())), preferred_element_type=jnp.float32
    )


def plain_product(left, right):
    return jnp.dot(left, right, preferred_element_type=jnp.float32)


def swapped(value, step):
    count = lax.axis_size("ctx")
    return lax.ppermute(value, "ctx", [(i, i ^ step) for i in range(count)])


def turned(value, step):
    count = lax.axis_size("wa")
    return lax.ppermute(value, "wa", [(i, (i + step) % count) for i in range(count)])


def narrowed(value, width):
    return [value[:, at : at + width] for at in range(0, value.shape[1], width)]


def widened(value, count):
    rows = value.shape[0] // count
    return jnp.concatenate([value[rows * k : rows * (k + 1)] for k in range(count)], axis=1)


def ordered(*values):
    return lax.optimization_barrier(values)


def as_column(row):
    return jnp.broadcast_to(row, (TILE, row.shape[1])).T


def segment_of(tag):
    return jnp.floor(tag * 0.5)


def prepare_kernel(
    place, ww, we, ew, ee, key, value, *others
):
    *lines, inner, outer, output, mine, slot, sem = others
    rows = key.shape[0]
    half, quarter = rows // 2, rows // CHIPS
    slot_w = slot.shape[1]
    chip, core = place[0], place[1]
    index = 2 * chip + core
    copies = [
        (inner.at[:, pl.ds(pl.multiple_of(slot_w * index, TILE), slot_w)], slot.at[pl.ds(0, rows), :])
    ]
    for v in range(2):
        copies.append(
            (
                outer.at[pl.ds(pl.multiple_of(half * index, 16), half), pl.ds(slot_w * v, slot_w)],
                slot.at[pl.ds(rows + half * v, half), :],
            )
        )
    copies.append(
        (
            output.at[
                pl.ds(pl.multiple_of(quarter * chip, 16), quarter),
                pl.ds(pl.multiple_of(slot_w * core, TILE), slot_w),
            ],
            slot.at[pl.ds(2 * rows, quarter), :],
        )
    )
    copies = [pltpu.make_async_copy(a, b, sem.at[k]) for k, (a, b) in enumerate(copies)]
    for copy in copies:
        copy.start()
    at = pl.ds(pl.multiple_of(half * core, 16), half)
    for g in range(CHIPS):

        @pl.when(chip == g)
        def _():
            def heads(sources):
                return jnp.concatenate(
                    [
                        w[at, HD * (3 * g + h) : HD * (3 * g + h + 1)].astype(jnp.float32)
                        for h in range(3)
                        for w in sources
                    ],
                    axis=1,
                ).astype(jnp.bfloat16)

            mine[:half, : 4 * 3 * HD] = heads((ww, we, ew, ee))
            mine[:half, 4 * 3 * HD :] = heads((key, value))

    lines = [line[...].astype(jnp.float32).reshape(1, line.shape[0]) for line in lines]
    bias = [lines[k][:, HD * h : HD * (h + 1)] for h in range(3) for k in range(4)]
    for h in range(3):
        bias += [jnp.zeros((1, HD), jnp.float32), lines[4][:, HD * h : HD * (h + 1)]]
    six = jnp.concatenate(lines[5:11], axis=1)
    last = jnp.concatenate([lines[11], jnp.zeros((1, 2 * rows), jnp.float32)], axis=1)
    which = lax.broadcasted_iota(jnp.int32, (TAG_ROWS, 6 * rows), 0)
    below = jnp.where(which == 0, jnp.concatenate(bias, axis=1), jnp.where(which == 1, six, last))
    mine[half:] = jnp.where(which < 3, below, 0.0).astype(jnp.bfloat16)
    for copy in copies:
        copy.wait()


def project_kernel(place, t0, t1, t2, t3a, t3b, mine, theirs, weight, tokens, q_ref, kv_ref):
    parts, rows = mine.shape[0], mine.shape[1] - TAG_ROWS
    tok = q_ref.shape[1]
    chip, core, wa = place[0], place[1], place[2]
    cut = t3a.shape[0]
    tokens[0] = t0[...]
    tokens[1] = t1[...]
    tokens[2] = t2[...]
    tokens[3, :cut] = t3a[...]
    tokens[3, cut:] = t3b[...]
    for z in range(parts):
        k = lax.rem(wa - z + parts, parts)
        for source, side in ((mine, core), (theirs, 1 - core)):
            weight[pl.ds(pl.multiple_of(2 * rows * z + rows * side, 32), rows), :] = source[k, :rows]
    k = lax.rem(wa - chip + parts, parts)
    bias = mine[k, rows : rows + TAG_ROWS].astype(jnp.float32)[:1]
    wide = 2 * HD

    def piece(m, unused):
        to = jnp.bitwise_xor(chip, m)
        tags = tokens[m, tok : tok + TAG_ROWS].astype(jnp.float32)[:1, :tok]
        flag = as_column(tags - 2.0 * segment_of(tags)) == 1.0
        text = tokens[m, :tok]
        for h in range(3):
            at = 2 * wide * h
            both = plain_product(text, weight[:, at : at + 2 * wide]) + bias[:, at : at + 2 * wide]
            q = jnp.where(flag, both[:, wide:], both[:, :wide]).astype(jnp.bfloat16)
            q_ref[to, :, wide * h : wide * (h + 1)] = q * jnp.bfloat16(HD**-0.5)
        kv = plain_product(text, weight[:, 6 * wide :]) + bias[:, 6 * wide :]
        kv_ref[to, :tok] = kv.astype(jnp.bfloat16)
        kv_ref[to, tok:] = jnp.broadcast_to(tags, (TAG_ROWS, tok)).astype(jnp.bfloat16)
        return 0

    lax.fori_loop(0, CHIPS, piece, 0)


def ones_where(shape, test):
    row = lax.broadcasted_iota(jnp.int32, shape, 0)
    column = lax.broadcasted_iota(jnp.int32, shape, 1)
    return jnp.where(test(row, column), 1.0, 0.0).astype(jnp.bfloat16)


def unit(size):
    return ones_where((size, size), lambda row, column: row == column)


def attend_kernel(place, q_ref, own, other, out, turned_out, lse, bounds, keys, values, seg_col, seg_row, acc):
    tok = q_ref.shape[1]
    core = place[1]
    twice = ones_where((2 * HD, 2 * HD), lambda row, column: row == lax.rem(column, HD))
    upper = ones_where((HD, 2 * HD), lambda row, column: column == row + HD)

    def prepare(j, unused):
        for source, side in ((own, core), (other, 1 - core)):
            shard = 2 * j + side
            at = pl.ds(pl.multiple_of(shard * tok, TILE), tok)
            tags = source[j, tok : tok + TAG_ROWS].astype(jnp.float32)[:1]
            seg_row[shard] = jnp.broadcast_to(segment_of(tags), (8, tok))
            column = as_column(tags)
            segment = segment_of(column)
            seg_col[at, :] = segment
            flag = column - 2.0 * segment == 1.0
            for h in range(3):
                kv = source[j, :tok, 2 * HD * h : 2 * HD * (h + 1)]
                low = lax.broadcasted_iota(jnp.int32, kv.shape, 1) < HD
                keys[h, at, :] = jnp.where(low == flag, 0.0, plain_product(kv, twice)).astype(jnp.bfloat16)
                values[h, :, at] = lanes_product(upper, kv).astype(jnp.bfloat16)
        return 0

    lax.fori_loop(0, CHIPS, prepare, 0)

    def queries(j, unused):
        seg = seg_row[2 * j + core][:1]
        everyone = seg_row[...][:, 0, :]
        before = jnp.sum((everyone < jnp.min(seg)).astype(jnp.float32)).astype(jnp.int32)
        through = jnp.sum((everyone <= jnp.max(seg)).astype(jnp.float32)).astype(jnp.int32)
        first = before // KEY_BLOCK
        last = (through + KEY_BLOCK - 1) // KEY_BLOCK
        bounds[0, j] = first
        bounds[1, j] = last
        acc[...] = jnp.zeros_like(acc)

        def step(t, carry):
            at = pl.ds(pl.multiple_of(t * KEY_BLOCK, KEY_BLOCK), KEY_BLOCK)
            column = seg_col[at, :]
            same = jnp.concatenate([column] * (tok // TILE), axis=1) == seg
            after = []
            queries = [q_ref[j, :, 2 * HD * h : 2 * HD * (h + 1)] for h in range(3)]
            scores = [
                jnp.where(same, lanes_product(keys[h, at, :], queries[h]), NEGATIVE) for h in range(3)
            ]
            peaks = [
                jnp.maximum(carry[2 * h], jnp.max(scores[h], axis=0, keepdims=True)) for h in range(3)
            ]
            expo = [jnp.exp(scores[h] - peaks[h]) for h in range(3)]
            for h in range(3):
                fade = jnp.exp(carry[2 * h] - peaks[h])
                total = carry[2 * h + 1] * fade + jnp.sum(expo[h], axis=0, keepdims=True)
                acc[h] = acc[h] * fade + plain_product(values[h, :, at], expo[h].astype(jnp.bfloat16))
                after += [peaks[h], total]
            return tuple(after)

        start = (jnp.full((1, tok), NEGATIVE, jnp.float32), jnp.zeros((1, tok), jnp.float32)) * 3
        done = lax.fori_loop(first, last, step, start)
        for h in range(3):
            turned_out[j, HD * h : HD * (h + 1), :] = acc[h] / done[2 * h + 1]
            lse[j, h] = done[2 * h] + jnp.log(done[2 * h + 1])
        out[jnp.bitwise_xor(place[0], j)] = turned_out[j].T.astype(jnp.bfloat16)
        return 0

    lax.fori_loop(0, CHIPS, queries, 0)


def attend_back_kernel(
    place,
    bounds,
    q_ref,
    own,
    other,
    turned_out,
    lse,
    grad0,
    grad1,
    grad2,
    grad3,
    dq_ref,
    dkv_own,
    dkv_other,
    sources,
    turned_keys,
    grads,
    seg_col,
    seg_row,
    acc,
    grad,
    pair,
    mixed,
):
    tok = q_ref.shape[1]
    chip, core = place[0], place[1]
    wide = 2 * HD
    for m, piece in enumerate((grad0, grad1, grad2, grad3)):
        grad[jnp.bitwise_xor(chip, m)] = piece[...]
    twice = ones_where((wide, wide), lambda row, column: row == lax.rem(column, HD))
    turned_twice = ones_where((wide, wide), lambda row, column: column == lax.rem(row, HD))
    folded = ones_where((wide, wide), lambda row, column: column == lax.rem(row, HD))
    all_rows, group = unit(tok), unit(3 * HD)
    pair[...] = jnp.zeros_like(pair)

    def prepare(j, unused):
        for source, side in ((own, core), (other, 1 - core)):
            shard = 2 * j + side
            at = pl.ds(pl.multiple_of(shard * tok, TILE), tok)
            tags = source[j, tok : tok + TAG_ROWS].astype(jnp.float32)[:1]
            seg_row[shard] = jnp.broadcast_to(tags, (8, tok))
            column = as_column(tags)
            segment = segment_of(column)
            seg_col[at, :] = segment
            flag = column - 2.0 * segment == 1.0
            row_flag = tags - 2.0 * segment_of(tags) == 1.0
            for h in range(3):
                kv = source[j, :tok, wide * h : wide * (h + 1)]
                low = lax.broadcasted_iota(jnp.int32, kv.shape, 1) < HD
                sources[h, at, :wide] = jnp.where(low == flag, 0.0, plain_product(kv, twice)).astype(
                    jnp.bfloat16
                )
                sources[h, at, wide:] = kv
                both = lanes_product(turned_twice, kv)
                low = lax.broadcasted_iota(jnp.int32, both.shape, 0) < HD
                turned_keys[h, :, at] = jnp.where(low == row_flag, 0.0, both).astype(jnp.bfloat16)
                grads[h, at, :] = jnp.zeros((tok, 2 * wide), jnp.float32)
        return 0

    lax.fori_loop(0, CHIPS, prepare, 0)

    def queries(j, unused):
        tags = seg_row[2 * j + core][:1]
        seg = segment_of(tags)
        slot = jnp.bitwise_xor(chip, j)
        flag = as_column(tags - 2.0 * seg) == 1.0
        turned_grad = lanes_product(group, grad[j])
        deltas, shifts = [], []
        for h in range(3):
            rows = slice(HD * h, HD * (h + 1))
            deltas.append(jnp.sum(turned_grad[rows] * turned_out[j, rows, :], axis=0, keepdims=True))
            shifts.append(lse[j, h])
            pair[h, :tok, :wide] = q_ref[j, :, wide * h : wide * (h + 1)]
            pair[h, tok:, wide + HD :] = grad[j, :, rows]
        acc[...] = jnp.zeros_like(acc)

        def step(t, carry):
            at = pl.ds(pl.multiple_of(t * KEY_BLOCK, KEY_BLOCK), KEY_BLOCK)
            column = seg_col[at, :]
            same = jnp.concatenate([column] * (tok // TILE), axis=1) == seg
            both = [lanes_product(sources[h, at, :], pair[h]) for h in range(3)]
            for h in range(3):
                probs = jnp.where(same, jnp.exp(both[h][:, :tok] - shifts[h]), 0.0)
                mixed[h, :, :tok] = (probs * (both[h][:, tok:] - deltas[h])).astype(jnp.bfloat16)
                mixed[h, :, tok:] = probs.astype(jnp.bfloat16)
            for h in range(3):
                grads[h, at, :] += plain_product(mixed[h], pair[h])
                acc[h] += plain_product(turned_keys[h, :, at], mixed[h, :, :tok])
            return carry

        lax.fori_loop(bounds[0, j], bounds[1, j], step, 0)
        for h in range(3):
            dq = lanes_product(all_rows, (acc[h] * (HD**-0.5)).astype(jnp.bfloat16))
            at = 2 * wide * h
            dq_ref[slot, :, at : at + wide] = jnp.where(flag, 0.0, dq).astype(jnp.bfloat16)
            dq_ref[slot, :, at + wide : at + 2 * wide] = jnp.where(flag, dq, 0.0).astype(jnp.bfloat16)
        return 0

    lax.fori_loop(0, CHIPS, queries, 0)

    def finish(j, unused):
        slot = jnp.bitwise_xor(chip, j)
        for target, side in ((dkv_own, core), (dkv_other, 1 - core)):
            shard = 2 * j + side
            at = pl.ds(pl.multiple_of(shard * tok, TILE), tok)
            tags = seg_row[shard][:1]
            flag = as_column(tags - 2.0 * segment_of(tags)) == 1.0
            for h in range(3):
                low = lax.broadcasted_iota(jnp.int32, (tok, wide), 1) < HD
                dk = jnp.where(low == flag, 0.0, grads[h, at, :wide]).astype(jnp.bfloat16)
                target[slot, :, wide * h : wide * (h + 1)] = jnp.where(
                    low, plain_product(dk, folded), grads[h, at, wide:]
                ).astype(jnp.bfloat16)
        return 0

    lax.fori_loop(0, CHIPS, finish, 0)


def normed(total, gain, shift):
    center = total - jnp.mean(total, axis=-1, keepdims=True)
    spread = jnp.mean(center * center, axis=-1, keepdims=True)
    inverse = lax.rsqrt(spread + EPSILON)
    unit = center * inverse
    return unit * gain + shift, unit, inverse


def normed_back(grad, unit, inverse, gain):
    scaled = grad * gain
    mean = jnp.mean(scaled, axis=-1, keepdims=True)
    along = jnp.mean(scaled * unit, axis=-1, keepdims=True)
    return inverse * (scaled - mean - unit * along)


def summed_rows(value):
    return jnp.sum(value, axis=0, keepdims=True)


def dense_kernel(
    place,
    context0,
    context1,
    context2,
    context3,
    text,
    cotangent,
    vectors,
    inner_bias,
    inner_shard,
    outer_shard,
    output_shard,
    near_own,
    near_other,
    far_own,
    far_other,
    result,
    grad_sum,
    grad_context,
    kept,
    sent_far,
    sent_near,
    inner_w,
    outer_w,
    output_w,
    hidden,
    slope,
    inner_g,
    outer_g,
    output_g,
    small,
    sums,
    in_sems,
    out_sems,
):
    bf16, f32 = jnp.bfloat16, jnp.float32
    chip, core, wa = place[0], place[1], place[2]
    tok, dmod = result.shape
    ff = hidden.shape[1]
    group = dmod // CHIPS
    parts = CHIPS
    rows = dmod // parts
    half = rows // 2
    quarter = rows // CHIPS
    slot_w = ff // (2 * CHIPS)

    context = (context0, context1, context2, context3)

    def head_rows(m):
        return pl.ds(pl.multiple_of(group * jnp.bitwise_xor(chip, m), 64), group)

    pltpu.make_async_copy(
        output_shard, output_w.at[pl.ds(pl.multiple_of(rows * wa, 16), rows), :], in_sems.at[0]
    ).start()
    pltpu.make_async_copy(
        inner_shard, inner_w.at[pl.ds(pl.multiple_of(rows * wa, 16), rows), :], in_sems.at[1]
    ).start()
    pltpu.make_async_copy(
        outer_shard, outer_w.at[pl.ds(pl.multiple_of(dmod * wa, 16), dmod), :], in_sems.at[2]
    ).start()

    def fetch(m, unused):
        g = jnp.bitwise_xor(chip, m)
        for source, side, far in (
            (near_own, core, 0),
            (near_other, 1 - core, 0),
            (far_own, core, 1),
            (far_other, 1 - core, 1),
        ):
            s = 2 * g + side
            for u in range(2 - far):
                z = lax.rem(wa - 1 - far - 2 * u + parts, parts)
                piece = source.at[m] if far else source.at[m, u]
                pltpu.make_async_copy(
                    piece.at[pl.ds(2 * rows, quarter), :],
                    output_w.at[
                        pl.ds(pl.multiple_of(rows * z + quarter * g, 16), quarter),
                        pl.ds(pl.multiple_of(slot_w * side, TILE), slot_w),
                    ],
                    in_sems.at[0],
                ).start()
                pltpu.make_async_copy(
                    piece.at[pl.ds(0, rows), :],
                    inner_w.at[
                        pl.ds(pl.multiple_of(rows * z, 16), rows),
                        pl.ds(pl.multiple_of(slot_w * s, TILE), slot_w),
                    ],
                    in_sems.at[1],
                ).start()
                for v in range(2):
                    pltpu.make_async_copy(
                        piece.at[pl.ds(rows + half * v, half), :],
                        outer_w.at[
                            pl.ds(pl.multiple_of(dmod * z + half * s, 16), half),
                            pl.ds(slot_w * v, slot_w),
                        ],
                        in_sems.at[2],
                    ).start()
        return 0

    lax.fori_loop(0, CHIPS, fetch, 0)
    names = ("outb", "g1", "s1", "outerb", "g2", "s2")
    vec = {name: vectors[k : k + 1, :] for k, name in enumerate(names)}

    pltpu.make_async_copy(output_w, output_w, in_sems.at[0]).wait()
    branch = vec["outb"]
    for m in range(CHIPS):
        branch = branch + plain_product(context[m][...], output_w[head_rows(m), :])
    first, unit_one, inverse_one = normed(text[:tok, :].astype(f32) + branch, vec["g1"], vec["s1"])
    low = first.astype(bf16)

    pltpu.make_async_copy(inner_w, inner_w, in_sems.at[1]).wait()
    pltpu.make_async_copy(outer_w, outer_w, in_sems.at[2]).wait()

    def forward(s, ffn):
        at = pl.ds(pl.multiple_of(slot_w * s, TILE), slot_w)
        inner = plain_product(low, inner_w[:, at]) + inner_bias[:, at]
        cdf = 0.5 + 0.5 * lax.erf(inner * (0.5**0.5))
        active = (inner * cdf).astype(bf16)
        hidden[:, at] = active
        slope[:, at] = cdf + inner * (jnp.exp(-0.5 * inner * inner) * (0.5 / jnp.pi) ** 0.5)
        return ffn + plain_product(active, outer_w[at, :])

    ffn = lax.fori_loop(0, 2 * CHIPS, forward, jnp.broadcast_to(vec["outerb"], (tok, dmod)))
    second, unit_two, inverse_two = normed(first + ffn, vec["g2"], vec["s2"])
    result[...] = second.astype(bf16)
    grad_out = cotangent[...].astype(f32)
    grad_two = normed_back(grad_out, unit_two, inverse_two, vec["g2"])
    low_two = grad_two.astype(bf16)

    sums[...] = jnp.zeros_like(sums)

    def put(row, value):
        for v in range(2):
            for z in range(parts):
                sums[z, row + v : row + v + 1, :] = value[:, slot_w * v : slot_w * (v + 1)]

    put(6, summed_rows(low_two.astype(f32)))
    put(8, summed_rows(grad_out * unit_two))
    put(10, summed_rows(grad_out))
    low_turned = low.astype(f32).T.astype(bf16)

    def backward(s, grad_first):
        at = pl.ds(pl.multiple_of(slot_w * s, TILE), slot_w)
        grad_hidden = lanes_product(low_two, outer_w[at, :])
        grad_inner = (grad_hidden * slope[:, at]).astype(bf16)
        outer_g[at, :] = rows_product(hidden[:, at], low_two).astype(bf16)
        inner_g[:, at] = plain_product(low_turned, grad_inner).astype(bf16)
        sums[s // 2, pl.ds(12 + lax.rem(s, 2), 1), :] = summed_rows(grad_inner.astype(f32))
        return grad_first + lanes_product(grad_inner, inner_w[:, at])

    grad_first = lax.fori_loop(0, 2 * CHIPS, backward, grad_two)

    def targets():
        for m in range(CHIPS):
            far = sent_far if m == CHIPS - 1 else sent_near.at[m]
            for target, side, sem in ((kept.at[m], core, 0), (far, 1 - core, 1 + (m < CHIPS - 1))):
                yield target, jnp.bitwise_xor(chip, m), side, sem

    inner_view = inner_g.reshape(parts, rows, ff)
    outer_view = outer_g.reshape(parts, dmod, dmod)
    output_view = output_g.reshape(parts, rows, dmod)
    for target, g, side, sem in targets():
        s = 2 * g + side
        pltpu.make_async_copy(
            inner_view.at[:, :, pl.ds(pl.multiple_of(slot_w * s, TILE), slot_w)],
            target.at[:, pl.ds(0, rows), :],
            out_sems.at[sem],
        ).start()
        for v in range(2):
            pltpu.make_async_copy(
                outer_view.at[:, pl.ds(pl.multiple_of(half * s, 16), half), pl.ds(slot_w * v, slot_w)],
                target.at[:, pl.ds(rows + half * v, half), :],
                out_sems.at[sem],
            ).start()

    put(2, summed_rows(grad_first * unit_one))
    put(4, summed_rows(grad_first))
    grad_one = normed_back(grad_first, unit_one, inverse_one, vec["g1"])
    grad_sum[...] = grad_one
    low_one = grad_one.astype(bf16)
    put(0, summed_rows(low_one.astype(f32)))
    small[0] = jnp.zeros_like(small[0])
    small[1] = sums[...].astype(bf16)
    for m in range(CHIPS):
        at = head_rows(m)
        output_g[at, :] = rows_product(context[m][...], low_one).astype(bf16)
        grad_context[m] = lanes_product(low_one, output_w[at, :]).astype(bf16)
    for target, g, side, sem in targets():
        pltpu.make_async_copy(
            output_view.at[
                :,
                pl.ds(pl.multiple_of(quarter * g, 16), quarter),
                pl.ds(pl.multiple_of(slot_w * side, TILE), slot_w),
            ],
            target.at[:, pl.ds(2 * rows, quarter), :],
            out_sems.at[sem],
        ).start()
        filled = jnp.where(2 * g + side == 0, 1, 0)
        pltpu.make_async_copy(
            small.at[filled], target.at[:, pl.ds(2 * rows + quarter, TAG_ROWS), :], out_sems.at[sem]
        ).start()
    for sem, target in enumerate((kept, sent_far, sent_near)):
        pltpu.make_async_copy(target, target, out_sems.at[sem]).wait()


def head_grads_kernel(place, tokens, dq, dkv, kept, sent, acc):
    tok = dq.shape[1]
    core = place[1]
    wide = dq.shape[2]
    parts, rows = kept.shape[0], kept.shape[1] - TAG_ROWS
    acc[...] = jnp.zeros_like(acc)

    def piece(m, carry):
        text = tokens[m, :tok]
        text_turned = text.astype(jnp.float32).T.astype(jnp.bfloat16)
        acc[:, :wide] += plain_product(text_turned, dq[m])
        acc[:, wide:] += plain_product(text_turned, dkv[m])
        return (
            carry[0] + summed_rows(dq[m].astype(jnp.float32)),
            carry[1] + summed_rows(dkv[m].astype(jnp.float32)),
        )

    start = (jnp.zeros((1, wide), jnp.float32), jnp.zeros((1, wide // 2), jnp.float32))
    sums = jnp.concatenate(lax.fori_loop(0, CHIPS, piece, start), axis=1)
    sums = jnp.broadcast_to(sums, (TAG_ROWS, sums.shape[1]))
    for z in range(parts):
        for target, side in ((kept, core), (sent, 1 - core)):
            at = pl.ds(pl.multiple_of(2 * rows * z + rows * side, 32), rows)
            target[z, :rows] = acc[at, :].astype(jnp.bfloat16)
            target[z, rows:] = jnp.where(side == 0, sums, 0.0).astype(jnp.bfloat16)


def token_grads_kernel(dq, dkv_own, dkv_other, weight, dkv, partial):
    wide = dq.shape[2]

    def piece(m, carry):
        both = dkv_own[m].astype(jnp.float32) + dkv_other[m].astype(jnp.float32)
        dkv[m] = both.astype(jnp.bfloat16)
        partial[m] = (
            lanes_product(dq[m], weight[:, :wide]) + lanes_product(dkv[m], weight[:, wide:])
        ).astype(jnp.bfloat16)
        return carry

    lax.fori_loop(0, CHIPS, piece, 0)


def picked_piece(place, own, other, g, side, rows):
    m = jnp.bitwise_xor(place[0], g)
    here = own[m, rows, :].astype(jnp.float32)
    there = other[m, rows, :].astype(jnp.float32)
    return jnp.where(place[1] == side, here, there)


def unpack_dense_kernel(place, own, other, inner, outer, output, small):
    rows = inner.shape[0]
    half, quarter = rows // 2, rows // CHIPS
    slot_w = own.shape[2]
    for g in range(CHIPS):
        for side in range(2):
            s = 2 * g + side
            at = slice(slot_w * s, slot_w * (s + 1))
            inner[:, at] = picked_piece(place, own, other, g, side, slice(0, rows))
            for v in range(2):
                outer[half * s : half * (s + 1), slot_w * v : slot_w * (v + 1)] = picked_piece(
                    place, own, other, g, side, slice(rows + half * v, rows + half * (v + 1))
                )
            output[quarter * g : quarter * (g + 1), slot_w * side : slot_w * (side + 1)] = picked_piece(
                place, own, other, g, side, slice(2 * rows, 2 * rows + quarter)
            )
    small[...] = picked_piece(place, own, other, 0, 0, slice(2 * rows + quarter, own.shape[1]))


def unpack_heads_kernel(place, own, other, ww, we, ew, ee, key, value, sums):
    rows = own.shape[1] - TAG_ROWS
    wide = 4 * 3 * HD
    for side in range(2):
        at = slice(rows * side, rows * (side + 1))
        pieces = [picked_piece(place, own, other, g, side, slice(0, rows)) for g in range(CHIPS)]
        for k, target in enumerate((ww, we, ew, ee)):
            target[at, :] = jnp.concatenate(
                [p[:, HD * (4 * h + k) : HD * (4 * h + k + 1)] for p in pieces for h in range(3)], axis=1
            )
        for k, target in enumerate((key, value)):
            target[at, :] = jnp.concatenate(
                [
                    p[:, wide + HD * (2 * h + k) : wide + HD * (2 * h + k + 1)]
                    for p in pieces
                    for h in range(3)
                ],
                axis=1,
            )
    sums[...] = picked_piece(place, own, other, place[2], 0, slice(rows, rows + TAG_ROWS))


def smem():
    return pl.BlockSpec(memory_space=pltpu.SMEM)


def vmem():
    return pl.BlockSpec(memory_space=pltpu.VMEM)


def hbm():
    return pl.BlockSpec(memory_space=pl.ANY)


def whole_call(kernel, operands, outs, scratch=(), micros=1, mebibytes=16):
    return pl.pallas_call(
        kernel,
        out_shape=[jax.ShapeDtypeStruct(shape, dtype) for shape, dtype, _ in outs],
        in_specs=[spec() for _, spec in operands],
        out_specs=[spec() for _, _, spec in outs],
        scratch_shapes=list(scratch),
        compiler_params=pltpu.CompilerParams(vmem_limit_bytes=mebibytes << 20),
        cost_estimate=pl.CostEstimate(
            flops=micros * FLOPS_PER_MICRO, bytes_accessed=micros << 20, transcendentals=0
        ),
    )(*(value for value, _ in operands))


def grouped_device(
    tokens,
    cotangent,
    segment_ids,
    token_types,
    query_wordword,
    query_wordentity,
    query_entityword,
    query_entityentity,
    bias_wordword,
    bias_wordentity,
    bias_entityword,
    bias_entityentity,
    key_weight,
    value_weight,
    value_bias,
    output_weight,
    output_bias,
    first_gain,
    first_bias,
    inner_weight,
    inner_bias,
    outer_weight,
    outer_bias,
    second_gain,
    second_bias,
):
    bf16, f32 = jnp.bfloat16, jnp.float32
    index = lax.axis_index("ctx")
    chip, core = index // 2, index % 2
    wa = lax.axis_index("wa")
    parts = lax.axis_size("wa")
    place = jnp.stack([chip, core, wa]).astype(jnp.int32)
    inputs = tokens[0]
    tok, dmod = inputs.shape
    length = 2 * CHIPS * tok
    rows = key_weight.shape[0]
    half, quarter = rows // 2, rows // CHIPS
    group = dmod // CHIPS
    ff = inner_weight.shape[1]
    slot_w = ff // (2 * CHIPS)

    tags = (segment_ids[0] * 2 + token_types[0]).astype(bf16)
    tag_rows = jnp.pad(tags[None], ((0, TAG_ROWS - 1), (0, dmod - tok)))
    text = jnp.concatenate([inputs, tag_rows], axis=0)
    cut = tok // 2
    text_x, text_y = swapped(text, 2), swapped(text, 4)

    lines = (
        bias_wordword,
        bias_wordentity,
        bias_entityword,
        bias_entityentity,
        value_bias,
        output_bias,
        first_gain,
        first_bias,
        outer_bias,
        second_gain,
        second_bias,
        inner_bias,
    )
    six = (query_wordword, query_wordentity, query_entityword, query_entityentity, key_weight, value_weight)
    mine, slot = whole_call(
        prepare_kernel,
        [(place, smem)]
        + [(a, vmem) for a in (*six, *lines)]
        + [(a, hbm) for a in (inner_weight, outer_weight, output_weight)],
        [((half + TAG_ROWS, 6 * group), bf16, vmem), ((2 * rows + quarter, slot_w), bf16, vmem)],
        [pltpu.SemaphoreType.DMA((4,))],
        micros=3,
        mebibytes=58,
    )
    one, three = turned(mine, 1), turned(mine, 3)
    text_x, text_y, one, three, slot = ordered(text_x, text_y, one, three, slot)
    text_far = swapped(text_x[:cut], 4), swapped(text_y[cut:], 2)

    split, wide = half // 2, 6 * group // slot_w
    right = jnp.concatenate([*narrowed(one[:split], slot_w), slot], axis=0)
    left = jnp.concatenate([*narrowed(three[split:], slot_w), slot], axis=0)
    right, left = turned(right, 1), turned(left, 3)
    *text_far, right, left = ordered(*text_far, right, left)
    cut_right, cut_left = split * wide, (half + TAG_ROWS - split) * wide
    two = jnp.concatenate([widened(right[:cut_right], wide), widened(left[:cut_left], wide)], axis=0)
    near_slot = jnp.stack([right[cut_right:], left[cut_left:]])
    middle = TAG_ROWS * (slot.shape[0] // TAG_ROWS // 2)
    far_slot = turned(near_slot[0, :middle], 1), turned(near_slot[1, middle:], 3)
    mine = jnp.stack([mine, one, two, three])
    theirs = swapped(mine, 1)
    near_x, near_y = swapped(near_slot, 2), swapped(near_slot, 4)
    theirs, *far_slot = ordered(theirs, *far_slot)
    far_slot = jnp.concatenate(far_slot, axis=0)
    order = (wa - jnp.arange(parts)) % parts
    vectors = jnp.take(mine[:, half + 1], order, axis=0).reshape(parts, 6, rows)
    vectors = jnp.pad(jnp.transpose(vectors, (1, 0, 2)).reshape(6, dmod), ((0, 2), (0, 0))).astype(f32)
    full_inner_bias = jnp.take(mine[:, half + 2, : ff // parts], order, axis=0).reshape(1, ff).astype(f32)

    weight, all_text, q, kv = whole_call(
        project_kernel,
        [(place, smem)] + [(a, vmem) for a in (text, text_x, text_y, *text_far, mine, theirs)],
        [
            ((dmod, 6 * group), bf16, vmem),
            ((CHIPS, tok + TAG_ROWS, dmod), bf16, vmem),
            ((CHIPS, tok, 2 * group), bf16, vmem),
            ((CHIPS, tok + TAG_ROWS, 2 * group), bf16, vmem),
        ],
        micros=8,
        mebibytes=16,
    )
    kv, near_x, near_y, far_slot = ordered(kv, near_x, near_y, far_slot)
    kv_other = swapped(kv, 1)
    to_x = jnp.concatenate([far_slot, near_y[1]], axis=0)
    to_y = jnp.concatenate([far_slot, near_x[0]], axis=0)
    kv_other, to_x, to_y = ordered(kv_other, to_x, to_y)
    to_x, to_y, to_far = swapped(to_x, 2), swapped(to_y, 4), swapped(far_slot, 6)

    context, turned_out, lse, bounds = whole_call(
        attend_kernel,
        [(place, smem), (q, vmem), (kv, vmem), (kv_other, vmem)],
        [
            ((CHIPS, tok, group), bf16, vmem),
            ((CHIPS, group, tok), f32, vmem),
            ((CHIPS, 3, 1, tok), f32, vmem),
            ((2, CHIPS), jnp.int32, smem),
        ],
        [
            pltpu.VMEM((3, length, 2 * HD), bf16),
            pltpu.VMEM((3, HD, length), bf16),
            pltpu.VMEM((length, TILE), f32),
            pltpu.VMEM((2 * CHIPS, 8, tok), f32),
            pltpu.VMEM((3, HD, tok), f32),
        ],
        micros=25,
        mebibytes=20,
    )
    context, to_x, to_y, to_far = ordered(context, to_x, to_y, to_far)

    def exchanged(value):
        return [value[0]] + [swapped(value[m], 2 * m) for m in range(1, CHIPS)]

    contexts = exchanged(context)
    deep = slot.shape[0]
    near_slots = jnp.stack([near_slot, near_x, near_y, jnp.stack([to_y[deep:], to_x[deep:]])])
    near_slots = near_slots, swapped(near_slots, 1)
    far_slots = jnp.stack([far_slot, to_x[:deep], to_y[:deep], to_far])
    far_slots = far_slots, swapped(far_slots, 1)

    slot_rows = 2 * rows + quarter + TAG_ROWS
    result, grad_sum, grad_context, kept, sent_far, sent_near = whole_call(
        dense_kernel,
        [(place, smem)]
        + [(a, vmem) for a in (*contexts, text, cotangent[0], vectors, full_inner_bias)]
        + [
            (a, hbm)
            for a in (inner_weight, outer_weight, output_weight, *near_slots, *far_slots)
        ],
        [
            ((tok, dmod), bf16, vmem),
            ((tok, dmod), f32, vmem),
            ((CHIPS, tok, group), bf16, vmem),
            ((CHIPS, parts, slot_rows, slot_w), bf16, hbm),
            ((parts, slot_rows, slot_w), bf16, hbm),
            ((CHIPS - 1, parts, slot_rows, slot_w), bf16, hbm),
        ],
        [
            pltpu.VMEM((dmod, ff), bf16),
            pltpu.VMEM((ff, dmod), bf16),
            pltpu.VMEM((dmod, dmod), bf16),
            pltpu.VMEM((tok, ff), bf16),
            pltpu.VMEM((tok, ff), f32),
            pltpu.VMEM((dmod, ff), bf16),
            pltpu.VMEM((ff, dmod), bf16),
            pltpu.VMEM((dmod, dmod), bf16),
            pltpu.VMEM((2, parts, TAG_ROWS, slot_w), bf16),
            pltpu.VMEM((parts, TAG_ROWS, slot_w), f32),
            pltpu.SemaphoreType.DMA((3,)),
            pltpu.SemaphoreType.DMA((3,)),
        ],
        micros=35,
        mebibytes=50,
    )
    grad_pieces = exchanged(grad_context)

    def added(*values):
        total = values[0].astype(f32)
        for v in values[1:]:
            total = total + v.astype(f32)
        return total

    middle = parts // 2
    upper, lower = slice(0, middle), slice(middle, None)
    received_far = swapped(sent_far, 1)
    received = swapped(sent_near, 1)
    far_x = added(kept[CHIPS - 1, upper], received_far[upper]).astype(bf16)
    far_y = added(kept[CHIPS - 1, lower], received_far[lower]).astype(bf16)
    near_x = added(kept[1, upper], received[1, upper]).astype(bf16)
    near_y = added(kept[2, lower], received[2, lower]).astype(bf16)
    *grad_pieces, far_x, far_y, near_x, near_y = lax.optimization_barrier(
        (*grad_pieces, far_x, far_y, near_x, near_y)
    )
    far_x, far_y = swapped(far_x, 2), swapped(far_y, 4)
    near_x, near_y = swapped(near_x, 2), swapped(near_y, 4)

    dq, dkv, dkv_sent = whole_call(
        attend_back_kernel,
        [(place, smem), (bounds, smem)]
        + [(a, vmem) for a in (q, kv, kv_other, turned_out, lse, *grad_pieces)],
        [
            ((CHIPS, tok, 4 * group), bf16, vmem),
            ((CHIPS, tok, 2 * group), bf16, vmem),
            ((CHIPS, tok, 2 * group), bf16, vmem),
        ],
        [
            pltpu.VMEM((3, length, 4 * HD), bf16),
            pltpu.VMEM((3, 2 * HD, length), bf16),
            pltpu.VMEM((3, length, 4 * HD), f32),
            pltpu.VMEM((length, TILE), f32),
            pltpu.VMEM((2 * CHIPS, 8, tok), f32),
            pltpu.VMEM((3, 2 * HD, tok), f32),
            pltpu.VMEM((CHIPS, tok, group), bf16),
            pltpu.VMEM((3, 2 * tok, 4 * HD), bf16),
            pltpu.VMEM((3, KEY_BLOCK, 2 * tok), bf16),
        ],
        micros=40,
        mebibytes=36,
    )
    dq, dkv, dkv_sent, far_x, far_y, near_x, near_y = lax.optimization_barrier(
        (dq, dkv, dkv_sent, far_x, far_y, near_x, near_y)
    )
    dkv_received = swapped(dkv_sent, 1)
    last_x = added(kept[1, lower], received[1, lower], far_y).astype(bf16)
    last_y = added(kept[2, upper], received[2, upper], far_x).astype(bf16)
    last_x, last_y = ordered(last_x, last_y)
    last_x, last_y = swapped(last_x, 2), swapped(last_y, 4)
    dkv, partial = whole_call(
        token_grads_kernel,
        [(a, vmem) for a in (dq, dkv, dkv_received, weight)],
        [((CHIPS, tok, 2 * group), bf16, vmem), ((CHIPS, tok, dmod), bf16, vmem)],
        micros=8,
        mebibytes=16,
    )
    head_kept, head_sent = whole_call(
        head_grads_kernel,
        [(place, smem)] + [(a, vmem) for a in (all_text, dq, dkv)],
        [
            ((parts, half + TAG_ROWS, 6 * group), bf16, vmem),
            ((parts, half + TAG_ROWS, 6 * group), bf16, vmem),
        ],
        [pltpu.VMEM((dmod, 6 * group), f32)],
        micros=10,
        mebibytes=20,
    )
    head_kept, head_sent, last_x, last_y = ordered(head_kept, head_sent, last_x, last_y)

    def parts_sent(*values):
        shards = [
            added(*(lax.dynamic_index_in_dim(v, (wa + k) % parts, 0, keepdims=False) for v in values))
            for k in range(parts)
        ]
        return [v.astype(bf16) for v in shards]

    def parts_moved(values):
        return [turned(v, k) for k, v in enumerate(values) if k]

    def chips_moved(value):
        return [swapped(value, 2 * m) for m in range(1, CHIPS)]

    low, high = slice(0, cut), slice(cut, None)
    summed = jnp.concatenate(
        [
            added(kept[0, upper], received[0, upper], near_x, last_y),
            added(kept[0, lower], received[0, lower], last_x, near_y),
        ],
        axis=0,
    ).astype(bf16)
    dense_parts = parts_sent(summed)
    text_x = jnp.stack([partial[3, low], partial[1, low]])
    text_y = jnp.stack([partial[3, high], partial[2, high]])
    *dense_parts, text_x, text_y = ordered(*dense_parts, text_x, text_y)
    dense_moved = parts_moved(dense_parts)
    head_received = swapped(head_sent, 1)
    text_x, text_y = swapped(text_x, 2), swapped(text_y, 4)
    *dense_moved, text_x, text_y, head_received = ordered(*dense_moved, text_x, text_y, head_received)

    count = dmod // slot_w
    dense_summed = added(dense_parts[0], *dense_moved).astype(bf16)
    (far_x, near_x), (far_y, near_y) = text_x, text_y
    last_x = added(partial[1, high], far_y).astype(bf16)
    last_y = added(partial[2, low], far_x).astype(bf16)
    to_x = jnp.concatenate([dense_summed, *narrowed(last_x, slot_w)], axis=0)
    to_y = jnp.concatenate([dense_summed, *narrowed(last_y, slot_w)], axis=0)
    head_parts = parts_sent(head_kept, head_received)
    *head_parts, to_x, to_y, dense_summed = ordered(*head_parts, to_x, to_y, dense_summed)
    head_moved = parts_moved(head_parts)
    to_x, to_y, dense_far = swapped(to_x, 2), swapped(to_y, 4), swapped(dense_summed, 6)
    *head_moved, to_x, to_y, dense_far = ordered(*head_moved, to_x, to_y, dense_far)

    deep = dense_summed.shape[0]
    dense_all = jnp.stack([dense_summed, to_x[:deep], to_y[:deep], dense_far])
    head_summed = added(head_parts[0], *head_moved).astype(bf16)
    head_summed, dense_all = ordered(head_summed, dense_all)
    head_moved = chips_moved(head_summed)
    dense_other = swapped(dense_all, 1)
    out_inner, out_outer, out_output, small = whole_call(
        unpack_dense_kernel,
        [(place, smem), (dense_all, vmem), (dense_other, vmem)],
        [
            ((rows, ff), f32, vmem),
            (outer_weight.shape, f32, vmem),
            ((rows, dmod), f32, vmem),
            ((TAG_ROWS, slot_w), f32, vmem),
        ],
        micros=4,
    )
    last_x, last_y = widened(to_x[deep:], count), widened(to_y[deep:], count)
    input_grads = grad_sum + jnp.concatenate(
        [added(partial[0, low], near_x, last_y), added(partial[0, high], last_x, near_y)], axis=0
    )
    *head_moved, out_inner, out_outer, out_output, small, input_grads = ordered(
        *head_moved, out_inner, out_outer, out_output, small, input_grads
    )
    head_all = jnp.stack([head_summed, *head_moved])
    *out_heads, sums = whole_call(
        unpack_heads_kernel,
        [(place, smem), (head_all, vmem), (swapped(head_all, 1), vmem)],
        [((rows, dmod), f32, vmem) for _ in range(6)] + [((TAG_ROWS, 6 * group), f32, vmem)],
        micros=4,
    )

    sum_q = sums[0, : 4 * group].reshape(3, 4, HD)
    sum_v = sums[0, 4 * group :].reshape(3, 2, HD)[:, 1].reshape(rows)
    own_small = lax.dynamic_slice(small[:12].reshape(6, dmod), (0, wa * rows), (6, rows))
    return (
        result[None],
        input_grads[None],
        *out_heads[:4],
        *(sum_q[:, k].reshape(rows) for k in range(4)),
        *out_heads[4:],
        sum_v,
        out_output,
        own_small[0],
        own_small[1],
        own_small[2],
        out_inner,
        small[12:14].reshape(ff // parts),
        out_outer,
        own_small[3],
        own_small[4],
        own_small[5],
    )


def solution(mesh):
    in_specs = (
        P("wa", "ctx", None),
        P("wa", "ctx", None),
        P("wa", "ctx"),
        P("wa", "ctx"),
        P("wa", None),
        P("wa", None),
        P("wa", None),
        P("wa", None),
        P("wa"),
        P("wa"),
        P("wa"),
        P("wa"),
        P("wa", None),
        P("wa", None),
        P("wa"),
        P("wa", None),
        P("wa"),
        P("wa"),
        P("wa"),
        P("wa", None),
        P("wa"),
        P("wa", None),
        P("wa"),
        P("wa"),
        P("wa"),
    )
    out_specs = (
        P("wa", "ctx", None),
        P("wa", "ctx", None),
        P("wa", None),
        P("wa", None),
        P("wa", None),
        P("wa", None),
        P("wa"),
        P("wa"),
        P("wa"),
        P("wa"),
        P("wa", None),
        P("wa", None),
        P("wa"),
        P("wa", None),
        P("wa"),
        P("wa"),
        P("wa"),
        P("wa", None),
        P("wa"),
        P("wa", None),
        P("wa"),
        P("wa"),
        P("wa"),
    )
    body = grouped_device if mesh.shape["ctx"] == 2 * CHIPS else windowed_device
    return jax.shard_map(
        body, mesh=mesh, in_specs=in_specs, out_specs=out_specs, check_vma=False
    )
```

```python
import jax
import jax.numpy as jnp
from jax import lax
from jax.experimental import pallas as pl
from jax.experimental.pallas import tpu as pltpu
from jax.sharding import PartitionSpec as P

HD = 64


EPSILON = 1e-12
MASKED = -1e30


def as_sent(shard):
    return jax.tree.map(lambda a: a.astype(jnp.bfloat16) if a.dtype == jnp.float32 else a, shard)


def passed_along(value, axis, steps):
    count = lax.axis_size(axis)
    leading, last = (max(0, -steps), min(count, count - steps))
    return lax.ppermute(value, axis, [(source, source + steps) for source in range(leading, last)])


def layer_norm(values, gain, shift):
    center = values - jnp.mean(values, axis=-1, keepdims=True)
    spread = jnp.mean(center * center, axis=-1, keepdims=True)
    return center * lax.rsqrt(spread + EPSILON) * gain + shift


def gelu_exact(values):
    return jax.nn.gelu(values, approximate=False)


def matmul(left, right):
    return jnp.dot(left, right, preferred_element_type=jnp.float32)


def left_product(left, right):
    return lax.dot_general(
        left, right, (((0,), (0,)), ((), ())), preferred_element_type=jnp.float32
    )


def right_product(left, right):
    return lax.dot_general(
        left, right, (((1,), (1,)), ((), ())), preferred_element_type=jnp.float32
    )


def column_sums(values):
    return jnp.sum(values.astype(jnp.float32), axis=0)


def columns(values, start):
    return lax.dynamic_slice_in_dim(values, start, HD, 1)


def head_scores(query_word, query_entity, keys_head, key_entity, allowed, scale):
    word_scores = right_product(query_word, keys_head)
    entity_scores = right_product(query_entity, keys_head)
    raw = jnp.where(key_entity[None, :], entity_scores, word_scores) * scale
    return jnp.where(allowed, raw, MASKED)


def merge_heads(stacked):
    return jnp.transpose(stacked, (1, 0, 2)).reshape(
        stacked.shape[1], stacked.shape[0] * stacked.shape[2]
    )


def windowed_device(
    tokens,
    cotangent,
    segment_ids,
    token_types,
    query_wordword,
    query_wordentity,
    query_entityword,
    query_entityentity,
    bias_wordword,
    bias_wordentity,
    bias_entityword,
    bias_entityentity,
    key_weight,
    value_weight,
    value_bias,
    output_weight,
    output_bias,
    first_gain,
    first_bias,
    inner_weight,
    inner_bias,
    outer_weight,
    outer_bias,
    second_gain,
    second_bias,
):
    attention = (
        lax.all_gather(query_wordword, "wa", axis=0, tiled=True),
        lax.all_gather(query_wordentity, "wa", axis=0, tiled=True),
        lax.all_gather(query_entityword, "wa", axis=0, tiled=True),
        lax.all_gather(query_entityentity, "wa", axis=0, tiled=True),
        lax.all_gather(bias_wordword, "wa", axis=0, tiled=True),
        lax.all_gather(bias_wordentity, "wa", axis=0, tiled=True),
        lax.all_gather(bias_entityword, "wa", axis=0, tiled=True),
        lax.all_gather(bias_entityentity, "wa", axis=0, tiled=True),
        lax.all_gather(key_weight, "wa", axis=0, tiled=True),
        lax.all_gather(value_weight, "wa", axis=0, tiled=True),
        lax.all_gather(value_bias, "wa", axis=0, tiled=True),
        lax.all_gather(output_weight, "wa", axis=0, tiled=True),
        lax.all_gather(output_bias, "wa", axis=0, tiled=True),
        lax.all_gather(first_gain, "wa", axis=0, tiled=True),
        lax.all_gather(first_bias, "wa", axis=0, tiled=True),
    )
    (
        full_ww,
        full_we,
        full_ew,
        full_ee,
        shift_ww,
        shift_we,
        shift_ew,
        shift_ee,
        full_key,
        full_value,
        shift_value,
        full_output,
        shift_output,
        gain_one,
        shift_one,
    ) = attention
    feedforward = (
        lax.all_gather(inner_weight, "wa", axis=0, tiled=True),
        lax.all_gather(inner_bias, "wa", axis=0, tiled=True),
        lax.all_gather(outer_weight, "wa", axis=0, tiled=True),
        lax.all_gather(outer_bias, "wa", axis=0, tiled=True),
        lax.all_gather(second_gain, "wa", axis=0, tiled=True),
        lax.all_gather(second_bias, "wa", axis=0, tiled=True),
    )
    full_inner, shift_inner, full_outer, shift_outer, gain_two, shift_two = feedforward
    inputs = tokens[0]
    seg = segment_ids[0]
    types = token_types[0]
    tok = inputs.shape[0]
    dmod = inputs.shape[1]
    heads = dmod // HD
    scale = HD ** (-0.5)
    length = tok * lax.axis_size("ctx")
    doc_max = min(2048, 4 * tok, length // 2)
    reach = (doc_max - 2) // tok + 1
    entity = (types == 1)[:, None]
    proj_ww = matmul(inputs, full_ww) + shift_ww
    proj_we = matmul(inputs, full_we) + shift_we
    proj_ew = matmul(inputs, full_ew) + shift_ew
    proj_ee = matmul(inputs, full_ee) + shift_ee
    query_word = jnp.where(entity, proj_ew, proj_ww).astype(jnp.bfloat16)
    query_entity = jnp.where(entity, proj_ee, proj_we).astype(jnp.bfloat16)
    keys = matmul(inputs, full_key).astype(jnp.bfloat16)
    values = (matmul(inputs, full_value) + shift_value).astype(jnp.bfloat16)
    own_kv = jnp.concatenate([keys, values], axis=1)
    own_seg = seg + 1
    tags = own_seg * 2 + types

    def pass_left(packet, unused):
        moved = jax.tree.map(
            lambda part, own: part.astype(own.dtype),
            passed_along(as_sent(packet), "ctx", 1),
            packet,
        )
        return (moved, moved)

    def pass_right(packet, unused):
        moved = jax.tree.map(
            lambda part, own: part.astype(own.dtype),
            passed_along(as_sent(packet), "ctx", -1),
            packet,
        )
        return (moved, moved)

    _, (left_kv, left_tags) = lax.scan(pass_left, (own_kv, tags), None, length=reach)
    _, (right_kv, right_tags) = lax.scan(pass_right, (own_kv, tags), None, length=reach)
    window = jnp.concatenate(
        [jnp.flip(left_kv, 0).reshape(-1, 2 * dmod), own_kv, right_kv.reshape(-1, 2 * dmod)], axis=0
    )
    window_tags = jnp.concatenate(
        [jnp.flip(left_tags, 0).reshape(-1), tags, right_tags.reshape(-1)], axis=0
    )
    key_entity = window_tags % 2 == 1
    allowed = own_seg[:, None] == (window_tags // 2)[None, :]

    def head_forward(index):
        start = index * HD
        scores = head_scores(
            columns(query_word, start),
            columns(query_entity, start),
            columns(window, start),
            key_entity,
            allowed,
            scale,
        )
        top = jnp.max(scores, axis=1, keepdims=True)
        expo = jnp.exp(scores - top)
        total = jnp.sum(expo, axis=1, keepdims=True)
        probs = (expo / total).astype(jnp.bfloat16)
        return (matmul(probs, columns(window, dmod + start)), (top + jnp.log(total))[:, 0])

    head_context, lse = lax.map(head_forward, jnp.arange(heads))
    context = merge_heads(head_context).astype(jnp.bfloat16)
    branch = matmul(context, full_output) + shift_output
    first, pull_one = jax.vjp(
        layer_norm,
        inputs.astype(jnp.float32) + branch,
        gain_one.astype(jnp.float32),
        shift_one.astype(jnp.float32),
    )
    first_low = first.astype(jnp.bfloat16)
    inner = matmul(first_low, full_inner) + shift_inner
    activated, pull_gelu = jax.vjp(gelu_exact, inner)
    hidden = activated.astype(jnp.bfloat16)
    ffn = matmul(hidden, full_outer) + shift_outer
    result, pull_two = jax.vjp(
        layer_norm, first + ffn, gain_two.astype(jnp.float32), shift_two.astype(jnp.float32)
    )
    grad_sum_two, grad_gain_two, grad_shift_two = pull_two(cotangent[0].astype(jnp.float32))
    grad_ffn = grad_sum_two.astype(jnp.bfloat16)
    grad_outer = left_product(hidden, grad_ffn)
    grad_outer_shift = column_sums(grad_ffn)
    grad_inner = pull_gelu(right_product(grad_ffn, full_outer))[0].astype(jnp.bfloat16)
    grad_inner_full = left_product(first_low, grad_inner)
    grad_inner_shift = column_sums(grad_inner)
    grad_first = grad_sum_two + right_product(grad_inner, full_inner)
    grad_sum_one, grad_gain_one, grad_shift_one = pull_one(grad_first)
    grad_branch = grad_sum_one.astype(jnp.bfloat16)
    grad_output = left_product(context, grad_branch)
    grad_output_shift = column_sums(grad_branch)
    grad_context = right_product(grad_branch, full_output).astype(jnp.bfloat16)

    def head_backward(index):
        start = index * HD
        word_head = columns(query_word, start)
        entity_head = columns(query_entity, start)
        keys_head = columns(window, start)
        values_head = columns(window, dmod + start)
        context_head = columns(grad_context, start)
        scores = head_scores(word_head, entity_head, keys_head, key_entity, allowed, scale)
        probs = jnp.exp(scores - lse[index][:, None])
        grad_probs = right_product(context_head, values_head)
        delta = jnp.sum(probs * grad_probs, axis=1)
        grad_scores = (probs * (grad_probs - delta[:, None])).astype(jnp.bfloat16)
        zero = jnp.zeros_like(grad_scores)
        grad_word = jnp.where(key_entity[None, :], zero, grad_scores)
        grad_entity = jnp.where(key_entity[None, :], grad_scores, zero)
        grad_qword = matmul(grad_word, keys_head) * scale
        grad_qentity = matmul(grad_entity, keys_head) * scale
        grad_keys = (
            left_product(grad_word, word_head) + left_product(grad_entity, entity_head)
        ) * scale
        grad_values = left_product(probs.astype(jnp.bfloat16), context_head)
        return (grad_qword, grad_qentity, delta, grad_keys, grad_values)

    grad_qword, grad_qentity, delta, window_keys, window_values = lax.map(
        lambda index: head_backward(index), jnp.arange(heads)
    )
    parts_keys = merge_heads(window_keys).reshape(2 * reach + 1, tok, dmod)
    parts_values = merge_heads(window_values).reshape(2 * reach + 1, tok, dmod)

    def back_left(total, piece):
        return (
            (
                passed_along((total[0] + piece[0]).astype(jnp.bfloat16), "ctx", -1).astype(
                    jnp.float32
                ),
                passed_along((total[1] + piece[1]).astype(jnp.bfloat16), "ctx", -1).astype(
                    jnp.float32
                ),
            ),
            None,
        )

    def back_right(total, piece):
        return (
            (
                passed_along((total[0] + piece[0]).astype(jnp.bfloat16), "ctx", 1).astype(
                    jnp.float32
                ),
                passed_along((total[1] + piece[1]).astype(jnp.bfloat16), "ctx", 1).astype(
                    jnp.float32
                ),
            ),
            None,
        )

    empty = jnp.zeros((tok, dmod), jnp.float32)
    from_above, _ = lax.scan(back_left, (empty, empty), (parts_keys[:reach], parts_values[:reach]))
    from_below, _ = lax.scan(
        back_right,
        (empty, empty),
        (jnp.flip(parts_keys[reach + 1 :], 0), jnp.flip(parts_values[reach + 1 :], 0)),
    )
    own_keys = parts_keys[reach] + from_above[0] + from_below[0]
    own_values = parts_values[reach] + from_above[1] + from_below[1]
    grad_keys = own_keys.astype(jnp.bfloat16)
    grad_values = own_values.astype(jnp.bfloat16)
    grad_qword = merge_heads(grad_qword).astype(jnp.bfloat16)
    grad_qentity = merge_heads(grad_qentity).astype(jnp.bfloat16)
    zeros = jnp.zeros_like(grad_qword)
    grad_pww = jnp.where(entity, zeros, grad_qword)
    grad_pew = jnp.where(entity, grad_qword, zeros)
    grad_pwe = jnp.where(entity, zeros, grad_qentity)
    grad_pee = jnp.where(entity, grad_qentity, zeros)
    input_grads = grad_sum_one + right_product(grad_pww, full_ww) + right_product(grad_pwe, full_we)
    input_grads = input_grads + right_product(grad_pew, full_ew) + right_product(grad_pee, full_ee)
    input_grads = (
        input_grads + right_product(grad_keys, full_key) + right_product(grad_values, full_value)
    )
    local_grads = (
        left_product(inputs, grad_pww),
        left_product(inputs, grad_pwe),
        left_product(inputs, grad_pew),
        left_product(inputs, grad_pee),
        column_sums(grad_pww),
        column_sums(grad_pwe),
        column_sums(grad_pew),
        column_sums(grad_pee),
        left_product(inputs, grad_keys),
        left_product(inputs, grad_values),
        column_sums(grad_values),
        grad_output,
        grad_output_shift,
        grad_gain_one,
        grad_shift_one,
        grad_inner_full,
        grad_inner_shift,
        grad_outer,
        grad_outer_shift,
        grad_gain_two,
        grad_shift_two,
    )
    shards = (
        lax.psum_scatter(
            local_grads[0].astype(jnp.bfloat16), "wa", scatter_dimension=0, tiled=True
        ).astype(jnp.float32),
        lax.psum_scatter(
            local_grads[1].astype(jnp.bfloat16), "wa", scatter_dimension=0, tiled=True
        ).astype(jnp.float32),
        lax.psum_scatter(
            local_grads[2].astype(jnp.bfloat16), "wa", scatter_dimension=0, tiled=True
        ).astype(jnp.float32),
        lax.psum_scatter(
            local_grads[3].astype(jnp.bfloat16), "wa", scatter_dimension=0, tiled=True
        ).astype(jnp.float32),
        lax.psum_scatter(
            local_grads[4].astype(jnp.bfloat16), "wa", scatter_dimension=0, tiled=True
        ).astype(jnp.float32),
        lax.psum_scatter(
            local_grads[5].astype(jnp.bfloat16), "wa", scatter_dimension=0, tiled=True
        ).astype(jnp.float32),
        lax.psum_scatter(
            local_grads[6].astype(jnp.bfloat16), "wa", scatter_dimension=0, tiled=True
        ).astype(jnp.float32),
        lax.psum_scatter(
            local_grads[7].astype(jnp.bfloat16), "wa", scatter_dimension=0, tiled=True
        ).astype(jnp.float32),
        lax.psum_scatter(
            local_grads[8].astype(jnp.bfloat16), "wa", scatter_dimension=0, tiled=True
        ).astype(jnp.float32),
        lax.psum_scatter(
            local_grads[9].astype(jnp.bfloat16), "wa", scatter_dimension=0, tiled=True
        ).astype(jnp.float32),
        lax.psum_scatter(
            local_grads[10].astype(jnp.bfloat16), "wa", scatter_dimension=0, tiled=True
        ).astype(jnp.float32),
        lax.psum_scatter(
            local_grads[11].astype(jnp.bfloat16), "wa", scatter_dimension=0, tiled=True
        ).astype(jnp.float32),
        lax.psum_scatter(
            local_grads[12].astype(jnp.bfloat16), "wa", scatter_dimension=0, tiled=True
        ).astype(jnp.float32),
        lax.psum_scatter(
            local_grads[13].astype(jnp.bfloat16), "wa", scatter_dimension=0, tiled=True
        ).astype(jnp.float32),
        lax.psum_scatter(
            local_grads[14].astype(jnp.bfloat16), "wa", scatter_dimension=0, tiled=True
        ).astype(jnp.float32),
        lax.psum_scatter(
            local_grads[15].astype(jnp.bfloat16), "wa", scatter_dimension=0, tiled=True
        ).astype(jnp.float32),
        lax.psum_scatter(
            local_grads[16].astype(jnp.bfloat16), "wa", scatter_dimension=0, tiled=True
        ).astype(jnp.float32),
        lax.psum_scatter(
            local_grads[17].astype(jnp.bfloat16), "wa", scatter_dimension=0, tiled=True
        ).astype(jnp.float32),
        lax.psum_scatter(
            local_grads[18].astype(jnp.bfloat16), "wa", scatter_dimension=0, tiled=True
        ).astype(jnp.float32),
        lax.psum_scatter(
            local_grads[19].astype(jnp.bfloat16), "wa", scatter_dimension=0, tiled=True
        ).astype(jnp.float32),
        lax.psum_scatter(
            local_grads[20].astype(jnp.bfloat16), "wa", scatter_dimension=0, tiled=True
        ).astype(jnp.float32),
    )
    totals = lax.psum(
        (
            shards[0],
            shards[1],
            shards[2],
            shards[3],
            shards[4],
            shards[5],
            shards[6],
            shards[7],
            shards[8],
            shards[9],
            shards[10],
            shards[11],
            shards[12],
            shards[13],
            shards[14],
            shards[15],
            shards[16],
            shards[17],
            shards[18],
            shards[19],
            shards[20],
        ),
        "ctx",
    )
    return (
        result.astype(jnp.bfloat16)[None],
        input_grads[None],
        totals[0],
        totals[1],
        totals[2],
        totals[3],
        totals[4],
        totals[5],
        totals[6],
        totals[7],
        totals[8],
        totals[9],
        totals[10],
        totals[11],
        totals[12],
        totals[13],
        totals[14],
        totals[15],
        totals[16],
        totals[17],
        totals[18],
        totals[19],
        totals[20],
    )


CHIPS = 4
KEY_BLOCK = 256
NEGATIVE = -1e30
TAG_ROWS = 16
TILE = 128
FLOPS_PER_MICRO = 1_100_000_000


def lanes_product(left, right):
    return lax.dot_general(
        left, right, (((1,), (1,)), ((), ())), preferred_element_type=jnp.float32
    )


def rows_product(left, right):
    return lax.dot_general(
        left, right, (((0,), (0,)), ((), ())), preferred_element_type=jnp.float32
    )


def plain_product(left, right):
    return jnp.dot(left, right, preferred_element_type=jnp.float32)


def swapped(value, step):
    count = lax.axis_size("ctx")
    return lax.ppermute(value, "ctx", [(i, i ^ step) for i in range(count)])


def turned(value, step):
    count = lax.axis_size("wa")
    return lax.ppermute(value, "wa", [(i, (i + step) % count) for i in range(count)])


def narrowed(value, width):
    return [value[:, at : at + width] for at in range(0, value.shape[1], width)]


def widened(value, count):
    rows = value.shape[0] // count
    return jnp.concatenate([value[rows * k : rows * (k + 1)] for k in range(count)], axis=1)


def ordered(*values):
    return lax.optimization_barrier(values)


def as_column(row):
    return jnp.broadcast_to(row, (TILE, row.shape[1])).T


def segment_of(tag):
    return jnp.floor(tag * 0.5)


def prepare_kernel(
    place, ww, we, ew, ee, key, value, *others
):
    *lines, inner, outer, output, mine, slot, sem = others
    rows = key.shape[0]
    half, quarter = rows // 2, rows // CHIPS
    slot_w = slot.shape[1]
    chip, core = place[0], place[1]
    index = 2 * chip + core
    copies = [
        (inner.at[:, pl.ds(pl.multiple_of(slot_w * index, TILE), slot_w)], slot.at[pl.ds(0, rows), :])
    ]
    for v in range(2):
        copies.append(
            (
                outer.at[pl.ds(pl.multiple_of(half * index, 16), half), pl.ds(slot_w * v, slot_w)],
                slot.at[pl.ds(rows + half * v, half), :],
            )
        )
    copies.append(
        (
            output.at[
                pl.ds(pl.multiple_of(quarter * chip, 16), quarter),
                pl.ds(pl.multiple_of(slot_w * core, TILE), slot_w),
            ],
            slot.at[pl.ds(2 * rows, quarter), :],
        )
    )
    copies = [pltpu.make_async_copy(a, b, sem.at[k]) for k, (a, b) in enumerate(copies)]
    for copy in copies:
        copy.start()
    at = pl.ds(pl.multiple_of(half * core, 16), half)
    for g in range(CHIPS):

        @pl.when(chip == g)
        def _():
            def heads(sources):
                return jnp.concatenate(
                    [
                        w[at, HD * (3 * g + h) : HD * (3 * g + h + 1)].astype(jnp.float32)
                        for h in range(3)
                        for w in sources
                    ],
                    axis=1,
                ).astype(jnp.bfloat16)

            mine[:half, : 4 * 3 * HD] = heads((ww, we, ew, ee))
            mine[:half, 4 * 3 * HD :] = heads((key, value))

    lines = [line[...].astype(jnp.float32).reshape(1, line.shape[0]) for line in lines]
    bias = [lines[k][:, HD * h : HD * (h + 1)] for h in range(3) for k in range(4)]
    for h in range(3):
        bias += [jnp.zeros((1, HD), jnp.float32), lines[4][:, HD * h : HD * (h + 1)]]
    six = jnp.concatenate(lines[5:11], axis=1)
    last = jnp.concatenate([lines[11], jnp.zeros((1, 2 * rows), jnp.float32)], axis=1)
    which = lax.broadcasted_iota(jnp.int32, (TAG_ROWS, 6 * rows), 0)
    below = jnp.where(which == 0, jnp.concatenate(bias, axis=1), jnp.where(which == 1, six, last))
    mine[half:] = jnp.where(which < 3, below, 0.0).astype(jnp.bfloat16)
    for copy in copies:
        copy.wait()


def project_kernel(place, t0, t1, t2, t3a, t3b, mine, theirs, weight, tokens, q_ref, kv_ref):
    parts, rows = mine.shape[0], mine.shape[1] - TAG_ROWS
    tok = q_ref.shape[1]
    chip, core, wa = place[0], place[1], place[2]
    cut = t3a.shape[0]
    tokens[0] = t0[...]
    tokens[1] = t1[...]
    tokens[2] = t2[...]
    tokens[3, :cut] = t3a[...]
    tokens[3, cut:] = t3b[...]
    for z in range(parts):
        k = lax.rem(wa - z + parts, parts)
        for source, side in ((mine, core), (theirs, 1 - core)):
            weight[pl.ds(pl.multiple_of(2 * rows * z + rows * side, 32), rows), :] = source[k, :rows]
    k = lax.rem(wa - chip + parts, parts)
    bias = mine[k, rows : rows + TAG_ROWS].astype(jnp.float32)[:1]
    wide = 2 * HD

    def piece(m, unused):
        to = jnp.bitwise_xor(chip, m)
        tags = tokens[m, tok : tok + TAG_ROWS].astype(jnp.float32)[:1, :tok]
        flag = as_column(tags - 2.0 * segment_of(tags)) == 1.0
        text = tokens[m, :tok]
        for h in range(3):
            at = 2 * wide * h
            both = plain_product(text, weight[:, at : at + 2 * wide]) + bias[:, at : at + 2 * wide]
            q = jnp.where(flag, both[:, wide:], both[:, :wide]).astype(jnp.bfloat16)
            q_ref[to, :, wide * h : wide * (h + 1)] = q * jnp.bfloat16(HD**-0.5)
        kv = plain_product(text, weight[:, 6 * wide :]) + bias[:, 6 * wide :]
        kv_ref[to, :tok] = kv.astype(jnp.bfloat16)
        kv_ref[to, tok:] = jnp.broadcast_to(tags, (TAG_ROWS, tok)).astype(jnp.bfloat16)
        return 0

    lax.fori_loop(0, CHIPS, piece, 0)


def ones_where(shape, test):
    row = lax.broadcasted_iota(jnp.int32, shape, 0)
    column = lax.broadcasted_iota(jnp.int32, shape, 1)
    return jnp.where(test(row, column), 1.0, 0.0).astype(jnp.bfloat16)


def unit(size):
    return ones_where((size, size), lambda row, column: row == column)


def attend_kernel(place, q_ref, own, other, out, turned_out, lse, bounds, keys, values, seg_col, seg_row, acc):
    tok = q_ref.shape[1]
    core = place[1]
    twice = ones_where((2 * HD, 2 * HD), lambda row, column: row == lax.rem(column, HD))
    upper = ones_where((HD, 2 * HD), lambda row, column: column == row + HD)

    def prepare(j, unused):
        for source, side in ((own, core), (other, 1 - core)):
            shard = 2 * j + side
            at = pl.ds(pl.multiple_of(shard * tok, TILE), tok)
            tags = source[j, tok : tok + TAG_ROWS].astype(jnp.float32)[:1]
            seg_row[shard] = jnp.broadcast_to(segment_of(tags), (8, tok))
            column = as_column(tags)
            segment = segment_of(column)
            seg_col[at, :] = segment
            flag = column - 2.0 * segment == 1.0
            for h in range(3):
                kv = source[j, :tok, 2 * HD * h : 2 * HD * (h + 1)]
                low = lax.broadcasted_iota(jnp.int32, kv.shape, 1) < HD
                keys[h, at, :] = jnp.where(low == flag, 0.0, plain_product(kv, twice)).astype(jnp.bfloat16)
                values[h, :, at] = lanes_product(upper, kv).astype(jnp.bfloat16)
        return 0

    lax.fori_loop(0, CHIPS, prepare, 0)

    def queries(j, unused):
        seg = seg_row[2 * j + core][:1]
        everyone = seg_row[...][:, 0, :]
        before = jnp.sum((everyone < jnp.min(seg)).astype(jnp.float32)).astype(jnp.int32)
        through = jnp.sum((everyone <= jnp.max(seg)).astype(jnp.float32)).astype(jnp.int32)
        first = before // KEY_BLOCK
        last = (through + KEY_BLOCK - 1) // KEY_BLOCK
        bounds[0, j] = first
        bounds[1, j] = last
        acc[...] = jnp.zeros_like(acc)

        def step(t, carry):
            at = pl.ds(pl.multiple_of(t * KEY_BLOCK, KEY_BLOCK), KEY_BLOCK)
            column = seg_col[at, :]
            same = jnp.concatenate([column] * (tok // TILE), axis=1) == seg
            after = []
            queries = [q_ref[j, :, 2 * HD * h : 2 * HD * (h + 1)] for h in range(3)]
            scores = [
                jnp.where(same, lanes_product(keys[h, at, :], queries[h]), NEGATIVE) for h in range(3)
            ]
            peaks = [
                jnp.maximum(carry[2 * h], jnp.max(scores[h], axis=0, keepdims=True)) for h in range(3)
            ]
            expo = [jnp.exp(scores[h] - peaks[h]) for h in range(3)]
            for h in range(3):
                fade = jnp.exp(carry[2 * h] - peaks[h])
                total = carry[2 * h + 1] * fade + jnp.sum(expo[h], axis=0, keepdims=True)
                acc[h] = acc[h] * fade + plain_product(values[h, :, at], expo[h].astype(jnp.bfloat16))
                after += [peaks[h], total]
            return tuple(after)

        start = (jnp.full((1, tok), NEGATIVE, jnp.float32), jnp.zeros((1, tok), jnp.float32)) * 3
        done = lax.fori_loop(first, last, step, start)
        for h in range(3):
            turned_out[j, HD * h : HD * (h + 1), :] = acc[h] / done[2 * h + 1]
            lse[j, h] = done[2 * h] + jnp.log(done[2 * h + 1])
        out[jnp.bitwise_xor(place[0], j)] = turned_out[j].T.astype(jnp.bfloat16)
        return 0

    lax.fori_loop(0, CHIPS, queries, 0)


def attend_back_kernel(
    place,
    bounds,
    q_ref,
    own,
    other,
    turned_out,
    lse,
    grad0,
    grad1,
    grad2,
    grad3,
    dq_ref,
    dkv_own,
    dkv_other,
    sources,
    turned_keys,
    grads,
    seg_col,
    seg_row,
    acc,
    grad,
    pair,
    mixed,
):
    tok = q_ref.shape[1]
    chip, core = place[0], place[1]
    wide = 2 * HD
    for m, piece in enumerate((grad0, grad1, grad2, grad3)):
        grad[jnp.bitwise_xor(chip, m)] = piece[...]
    twice = ones_where((wide, wide), lambda row, column: row == lax.rem(column, HD))
    turned_twice = ones_where((wide, wide), lambda row, column: column == lax.rem(row, HD))
    folded = ones_where((wide, wide), lambda row, column: column == lax.rem(row, HD))
    all_rows, group = unit(tok), unit(3 * HD)
    pair[...] = jnp.zeros_like(pair)

    def prepare(j, unused):
        for source, side in ((own, core), (other, 1 - core)):
            shard = 2 * j + side
            at = pl.ds(pl.multiple_of(shard * tok, TILE), tok)
            tags = source[j, tok : tok + TAG_ROWS].astype(jnp.float32)[:1]
            seg_row[shard] = jnp.broadcast_to(tags, (8, tok))
            column = as_column(tags)
            segment = segment_of(column)
            seg_col[at, :] = segment
            flag = column - 2.0 * segment == 1.0
            row_flag = tags - 2.0 * segment_of(tags) == 1.0
            for h in range(3):
                kv = source[j, :tok, wide * h : wide * (h + 1)]
                low = lax.broadcasted_iota(jnp.int32, kv.shape, 1) < HD
                sources[h, at, :wide] = jnp.where(low == flag, 0.0, plain_product(kv, twice)).astype(
                    jnp.bfloat16
                )
                sources[h, at, wide:] = kv
                both = lanes_product(turned_twice, kv)
                low = lax.broadcasted_iota(jnp.int32, both.shape, 0) < HD
                turned_keys[h, :, at] = jnp.where(low == row_flag, 0.0, both).astype(jnp.bfloat16)
                grads[h, at, :] = jnp.zeros((tok, 2 * wide), jnp.float32)
        return 0

    lax.fori_loop(0, CHIPS, prepare, 0)

    def queries(j, unused):
        tags = seg_row[2 * j + core][:1]
        seg = segment_of(tags)
        slot = jnp.bitwise_xor(chip, j)
        flag = as_column(tags - 2.0 * seg) == 1.0
        turned_grad = lanes_product(group, grad[j])
        deltas, shifts = [], []
        for h in range(3):
            rows = slice(HD * h, HD * (h + 1))
            deltas.append(jnp.sum(turned_grad[rows] * turned_out[j, rows, :], axis=0, keepdims=True))
            shifts.append(lse[j, h])
            pair[h, :tok, :wide] = q_ref[j, :, wide * h : wide * (h + 1)]
            pair[h, tok:, wide + HD :] = grad[j, :, rows]
        acc[...] = jnp.zeros_like(acc)

        def step(t, carry):
            at = pl.ds(pl.multiple_of(t * KEY_BLOCK, KEY_BLOCK), KEY_BLOCK)
            column = seg_col[at, :]
            same = jnp.concatenate([column] * (tok // TILE), axis=1) == seg
            both = [lanes_product(sources[h, at, :], pair[h]) for h in range(3)]
            for h in range(3):
                probs = jnp.where(same, jnp.exp(both[h][:, :tok] - shifts[h]), 0.0)
                mixed[h, :, :tok] = (probs * (both[h][:, tok:] - deltas[h])).astype(jnp.bfloat16)
                mixed[h, :, tok:] = probs.astype(jnp.bfloat16)
            for h in range(3):
                grads[h, at, :] += plain_product(mixed[h], pair[h])
                acc[h] += plain_product(turned_keys[h, :, at], mixed[h, :, :tok])
            return carry

        lax.fori_loop(bounds[0, j], bounds[1, j], step, 0)
        for h in range(3):
            dq = lanes_product(all_rows, (acc[h] * (HD**-0.5)).astype(jnp.bfloat16))
            at = 2 * wide * h
            dq_ref[slot, :, at : at + wide] = jnp.where(flag, 0.0, dq).astype(jnp.bfloat16)
            dq_ref[slot, :, at + wide : at + 2 * wide] = jnp.where(flag, dq, 0.0).astype(jnp.bfloat16)
        return 0

    lax.fori_loop(0, CHIPS, queries, 0)

    def finish(j, unused):
        slot = jnp.bitwise_xor(chip, j)
        for target, side in ((dkv_own, core), (dkv_other, 1 - core)):
            shard = 2 * j + side
            at = pl.ds(pl.multiple_of(shard * tok, TILE), tok)
            tags = seg_row[shard][:1]
            flag = as_column(tags - 2.0 * segment_of(tags)) == 1.0
            for h in range(3):
                low = lax.broadcasted_iota(jnp.int32, (tok, wide), 1) < HD
                dk = jnp.where(low == flag, 0.0, grads[h, at, :wide]).astype(jnp.bfloat16)
                target[slot, :, wide * h : wide * (h + 1)] = jnp.where(
                    low, plain_product(dk, folded), grads[h, at, wide:]
                ).astype(jnp.bfloat16)
        return 0

    lax.fori_loop(0, CHIPS, finish, 0)


def normed(total, gain, shift):
    center = total - jnp.mean(total, axis=-1, keepdims=True)
    spread = jnp.mean(center * center, axis=-1, keepdims=True)
    inverse = lax.rsqrt(spread + EPSILON)
    unit = center * inverse
    return unit * gain + shift, unit, inverse


def normed_back(grad, unit, inverse, gain):
    scaled = grad * gain
    mean = jnp.mean(scaled, axis=-1, keepdims=True)
    along = jnp.mean(scaled * unit, axis=-1, keepdims=True)
    return inverse * (scaled - mean - unit * along)


def summed_rows(value):
    return jnp.sum(value, axis=0, keepdims=True)


def dense_kernel(
    place,
    context0,
    context1,
    context2,
    context3,
    text,
    cotangent,
    vectors,
    inner_bias,
    inner_shard,
    outer_shard,
    output_shard,
    first_own,
    first_other,
    second_own,
    second_other,
    result,
    grad_sum,
    grad_context,
    kept,
    sent_far,
    sent_near,
    inner_w,
    outer_w,
    output_w,
    hidden,
    slope,
    inner_g,
    outer_g,
    output_g,
    small,
    sums,
    in_sems,
    out_sems,
):
    bf16, f32 = jnp.bfloat16, jnp.float32
    chip, core, wa = place[0], place[1], place[2]
    tok, dmod = result.shape
    ff = hidden.shape[1]
    group = dmod // CHIPS
    parts = CHIPS
    rows = dmod // parts
    half = rows // 2
    quarter = rows // CHIPS
    slot_w = ff // (2 * CHIPS)

    context = (context0, context1, context2, context3)

    def head_rows(m):
        return pl.ds(pl.multiple_of(group * jnp.bitwise_xor(chip, m), 64), group)

    pltpu.make_async_copy(
        output_shard, output_w.at[pl.ds(pl.multiple_of(rows * wa, 16), rows), :], in_sems.at[0]
    ).start()
    pltpu.make_async_copy(
        inner_shard, inner_w.at[pl.ds(pl.multiple_of(rows * wa, 16), rows), :], in_sems.at[1]
    ).start()
    deep = first_own.shape[0] // 7
    places = [(0, 0, 0, 1), (0, 1, 0, 3), (0, 2, 1, 1), (0, 3, 1, 3), (0, 4, 2, 1), (0, 5, 2, 3), (0, 6, 0, 2)]
    places += [(1, 0, 1, 2), (1, 1, 3, 3), (1, 2, 2, 2), (1, 3, 3, 1), (1, 4, 3, 2)]
    sides = []
    for which, at, m, k in places:
        g = jnp.bitwise_xor(chip, m)
        z = lax.rem(wa - k + parts, parts)
        sides.append(((first_own, second_own)[which], deep * at, g, core, z))
        sides.append(((first_other, second_other)[which], deep * at, g, 1 - core, z))
    for source, at, g, side, z in sides:
        pltpu.make_async_copy(
            source.at[pl.ds(at + 2 * rows, quarter), :],
            output_w.at[
                pl.ds(pl.multiple_of(rows * z + quarter * g, 16), quarter),
                pl.ds(pl.multiple_of(slot_w * side, TILE), slot_w),
            ],
            in_sems.at[0],
        ).start()
    for source, at, g, side, z in sides:
        pltpu.make_async_copy(
            source.at[pl.ds(at, rows), :],
            inner_w.at[
                pl.ds(pl.multiple_of(rows * z, 16), rows),
                pl.ds(pl.multiple_of(slot_w * (2 * g + side), TILE), slot_w),
            ],
            in_sems.at[1],
        ).start()
    pltpu.make_async_copy(
        outer_shard, outer_w.at[pl.ds(pl.multiple_of(dmod * wa, 16), dmod), :], in_sems.at[2]
    ).start()
    for source, at, g, side, z in sides:
        for v in range(2):
            pltpu.make_async_copy(
                source.at[pl.ds(at + rows + half * v, half), :],
                outer_w.at[
                    pl.ds(pl.multiple_of(dmod * z + half * (2 * g + side), 16), half),
                    pl.ds(slot_w * v, slot_w),
                ],
                in_sems.at[2],
            ).start()

    names = ("outb", "g1", "s1", "outerb", "g2", "s2")
    vec = {name: vectors[k : k + 1, :] for k, name in enumerate(names)}

    pltpu.make_async_copy(output_w, output_w, in_sems.at[0]).wait()
    branch = vec["outb"]
    for m in range(CHIPS):
        branch = branch + plain_product(context[m][...], output_w[head_rows(m), :])
    first, unit_one, inverse_one = normed(text[:tok, :].astype(f32) + branch, vec["g1"], vec["s1"])
    low = first.astype(bf16)

    pltpu.make_async_copy(inner_w, inner_w, in_sems.at[1]).wait()

    def forward(s, carry):
        at = pl.ds(pl.multiple_of(2 * slot_w * s, TILE), 2 * slot_w)
        inner = plain_product(low, inner_w[:, at]) + inner_bias[:, at]
        cdf = 0.5 + 0.5 * lax.erf(inner * (0.5**0.5))
        hidden[:, at] = (inner * cdf).astype(bf16)
        slope[:, at] = cdf + inner * (jnp.exp(-0.5 * inner * inner) * (0.5 / jnp.pi) ** 0.5)
        return carry

    lax.fori_loop(0, CHIPS, forward, 0)
    pltpu.make_async_copy(outer_w, outer_w, in_sems.at[2]).wait()
    ffn = plain_product(hidden[...], outer_w[...]) + vec["outerb"]
    second, unit_two, inverse_two = normed(first + ffn, vec["g2"], vec["s2"])
    result[...] = second.astype(bf16)
    grad_out = cotangent[...].astype(f32)
    grad_two = normed_back(grad_out, unit_two, inverse_two, vec["g2"])
    low_two = grad_two.astype(bf16)

    sums[...] = jnp.zeros_like(sums)

    def put(row, value):
        for v in range(2):
            for z in range(parts):
                sums[z, row + v : row + v + 1, :] = value[:, slot_w * v : slot_w * (v + 1)]

    put(6, summed_rows(low_two.astype(f32)))
    put(8, summed_rows(grad_out * unit_two))
    put(10, summed_rows(grad_out))
    low_turned = low.astype(f32).T.astype(bf16)

    def backward(s, carry):
        at = pl.ds(pl.multiple_of(2 * slot_w * s, TILE), 2 * slot_w)
        grad_hidden = lanes_product(low_two, outer_w[at, :])
        grad_inner = (grad_hidden * slope[:, at]).astype(bf16)
        outer_g[at, :] = rows_product(hidden[:, at], low_two).astype(bf16)
        hidden[:, at] = grad_inner
        inner_g[:, at] = plain_product(low_turned, grad_inner).astype(bf16)
        totals = summed_rows(grad_inner.astype(f32))
        sums[s, 12:13, :] = totals[:, :slot_w]
        sums[s, 13:14, :] = totals[:, slot_w:]
        return carry

    lax.fori_loop(0, CHIPS, backward, 0)

    def targets():
        for m in range(CHIPS):
            far = sent_far if m == CHIPS - 1 else sent_near.at[m]
            for target, side, sem in ((kept.at[m], core, 0), (far, 1 - core, 1 + (m < CHIPS - 1))):
                yield target, jnp.bitwise_xor(chip, m), side, sem

    inner_view = inner_g.reshape(parts, rows, ff)
    outer_view = outer_g.reshape(parts, dmod, dmod)
    output_view = output_g.reshape(parts, rows, dmod)
    for target, g, side, sem in targets():
        s = 2 * g + side
        pltpu.make_async_copy(
            inner_view.at[:, :, pl.ds(pl.multiple_of(slot_w * s, TILE), slot_w)],
            target.at[:, pl.ds(0, rows), :],
            out_sems.at[sem],
        ).start()
        for v in range(2):
            pltpu.make_async_copy(
                outer_view.at[:, pl.ds(pl.multiple_of(half * s, 16), half), pl.ds(slot_w * v, slot_w)],
                target.at[:, pl.ds(rows + half * v, half), :],
                out_sems.at[sem],
            ).start()

    grad_first = grad_two + lanes_product(hidden[...], inner_w[...])
    put(2, summed_rows(grad_first * unit_one))
    put(4, summed_rows(grad_first))
    grad_one = normed_back(grad_first, unit_one, inverse_one, vec["g1"])
    grad_sum[...] = grad_one
    low_one = grad_one.astype(bf16)
    put(0, summed_rows(low_one.astype(f32)))
    small[0] = jnp.zeros_like(small[0])
    small[1] = sums[...].astype(bf16)
    for m in range(CHIPS):
        at = head_rows(m)
        output_g[at, :] = rows_product(context[m][...], low_one).astype(bf16)
        grad_context[m] = lanes_product(low_one, output_w[at, :]).astype(bf16)
    for target, g, side, sem in targets():
        pltpu.make_async_copy(
            output_view.at[
                :,
                pl.ds(pl.multiple_of(quarter * g, 16), quarter),
                pl.ds(pl.multiple_of(slot_w * side, TILE), slot_w),
            ],
            target.at[:, pl.ds(2 * rows, quarter), :],
            out_sems.at[sem],
        ).start()
        filled = jnp.where(2 * g + side == 0, 1, 0)
        pltpu.make_async_copy(
            small.at[filled], target.at[:, pl.ds(2 * rows + quarter, TAG_ROWS), :], out_sems.at[sem]
        ).start()
    for sem, target in enumerate((kept, sent_far, sent_near)):
        pltpu.make_async_copy(target, target, out_sems.at[sem]).wait()


def head_grads_kernel(place, tokens, dq, dkv, kept, sent, acc):
    tok = dq.shape[1]
    core = place[1]
    wide = dq.shape[2]
    parts, rows = kept.shape[0], kept.shape[1] - TAG_ROWS
    acc[...] = jnp.zeros_like(acc)

    def piece(m, carry):
        text = tokens[m, :tok]
        text_turned = text.astype(jnp.float32).T.astype(jnp.bfloat16)
        acc[:, :wide] += plain_product(text_turned, dq[m])
        acc[:, wide:] += plain_product(text_turned, dkv[m])
        return (
            carry[0] + summed_rows(dq[m].astype(jnp.float32)),
            carry[1] + summed_rows(dkv[m].astype(jnp.float32)),
        )

    start = (jnp.zeros((1, wide), jnp.float32), jnp.zeros((1, wide // 2), jnp.float32))
    sums = jnp.concatenate(lax.fori_loop(0, CHIPS, piece, start), axis=1)
    sums = jnp.broadcast_to(sums, (TAG_ROWS, sums.shape[1]))
    for z in range(parts):
        for target, side in ((kept, core), (sent, 1 - core)):
            at = pl.ds(pl.multiple_of(2 * rows * z + rows * side, 32), rows)
            target[z, :rows] = acc[at, :].astype(jnp.bfloat16)
            target[z, rows:] = jnp.where(side == 0, sums, 0.0).astype(jnp.bfloat16)


def token_grads_kernel(dq, dkv_own, dkv_other, weight, dkv, partial):
    wide = dq.shape[2]

    def piece(m, carry):
        both = dkv_own[m].astype(jnp.float32) + dkv_other[m].astype(jnp.float32)
        dkv[m] = both.astype(jnp.bfloat16)
        partial[m] = (
            lanes_product(dq[m], weight[:, :wide]) + lanes_product(dkv[m], weight[:, wide:])
        ).astype(jnp.bfloat16)
        return carry

    lax.fori_loop(0, CHIPS, piece, 0)


def picked_piece(place, own, other, g, side, rows):
    m = jnp.bitwise_xor(place[0], g)
    here = own[m, rows, :].astype(jnp.float32)
    there = other[m, rows, :].astype(jnp.float32)
    return jnp.where(place[1] == side, here, there)


def unpack_dense_kernel(place, own, other, inner, outer, output, small):
    rows = inner.shape[0]
    half, quarter = rows // 2, rows // CHIPS
    slot_w = own.shape[2]
    for g in range(CHIPS):
        for side in range(2):
            s = 2 * g + side
            at = slice(slot_w * s, slot_w * (s + 1))
            inner[:, at] = picked_piece(place, own, other, g, side, slice(0, rows))
            for v in range(2):
                outer[half * s : half * (s + 1), slot_w * v : slot_w * (v + 1)] = picked_piece(
                    place, own, other, g, side, slice(rows + half * v, rows + half * (v + 1))
                )
            output[quarter * g : quarter * (g + 1), slot_w * side : slot_w * (side + 1)] = picked_piece(
                place, own, other, g, side, slice(2 * rows, 2 * rows + quarter)
            )
    small[...] = picked_piece(place, own, other, 0, 0, slice(2 * rows + quarter, own.shape[1]))


def unpack_heads_kernel(place, own, other, ww, we, ew, ee, key, value, sums):
    rows = own.shape[1] - TAG_ROWS
    wide = 4 * 3 * HD
    for side in range(2):
        at = slice(rows * side, rows * (side + 1))
        pieces = [picked_piece(place, own, other, g, side, slice(0, rows)) for g in range(CHIPS)]
        for k, target in enumerate((ww, we, ew, ee)):
            target[at, :] = jnp.concatenate(
                [p[:, HD * (4 * h + k) : HD * (4 * h + k + 1)] for p in pieces for h in range(3)], axis=1
            )
        for k, target in enumerate((key, value)):
            target[at, :] = jnp.concatenate(
                [
                    p[:, wide + HD * (2 * h + k) : wide + HD * (2 * h + k + 1)]
                    for p in pieces
                    for h in range(3)
                ],
                axis=1,
            )
    sums[...] = picked_piece(place, own, other, place[2], 0, slice(rows, rows + TAG_ROWS))


def smem():
    return pl.BlockSpec(memory_space=pltpu.SMEM)


def vmem():
    return pl.BlockSpec(memory_space=pltpu.VMEM)


def hbm():
    return pl.BlockSpec(memory_space=pl.ANY)


def whole_call(kernel, operands, outs, scratch=(), micros=1, mebibytes=16):
    return pl.pallas_call(
        kernel,
        out_shape=[jax.ShapeDtypeStruct(shape, dtype) for shape, dtype, _ in outs],
        in_specs=[spec() for _, spec in operands],
        out_specs=[spec() for _, _, spec in outs],
        scratch_shapes=list(scratch),
        compiler_params=pltpu.CompilerParams(vmem_limit_bytes=mebibytes << 20),
        cost_estimate=pl.CostEstimate(
            flops=micros * FLOPS_PER_MICRO, bytes_accessed=micros << 20, transcendentals=0
        ),
    )(*(value for value, _ in operands))


def grouped_device(
    tokens,
    cotangent,
    segment_ids,
    token_types,
    query_wordword,
    query_wordentity,
    query_entityword,
    query_entityentity,
    bias_wordword,
    bias_wordentity,
    bias_entityword,
    bias_entityentity,
    key_weight,
    value_weight,
    value_bias,
    output_weight,
    output_bias,
    first_gain,
    first_bias,
    inner_weight,
    inner_bias,
    outer_weight,
    outer_bias,
    second_gain,
    second_bias,
):
    bf16, f32 = jnp.bfloat16, jnp.float32
    index = lax.axis_index("ctx")
    chip, core = index // 2, index % 2
    wa = lax.axis_index("wa")
    parts = lax.axis_size("wa")
    place = jnp.stack([chip, core, wa]).astype(jnp.int32)
    inputs = tokens[0]
    tok, dmod = inputs.shape
    length = 2 * CHIPS * tok
    rows = key_weight.shape[0]
    half, quarter = rows // 2, rows // CHIPS
    group = dmod // CHIPS
    ff = inner_weight.shape[1]
    slot_w = ff // (2 * CHIPS)

    lines = (
        bias_wordword,
        bias_wordentity,
        bias_entityword,
        bias_entityentity,
        value_bias,
        output_bias,
        first_gain,
        first_bias,
        outer_bias,
        second_gain,
        second_bias,
        inner_bias,
    )
    six = (query_wordword, query_wordentity, query_entityword, query_entityentity, key_weight, value_weight)
    mine, slot = whole_call(
        prepare_kernel,
        [(place, smem)]
        + [(a, vmem) for a in (*six, *lines)]
        + [(a, hbm) for a in (inner_weight, outer_weight, output_weight)],
        [((half + TAG_ROWS, 6 * group), bf16, vmem), ((2 * rows + quarter, slot_w), bf16, vmem)],
        [pltpu.SemaphoreType.DMA((4,))],
        micros=3,
        mebibytes=58,
    )
    inputs, mine, slot = ordered(inputs, mine, slot)
    tags = (segment_ids[0] * 2 + token_types[0]).astype(bf16)
    tag_rows = jnp.pad(tags[None], ((0, TAG_ROWS - 1), (0, dmod - tok)))
    text = jnp.concatenate([inputs, tag_rows], axis=0)
    cut = tok // 2
    text_x, text_y = swapped(text, 2), swapped(text, 4)

    one, three = turned(mine, 1), turned(mine, 3)
    text_x, text_y, one, three, slot = ordered(text_x, text_y, one, three, slot)
    text_far = swapped(text_x[:cut], 4), swapped(text_y[cut:], 2)

    split, wide = half // 2, 6 * group // slot_w
    right = jnp.concatenate([*narrowed(one[:split], slot_w), slot], axis=0)
    left = jnp.concatenate([*narrowed(three[split:], slot_w), slot], axis=0)
    right, left = turned(right, 1), turned(left, 3)
    *text_far, right, left = ordered(*text_far, right, left)
    cut_right, cut_left = split * wide, (half + TAG_ROWS - split) * wide
    two = jnp.concatenate([widened(right[:cut_right], wide), widened(left[:cut_left], wide)], axis=0)
    near_slot = jnp.stack([right[cut_right:], left[cut_left:]])
    middle = TAG_ROWS * (slot.shape[0] // TAG_ROWS // 2)
    far_slot = turned(near_slot[0, :middle], 1), turned(near_slot[1, middle:], 3)
    mine = jnp.stack([mine, one, two, three])
    theirs = swapped(mine, 1)
    near_x, near_y = swapped(near_slot, 2), swapped(near_slot, 4)
    theirs, *far_slot = ordered(theirs, *far_slot)
    far_slot = jnp.concatenate(far_slot, axis=0)
    order = (wa - jnp.arange(parts)) % parts
    vectors = jnp.take(mine[:, half + 1], order, axis=0).reshape(parts, 6, rows)
    vectors = jnp.pad(jnp.transpose(vectors, (1, 0, 2)).reshape(6, dmod), ((0, 2), (0, 0))).astype(f32)
    full_inner_bias = jnp.take(mine[:, half + 2, : ff // parts], order, axis=0).reshape(1, ff).astype(f32)

    weight, all_text, q, kv = whole_call(
        project_kernel,
        [(place, smem)] + [(a, vmem) for a in (text, text_x, text_y, *text_far, mine, theirs)],
        [
            ((dmod, 6 * group), bf16, vmem),
            ((CHIPS, tok + TAG_ROWS, dmod), bf16, vmem),
            ((CHIPS, tok, 2 * group), bf16, vmem),
            ((CHIPS, tok + TAG_ROWS, 2 * group), bf16, vmem),
        ],
        micros=8,
        mebibytes=16,
    )
    kv, near_x, near_y, far_slot = ordered(kv, near_x, near_y, far_slot)
    kv_other = swapped(kv, 1)
    first_slots = jnp.concatenate([*near_slot, *near_x, *near_y, far_slot], axis=0)
    to_x = jnp.concatenate([far_slot, near_y[1]], axis=0)
    to_y = jnp.concatenate([far_slot, near_x[0]], axis=0)
    kv_other, to_x, to_y, first_slots = ordered(kv_other, to_x, to_y, first_slots)
    to_x, to_y, to_far = swapped(to_x, 2), swapped(to_y, 4), swapped(far_slot, 6)
    first_other = swapped(first_slots, 1)

    context, turned_out, lse, bounds = whole_call(
        attend_kernel,
        [(place, smem), (q, vmem), (kv, vmem), (kv_other, vmem)],
        [
            ((CHIPS, tok, group), bf16, vmem),
            ((CHIPS, group, tok), f32, vmem),
            ((CHIPS, 3, 1, tok), f32, vmem),
            ((2, CHIPS), jnp.int32, smem),
        ],
        [
            pltpu.VMEM((3, length, 2 * HD), bf16),
            pltpu.VMEM((3, HD, length), bf16),
            pltpu.VMEM((length, TILE), f32),
            pltpu.VMEM((2 * CHIPS, 8, tok), f32),
            pltpu.VMEM((3, HD, tok), f32),
        ],
        micros=25,
        mebibytes=20,
    )
    context, to_x, to_y, to_far, first_other = ordered(context, to_x, to_y, to_far, first_other)

    def exchanged(value):
        return [value[0]] + [swapped(value[m], 2 * m) for m in range(1, CHIPS)]

    contexts = exchanged(context)
    second_slots = jnp.concatenate([to_x, to_y, to_far], axis=0)
    second_other = swapped(second_slots, 1)

    slot_rows = 2 * rows + quarter + TAG_ROWS
    result, grad_sum, grad_context, kept, sent_far, sent_near = whole_call(
        dense_kernel,
        [(place, smem)]
        + [(a, vmem) for a in (*contexts, text, cotangent[0], vectors, full_inner_bias)]
        + [
            (a, hbm)
            for a in (inner_weight, outer_weight, output_weight, first_slots, first_other, second_slots, second_other)
        ],
        [
            ((tok, dmod), bf16, vmem),
            ((tok, dmod), f32, vmem),
            ((CHIPS, tok, group), bf16, vmem),
            ((CHIPS, parts, slot_rows, slot_w), bf16, hbm),
            ((parts, slot_rows, slot_w), bf16, hbm),
            ((CHIPS - 1, parts, slot_rows, slot_w), bf16, hbm),
        ],
        [
            pltpu.VMEM((dmod, ff), bf16),
            pltpu.VMEM((ff, dmod), bf16),
            pltpu.VMEM((dmod, dmod), bf16),
            pltpu.VMEM((tok, ff), bf16),
            pltpu.VMEM((tok, ff), f32),
            pltpu.VMEM((dmod, ff), bf16),
            pltpu.VMEM((ff, dmod), bf16),
            pltpu.VMEM((dmod, dmod), bf16),
            pltpu.VMEM((2, parts, TAG_ROWS, slot_w), bf16),
            pltpu.VMEM((parts, TAG_ROWS, slot_w), f32),
            pltpu.SemaphoreType.DMA((3,)),
            pltpu.SemaphoreType.DMA((3,)),
        ],
        micros=26,
        mebibytes=50,
    )
    grad_pieces = exchanged(grad_context)

    def added(*values):
        total = values[0].astype(f32)
        for v in values[1:]:
            total = total + v.astype(f32)
        return total

    middle = parts // 2
    upper, lower = slice(0, middle), slice(middle, None)
    received_far = swapped(sent_far, 1)
    received = swapped(sent_near, 1)
    far_x = added(kept[CHIPS - 1, upper], received_far[upper]).astype(bf16)
    far_y = added(kept[CHIPS - 1, lower], received_far[lower]).astype(bf16)
    near_x = added(kept[1, upper], received[1, upper]).astype(bf16)
    near_y = added(kept[2, lower], received[2, lower]).astype(bf16)
    *grad_pieces, far_x, far_y, near_x, near_y = lax.optimization_barrier(
        (*grad_pieces, far_x, far_y, near_x, near_y)
    )
    far_x, far_y = swapped(far_x, 2), swapped(far_y, 4)
    near_x, near_y = swapped(near_x, 2), swapped(near_y, 4)

    dq, dkv, dkv_sent = whole_call(
        attend_back_kernel,
        [(place, smem), (bounds, smem)]
        + [(a, vmem) for a in (q, kv, kv_other, turned_out, lse, *grad_pieces)],
        [
            ((CHIPS, tok, 4 * group), bf16, vmem),
            ((CHIPS, tok, 2 * group), bf16, vmem),
            ((CHIPS, tok, 2 * group), bf16, vmem),
        ],
        [
            pltpu.VMEM((3, length, 4 * HD), bf16),
            pltpu.VMEM((3, 2 * HD, length), bf16),
            pltpu.VMEM((3, length, 4 * HD), f32),
            pltpu.VMEM((length, TILE), f32),
            pltpu.VMEM((2 * CHIPS, 8, tok), f32),
            pltpu.VMEM((3, 2 * HD, tok), f32),
            pltpu.VMEM((CHIPS, tok, group), bf16),
            pltpu.VMEM((3, 2 * tok, 4 * HD), bf16),
            pltpu.VMEM((3, KEY_BLOCK, 2 * tok), bf16),
        ],
        micros=34,
        mebibytes=36,
    )
    dq, dkv, dkv_sent, far_x, far_y, near_x, near_y = lax.optimization_barrier(
        (dq, dkv, dkv_sent, far_x, far_y, near_x, near_y)
    )
    dkv_received = swapped(dkv_sent, 1)
    last_x = added(kept[1, lower], received[1, lower], far_y).astype(bf16)
    last_y = added(kept[2, upper], received[2, upper], far_x).astype(bf16)
    last_x, last_y = ordered(last_x, last_y)
    last_x, last_y = swapped(last_x, 2), swapped(last_y, 4)
    dkv, partial = whole_call(
        token_grads_kernel,
        [(a, vmem) for a in (dq, dkv, dkv_received, weight)],
        [((CHIPS, tok, 2 * group), bf16, vmem), ((CHIPS, tok, dmod), bf16, vmem)],
        micros=8,
        mebibytes=16,
    )
    head_kept, head_sent = whole_call(
        head_grads_kernel,
        [(place, smem)] + [(a, vmem) for a in (all_text, dq, dkv)],
        [
            ((parts, half + TAG_ROWS, 6 * group), bf16, vmem),
            ((parts, half + TAG_ROWS, 6 * group), bf16, vmem),
        ],
        [pltpu.VMEM((dmod, 6 * group), f32)],
        micros=10,
        mebibytes=20,
    )
    head_kept, head_sent, last_x, last_y = ordered(head_kept, head_sent, last_x, last_y)

    def parts_sent(*values):
        shards = [
            added(*(lax.dynamic_index_in_dim(v, (wa + k) % parts, 0, keepdims=False) for v in values))
            for k in range(parts)
        ]
        return [v.astype(bf16) for v in shards]

    def parts_moved(values):
        return [turned(v, k) for k, v in enumerate(values) if k]

    def chips_moved(value):
        return [swapped(value, 2 * m) for m in range(1, CHIPS)]

    low, high = slice(0, cut), slice(cut, None)
    summed = jnp.concatenate(
        [
            added(kept[0, upper], received[0, upper], near_x, last_y),
            added(kept[0, lower], received[0, lower], last_x, near_y),
        ],
        axis=0,
    ).astype(bf16)
    dense_parts = parts_sent(summed)
    text_x = jnp.stack([partial[3, low], partial[1, low]])
    text_y = jnp.stack([partial[3, high], partial[2, high]])
    *dense_parts, text_x, text_y = ordered(*dense_parts, text_x, text_y)
    dense_moved = parts_moved(dense_parts)
    head_received = swapped(head_sent, 1)
    text_x, text_y = swapped(text_x, 2), swapped(text_y, 4)
    *dense_moved, text_x, text_y, head_received = ordered(*dense_moved, text_x, text_y, head_received)

    count = dmod // slot_w
    dense_summed = added(dense_parts[0], *dense_moved).astype(bf16)
    (far_x, near_x), (far_y, near_y) = text_x, text_y
    last_x = added(partial[1, high], far_y).astype(bf16)
    last_y = added(partial[2, low], far_x).astype(bf16)
    to_x = jnp.concatenate([dense_summed, *narrowed(last_x, slot_w)], axis=0)
    to_y = jnp.concatenate([dense_summed, *narrowed(last_y, slot_w)], axis=0)
    head_parts = parts_sent(head_kept, head_received)
    *head_parts, to_x, to_y, dense_summed = ordered(*head_parts, to_x, to_y, dense_summed)
    head_moved = parts_moved(head_parts)
    to_x, to_y, dense_far = swapped(to_x, 2), swapped(to_y, 4), swapped(dense_summed, 6)
    *head_moved, to_x, to_y, dense_far = ordered(*head_moved, to_x, to_y, dense_far)

    deep = dense_summed.shape[0]
    dense_all = jnp.stack([dense_summed, to_x[:deep], to_y[:deep], dense_far])
    head_summed = added(head_parts[0], *head_moved).astype(bf16)
    head_summed, dense_all = ordered(head_summed, dense_all)
    head_moved = chips_moved(head_summed)
    dense_other = swapped(dense_all, 1)
    out_inner, out_outer, out_output, small = whole_call(
        unpack_dense_kernel,
        [(place, smem), (dense_all, vmem), (dense_other, vmem)],
        [
            ((rows, ff), f32, vmem),
            (outer_weight.shape, f32, vmem),
            ((rows, dmod), f32, vmem),
            ((TAG_ROWS, slot_w), f32, vmem),
        ],
        micros=4,
    )
    last_x, last_y = widened(to_x[deep:], count), widened(to_y[deep:], count)
    input_grads = grad_sum + jnp.concatenate(
        [added(partial[0, low], near_x, last_y), added(partial[0, high], last_x, near_y)], axis=0
    )
    *head_moved, out_inner, out_outer, out_output, small, input_grads = ordered(
        *head_moved, out_inner, out_outer, out_output, small, input_grads
    )
    head_all = jnp.stack([head_summed, *head_moved])
    *out_heads, sums = whole_call(
        unpack_heads_kernel,
        [(place, smem), (head_all, vmem), (swapped(head_all, 1), vmem)],
        [((rows, dmod), f32, vmem) for _ in range(6)] + [((TAG_ROWS, 6 * group), f32, vmem)],
        micros=4,
    )

    sum_q = sums[0, : 4 * group].reshape(3, 4, HD)
    sum_v = sums[0, 4 * group :].reshape(3, 2, HD)[:, 1].reshape(rows)
    own_small = lax.dynamic_slice(small[:12].reshape(6, dmod), (0, wa * rows), (6, rows))
    return (
        result[None],
        input_grads[None],
        *out_heads[:4],
        *(sum_q[:, k].reshape(rows) for k in range(4)),
        *out_heads[4:],
        sum_v,
        out_output,
        own_small[0],
        own_small[1],
        own_small[2],
        out_inner,
        small[12:14].reshape(ff // parts),
        out_outer,
        own_small[3],
        own_small[4],
        own_small[5],
    )


def solution(mesh):
    in_specs = (
        P("wa", "ctx", None),
        P("wa", "ctx", None),
        P("wa", "ctx"),
        P("wa", "ctx"),
        P("wa", None),
        P("wa", None),
        P("wa", None),
        P("wa", None),
        P("wa"),
        P("wa"),
        P("wa"),
        P("wa"),
        P("wa", None),
        P("wa", None),
        P("wa"),
        P("wa", None),
        P("wa"),
        P("wa"),
        P("wa"),
        P("wa", None),
        P("wa"),
        P("wa", None),
        P("wa"),
        P("wa"),
        P("wa"),
    )
    out_specs = (
        P("wa", "ctx", None),
        P("wa", "ctx", None),
        P("wa", None),
        P("wa", None),
        P("wa", None),
        P("wa", None),
        P("wa"),
        P("wa"),
        P("wa"),
        P("wa"),
        P("wa", None),
        P("wa", None),
        P("wa"),
        P("wa", None),
        P("wa"),
        P("wa"),
        P("wa"),
        P("wa", None),
        P("wa"),
        P("wa", None),
        P("wa"),
        P("wa"),
        P("wa"),
    )
    body = grouped_device if mesh.shape["ctx"] == 2 * CHIPS else windowed_device
    return jax.shard_map(
        body, mesh=mesh, in_specs=in_specs, out_specs=out_specs, check_vma=False
    )
```

```python
import jax
import jax.numpy as jnp
from jax import lax
from jax.experimental import pallas as pl
from jax.experimental.pallas import tpu as pltpu
from jax.sharding import PartitionSpec as P

HD = 64


EPSILON = 1e-12
MASKED = -1e30


def as_sent(shard):
    return jax.tree.map(lambda a: a.astype(jnp.bfloat16) if a.dtype == jnp.float32 else a, shard)


def passed_along(value, axis, steps):
    count = lax.axis_size(axis)
    leading, last = (max(0, -steps), min(count, count - steps))
    return lax.ppermute(value, axis, [(source, source + steps) for source in range(leading, last)])


def layer_norm(values, gain, shift):
    center = values - jnp.mean(values, axis=-1, keepdims=True)
    spread = jnp.mean(center * center, axis=-1, keepdims=True)
    return center * lax.rsqrt(spread + EPSILON) * gain + shift


def gelu_exact(values):
    return jax.nn.gelu(values, approximate=False)


def matmul(left, right):
    return jnp.dot(left, right, preferred_element_type=jnp.float32)


def left_product(left, right):
    return lax.dot_general(
        left, right, (((0,), (0,)), ((), ())), preferred_element_type=jnp.float32
    )


def right_product(left, right):
    return lax.dot_general(
        left, right, (((1,), (1,)), ((), ())), preferred_element_type=jnp.float32
    )


def column_sums(values):
    return jnp.sum(values.astype(jnp.float32), axis=0)


def columns(values, start):
    return lax.dynamic_slice_in_dim(values, start, HD, 1)


def head_scores(query_word, query_entity, keys_head, key_entity, allowed, scale):
    word_scores = right_product(query_word, keys_head)
    entity_scores = right_product(query_entity, keys_head)
    raw = jnp.where(key_entity[None, :], entity_scores, word_scores) * scale
    return jnp.where(allowed, raw, MASKED)


def merge_heads(stacked):
    return jnp.transpose(stacked, (1, 0, 2)).reshape(
        stacked.shape[1], stacked.shape[0] * stacked.shape[2]
    )


def windowed_device(
    tokens,
    cotangent,
    segment_ids,
    token_types,
    query_wordword,
    query_wordentity,
    query_entityword,
    query_entityentity,
    bias_wordword,
    bias_wordentity,
    bias_entityword,
    bias_entityentity,
    key_weight,
    value_weight,
    value_bias,
    output_weight,
    output_bias,
    first_gain,
    first_bias,
    inner_weight,
    inner_bias,
    outer_weight,
    outer_bias,
    second_gain,
    second_bias,
):
    attention = (
        lax.all_gather(query_wordword, "wa", axis=0, tiled=True),
        lax.all_gather(query_wordentity, "wa", axis=0, tiled=True),
        lax.all_gather(query_entityword, "wa", axis=0, tiled=True),
        lax.all_gather(query_entityentity, "wa", axis=0, tiled=True),
        lax.all_gather(bias_wordword, "wa", axis=0, tiled=True),
        lax.all_gather(bias_wordentity, "wa", axis=0, tiled=True),
        lax.all_gather(bias_entityword, "wa", axis=0, tiled=True),
        lax.all_gather(bias_entityentity, "wa", axis=0, tiled=True),
        lax.all_gather(key_weight, "wa", axis=0, tiled=True),
        lax.all_gather(value_weight, "wa", axis=0, tiled=True),
        lax.all_gather(value_bias, "wa", axis=0, tiled=True),
        lax.all_gather(output_weight, "wa", axis=0, tiled=True),
        lax.all_gather(output_bias, "wa", axis=0, tiled=True),
        lax.all_gather(first_gain, "wa", axis=0, tiled=True),
        lax.all_gather(first_bias, "wa", axis=0, tiled=True),
    )
    (
        full_ww,
        full_we,
        full_ew,
        full_ee,
        shift_ww,
        shift_we,
        shift_ew,
        shift_ee,
        full_key,
        full_value,
        shift_value,
        full_output,
        shift_output,
        gain_one,
        shift_one,
    ) = attention
    feedforward = (
        lax.all_gather(inner_weight, "wa", axis=0, tiled=True),
        lax.all_gather(inner_bias, "wa", axis=0, tiled=True),
        lax.all_gather(outer_weight, "wa", axis=0, tiled=True),
        lax.all_gather(outer_bias, "wa", axis=0, tiled=True),
        lax.all_gather(second_gain, "wa", axis=0, tiled=True),
        lax.all_gather(second_bias, "wa", axis=0, tiled=True),
    )
    full_inner, shift_inner, full_outer, shift_outer, gain_two, shift_two = feedforward
    inputs = tokens[0]
    seg = segment_ids[0]
    types = token_types[0]
    tok = inputs.shape[0]
    dmod = inputs.shape[1]
    heads = dmod // HD
    scale = HD ** (-0.5)
    length = tok * lax.axis_size("ctx")
    doc_max = min(2048, 4 * tok, length // 2)
    reach = (doc_max - 2) // tok + 1
    entity = (types == 1)[:, None]
    proj_ww = matmul(inputs, full_ww) + shift_ww
    proj_we = matmul(inputs, full_we) + shift_we
    proj_ew = matmul(inputs, full_ew) + shift_ew
    proj_ee = matmul(inputs, full_ee) + shift_ee
    query_word = jnp.where(entity, proj_ew, proj_ww).astype(jnp.bfloat16)
    query_entity = jnp.where(entity, proj_ee, proj_we).astype(jnp.bfloat16)
    keys = matmul(inputs, full_key).astype(jnp.bfloat16)
    values = (matmul(inputs, full_value) + shift_value).astype(jnp.bfloat16)
    own_kv = jnp.concatenate([keys, values], axis=1)
    own_seg = seg + 1
    tags = own_seg * 2 + types

    def pass_left(packet, unused):
        moved = jax.tree.map(
            lambda part, own: part.astype(own.dtype),
            passed_along(as_sent(packet), "ctx", 1),
            packet,
        )
        return (moved, moved)

    def pass_right(packet, unused):
        moved = jax.tree.map(
            lambda part, own: part.astype(own.dtype),
            passed_along(as_sent(packet), "ctx", -1),
            packet,
        )
        return (moved, moved)

    _, (left_kv, left_tags) = lax.scan(pass_left, (own_kv, tags), None, length=reach)
    _, (right_kv, right_tags) = lax.scan(pass_right, (own_kv, tags), None, length=reach)
    window = jnp.concatenate(
        [jnp.flip(left_kv, 0).reshape(-1, 2 * dmod), own_kv, right_kv.reshape(-1, 2 * dmod)], axis=0
    )
    window_tags = jnp.concatenate(
        [jnp.flip(left_tags, 0).reshape(-1), tags, right_tags.reshape(-1)], axis=0
    )
    key_entity = window_tags % 2 == 1
    allowed = own_seg[:, None] == (window_tags // 2)[None, :]

    def head_forward(index):
        start = index * HD
        scores = head_scores(
            columns(query_word, start),
            columns(query_entity, start),
            columns(window, start),
            key_entity,
            allowed,
            scale,
        )
        top = jnp.max(scores, axis=1, keepdims=True)
        expo = jnp.exp(scores - top)
        total = jnp.sum(expo, axis=1, keepdims=True)
        probs = (expo / total).astype(jnp.bfloat16)
        return (matmul(probs, columns(window, dmod + start)), (top + jnp.log(total))[:, 0])

    head_context, lse = lax.map(head_forward, jnp.arange(heads))
    context = merge_heads(head_context).astype(jnp.bfloat16)
    branch = matmul(context, full_output) + shift_output
    first, pull_one = jax.vjp(
        layer_norm,
        inputs.astype(jnp.float32) + branch,
        gain_one.astype(jnp.float32),
        shift_one.astype(jnp.float32),
    )
    first_low = first.astype(jnp.bfloat16)
    inner = matmul(first_low, full_inner) + shift_inner
    activated, pull_gelu = jax.vjp(gelu_exact, inner)
    hidden = activated.astype(jnp.bfloat16)
    ffn = matmul(hidden, full_outer) + shift_outer
    result, pull_two = jax.vjp(
        layer_norm, first + ffn, gain_two.astype(jnp.float32), shift_two.astype(jnp.float32)
    )
    grad_sum_two, grad_gain_two, grad_shift_two = pull_two(cotangent[0].astype(jnp.float32))
    grad_ffn = grad_sum_two.astype(jnp.bfloat16)
    grad_outer = left_product(hidden, grad_ffn)
    grad_outer_shift = column_sums(grad_ffn)
    grad_inner = pull_gelu(right_product(grad_ffn, full_outer))[0].astype(jnp.bfloat16)
    grad_inner_full = left_product(first_low, grad_inner)
    grad_inner_shift = column_sums(grad_inner)
    grad_first = grad_sum_two + right_product(grad_inner, full_inner)
    grad_sum_one, grad_gain_one, grad_shift_one = pull_one(grad_first)
    grad_branch = grad_sum_one.astype(jnp.bfloat16)
    grad_output = left_product(context, grad_branch)
    grad_output_shift = column_sums(grad_branch)
    grad_context = right_product(grad_branch, full_output).astype(jnp.bfloat16)

    def head_backward(index):
        start = index * HD
        word_head = columns(query_word, start)
        entity_head = columns(query_entity, start)
        keys_head = columns(window, start)
        values_head = columns(window, dmod + start)
        context_head = columns(grad_context, start)
        scores = head_scores(word_head, entity_head, keys_head, key_entity, allowed, scale)
        probs = jnp.exp(scores - lse[index][:, None])
        grad_probs = right_product(context_head, values_head)
        delta = jnp.sum(probs * grad_probs, axis=1)
        grad_scores = (probs * (grad_probs - delta[:, None])).astype(jnp.bfloat16)
        zero = jnp.zeros_like(grad_scores)
        grad_word = jnp.where(key_entity[None, :], zero, grad_scores)
        grad_entity = jnp.where(key_entity[None, :], grad_scores, zero)
        grad_qword = matmul(grad_word, keys_head) * scale
        grad_qentity = matmul(grad_entity, keys_head) * scale
        grad_keys = (
            left_product(grad_word, word_head) + left_product(grad_entity, entity_head)
        ) * scale
        grad_values = left_product(probs.astype(jnp.bfloat16), context_head)
        return (grad_qword, grad_qentity, delta, grad_keys, grad_values)

    grad_qword, grad_qentity, delta, window_keys, window_values = lax.map(
        lambda index: head_backward(index), jnp.arange(heads)
    )
    parts_keys = merge_heads(window_keys).reshape(2 * reach + 1, tok, dmod)
    parts_values = merge_heads(window_values).reshape(2 * reach + 1, tok, dmod)

    def back_left(total, piece):
        return (
            (
                passed_along((total[0] + piece[0]).astype(jnp.bfloat16), "ctx", -1).astype(
                    jnp.float32
                ),
                passed_along((total[1] + piece[1]).astype(jnp.bfloat16), "ctx", -1).astype(
                    jnp.float32
                ),
            ),
            None,
        )

    def back_right(total, piece):
        return (
            (
                passed_along((total[0] + piece[0]).astype(jnp.bfloat16), "ctx", 1).astype(
                    jnp.float32
                ),
                passed_along((total[1] + piece[1]).astype(jnp.bfloat16), "ctx", 1).astype(
                    jnp.float32
                ),
            ),
            None,
        )

    empty = jnp.zeros((tok, dmod), jnp.float32)
    from_above, _ = lax.scan(back_left, (empty, empty), (parts_keys[:reach], parts_values[:reach]))
    from_below, _ = lax.scan(
        back_right,
        (empty, empty),
        (jnp.flip(parts_keys[reach + 1 :], 0), jnp.flip(parts_values[reach + 1 :], 0)),
    )
    own_keys = parts_keys[reach] + from_above[0] + from_below[0]
    own_values = parts_values[reach] + from_above[1] + from_below[1]
    grad_keys = own_keys.astype(jnp.bfloat16)
    grad_values = own_values.astype(jnp.bfloat16)
    grad_qword = merge_heads(grad_qword).astype(jnp.bfloat16)
    grad_qentity = merge_heads(grad_qentity).astype(jnp.bfloat16)
    zeros = jnp.zeros_like(grad_qword)
    grad_pww = jnp.where(entity, zeros, grad_qword)
    grad_pew = jnp.where(entity, grad_qword, zeros)
    grad_pwe = jnp.where(entity, zeros, grad_qentity)
    grad_pee = jnp.where(entity, grad_qentity, zeros)
    input_grads = grad_sum_one + right_product(grad_pww, full_ww) + right_product(grad_pwe, full_we)
    input_grads = input_grads + right_product(grad_pew, full_ew) + right_product(grad_pee, full_ee)
    input_grads = (
        input_grads + right_product(grad_keys, full_key) + right_product(grad_values, full_value)
    )
    local_grads = (
        left_product(inputs, grad_pww),
        left_product(inputs, grad_pwe),
        left_product(inputs, grad_pew),
        left_product(inputs, grad_pee),
        column_sums(grad_pww),
        column_sums(grad_pwe),
        column_sums(grad_pew),
        column_sums(grad_pee),
        left_product(inputs, grad_keys),
        left_product(inputs, grad_values),
        column_sums(grad_values),
        grad_output,
        grad_output_shift,
        grad_gain_one,
        grad_shift_one,
        grad_inner_full,
        grad_inner_shift,
        grad_outer,
        grad_outer_shift,
        grad_gain_two,
        grad_shift_two,
    )
    shards = (
        lax.psum_scatter(
            local_grads[0].astype(jnp.bfloat16), "wa", scatter_dimension=0, tiled=True
        ).astype(jnp.float32),
        lax.psum_scatter(
            local_grads[1].astype(jnp.bfloat16), "wa", scatter_dimension=0, tiled=True
        ).astype(jnp.float32),
        lax.psum_scatter(
            local_grads[2].astype(jnp.bfloat16), "wa", scatter_dimension=0, tiled=True
        ).astype(jnp.float32),
        lax.psum_scatter(
            local_grads[3].astype(jnp.bfloat16), "wa", scatter_dimension=0, tiled=True
        ).astype(jnp.float32),
        lax.psum_scatter(
            local_grads[4].astype(jnp.bfloat16), "wa", scatter_dimension=0, tiled=True
        ).astype(jnp.float32),
        lax.psum_scatter(
            local_grads[5].astype(jnp.bfloat16), "wa", scatter_dimension=0, tiled=True
        ).astype(jnp.float32),
        lax.psum_scatter(
            local_grads[6].astype(jnp.bfloat16), "wa", scatter_dimension=0, tiled=True
        ).astype(jnp.float32),
        lax.psum_scatter(
            local_grads[7].astype(jnp.bfloat16), "wa", scatter_dimension=0, tiled=True
        ).astype(jnp.float32),
        lax.psum_scatter(
            local_grads[8].astype(jnp.bfloat16), "wa", scatter_dimension=0, tiled=True
        ).astype(jnp.float32),
        lax.psum_scatter(
            local_grads[9].astype(jnp.bfloat16), "wa", scatter_dimension=0, tiled=True
        ).astype(jnp.float32),
        lax.psum_scatter(
            local_grads[10].astype(jnp.bfloat16), "wa", scatter_dimension=0, tiled=True
        ).astype(jnp.float32),
        lax.psum_scatter(
            local_grads[11].astype(jnp.bfloat16), "wa", scatter_dimension=0, tiled=True
        ).astype(jnp.float32),
        lax.psum_scatter(
            local_grads[12].astype(jnp.bfloat16), "wa", scatter_dimension=0, tiled=True
        ).astype(jnp.float32),
        lax.psum_scatter(
            local_grads[13].astype(jnp.bfloat16), "wa", scatter_dimension=0, tiled=True
        ).astype(jnp.float32),
        lax.psum_scatter(
            local_grads[14].astype(jnp.bfloat16), "wa", scatter_dimension=0, tiled=True
        ).astype(jnp.float32),
        lax.psum_scatter(
            local_grads[15].astype(jnp.bfloat16), "wa", scatter_dimension=0, tiled=True
        ).astype(jnp.float32),
        lax.psum_scatter(
            local_grads[16].astype(jnp.bfloat16), "wa", scatter_dimension=0, tiled=True
        ).astype(jnp.float32),
        lax.psum_scatter(
            local_grads[17].astype(jnp.bfloat16), "wa", scatter_dimension=0, tiled=True
        ).astype(jnp.float32),
        lax.psum_scatter(
            local_grads[18].astype(jnp.bfloat16), "wa", scatter_dimension=0, tiled=True
        ).astype(jnp.float32),
        lax.psum_scatter(
            local_grads[19].astype(jnp.bfloat16), "wa", scatter_dimension=0, tiled=True
        ).astype(jnp.float32),
        lax.psum_scatter(
            local_grads[20].astype(jnp.bfloat16), "wa", scatter_dimension=0, tiled=True
        ).astype(jnp.float32),
    )
    totals = lax.psum(
        (
            shards[0],
            shards[1],
            shards[2],
            shards[3],
            shards[4],
            shards[5],
            shards[6],
            shards[7],
            shards[8],
            shards[9],
            shards[10],
            shards[11],
            shards[12],
            shards[13],
            shards[14],
            shards[15],
            shards[16],
            shards[17],
            shards[18],
            shards[19],
            shards[20],
        ),
        "ctx",
    )
    return (
        result.astype(jnp.bfloat16)[None],
        input_grads[None],
        totals[0],
        totals[1],
        totals[2],
        totals[3],
        totals[4],
        totals[5],
        totals[6],
        totals[7],
        totals[8],
        totals[9],
        totals[10],
        totals[11],
        totals[12],
        totals[13],
        totals[14],
        totals[15],
        totals[16],
        totals[17],
        totals[18],
        totals[19],
        totals[20],
    )


CHIPS = 4
KEY_BLOCK = 256
NEGATIVE = -1e30
TAG_ROWS = 16
TILE = 128
FLOPS_PER_MICRO = 1_100_000_000


def lanes_product(left, right):
    return lax.dot_general(
        left, right, (((1,), (1,)), ((), ())), preferred_element_type=jnp.float32
    )


def rows_product(left, right):
    return lax.dot_general(
        left, right, (((0,), (0,)), ((), ())), preferred_element_type=jnp.float32
    )


def plain_product(left, right):
    return jnp.dot(left, right, preferred_element_type=jnp.float32)


def swapped(value, step):
    count = lax.axis_size("ctx")
    return lax.ppermute(value, "ctx", [(i, i ^ step) for i in range(count)])


def turned(value, step):
    count = lax.axis_size("wa")
    return lax.ppermute(value, "wa", [(i, (i + step) % count) for i in range(count)])


def narrowed(value, width):
    return [value[:, at : at + width] for at in range(0, value.shape[1], width)]


def widened(value, count):
    rows = value.shape[0] // count
    return jnp.concatenate([value[rows * k : rows * (k + 1)] for k in range(count)], axis=1)


def ordered(*values):
    return lax.optimization_barrier(values)


def as_column(row):
    return jnp.broadcast_to(row, (TILE, row.shape[1])).T


def segment_of(tag):
    return jnp.floor(tag * 0.5)


def prepare_kernel(
    place, ww, we, ew, ee, key, value, *others
):
    *lines, inner, outer, output, mine, slot, sem = others
    rows = key.shape[0]
    half, quarter = rows // 2, rows // CHIPS
    slot_w = slot.shape[1]
    chip, core = place[0], place[1]
    index = 2 * chip + core
    copies = [
        (inner.at[:, pl.ds(pl.multiple_of(slot_w * index, TILE), slot_w)], slot.at[pl.ds(0, rows), :])
    ]
    for v in range(2):
        copies.append(
            (
                outer.at[pl.ds(pl.multiple_of(half * index, 16), half), pl.ds(slot_w * v, slot_w)],
                slot.at[pl.ds(rows + half * v, half), :],
            )
        )
    copies.append(
        (
            output.at[
                pl.ds(pl.multiple_of(quarter * chip, 16), quarter),
                pl.ds(pl.multiple_of(slot_w * core, TILE), slot_w),
            ],
            slot.at[pl.ds(2 * rows, quarter), :],
        )
    )
    copies = [pltpu.make_async_copy(a, b, sem.at[k]) for k, (a, b) in enumerate(copies)]
    for copy in copies:
        copy.start()
    at = pl.ds(pl.multiple_of(half * core, 16), half)
    for g in range(CHIPS):

        @pl.when(chip == g)
        def _():
            def heads(sources):
                return jnp.concatenate(
                    [
                        w[at, HD * (3 * g + h) : HD * (3 * g + h + 1)].astype(jnp.float32)
                        for h in range(3)
                        for w in sources
                    ],
                    axis=1,
                ).astype(jnp.bfloat16)

            mine[:half, : 4 * 3 * HD] = heads((ww, we, ew, ee))
            mine[:half, 4 * 3 * HD :] = heads((key, value))

    lines = [line[...].astype(jnp.float32).reshape(1, line.shape[0]) for line in lines]
    bias = [lines[k][:, HD * h : HD * (h + 1)] for h in range(3) for k in range(4)]
    for h in range(3):
        bias += [jnp.zeros((1, HD), jnp.float32), lines[4][:, HD * h : HD * (h + 1)]]
    six = jnp.concatenate(lines[5:11], axis=1)
    last = jnp.concatenate([lines[11], jnp.zeros((1, 2 * rows), jnp.float32)], axis=1)
    which = lax.broadcasted_iota(jnp.int32, (TAG_ROWS, 6 * rows), 0)
    below = jnp.where(which == 0, jnp.concatenate(bias, axis=1), jnp.where(which == 1, six, last))
    mine[half:] = jnp.where(which < 3, below, 0.0).astype(jnp.bfloat16)
    for copy in copies:
        copy.wait()


def project_kernel(
    place, t0, t1, t2, t3a, t3b, mine3, mine_two, theirs3, theirs_two, weight, tokens, q_ref, kv_ref, mine, theirs
):
    parts, rows = mine.shape[0], mine.shape[1] - TAG_ROWS
    for target, three, two in ((mine, mine3, mine_two), (theirs, theirs3, theirs_two)):
        target[0] = three[0]
        target[1] = three[1]
        target[2] = two[...]
        target[3] = three[2]
    tok = q_ref.shape[1]
    chip, core, wa = place[0], place[1], place[2]
    cut = t3a.shape[0]
    tokens[0] = t0[...]
    tokens[1] = t1[...]
    tokens[2] = t2[...]
    tokens[3, :cut] = t3a[...]
    tokens[3, cut:] = t3b[...]
    for z in range(parts):
        k = lax.rem(wa - z + parts, parts)
        for source, side in ((mine, core), (theirs, 1 - core)):
            weight[pl.ds(pl.multiple_of(2 * rows * z + rows * side, 32), rows), :] = source[k, :rows]
    k = lax.rem(wa - chip + parts, parts)
    bias = mine[k, rows : rows + TAG_ROWS].astype(jnp.float32)[:1]
    wide = 2 * HD

    def piece(m, unused):
        to = jnp.bitwise_xor(chip, m)
        tags = tokens[m, tok : tok + TAG_ROWS].astype(jnp.float32)[:1, :tok]
        flag = as_column(tags - 2.0 * segment_of(tags)) == 1.0
        text = tokens[m, :tok]
        for h in range(3):
            at = 2 * wide * h
            both = plain_product(text, weight[:, at : at + 2 * wide]) + bias[:, at : at + 2 * wide]
            q = jnp.where(flag, both[:, wide:], both[:, :wide]).astype(jnp.bfloat16)
            q_ref[to, :, wide * h : wide * (h + 1)] = q * jnp.bfloat16(HD**-0.5)
        kv = plain_product(text, weight[:, 6 * wide :]) + bias[:, 6 * wide :]
        kv_ref[to, :tok] = kv.astype(jnp.bfloat16)
        kv_ref[to, tok:] = jnp.broadcast_to(tags, (TAG_ROWS, tok)).astype(jnp.bfloat16)
        return 0

    lax.fori_loop(0, CHIPS, piece, 0)


def ones_where(shape, test):
    row = lax.broadcasted_iota(jnp.int32, shape, 0)
    column = lax.broadcasted_iota(jnp.int32, shape, 1)
    return jnp.where(test(row, column), 1.0, 0.0).astype(jnp.bfloat16)


def unit(size):
    return ones_where((size, size), lambda row, column: row == column)


def attend_kernel(
    place, q_ref, own, other, out0, out1, out2, out3, turned_out, lse, bounds, keys, values, seg_col, seg_row, acc, out
):
    tok = q_ref.shape[1]
    core = place[1]
    twice = ones_where((2 * HD, 2 * HD), lambda row, column: row == lax.rem(column, HD))
    upper = ones_where((HD, 2 * HD), lambda row, column: column == row + HD)

    def prepare(j, unused):
        for source, side in ((own, core), (other, 1 - core)):
            shard = 2 * j + side
            at = pl.ds(pl.multiple_of(shard * tok, TILE), tok)
            tags = source[j, tok : tok + TAG_ROWS].astype(jnp.float32)[:1]
            seg_row[shard] = jnp.broadcast_to(segment_of(tags), (8, tok))
            column = as_column(tags)
            segment = segment_of(column)
            seg_col[at, :] = segment
            flag = column - 2.0 * segment == 1.0
            for h in range(3):
                kv = source[j, :tok, 2 * HD * h : 2 * HD * (h + 1)]
                low = lax.broadcasted_iota(jnp.int32, kv.shape, 1) < HD
                keys[h, at, :] = jnp.where(low == flag, 0.0, plain_product(kv, twice)).astype(jnp.bfloat16)
                values[h, :, at] = lanes_product(upper, kv).astype(jnp.bfloat16)
        return 0

    lax.fori_loop(0, CHIPS, prepare, 0)

    def queries(j, unused):
        seg = seg_row[2 * j + core][:1]
        everyone = seg_row[...][:, 0, :]
        before = jnp.sum((everyone < jnp.min(seg)).astype(jnp.float32)).astype(jnp.int32)
        through = jnp.sum((everyone <= jnp.max(seg)).astype(jnp.float32)).astype(jnp.int32)
        first = before // KEY_BLOCK
        last = (through + KEY_BLOCK - 1) // KEY_BLOCK
        bounds[0, j] = first
        bounds[1, j] = last
        acc[...] = jnp.zeros_like(acc)

        def step(t, carry):
            at = pl.ds(pl.multiple_of(t * KEY_BLOCK, KEY_BLOCK), KEY_BLOCK)
            column = seg_col[at, :]
            same = jnp.concatenate([column] * (tok // TILE), axis=1) == seg
            after = []
            queries = [q_ref[j, :, 2 * HD * h : 2 * HD * (h + 1)] for h in range(3)]
            scores = [
                jnp.where(same, lanes_product(keys[h, at, :], queries[h]), NEGATIVE) for h in range(3)
            ]
            peaks = [
                jnp.maximum(carry[2 * h], jnp.max(scores[h], axis=0, keepdims=True)) for h in range(3)
            ]
            expo = [jnp.exp(scores[h] - peaks[h]) for h in range(3)]
            for h in range(3):
                fade = jnp.exp(carry[2 * h] - peaks[h])
                total = carry[2 * h + 1] * fade + jnp.sum(expo[h], axis=0, keepdims=True)
                acc[h] = acc[h] * fade + plain_product(values[h, :, at], expo[h].astype(jnp.bfloat16))
                after += [peaks[h], total]
            return tuple(after)

        start = (jnp.full((1, tok), NEGATIVE, jnp.float32), jnp.zeros((1, tok), jnp.float32)) * 3
        done = lax.fori_loop(first, last, step, start)
        for h in range(3):
            turned_out[j, HD * h : HD * (h + 1), :] = acc[h] / done[2 * h + 1]
            lse[j, h] = done[2 * h] + jnp.log(done[2 * h + 1])
        out[jnp.bitwise_xor(place[0], j)] = turned_out[j].T.astype(jnp.bfloat16)
        return 0

    lax.fori_loop(0, CHIPS, queries, 0)
    for m, target in enumerate((out0, out1, out2, out3)):
        target[...] = out[m]


def attend_back_kernel(
    place,
    bounds,
    q_ref,
    own,
    other,
    turned_out,
    lse,
    grad0,
    grad1,
    grad2,
    grad3,
    dq_ref,
    dkv_own,
    dkv_other,
    sources,
    turned_keys,
    grads,
    seg_col,
    seg_row,
    acc,
    grad,
    pair,
    mixed,
):
    tok = q_ref.shape[1]
    chip, core = place[0], place[1]
    wide = 2 * HD
    for m, piece in enumerate((grad0, grad1, grad2, grad3)):
        grad[jnp.bitwise_xor(chip, m)] = piece[...]
    twice = ones_where((wide, wide), lambda row, column: row == lax.rem(column, HD))
    turned_twice = ones_where((wide, wide), lambda row, column: column == lax.rem(row, HD))
    folded = ones_where((wide, wide), lambda row, column: column == lax.rem(row, HD))
    all_rows, group = unit(tok), unit(3 * HD)
    pair[...] = jnp.zeros_like(pair)

    def prepare(j, unused):
        for source, side in ((own, core), (other, 1 - core)):
            shard = 2 * j + side
            at = pl.ds(pl.multiple_of(shard * tok, TILE), tok)
            tags = source[j, tok : tok + TAG_ROWS].astype(jnp.float32)[:1]
            seg_row[shard] = jnp.broadcast_to(tags, (8, tok))
            column = as_column(tags)
            segment = segment_of(column)
            seg_col[at, :] = segment
            flag = column - 2.0 * segment == 1.0
            row_flag = tags - 2.0 * segment_of(tags) == 1.0
            for h in range(3):
                kv = source[j, :tok, wide * h : wide * (h + 1)]
                low = lax.broadcasted_iota(jnp.int32, kv.shape, 1) < HD
                sources[h, at, :wide] = jnp.where(low == flag, 0.0, plain_product(kv, twice)).astype(
                    jnp.bfloat16
                )
                sources[h, at, wide:] = kv
                both = lanes_product(turned_twice, kv)
                low = lax.broadcasted_iota(jnp.int32, both.shape, 0) < HD
                turned_keys[h, :, at] = jnp.where(low == row_flag, 0.0, both).astype(jnp.bfloat16)
                grads[h, at, :] = jnp.zeros((tok, 2 * wide), jnp.float32)
        return 0

    lax.fori_loop(0, CHIPS, prepare, 0)

    def queries(j, unused):
        tags = seg_row[2 * j + core][:1]
        seg = segment_of(tags)
        slot = jnp.bitwise_xor(chip, j)
        flag = as_column(tags - 2.0 * seg) == 1.0
        turned_grad = lanes_product(group, grad[j])
        deltas, shifts = [], []
        for h in range(3):
            rows = slice(HD * h, HD * (h + 1))
            deltas.append(jnp.sum(turned_grad[rows] * turned_out[j, rows, :], axis=0, keepdims=True))
            shifts.append(lse[j, h])
            pair[h, :tok, :wide] = q_ref[j, :, wide * h : wide * (h + 1)]
            pair[h, tok:, wide + HD :] = grad[j, :, rows]
        acc[...] = jnp.zeros_like(acc)

        def step(t, carry):
            at = pl.ds(pl.multiple_of(t * KEY_BLOCK, KEY_BLOCK), KEY_BLOCK)
            column = seg_col[at, :]
            same = jnp.concatenate([column] * (tok // TILE), axis=1) == seg
            both = [lanes_product(sources[h, at, :], pair[h]) for h in range(3)]
            for h in range(3):
                probs = jnp.where(same, jnp.exp(both[h][:, :tok] - shifts[h]), 0.0)
                mixed[h, :, :tok] = (probs * (both[h][:, tok:] - deltas[h])).astype(jnp.bfloat16)
                mixed[h, :, tok:] = probs.astype(jnp.bfloat16)
            for h in range(3):
                grads[h, at, :] += plain_product(mixed[h], pair[h])
                acc[h] += plain_product(turned_keys[h, :, at], mixed[h, :, :tok])
            return carry

        lax.fori_loop(bounds[0, j], bounds[1, j], step, 0)
        for h in range(3):
            dq = lanes_product(all_rows, (acc[h] * (HD**-0.5)).astype(jnp.bfloat16))
            at = 2 * wide * h
            dq_ref[slot, :, at : at + wide] = jnp.where(flag, 0.0, dq).astype(jnp.bfloat16)
            dq_ref[slot, :, at + wide : at + 2 * wide] = jnp.where(flag, dq, 0.0).astype(jnp.bfloat16)
        return 0

    lax.fori_loop(0, CHIPS, queries, 0)

    def finish(j, unused):
        slot = jnp.bitwise_xor(chip, j)
        for target, side in ((dkv_own, core), (dkv_other, 1 - core)):
            shard = 2 * j + side
            at = pl.ds(pl.multiple_of(shard * tok, TILE), tok)
            tags = seg_row[shard][:1]
            flag = as_column(tags - 2.0 * segment_of(tags)) == 1.0
            for h in range(3):
                low = lax.broadcasted_iota(jnp.int32, (tok, wide), 1) < HD
                dk = jnp.where(low == flag, 0.0, grads[h, at, :wide]).astype(jnp.bfloat16)
                target[slot, :, wide * h : wide * (h + 1)] = jnp.where(
                    low, plain_product(dk, folded), grads[h, at, wide:]
                ).astype(jnp.bfloat16)
        return 0

    lax.fori_loop(0, CHIPS, finish, 0)


def normed(total, gain, shift):
    center = total - jnp.mean(total, axis=-1, keepdims=True)
    spread = jnp.mean(center * center, axis=-1, keepdims=True)
    inverse = lax.rsqrt(spread + EPSILON)
    unit = center * inverse
    return unit * gain + shift, unit, inverse


def normed_back(grad, unit, inverse, gain):
    scaled = grad * gain
    mean = jnp.mean(scaled, axis=-1, keepdims=True)
    along = jnp.mean(scaled * unit, axis=-1, keepdims=True)
    return inverse * (scaled - mean - unit * along)


def summed_rows(value):
    return jnp.sum(value, axis=0, keepdims=True)


def dense_kernel(
    place,
    context0,
    context1,
    context2,
    context3,
    text,
    cotangent,
    lines,
    inner_shard,
    outer_shard,
    output_shard,
    first_own,
    first_other,
    second_own,
    second_other,
    result,
    grad_sum,
    grad0,
    grad1,
    grad2,
    grad3,
    kept,
    sent_first,
    sent_second,
    inner_w,
    outer_w,
    output_w,
    hidden,
    slope,
    inner_g,
    outer_g,
    output_g,
    small,
    sums,
    inner_bias,
    in_sems,
    out_sems,
):
    bf16, f32 = jnp.bfloat16, jnp.float32
    chip, core, wa = place[0], place[1], place[2]
    tok, dmod = result.shape
    ff = hidden.shape[1]
    group = dmod // CHIPS
    parts = CHIPS
    rows = dmod // parts
    half = rows // 2
    quarter = rows // CHIPS
    slot_w = ff // (2 * CHIPS)

    context = (context0, context1, context2, context3)

    def head_rows(m):
        return pl.ds(pl.multiple_of(group * jnp.bitwise_xor(chip, m), 64), group)

    pltpu.make_async_copy(
        output_shard, output_w.at[pl.ds(pl.multiple_of(rows * wa, 16), rows), :], in_sems.at[0]
    ).start()
    pltpu.make_async_copy(
        inner_shard, inner_w.at[pl.ds(pl.multiple_of(rows * wa, 16), rows), :], in_sems.at[1]
    ).start()
    deep = first_own.shape[0] // 7
    places = [(0, 0, 0, 1), (0, 1, 0, 3), (0, 2, 1, 1), (0, 3, 1, 3), (0, 4, 2, 1), (0, 5, 2, 3), (0, 6, 0, 2)]
    places += [(1, 0, 1, 2), (1, 1, 3, 3), (1, 2, 2, 2), (1, 3, 3, 1), (1, 4, 3, 2)]
    sides = []
    for which, at, m, k in places:
        g = jnp.bitwise_xor(chip, m)
        z = lax.rem(wa - k + parts, parts)
        sides.append(((first_own, second_own)[which], deep * at, g, core, z))
        sides.append(((first_other, second_other)[which], deep * at, g, 1 - core, z))
    for source, at, g, side, z in sides:
        pltpu.make_async_copy(
            source.at[pl.ds(at + 2 * rows, quarter), :],
            output_w.at[
                pl.ds(pl.multiple_of(rows * z + quarter * g, 16), quarter),
                pl.ds(pl.multiple_of(slot_w * side, TILE), slot_w),
            ],
            in_sems.at[0],
        ).start()
    for source, at, g, side, z in sides:
        pltpu.make_async_copy(
            source.at[pl.ds(at, rows), :],
            inner_w.at[
                pl.ds(pl.multiple_of(rows * z, 16), rows),
                pl.ds(pl.multiple_of(slot_w * (2 * g + side), TILE), slot_w),
            ],
            in_sems.at[1],
        ).start()
    pltpu.make_async_copy(
        outer_shard, outer_w.at[pl.ds(pl.multiple_of(dmod * wa, 16), dmod), :], in_sems.at[2]
    ).start()
    for source, at, g, side, z in sides:
        for v in range(2):
            pltpu.make_async_copy(
                source.at[pl.ds(at + rows + half * v, half), :],
                outer_w.at[
                    pl.ds(pl.multiple_of(dmod * z + half * (2 * g + side), 16), half),
                    pl.ds(slot_w * v, slot_w),
                ],
                in_sems.at[2],
            ).start()

    names = ("outb", "g1", "s1", "outerb", "g2", "s2")
    lined = [lines[lax.rem(wa - z + parts, parts)].astype(f32) for z in range(parts)]
    vec = {
        name: jnp.concatenate([line[1:2, rows * k : rows * (k + 1)] for line in lined], axis=1)
        for k, name in enumerate(names)
    }
    inner_bias[...] = jnp.concatenate([line[2:3, : ff // parts] for line in lined], axis=1)

    pltpu.make_async_copy(output_w, output_w, in_sems.at[0]).wait()
    branch = vec["outb"]
    for m in range(CHIPS):
        branch = branch + plain_product(context[m][...], output_w[head_rows(m), :])
    first, unit_one, inverse_one = normed(text[:tok, :].astype(f32) + branch, vec["g1"], vec["s1"])
    low = first.astype(bf16)

    pltpu.make_async_copy(inner_w, inner_w, in_sems.at[1]).wait()

    def forward(s, carry):
        at = pl.ds(pl.multiple_of(2 * slot_w * s, TILE), 2 * slot_w)
        inner = plain_product(low, inner_w[:, at]) + inner_bias[:, at]
        cdf = 0.5 + 0.5 * lax.erf(inner * (0.5**0.5))
        hidden[:, at] = (inner * cdf).astype(bf16)
        slope[:, at] = cdf + inner * (jnp.exp(-0.5 * inner * inner) * (0.5 / jnp.pi) ** 0.5)
        return carry

    lax.fori_loop(0, CHIPS, forward, 0)
    pltpu.make_async_copy(outer_w, outer_w, in_sems.at[2]).wait()
    ffn = plain_product(hidden[...], outer_w[...]) + vec["outerb"]
    second, unit_two, inverse_two = normed(first + ffn, vec["g2"], vec["s2"])
    result[...] = second.astype(bf16)
    grad_out = cotangent[...].astype(f32)
    grad_two = normed_back(grad_out, unit_two, inverse_two, vec["g2"])
    low_two = grad_two.astype(bf16)

    sums[...] = jnp.zeros_like(sums)

    def put(row, value):
        for v in range(2):
            for z in range(parts):
                sums[z, row + v : row + v + 1, :] = value[:, slot_w * v : slot_w * (v + 1)]

    put(6, summed_rows(low_two.astype(f32)))
    put(8, summed_rows(grad_out * unit_two))
    put(10, summed_rows(grad_out))
    low_turned = low.astype(f32).T.astype(bf16)

    def backward(s, carry):
        at = pl.ds(pl.multiple_of(2 * slot_w * s, TILE), 2 * slot_w)
        grad_hidden = lanes_product(low_two, outer_w[at, :])
        grad_inner = (grad_hidden * slope[:, at]).astype(bf16)
        outer_g[at, :] = rows_product(hidden[:, at], low_two).astype(bf16)
        hidden[:, at] = grad_inner
        inner_g[:, at] = plain_product(low_turned, grad_inner).astype(bf16)
        totals = summed_rows(grad_inner.astype(f32))
        sums[s, 12:13, :] = totals[:, :slot_w]
        sums[s, 13:14, :] = totals[:, slot_w:]
        return carry

    lax.fori_loop(0, CHIPS, backward, 0)

    def targets():
        spans = [(3, 0, 4, 0, 0), (1, 0, 2, 0, 4), (2, 2, 4, 0, 6), (0, 0, 4, 1, 0), (1, 2, 4, 1, 4), (2, 0, 2, 1, 6)]
        for m in range(CHIPS):
            yield kept.at[m], 0, parts, jnp.bitwise_xor(chip, m), core, 0
        for m, low_z, high_z, which, at in spans:
            target = (sent_first, sent_second)[which].at[pl.ds(at, high_z - low_z)]
            yield target, low_z, high_z - low_z, jnp.bitwise_xor(chip, m), 1 - core, 1 + which

    inner_view = inner_g.reshape(parts, rows, ff)
    outer_view = outer_g.reshape(parts, dmod, dmod)
    output_view = output_g.reshape(parts, rows, dmod)
    for target, z, count, g, side, sem in targets():
        s = 2 * g + side
        pltpu.make_async_copy(
            inner_view.at[pl.ds(z, count), :, pl.ds(pl.multiple_of(slot_w * s, TILE), slot_w)],
            target.at[:, pl.ds(0, rows), :],
            out_sems.at[sem],
        ).start()
        for v in range(2):
            pltpu.make_async_copy(
                outer_view.at[
                    pl.ds(z, count), pl.ds(pl.multiple_of(half * s, 16), half), pl.ds(slot_w * v, slot_w)
                ],
                target.at[:, pl.ds(rows + half * v, half), :],
                out_sems.at[sem],
            ).start()

    grad_first = grad_two + lanes_product(hidden[...], inner_w[...])
    put(2, summed_rows(grad_first * unit_one))
    put(4, summed_rows(grad_first))
    grad_one = normed_back(grad_first, unit_one, inverse_one, vec["g1"])
    grad_sum[...] = grad_one
    low_one = grad_one.astype(bf16)
    put(0, summed_rows(low_one.astype(f32)))
    small[0] = jnp.zeros_like(small[0])
    small[1] = sums[...].astype(bf16)
    for m in range(CHIPS):
        at = head_rows(m)
        output_g[at, :] = rows_product(context[m][...], low_one).astype(bf16)
        (grad0, grad1, grad2, grad3)[m][...] = lanes_product(low_one, output_w[at, :]).astype(bf16)
    for target, z, count, g, side, sem in targets():
        pltpu.make_async_copy(
            output_view.at[
                pl.ds(z, count),
                pl.ds(pl.multiple_of(quarter * g, 16), quarter),
                pl.ds(pl.multiple_of(slot_w * side, TILE), slot_w),
            ],
            target.at[:, pl.ds(2 * rows, quarter), :],
            out_sems.at[sem],
        ).start()
        filled = jnp.where(2 * g + side == 0, 1, 0)
        pltpu.make_async_copy(
            small.at[filled, pl.ds(z, count)],
            target.at[:, pl.ds(2 * rows + quarter, TAG_ROWS), :],
            out_sems.at[sem],
        ).start()
    for sem, target in enumerate((kept, sent_first, sent_second)):
        pltpu.make_async_copy(target, target, out_sems.at[sem]).wait()


def head_grads_kernel(place, tokens, dq, dkv, kept, sent, acc):
    tok = dq.shape[1]
    core = place[1]
    wide = dq.shape[2]
    parts, rows = kept.shape[0], kept.shape[1] - TAG_ROWS
    acc[...] = jnp.zeros_like(acc)

    def piece(m, carry):
        text = tokens[m, :tok]
        text_turned = text.astype(jnp.float32).T.astype(jnp.bfloat16)
        acc[:, :wide] += plain_product(text_turned, dq[m])
        acc[:, wide:] += plain_product(text_turned, dkv[m])
        return (
            carry[0] + summed_rows(dq[m].astype(jnp.float32)),
            carry[1] + summed_rows(dkv[m].astype(jnp.float32)),
        )

    start = (jnp.zeros((1, wide), jnp.float32), jnp.zeros((1, wide // 2), jnp.float32))
    sums = jnp.concatenate(lax.fori_loop(0, CHIPS, piece, start), axis=1)
    sums = jnp.broadcast_to(sums, (TAG_ROWS, sums.shape[1]))
    for z in range(parts):
        for target, side in ((kept, core), (sent, 1 - core)):
            at = pl.ds(pl.multiple_of(2 * rows * z + rows * side, 32), rows)
            target[z, :rows] = acc[at, :].astype(jnp.bfloat16)
            target[z, rows:] = jnp.where(side == 0, sums, 0.0).astype(jnp.bfloat16)


def token_grads_kernel(dq, dkv_own, dkv_other, weight, dkv, partial):
    wide = dq.shape[2]

    def piece(m, carry):
        both = dkv_own[m].astype(jnp.float32) + dkv_other[m].astype(jnp.float32)
        dkv[m] = both.astype(jnp.bfloat16)
        partial[m] = (
            lanes_product(dq[m], weight[:, :wide]) + lanes_product(dkv[m], weight[:, wide:])
        ).astype(jnp.bfloat16)
        return carry

    lax.fori_loop(0, CHIPS, piece, 0)


def picked_piece(place, own, other, g, side, rows):
    m = jnp.bitwise_xor(place[0], g)
    here = own[m, rows, :].astype(jnp.float32)
    there = other[m, rows, :].astype(jnp.float32)
    return jnp.where(place[1] == side, here, there)


def unpack_dense_kernel(place, own, other, inner, outer, output, small):
    rows = inner.shape[0]
    half, quarter = rows // 2, rows // CHIPS
    slot_w = own.shape[2]
    for g in range(CHIPS):
        for side in range(2):
            s = 2 * g + side
            at = slice(slot_w * s, slot_w * (s + 1))
            inner[:, at] = picked_piece(place, own, other, g, side, slice(0, rows))
            for v in range(2):
                outer[half * s : half * (s + 1), slot_w * v : slot_w * (v + 1)] = picked_piece(
                    place, own, other, g, side, slice(rows + half * v, rows + half * (v + 1))
                )
            output[quarter * g : quarter * (g + 1), slot_w * side : slot_w * (side + 1)] = picked_piece(
                place, own, other, g, side, slice(2 * rows, 2 * rows + quarter)
            )
    small[...] = picked_piece(place, own, other, 0, 0, slice(2 * rows + quarter, own.shape[1]))


def unpack_heads_kernel(
    place, own, other, ww, we, ew, ee, key, value, sum_ww, sum_we, sum_ew, sum_ee, sum_value
):
    rows = own.shape[1] - TAG_ROWS
    wide = 4 * 3 * HD
    for side in range(2):
        at = slice(rows * side, rows * (side + 1))
        pieces = [picked_piece(place, own, other, g, side, slice(0, rows)) for g in range(CHIPS)]
        for k, target in enumerate((ww, we, ew, ee)):
            target[at, :] = jnp.concatenate(
                [p[:, HD * (4 * h + k) : HD * (4 * h + k + 1)] for p in pieces for h in range(3)], axis=1
            )
        for k, target in enumerate((key, value)):
            target[at, :] = jnp.concatenate(
                [
                    p[:, wide + HD * (2 * h + k) : wide + HD * (2 * h + k + 1)]
                    for p in pieces
                    for h in range(3)
                ],
                axis=1,
            )
    sums = picked_piece(place, own, other, place[2], 0, slice(rows, rows + TAG_ROWS))[:1]
    for k, target in enumerate((sum_ww, sum_we, sum_ew, sum_ee)):
        line = [sums[:, HD * (4 * h + k) : HD * (4 * h + k + 1)] for h in range(3)]
        target[...] = jnp.concatenate(line, axis=1).reshape(target.shape[0])
    line = [sums[:, wide + HD * (2 * h + 1) : wide + HD * (2 * h + 2)] for h in range(3)]
    sum_value[...] = jnp.concatenate(line, axis=1).reshape(sum_value.shape[0])


def smem():
    return pl.BlockSpec(memory_space=pltpu.SMEM)


def vmem():
    return pl.BlockSpec(memory_space=pltpu.VMEM)


def hbm():
    return pl.BlockSpec(memory_space=pl.ANY)


def whole_call(kernel, operands, outs, scratch=(), micros=1, mebibytes=16):
    return pl.pallas_call(
        kernel,
        out_shape=[jax.ShapeDtypeStruct(shape, dtype) for shape, dtype, _ in outs],
        in_specs=[spec() for _, spec in operands],
        out_specs=[spec() for _, _, spec in outs],
        scratch_shapes=list(scratch),
        compiler_params=pltpu.CompilerParams(vmem_limit_bytes=mebibytes << 20),
        cost_estimate=pl.CostEstimate(
            flops=micros * FLOPS_PER_MICRO, bytes_accessed=micros << 20, transcendentals=0
        ),
    )(*(value for value, _ in operands))


def grouped_device(
    tokens,
    cotangent,
    segment_ids,
    token_types,
    query_wordword,
    query_wordentity,
    query_entityword,
    query_entityentity,
    bias_wordword,
    bias_wordentity,
    bias_entityword,
    bias_entityentity,
    key_weight,
    value_weight,
    value_bias,
    output_weight,
    output_bias,
    first_gain,
    first_bias,
    inner_weight,
    inner_bias,
    outer_weight,
    outer_bias,
    second_gain,
    second_bias,
):
    bf16, f32 = jnp.bfloat16, jnp.float32
    index = lax.axis_index("ctx")
    chip, core = index // 2, index % 2
    wa = lax.axis_index("wa")
    parts = lax.axis_size("wa")
    place = jnp.stack([chip, core, wa]).astype(jnp.int32)
    inputs = tokens[0]
    tok, dmod = inputs.shape
    length = 2 * CHIPS * tok
    rows = key_weight.shape[0]
    half, quarter = rows // 2, rows // CHIPS
    group = dmod // CHIPS
    ff = inner_weight.shape[1]
    slot_w = ff // (2 * CHIPS)

    lines = (
        bias_wordword,
        bias_wordentity,
        bias_entityword,
        bias_entityentity,
        value_bias,
        output_bias,
        first_gain,
        first_bias,
        outer_bias,
        second_gain,
        second_bias,
        inner_bias,
    )
    six = (query_wordword, query_wordentity, query_entityword, query_entityentity, key_weight, value_weight)
    mine, slot = whole_call(
        prepare_kernel,
        [(place, smem)]
        + [(a, vmem) for a in (*six, *lines)]
        + [(a, hbm) for a in (inner_weight, outer_weight, output_weight)],
        [((half + TAG_ROWS, 6 * group), bf16, vmem), ((2 * rows + quarter, slot_w), bf16, vmem)],
        [pltpu.SemaphoreType.DMA((4,))],
        micros=3,
        mebibytes=58,
    )
    inputs, mine, slot = ordered(inputs, mine, slot)
    tags = (segment_ids[0] * 2 + token_types[0]).astype(bf16)
    tag_rows = jnp.pad(tags[None], ((0, TAG_ROWS - 1), (0, dmod - tok)))
    text = jnp.concatenate([inputs, tag_rows], axis=0)
    cut = tok // 2
    text_x, text_y = swapped(text, 2), swapped(text, 4)

    one, three = turned(mine, 1), turned(mine, 3)
    text_x, text_y, one, three, slot = ordered(text_x, text_y, one, three, slot)
    text_far = swapped(text_x[:cut], 4), swapped(text_y[cut:], 2)

    right, left = turned(slot, 1), turned(slot, 3)
    *text_far, right, left = ordered(*text_far, right, left)
    near_slot = jnp.stack([right, left])
    split, wide = half // 2, 6 * group // slot_w
    middle = TAG_ROWS * (slot.shape[0] // TAG_ROWS // 2)
    right = jnp.concatenate([*narrowed(one[:split], slot_w), right[:middle]], axis=0)
    left = jnp.concatenate([*narrowed(three[split:], slot_w), left[middle:]], axis=0)
    mine3 = jnp.stack([mine, one, three])
    right, left, mine3 = ordered(right, left, mine3)
    right, left = turned(right, 1), turned(left, 3)
    theirs3 = swapped(mine3, 1)
    near_x, near_y = swapped(near_slot, 2), swapped(near_slot, 4)
    right, left, theirs3 = ordered(right, left, theirs3)
    cut_right, cut_left = split * wide, (half + TAG_ROWS - split) * wide
    two = jnp.concatenate([widened(right[:cut_right], wide), widened(left[:cut_left], wide)], axis=0)
    theirs_two = swapped(two, 1)
    far_slot = jnp.concatenate([right[cut_right:], left[cut_left:]], axis=0)
    lines = jnp.stack([mine3[0, half:], mine3[1, half:], two[half:], mine3[2, half:]])

    weight, all_text, q, kv = whole_call(
        project_kernel,
        [(place, smem)] + [(a, vmem) for a in (text, text_x, text_y, *text_far, mine3, two, theirs3, theirs_two)],
        [
            ((dmod, 6 * group), bf16, vmem),
            ((CHIPS, tok + TAG_ROWS, dmod), bf16, vmem),
            ((CHIPS, tok, 2 * group), bf16, vmem),
            ((CHIPS, tok + TAG_ROWS, 2 * group), bf16, vmem),
        ],
        [pltpu.VMEM((parts, half + TAG_ROWS, 6 * group), bf16)] * 2,
        micros=8,
        mebibytes=20,
    )
    kv, near_x, near_y, far_slot = ordered(kv, near_x, near_y, far_slot)
    kv_other = swapped(kv, 1)
    first_slots = jnp.concatenate([*near_slot, *near_x, *near_y, far_slot], axis=0)
    to_x = jnp.concatenate([far_slot, near_y[1]], axis=0)
    to_y = jnp.concatenate([far_slot, near_x[0]], axis=0)
    kv_other, to_x, to_y, first_slots = ordered(kv_other, to_x, to_y, first_slots)
    to_x, to_y, to_far = swapped(to_x, 2), swapped(to_y, 4), swapped(far_slot, 6)
    first_other = swapped(first_slots, 1)

    *context, turned_out, lse, bounds = whole_call(
        attend_kernel,
        [(place, smem), (q, vmem), (kv, vmem), (kv_other, vmem)],
        [
            *[((tok, group), bf16, vmem)] * CHIPS,
            ((CHIPS, group, tok), f32, vmem),
            ((CHIPS, 3, 1, tok), f32, vmem),
            ((2, CHIPS), jnp.int32, smem),
        ],
        [
            pltpu.VMEM((3, length, 2 * HD), bf16),
            pltpu.VMEM((3, HD, length), bf16),
            pltpu.VMEM((length, TILE), f32),
            pltpu.VMEM((2 * CHIPS, 8, tok), f32),
            pltpu.VMEM((3, HD, tok), f32),
            pltpu.VMEM((CHIPS, tok, group), bf16),
        ],
        micros=25,
        mebibytes=20,
    )
    *context, to_x, to_y, to_far, first_other = ordered(*context, to_x, to_y, to_far, first_other)

    def exchanged(value):
        return [value[0]] + [swapped(value[m], 2 * m) for m in range(1, CHIPS)]

    contexts = exchanged(context)
    second_slots = jnp.concatenate([to_x, to_y, to_far], axis=0)
    second_other = swapped(second_slots, 1)

    slot_rows = 2 * rows + quarter + TAG_ROWS
    result, grad_sum, *grad_context, kept, sent_first, sent_second = whole_call(
        dense_kernel,
        [(place, smem)]
        + [(a, vmem) for a in (*contexts, text, cotangent[0], lines)]
        + [
            (a, hbm)
            for a in (inner_weight, outer_weight, output_weight, first_slots, first_other, second_slots, second_other)
        ],
        [
            ((tok, dmod), bf16, vmem),
            ((tok, dmod), f32, vmem),
            *[((tok, group), bf16, vmem)] * CHIPS,
            ((CHIPS, parts, slot_rows, slot_w), bf16, hbm),
            ((2 * parts, slot_rows, slot_w), bf16, hbm),
            ((2 * parts, slot_rows, slot_w), bf16, hbm),
        ],
        [
            pltpu.VMEM((dmod, ff), bf16),
            pltpu.VMEM((ff, dmod), bf16),
            pltpu.VMEM((dmod, dmod), bf16),
            pltpu.VMEM((tok, ff), bf16),
            pltpu.VMEM((tok, ff), f32),
            pltpu.VMEM((dmod, ff), bf16),
            pltpu.VMEM((ff, dmod), bf16),
            pltpu.VMEM((dmod, dmod), bf16),
            pltpu.VMEM((2, parts, TAG_ROWS, slot_w), bf16),
            pltpu.VMEM((parts, TAG_ROWS, slot_w), f32),
            pltpu.VMEM((1, ff), f32),
            pltpu.SemaphoreType.DMA((3,)),
            pltpu.SemaphoreType.DMA((3,)),
        ],
        micros=26,
        mebibytes=50,
    )
    grad_pieces = exchanged(grad_context)

    def added(*values):
        total = values[0].astype(f32)
        for v in values[1:]:
            total = total + v.astype(f32)
        return total

    middle = parts // 2
    upper, lower = slice(0, middle), slice(middle, None)
    first, second = swapped(sent_first, 1), swapped(sent_second, 1)
    far_x = added(kept[3, upper], first[:2]).astype(bf16)
    far_y = added(kept[3, lower], first[2:4]).astype(bf16)
    near_x = added(kept[1, upper], first[4:6]).astype(bf16)
    near_y = added(kept[2, lower], first[6:]).astype(bf16)
    *grad_pieces, far_x, far_y, near_x, near_y = ordered(*grad_pieces, far_x, far_y, near_x, near_y)
    far_x, far_y = swapped(far_x, 2), swapped(far_y, 4)
    near_x, near_y = swapped(near_x, 2), swapped(near_y, 4)

    dq, dkv, dkv_sent = whole_call(
        attend_back_kernel,
        [(place, smem), (bounds, smem)]
        + [(a, vmem) for a in (q, kv, kv_other, turned_out, lse, *grad_pieces)],
        [
            ((CHIPS, tok, 4 * group), bf16, vmem),
            ((CHIPS, tok, 2 * group), bf16, vmem),
            ((CHIPS, tok, 2 * group), bf16, vmem),
        ],
        [
            pltpu.VMEM((3, length, 4 * HD), bf16),
            pltpu.VMEM((3, 2 * HD, length), bf16),
            pltpu.VMEM((3, length, 4 * HD), f32),
            pltpu.VMEM((length, TILE), f32),
            pltpu.VMEM((2 * CHIPS, 8, tok), f32),
            pltpu.VMEM((3, 2 * HD, tok), f32),
            pltpu.VMEM((CHIPS, tok, group), bf16),
            pltpu.VMEM((3, 2 * tok, 4 * HD), bf16),
            pltpu.VMEM((3, KEY_BLOCK, 2 * tok), bf16),
        ],
        micros=34,
        mebibytes=36,
    )
    dq, dkv, dkv_sent, far_x, far_y, near_x, near_y, second = ordered(
        dq, dkv, dkv_sent, far_x, far_y, near_x, near_y, second
    )
    dkv_received = swapped(dkv_sent, 1)
    last_x = added(kept[1, lower], second[4:6], far_y).astype(bf16)
    last_y = added(kept[2, upper], second[6:], far_x).astype(bf16)
    last_x, last_y = ordered(last_x, last_y)
    last_x, last_y = swapped(last_x, 2), swapped(last_y, 4)
    dkv, partial = whole_call(
        token_grads_kernel,
        [(a, vmem) for a in (dq, dkv, dkv_received, weight)],
        [((CHIPS, tok, 2 * group), bf16, vmem), ((CHIPS, tok, dmod), bf16, vmem)],
        micros=8,
        mebibytes=16,
    )
    head_kept, head_sent = whole_call(
        head_grads_kernel,
        [(place, smem)] + [(a, vmem) for a in (all_text, dq, dkv)],
        [
            ((parts, half + TAG_ROWS, 6 * group), bf16, vmem),
            ((parts, half + TAG_ROWS, 6 * group), bf16, vmem),
        ],
        [pltpu.VMEM((dmod, 6 * group), f32)],
        micros=10,
        mebibytes=20,
    )
    head_kept, head_sent, last_x, last_y = ordered(head_kept, head_sent, last_x, last_y)

    def parts_sent(*values):
        shards = [
            added(*(lax.dynamic_index_in_dim(v, (wa + k) % parts, 0, keepdims=False) for v in values))
            for k in range(parts)
        ]
        return [v.astype(bf16) for v in shards]

    def parts_moved(values):
        return [turned(v, k) for k, v in enumerate(values) if k]

    def chips_moved(value):
        return [swapped(value, 2 * m) for m in range(1, CHIPS)]

    low, high = slice(0, cut), slice(cut, None)
    summed = jnp.concatenate(
        [
            added(kept[0, upper], second[:2], near_x, last_y),
            added(kept[0, lower], second[2:4], last_x, near_y),
        ],
        axis=0,
    ).astype(bf16)
    dense_parts = parts_sent(summed)
    text_x = jnp.stack([partial[3, low], partial[1, low]])
    text_y = jnp.stack([partial[3, high], partial[2, high]])
    *dense_parts, text_x, text_y = ordered(*dense_parts, text_x, text_y)
    dense_moved = parts_moved(dense_parts)
    head_received = swapped(head_sent, 1)
    text_x, text_y = swapped(text_x, 2), swapped(text_y, 4)
    *dense_moved, text_x, text_y, head_received = ordered(*dense_moved, text_x, text_y, head_received)

    count = dmod // slot_w
    dense_summed = added(dense_parts[0], *dense_moved).astype(bf16)
    (far_x, near_x), (far_y, near_y) = text_x, text_y
    last_x = added(partial[1, high], far_y).astype(bf16)
    last_y = added(partial[2, low], far_x).astype(bf16)
    to_x = jnp.concatenate([dense_summed, *narrowed(last_x, slot_w)], axis=0)
    to_y = jnp.concatenate([dense_summed, *narrowed(last_y, slot_w)], axis=0)
    head_parts = parts_sent(head_kept, head_received)
    *head_parts, to_x, to_y, dense_summed = ordered(*head_parts, to_x, to_y, dense_summed)
    head_moved = parts_moved(head_parts)
    to_x, to_y, dense_far = swapped(to_x, 2), swapped(to_y, 4), swapped(dense_summed, 6)
    *head_moved, to_x, to_y, dense_far = ordered(*head_moved, to_x, to_y, dense_far)

    deep = dense_summed.shape[0]
    dense_all = jnp.stack([dense_summed, to_x[:deep], to_y[:deep], dense_far])
    head_summed = added(head_parts[0], *head_moved).astype(bf16)
    head_summed, dense_all = ordered(head_summed, dense_all)
    head_moved = chips_moved(head_summed)
    dense_other = swapped(dense_all, 1)
    out_inner, out_outer, out_output, small = whole_call(
        unpack_dense_kernel,
        [(place, smem), (dense_all, vmem), (dense_other, vmem)],
        [
            ((rows, ff), f32, vmem),
            (outer_weight.shape, f32, vmem),
            ((rows, dmod), f32, vmem),
            ((TAG_ROWS, slot_w), f32, vmem),
        ],
        micros=4,
    )
    last_x, last_y = widened(to_x[deep:], count), widened(to_y[deep:], count)
    input_grads = grad_sum + jnp.concatenate(
        [added(partial[0, low], near_x, last_y), added(partial[0, high], last_x, near_y)], axis=0
    )
    *head_moved, out_inner, out_outer, out_output, small, input_grads = ordered(
        *head_moved, out_inner, out_outer, out_output, small, input_grads
    )
    head_all = jnp.stack([head_summed, *head_moved])
    out_heads = whole_call(
        unpack_heads_kernel,
        [(place, smem), (head_all, vmem), (swapped(head_all, 1), vmem)],
        [((rows, dmod), f32, vmem)] * 6 + [((rows,), f32, vmem)] * 5,
        micros=4,
    )

    own_small = lax.dynamic_slice(small[:12].reshape(6, dmod), (0, wa * rows), (6, rows))
    return (
        result[None],
        input_grads[None],
        *out_heads[:4],
        *out_heads[6:10],
        *out_heads[4:6],
        out_heads[10],
        out_output,
        own_small[0],
        own_small[1],
        own_small[2],
        out_inner,
        small[12:14].reshape(ff // parts),
        out_outer,
        own_small[3],
        own_small[4],
        own_small[5],
    )


def solution(mesh):
    in_specs = (
        P("wa", "ctx", None),
        P("wa", "ctx", None),
        P("wa", "ctx"),
        P("wa", "ctx"),
        P("wa", None),
        P("wa", None),
        P("wa", None),
        P("wa", None),
        P("wa"),
        P("wa"),
        P("wa"),
        P("wa"),
        P("wa", None),
        P("wa", None),
        P("wa"),
        P("wa", None),
        P("wa"),
        P("wa"),
        P("wa"),
        P("wa", None),
        P("wa"),
        P("wa", None),
        P("wa"),
        P("wa"),
        P("wa"),
    )
    out_specs = (
        P("wa", "ctx", None),
        P("wa", "ctx", None),
        P("wa", None),
        P("wa", None),
        P("wa", None),
        P("wa", None),
        P("wa"),
        P("wa"),
        P("wa"),
        P("wa"),
        P("wa", None),
        P("wa", None),
        P("wa"),
        P("wa", None),
        P("wa"),
        P("wa"),
        P("wa"),
        P("wa", None),
        P("wa"),
        P("wa", None),
        P("wa"),
        P("wa"),
        P("wa"),
    )
    body = grouped_device if mesh.shape["ctx"] == 2 * CHIPS else windowed_device
    return jax.shard_map(
        body, mesh=mesh, in_specs=in_specs, out_specs=out_specs, check_vma=False
    )
```

```python
import jax
import jax.numpy as jnp
from jax import lax
from jax.experimental import pallas as pl
from jax.experimental.pallas import tpu as pltpu
from jax.sharding import PartitionSpec as P

HD = 64


EPSILON = 1e-12
MASKED = -1e30


def as_sent(shard):
    return jax.tree.map(lambda a: a.astype(jnp.bfloat16) if a.dtype == jnp.float32 else a, shard)


def passed_along(value, axis, steps):
    count = lax.axis_size(axis)
    leading, last = (max(0, -steps), min(count, count - steps))
    return lax.ppermute(value, axis, [(source, source + steps) for source in range(leading, last)])


def layer_norm(values, gain, shift):
    center = values - jnp.mean(values, axis=-1, keepdims=True)
    spread = jnp.mean(center * center, axis=-1, keepdims=True)
    return center * lax.rsqrt(spread + EPSILON) * gain + shift


def gelu_exact(values):
    return jax.nn.gelu(values, approximate=False)


def matmul(left, right):
    return jnp.dot(left, right, preferred_element_type=jnp.float32)


def left_product(left, right):
    return lax.dot_general(
        left, right, (((0,), (0,)), ((), ())), preferred_element_type=jnp.float32
    )


def right_product(left, right):
    return lax.dot_general(
        left, right, (((1,), (1,)), ((), ())), preferred_element_type=jnp.float32
    )


def column_sums(values):
    return jnp.sum(values.astype(jnp.float32), axis=0)


def columns(values, start):
    return lax.dynamic_slice_in_dim(values, start, HD, 1)


def head_scores(query_word, query_entity, keys_head, key_entity, allowed, scale):
    word_scores = right_product(query_word, keys_head)
    entity_scores = right_product(query_entity, keys_head)
    raw = jnp.where(key_entity[None, :], entity_scores, word_scores) * scale
    return jnp.where(allowed, raw, MASKED)


def merge_heads(stacked):
    return jnp.transpose(stacked, (1, 0, 2)).reshape(
        stacked.shape[1], stacked.shape[0] * stacked.shape[2]
    )


def windowed_device(
    tokens,
    cotangent,
    segment_ids,
    token_types,
    query_wordword,
    query_wordentity,
    query_entityword,
    query_entityentity,
    bias_wordword,
    bias_wordentity,
    bias_entityword,
    bias_entityentity,
    key_weight,
    value_weight,
    value_bias,
    output_weight,
    output_bias,
    first_gain,
    first_bias,
    inner_weight,
    inner_bias,
    outer_weight,
    outer_bias,
    second_gain,
    second_bias,
):
    attention = (
        lax.all_gather(query_wordword, "wa", axis=0, tiled=True),
        lax.all_gather(query_wordentity, "wa", axis=0, tiled=True),
        lax.all_gather(query_entityword, "wa", axis=0, tiled=True),
        lax.all_gather(query_entityentity, "wa", axis=0, tiled=True),
        lax.all_gather(bias_wordword, "wa", axis=0, tiled=True),
        lax.all_gather(bias_wordentity, "wa", axis=0, tiled=True),
        lax.all_gather(bias_entityword, "wa", axis=0, tiled=True),
        lax.all_gather(bias_entityentity, "wa", axis=0, tiled=True),
        lax.all_gather(key_weight, "wa", axis=0, tiled=True),
        lax.all_gather(value_weight, "wa", axis=0, tiled=True),
        lax.all_gather(value_bias, "wa", axis=0, tiled=True),
        lax.all_gather(output_weight, "wa", axis=0, tiled=True),
        lax.all_gather(output_bias, "wa", axis=0, tiled=True),
        lax.all_gather(first_gain, "wa", axis=0, tiled=True),
        lax.all_gather(first_bias, "wa", axis=0, tiled=True),
    )
    (
        full_ww,
        full_we,
        full_ew,
        full_ee,
        shift_ww,
        shift_we,
        shift_ew,
        shift_ee,
        full_key,
        full_value,
        shift_value,
        full_output,
        shift_output,
        gain_one,
        shift_one,
    ) = attention
    feedforward = (
        lax.all_gather(inner_weight, "wa", axis=0, tiled=True),
        lax.all_gather(inner_bias, "wa", axis=0, tiled=True),
        lax.all_gather(outer_weight, "wa", axis=0, tiled=True),
        lax.all_gather(outer_bias, "wa", axis=0, tiled=True),
        lax.all_gather(second_gain, "wa", axis=0, tiled=True),
        lax.all_gather(second_bias, "wa", axis=0, tiled=True),
    )
    full_inner, shift_inner, full_outer, shift_outer, gain_two, shift_two = feedforward
    inputs = tokens[0]
    seg = segment_ids[0]
    types = token_types[0]
    tok = inputs.shape[0]
    dmod = inputs.shape[1]
    heads = dmod // HD
    scale = HD ** (-0.5)
    length = tok * lax.axis_size("ctx")
    doc_max = min(2048, 4 * tok, length // 2)
    reach = (doc_max - 2) // tok + 1
    entity = (types == 1)[:, None]
    proj_ww = matmul(inputs, full_ww) + shift_ww
    proj_we = matmul(inputs, full_we) + shift_we
    proj_ew = matmul(inputs, full_ew) + shift_ew
    proj_ee = matmul(inputs, full_ee) + shift_ee
    query_word = jnp.where(entity, proj_ew, proj_ww).astype(jnp.bfloat16)
    query_entity = jnp.where(entity, proj_ee, proj_we).astype(jnp.bfloat16)
    keys = matmul(inputs, full_key).astype(jnp.bfloat16)
    values = (matmul(inputs, full_value) + shift_value).astype(jnp.bfloat16)
    own_kv = jnp.concatenate([keys, values], axis=1)
    own_seg = seg + 1
    tags = own_seg * 2 + types

    def pass_left(packet, unused):
        moved = jax.tree.map(
            lambda part, own: part.astype(own.dtype),
            passed_along(as_sent(packet), "ctx", 1),
            packet,
        )
        return (moved, moved)

    def pass_right(packet, unused):
        moved = jax.tree.map(
            lambda part, own: part.astype(own.dtype),
            passed_along(as_sent(packet), "ctx", -1),
            packet,
        )
        return (moved, moved)

    _, (left_kv, left_tags) = lax.scan(pass_left, (own_kv, tags), None, length=reach)
    _, (right_kv, right_tags) = lax.scan(pass_right, (own_kv, tags), None, length=reach)
    window = jnp.concatenate(
        [jnp.flip(left_kv, 0).reshape(-1, 2 * dmod), own_kv, right_kv.reshape(-1, 2 * dmod)], axis=0
    )
    window_tags = jnp.concatenate(
        [jnp.flip(left_tags, 0).reshape(-1), tags, right_tags.reshape(-1)], axis=0
    )
    key_entity = window_tags % 2 == 1
    allowed = own_seg[:, None] == (window_tags // 2)[None, :]

    def head_forward(index):
        start = index * HD
        scores = head_scores(
            columns(query_word, start),
            columns(query_entity, start),
            columns(window, start),
            key_entity,
            allowed,
            scale,
        )
        top = jnp.max(scores, axis=1, keepdims=True)
        expo = jnp.exp(scores - top)
        total = jnp.sum(expo, axis=1, keepdims=True)
        probs = (expo / total).astype(jnp.bfloat16)
        return (matmul(probs, columns(window, dmod + start)), (top + jnp.log(total))[:, 0])

    head_context, lse = lax.map(head_forward, jnp.arange(heads))
    context = merge_heads(head_context).astype(jnp.bfloat16)
    branch = matmul(context, full_output) + shift_output
    first, pull_one = jax.vjp(
        layer_norm,
        inputs.astype(jnp.float32) + branch,
        gain_one.astype(jnp.float32),
        shift_one.astype(jnp.float32),
    )
    first_low = first.astype(jnp.bfloat16)
    inner = matmul(first_low, full_inner) + shift_inner
    activated, pull_gelu = jax.vjp(gelu_exact, inner)
    hidden = activated.astype(jnp.bfloat16)
    ffn = matmul(hidden, full_outer) + shift_outer
    result, pull_two = jax.vjp(
        layer_norm, first + ffn, gain_two.astype(jnp.float32), shift_two.astype(jnp.float32)
    )
    grad_sum_two, grad_gain_two, grad_shift_two = pull_two(cotangent[0].astype(jnp.float32))
    grad_ffn = grad_sum_two.astype(jnp.bfloat16)
    grad_outer = left_product(hidden, grad_ffn)
    grad_outer_shift = column_sums(grad_ffn)
    grad_inner = pull_gelu(right_product(grad_ffn, full_outer))[0].astype(jnp.bfloat16)
    grad_inner_full = left_product(first_low, grad_inner)
    grad_inner_shift = column_sums(grad_inner)
    grad_first = grad_sum_two + right_product(grad_inner, full_inner)
    grad_sum_one, grad_gain_one, grad_shift_one = pull_one(grad_first)
    grad_branch = grad_sum_one.astype(jnp.bfloat16)
    grad_output = left_product(context, grad_branch)
    grad_output_shift = column_sums(grad_branch)
    grad_context = right_product(grad_branch, full_output).astype(jnp.bfloat16)

    def head_backward(index):
        start = index * HD
        word_head = columns(query_word, start)
        entity_head = columns(query_entity, start)
        keys_head = columns(window, start)
        values_head = columns(window, dmod + start)
        context_head = columns(grad_context, start)
        scores = head_scores(word_head, entity_head, keys_head, key_entity, allowed, scale)
        probs = jnp.exp(scores - lse[index][:, None])
        grad_probs = right_product(context_head, values_head)
        delta = jnp.sum(probs * grad_probs, axis=1)
        grad_scores = (probs * (grad_probs - delta[:, None])).astype(jnp.bfloat16)
        zero = jnp.zeros_like(grad_scores)
        grad_word = jnp.where(key_entity[None, :], zero, grad_scores)
        grad_entity = jnp.where(key_entity[None, :], grad_scores, zero)
        grad_qword = matmul(grad_word, keys_head) * scale
        grad_qentity = matmul(grad_entity, keys_head) * scale
        grad_keys = (
            left_product(grad_word, word_head) + left_product(grad_entity, entity_head)
        ) * scale
        grad_values = left_product(probs.astype(jnp.bfloat16), context_head)
        return (grad_qword, grad_qentity, delta, grad_keys, grad_values)

    grad_qword, grad_qentity, delta, window_keys, window_values = lax.map(
        lambda index: head_backward(index), jnp.arange(heads)
    )
    parts_keys = merge_heads(window_keys).reshape(2 * reach + 1, tok, dmod)
    parts_values = merge_heads(window_values).reshape(2 * reach + 1, tok, dmod)

    def back_left(total, piece):
        return (
            (
                passed_along((total[0] + piece[0]).astype(jnp.bfloat16), "ctx", -1).astype(
                    jnp.float32
                ),
                passed_along((total[1] + piece[1]).astype(jnp.bfloat16), "ctx", -1).astype(
                    jnp.float32
                ),
            ),
            None,
        )

    def back_right(total, piece):
        return (
            (
                passed_along((total[0] + piece[0]).astype(jnp.bfloat16), "ctx", 1).astype(
                    jnp.float32
                ),
                passed_along((total[1] + piece[1]).astype(jnp.bfloat16), "ctx", 1).astype(
                    jnp.float32
                ),
            ),
            None,
        )

    empty = jnp.zeros((tok, dmod), jnp.float32)
    from_above, _ = lax.scan(back_left, (empty, empty), (parts_keys[:reach], parts_values[:reach]))
    from_below, _ = lax.scan(
        back_right,
        (empty, empty),
        (jnp.flip(parts_keys[reach + 1 :], 0), jnp.flip(parts_values[reach + 1 :], 0)),
    )
    own_keys = parts_keys[reach] + from_above[0] + from_below[0]
    own_values = parts_values[reach] + from_above[1] + from_below[1]
    grad_keys = own_keys.astype(jnp.bfloat16)
    grad_values = own_values.astype(jnp.bfloat16)
    grad_qword = merge_heads(grad_qword).astype(jnp.bfloat16)
    grad_qentity = merge_heads(grad_qentity).astype(jnp.bfloat16)
    zeros = jnp.zeros_like(grad_qword)
    grad_pww = jnp.where(entity, zeros, grad_qword)
    grad_pew = jnp.where(entity, grad_qword, zeros)
    grad_pwe = jnp.where(entity, zeros, grad_qentity)
    grad_pee = jnp.where(entity, grad_qentity, zeros)
    input_grads = grad_sum_one + right_product(grad_pww, full_ww) + right_product(grad_pwe, full_we)
    input_grads = input_grads + right_product(grad_pew, full_ew) + right_product(grad_pee, full_ee)
    input_grads = (
        input_grads + right_product(grad_keys, full_key) + right_product(grad_values, full_value)
    )
    local_grads = (
        left_product(inputs, grad_pww),
        left_product(inputs, grad_pwe),
        left_product(inputs, grad_pew),
        left_product(inputs, grad_pee),
        column_sums(grad_pww),
        column_sums(grad_pwe),
        column_sums(grad_pew),
        column_sums(grad_pee),
        left_product(inputs, grad_keys),
        left_product(inputs, grad_values),
        column_sums(grad_values),
        grad_output,
        grad_output_shift,
        grad_gain_one,
        grad_shift_one,
        grad_inner_full,
        grad_inner_shift,
        grad_outer,
        grad_outer_shift,
        grad_gain_two,
        grad_shift_two,
    )
    shards = (
        lax.psum_scatter(
            local_grads[0].astype(jnp.bfloat16), "wa", scatter_dimension=0, tiled=True
        ).astype(jnp.float32),
        lax.psum_scatter(
            local_grads[1].astype(jnp.bfloat16), "wa", scatter_dimension=0, tiled=True
        ).astype(jnp.float32),
        lax.psum_scatter(
            local_grads[2].astype(jnp.bfloat16), "wa", scatter_dimension=0, tiled=True
        ).astype(jnp.float32),
        lax.psum_scatter(
            local_grads[3].astype(jnp.bfloat16), "wa", scatter_dimension=0, tiled=True
        ).astype(jnp.float32),
        lax.psum_scatter(
            local_grads[4].astype(jnp.bfloat16), "wa", scatter_dimension=0, tiled=True
        ).astype(jnp.float32),
        lax.psum_scatter(
            local_grads[5].astype(jnp.bfloat16), "wa", scatter_dimension=0, tiled=True
        ).astype(jnp.float32),
        lax.psum_scatter(
            local_grads[6].astype(jnp.bfloat16), "wa", scatter_dimension=0, tiled=True
        ).astype(jnp.float32),
        lax.psum_scatter(
            local_grads[7].astype(jnp.bfloat16), "wa", scatter_dimension=0, tiled=True
        ).astype(jnp.float32),
        lax.psum_scatter(
            local_grads[8].astype(jnp.bfloat16), "wa", scatter_dimension=0, tiled=True
        ).astype(jnp.float32),
        lax.psum_scatter(
            local_grads[9].astype(jnp.bfloat16), "wa", scatter_dimension=0, tiled=True
        ).astype(jnp.float32),
        lax.psum_scatter(
            local_grads[10].astype(jnp.bfloat16), "wa", scatter_dimension=0, tiled=True
        ).astype(jnp.float32),
        lax.psum_scatter(
            local_grads[11].astype(jnp.bfloat16), "wa", scatter_dimension=0, tiled=True
        ).astype(jnp.float32),
        lax.psum_scatter(
            local_grads[12].astype(jnp.bfloat16), "wa", scatter_dimension=0, tiled=True
        ).astype(jnp.float32),
        lax.psum_scatter(
            local_grads[13].astype(jnp.bfloat16), "wa", scatter_dimension=0, tiled=True
        ).astype(jnp.float32),
        lax.psum_scatter(
            local_grads[14].astype(jnp.bfloat16), "wa", scatter_dimension=0, tiled=True
        ).astype(jnp.float32),
        lax.psum_scatter(
            local_grads[15].astype(jnp.bfloat16), "wa", scatter_dimension=0, tiled=True
        ).astype(jnp.float32),
        lax.psum_scatter(
            local_grads[16].astype(jnp.bfloat16), "wa", scatter_dimension=0, tiled=True
        ).astype(jnp.float32),
        lax.psum_scatter(
            local_grads[17].astype(jnp.bfloat16), "wa", scatter_dimension=0, tiled=True
        ).astype(jnp.float32),
        lax.psum_scatter(
            local_grads[18].astype(jnp.bfloat16), "wa", scatter_dimension=0, tiled=True
        ).astype(jnp.float32),
        lax.psum_scatter(
            local_grads[19].astype(jnp.bfloat16), "wa", scatter_dimension=0, tiled=True
        ).astype(jnp.float32),
        lax.psum_scatter(
            local_grads[20].astype(jnp.bfloat16), "wa", scatter_dimension=0, tiled=True
        ).astype(jnp.float32),
    )
    totals = lax.psum(
        (
            shards[0],
            shards[1],
            shards[2],
            shards[3],
            shards[4],
            shards[5],
            shards[6],
            shards[7],
            shards[8],
            shards[9],
            shards[10],
            shards[11],
            shards[12],
            shards[13],
            shards[14],
            shards[15],
            shards[16],
            shards[17],
            shards[18],
            shards[19],
            shards[20],
        ),
        "ctx",
    )
    return (
        result.astype(jnp.bfloat16)[None],
        input_grads[None],
        totals[0],
        totals[1],
        totals[2],
        totals[3],
        totals[4],
        totals[5],
        totals[6],
        totals[7],
        totals[8],
        totals[9],
        totals[10],
        totals[11],
        totals[12],
        totals[13],
        totals[14],
        totals[15],
        totals[16],
        totals[17],
        totals[18],
        totals[19],
        totals[20],
    )


CHIPS = 4
KEY_BLOCK = 256
NEGATIVE = -1e30
TAG_ROWS = 16
TILE = 128
FLOPS_PER_MICRO = 1_100_000_000


def lanes_product(left, right):
    return lax.dot_general(
        left, right, (((1,), (1,)), ((), ())), preferred_element_type=jnp.float32
    )


def rows_product(left, right):
    return lax.dot_general(
        left, right, (((0,), (0,)), ((), ())), preferred_element_type=jnp.float32
    )


def plain_product(left, right):
    return jnp.dot(left, right, preferred_element_type=jnp.float32)


def swapped(value, step):
    count = lax.axis_size("ctx")
    return lax.ppermute(value, "ctx", [(i, i ^ step) for i in range(count)])


def turned(value, step):
    count = lax.axis_size("wa")
    return lax.ppermute(value, "wa", [(i, (i + step) % count) for i in range(count)])


def narrowed(value, width):
    return [value[:, at : at + width] for at in range(0, value.shape[1], width)]


def widened(value, count):
    rows = value.shape[0] // count
    return jnp.concatenate([value[rows * k : rows * (k + 1)] for k in range(count)], axis=1)


def ordered(*values):
    return lax.optimization_barrier(values)


def as_column(row):
    return jnp.broadcast_to(row, (TILE, row.shape[1])).T


def segment_of(tag):
    return jnp.floor(tag * 0.5)


def prepare_kernel(
    place, ww, we, ew, ee, key, value, *others
):
    *lines, inner, outer, output, mine, slot, sem = others
    rows = key.shape[0]
    half, quarter = rows // 2, rows // CHIPS
    slot_w = slot.shape[1]
    chip, core = place[0], place[1]
    index = 2 * chip + core
    copies = [
        (inner.at[:, pl.ds(pl.multiple_of(slot_w * index, TILE), slot_w)], slot.at[pl.ds(0, rows), :])
    ]
    for v in range(2):
        copies.append(
            (
                outer.at[pl.ds(pl.multiple_of(half * index, 16), half), pl.ds(slot_w * v, slot_w)],
                slot.at[pl.ds(rows + half * v, half), :],
            )
        )
    copies.append(
        (
            output.at[
                pl.ds(pl.multiple_of(quarter * chip, 16), quarter),
                pl.ds(pl.multiple_of(slot_w * core, TILE), slot_w),
            ],
            slot.at[pl.ds(2 * rows, quarter), :],
        )
    )
    copies = [pltpu.make_async_copy(a, b, sem.at[k]) for k, (a, b) in enumerate(copies)]
    for copy in copies:
        copy.start()
    at = pl.ds(pl.multiple_of(half * core, 16), half)
    for g in range(CHIPS):

        @pl.when(chip == g)
        def _():
            def heads(sources):
                return jnp.concatenate(
                    [
                        w[at, HD * (3 * g + h) : HD * (3 * g + h + 1)].astype(jnp.float32)
                        for h in range(3)
                        for w in sources
                    ],
                    axis=1,
                ).astype(jnp.bfloat16)

            mine[:half, : 4 * 3 * HD] = heads((ww, we, ew, ee))
            mine[:half, 4 * 3 * HD :] = heads((key, value))

    lines = [line[...].astype(jnp.float32).reshape(1, line.shape[0]) for line in lines]
    bias = [lines[k][:, HD * h : HD * (h + 1)] for h in range(3) for k in range(4)]
    for h in range(3):
        bias += [jnp.zeros((1, HD), jnp.float32), lines[4][:, HD * h : HD * (h + 1)]]
    six = jnp.concatenate(lines[5:11], axis=1)
    last = jnp.concatenate([lines[11], jnp.zeros((1, 2 * rows), jnp.float32)], axis=1)
    which = lax.broadcasted_iota(jnp.int32, (TAG_ROWS, 6 * rows), 0)
    below = jnp.where(which == 0, jnp.concatenate(bias, axis=1), jnp.where(which == 1, six, last))
    mine[half:] = jnp.where(which < 3, below, 0.0).astype(jnp.bfloat16)
    for copy in copies:
        copy.wait()


def project_kernel(
    place, t0, t1, t2, t3a, t3b, mine3, mine_two, theirs3, theirs_two, weight, tokens, q_ref, kv_ref, mine, theirs
):
    parts, rows = mine.shape[0], mine.shape[1] - TAG_ROWS
    for target, three, two in ((mine, mine3, mine_two), (theirs, theirs3, theirs_two)):
        target[0] = three[0]
        target[1] = three[1]
        target[2] = two[...]
        target[3] = three[2]
    tok = q_ref.shape[1]
    chip, core, wa = place[0], place[1], place[2]
    cut = t3a.shape[0]
    tokens[0] = t0[...]
    tokens[1] = t1[...]
    tokens[2] = t2[...]
    tokens[3, :cut] = t3a[...]
    tokens[3, cut:] = t3b[...]
    for z in range(parts):
        k = lax.rem(wa - z + parts, parts)
        for source, side in ((mine, core), (theirs, 1 - core)):
            weight[pl.ds(pl.multiple_of(2 * rows * z + rows * side, 32), rows), :] = source[k, :rows]
    k = lax.rem(wa - chip + parts, parts)
    bias = mine[k, rows : rows + TAG_ROWS].astype(jnp.float32)[:1]
    wide = 2 * HD

    def piece(m, unused):
        to = jnp.bitwise_xor(chip, m)
        tags = tokens[m, tok : tok + TAG_ROWS].astype(jnp.float32)[:1, :tok]
        flag = as_column(tags - 2.0 * segment_of(tags)) == 1.0
        text = tokens[m, :tok]
        for h in range(3):
            at = 2 * wide * h
            both = plain_product(text, weight[:, at : at + 2 * wide]) + bias[:, at : at + 2 * wide]
            q = jnp.where(flag, both[:, wide:], both[:, :wide]).astype(jnp.bfloat16)
            q_ref[to, :, wide * h : wide * (h + 1)] = q * jnp.bfloat16(HD**-0.5)
        kv = plain_product(text, weight[:, 6 * wide :]) + bias[:, 6 * wide :]
        kv_ref[to, :tok] = kv.astype(jnp.bfloat16)
        kv_ref[to, tok:] = jnp.broadcast_to(tags, (TAG_ROWS, tok)).astype(jnp.bfloat16)
        return 0

    lax.fori_loop(0, CHIPS, piece, 0)


def ones_where(shape, test):
    row = lax.broadcasted_iota(jnp.int32, shape, 0)
    column = lax.broadcasted_iota(jnp.int32, shape, 1)
    return jnp.where(test(row, column), 1.0, 0.0).astype(jnp.bfloat16)


def unit(size):
    return ones_where((size, size), lambda row, column: row == column)


def attend_kernel(
    place, q_ref, own, other, out0, out1, out2, out3, turned_out, lse, bounds, keys, values, seg_col, seg_row, acc, out
):
    tok = q_ref.shape[1]
    core = place[1]
    twice = ones_where((2 * HD, 2 * HD), lambda row, column: row == lax.rem(column, HD))
    upper = ones_where((HD, 2 * HD), lambda row, column: column == row + HD)

    def prepare(j, unused):
        for source, side in ((own, core), (other, 1 - core)):
            shard = 2 * j + side
            at = pl.ds(pl.multiple_of(shard * tok, TILE), tok)
            tags = source[j, tok : tok + TAG_ROWS].astype(jnp.float32)[:1]
            seg_row[shard] = jnp.broadcast_to(segment_of(tags), (8, tok))
            column = as_column(tags)
            segment = segment_of(column)
            seg_col[at, :] = segment
            flag = column - 2.0 * segment == 1.0
            for h in range(3):
                kv = source[j, :tok, 2 * HD * h : 2 * HD * (h + 1)]
                low = lax.broadcasted_iota(jnp.int32, kv.shape, 1) < HD
                keys[h, at, :] = jnp.where(low == flag, 0.0, plain_product(kv, twice)).astype(jnp.bfloat16)
                values[h, :, at] = lanes_product(upper, kv).astype(jnp.bfloat16)
        return 0

    lax.fori_loop(0, CHIPS, prepare, 0)

    def queries(j, unused):
        seg = seg_row[2 * j + core][:1]
        everyone = seg_row[...][:, 0, :]
        before = jnp.sum((everyone < jnp.min(seg)).astype(jnp.float32)).astype(jnp.int32)
        through = jnp.sum((everyone <= jnp.max(seg)).astype(jnp.float32)).astype(jnp.int32)
        first = before // KEY_BLOCK
        last = (through + KEY_BLOCK - 1) // KEY_BLOCK
        bounds[0, j] = first
        bounds[1, j] = last
        acc[...] = jnp.zeros_like(acc)

        def step(t, carry):
            at = pl.ds(pl.multiple_of(t * KEY_BLOCK, KEY_BLOCK), KEY_BLOCK)
            column = seg_col[at, :]
            same = jnp.concatenate([column] * (tok // TILE), axis=1) == seg
            after = []
            queries = [q_ref[j, :, 2 * HD * h : 2 * HD * (h + 1)] for h in range(3)]
            scores = [
                jnp.where(same, lanes_product(keys[h, at, :], queries[h]), NEGATIVE) for h in range(3)
            ]
            peaks = [
                jnp.maximum(carry[2 * h], jnp.max(scores[h], axis=0, keepdims=True)) for h in range(3)
            ]
            expo = [jnp.exp(scores[h] - peaks[h]) for h in range(3)]
            for h in range(3):
                fade = jnp.exp(carry[2 * h] - peaks[h])
                total = carry[2 * h + 1] * fade + jnp.sum(expo[h], axis=0, keepdims=True)
                acc[h] = acc[h] * fade + plain_product(values[h, :, at], expo[h].astype(jnp.bfloat16))
                after += [peaks[h], total]
            return tuple(after)

        start = (jnp.full((1, tok), NEGATIVE, jnp.float32), jnp.zeros((1, tok), jnp.float32)) * 3
        done = lax.fori_loop(first, last, step, start)
        for h in range(3):
            turned_out[j, HD * h : HD * (h + 1), :] = acc[h] / done[2 * h + 1]
            lse[j, h] = done[2 * h] + jnp.log(done[2 * h + 1])
        out[jnp.bitwise_xor(place[0], j)] = turned_out[j].T.astype(jnp.bfloat16)
        return 0

    lax.fori_loop(0, CHIPS, queries, 0)
    for m, target in enumerate((out0, out1, out2, out3)):
        target[...] = out[m]


def attend_back_kernel(
    place,
    bounds,
    q_ref,
    own,
    other,
    turned_out,
    lse,
    grad0,
    grad1,
    grad2,
    grad3,
    dq_ref,
    dkv_own,
    dkv_other,
    sources,
    turned_keys,
    grads,
    seg_col,
    seg_row,
    acc,
    grad,
    pair,
    mixed,
):
    tok = q_ref.shape[1]
    chip, core = place[0], place[1]
    wide = 2 * HD
    for m, piece in enumerate((grad0, grad1, grad2, grad3)):
        grad[jnp.bitwise_xor(chip, m)] = piece[...]
    twice = ones_where((wide, wide), lambda row, column: row == lax.rem(column, HD))
    turned_twice = ones_where((wide, wide), lambda row, column: column == lax.rem(row, HD))
    folded = ones_where((wide, wide), lambda row, column: column == lax.rem(row, HD))
    all_rows, group = unit(tok), unit(3 * HD)
    pair[...] = jnp.zeros_like(pair)

    def prepare(j, unused):
        for source, side in ((own, core), (other, 1 - core)):
            shard = 2 * j + side
            at = pl.ds(pl.multiple_of(shard * tok, TILE), tok)
            tags = source[j, tok : tok + TAG_ROWS].astype(jnp.float32)[:1]
            seg_row[shard] = jnp.broadcast_to(tags, (8, tok))
            column = as_column(tags)
            segment = segment_of(column)
            seg_col[at, :] = segment
            flag = column - 2.0 * segment == 1.0
            row_flag = tags - 2.0 * segment_of(tags) == 1.0
            for h in range(3):
                kv = source[j, :tok, wide * h : wide * (h + 1)]
                low = lax.broadcasted_iota(jnp.int32, kv.shape, 1) < HD
                sources[h, at, :wide] = jnp.where(low == flag, 0.0, plain_product(kv, twice)).astype(
                    jnp.bfloat16
                )
                sources[h, at, wide:] = kv
                both = lanes_product(turned_twice, kv)
                low = lax.broadcasted_iota(jnp.int32, both.shape, 0) < HD
                turned_keys[h, :, at] = jnp.where(low == row_flag, 0.0, both).astype(jnp.bfloat16)
                grads[h, at, :] = jnp.zeros((tok, 2 * wide), jnp.float32)
        return 0

    lax.fori_loop(0, CHIPS, prepare, 0)

    def queries(j, unused):
        tags = seg_row[2 * j + core][:1]
        seg = segment_of(tags)
        slot = jnp.bitwise_xor(chip, j)
        flag = as_column(tags - 2.0 * seg) == 1.0
        turned_grad = lanes_product(group, grad[j])
        deltas, shifts = [], []
        for h in range(3):
            rows = slice(HD * h, HD * (h + 1))
            deltas.append(jnp.sum(turned_grad[rows] * turned_out[j, rows, :], axis=0, keepdims=True))
            shifts.append(lse[j, h])
            pair[h, :tok, :wide] = q_ref[j, :, wide * h : wide * (h + 1)]
            pair[h, tok:, wide + HD :] = grad[j, :, rows]
        acc[...] = jnp.zeros_like(acc)

        def step(t, carry):
            at = pl.ds(pl.multiple_of(t * KEY_BLOCK, KEY_BLOCK), KEY_BLOCK)
            column = seg_col[at, :]
            same = jnp.concatenate([column] * (tok // TILE), axis=1) == seg
            both = [lanes_product(sources[h, at, :], pair[h]) for h in range(3)]
            for h in range(3):
                probs = jnp.where(same, jnp.exp(both[h][:, :tok] - shifts[h]), 0.0)
                mixed[h, :, :tok] = (probs * (both[h][:, tok:] - deltas[h])).astype(jnp.bfloat16)
                mixed[h, :, tok:] = probs.astype(jnp.bfloat16)
            for h in range(3):
                grads[h, at, :] += plain_product(mixed[h], pair[h])
                acc[h] += plain_product(turned_keys[h, :, at], mixed[h, :, :tok])
            return carry

        lax.fori_loop(bounds[0, j], bounds[1, j], step, 0)
        for h in range(3):
            dq = lanes_product(all_rows, (acc[h] * (HD**-0.5)).astype(jnp.bfloat16))
            at = 2 * wide * h
            dq_ref[slot, :, at : at + wide] = jnp.where(flag, 0.0, dq).astype(jnp.bfloat16)
            dq_ref[slot, :, at + wide : at + 2 * wide] = jnp.where(flag, dq, 0.0).astype(jnp.bfloat16)
        return 0

    lax.fori_loop(0, CHIPS, queries, 0)

    def finish(j, unused):
        slot = jnp.bitwise_xor(chip, j)
        for target, side in ((dkv_own, core), (dkv_other, 1 - core)):
            shard = 2 * j + side
            at = pl.ds(pl.multiple_of(shard * tok, TILE), tok)
            tags = seg_row[shard][:1]
            flag = as_column(tags - 2.0 * segment_of(tags)) == 1.0
            for h in range(3):
                low = lax.broadcasted_iota(jnp.int32, (tok, wide), 1) < HD
                dk = jnp.where(low == flag, 0.0, grads[h, at, :wide]).astype(jnp.bfloat16)
                target[slot, :, wide * h : wide * (h + 1)] = jnp.where(
                    low, plain_product(dk, folded), grads[h, at, wide:]
                ).astype(jnp.bfloat16)
        return 0

    lax.fori_loop(0, CHIPS, finish, 0)


def normed(total, gain, shift):
    center = total - jnp.mean(total, axis=-1, keepdims=True)
    spread = jnp.mean(center * center, axis=-1, keepdims=True)
    inverse = lax.rsqrt(spread + EPSILON)
    unit = center * inverse
    return unit * gain + shift, unit, inverse


def normed_back(grad, unit, inverse, gain):
    scaled = grad * gain
    mean = jnp.mean(scaled, axis=-1, keepdims=True)
    along = jnp.mean(scaled * unit, axis=-1, keepdims=True)
    return inverse * (scaled - mean - unit * along)


def summed_rows(value):
    return jnp.sum(value, axis=0, keepdims=True)


def dense_kernel(
    place,
    context0,
    context1,
    context2,
    context3,
    text,
    cotangent,
    lines,
    inner_shard,
    outer_shard,
    output_shard,
    first_own,
    first_other,
    second_own,
    second_other,
    result,
    grad_sum,
    grad0,
    grad1,
    grad2,
    grad3,
    kept,
    sent_first,
    sent_second,
    inner_w,
    outer_w,
    output_w,
    hidden,
    slope,
    inner_g,
    outer_g,
    output_g,
    small,
    sums,
    inner_bias,
    in_sems,
    out_sems,
):
    bf16, f32 = jnp.bfloat16, jnp.float32
    chip, core, wa = place[0], place[1], place[2]
    tok, dmod = result.shape
    ff = hidden.shape[1]
    group = dmod // CHIPS
    parts = CHIPS
    rows = dmod // parts
    half = rows // 2
    quarter = rows // CHIPS
    slot_w = ff // (2 * CHIPS)

    context = (context0, context1, context2, context3)

    def head_rows(m):
        return pl.ds(pl.multiple_of(group * jnp.bitwise_xor(chip, m), 64), group)

    pltpu.make_async_copy(
        output_shard, output_w.at[pl.ds(pl.multiple_of(rows * wa, 16), rows), :], in_sems.at[0]
    ).start()
    pltpu.make_async_copy(
        inner_shard, inner_w.at[pl.ds(pl.multiple_of(rows * wa, 16), rows), :], in_sems.at[1]
    ).start()
    deep = first_own.shape[0] // 7
    places = [(0, 0, 0, 1), (0, 1, 0, 3), (0, 2, 1, 1), (0, 3, 1, 3), (0, 4, 2, 1), (0, 5, 2, 3), (0, 6, 0, 2)]
    places += [(1, 0, 1, 2), (1, 1, 3, 3), (1, 2, 2, 2), (1, 3, 3, 1), (1, 4, 3, 2)]
    sides = []
    for which, at, m, k in places:
        g = jnp.bitwise_xor(chip, m)
        z = lax.rem(wa - k + parts, parts)
        sides.append(((first_own, second_own)[which], deep * at, g, core, z))
        sides.append(((first_other, second_other)[which], deep * at, g, 1 - core, z))
    for source, at, g, side, z in sides:
        pltpu.make_async_copy(
            source.at[pl.ds(at + 2 * rows, quarter), :],
            output_w.at[
                pl.ds(pl.multiple_of(rows * z + quarter * g, 16), quarter),
                pl.ds(pl.multiple_of(slot_w * side, TILE), slot_w),
            ],
            in_sems.at[0],
        ).start()
    for source, at, g, side, z in sides:
        pltpu.make_async_copy(
            source.at[pl.ds(at, rows), :],
            inner_w.at[
                pl.ds(pl.multiple_of(rows * z, 16), rows),
                pl.ds(pl.multiple_of(slot_w * (2 * g + side), TILE), slot_w),
            ],
            in_sems.at[1],
        ).start()
    pltpu.make_async_copy(
        outer_shard, outer_w.at[pl.ds(pl.multiple_of(dmod * wa, 16), dmod), :], in_sems.at[2]
    ).start()
    for source, at, g, side, z in sides:
        for v in range(2):
            pltpu.make_async_copy(
                source.at[pl.ds(at + rows + half * v, half), :],
                outer_w.at[
                    pl.ds(pl.multiple_of(dmod * z + half * (2 * g + side), 16), half),
                    pl.ds(slot_w * v, slot_w),
                ],
                in_sems.at[2],
            ).start()

    names = ("outb", "g1", "s1", "outerb", "g2", "s2")
    lined = [lines[lax.rem(wa - z + parts, parts)].astype(f32) for z in range(parts)]
    vec = {
        name: jnp.concatenate([line[1:2, rows * k : rows * (k + 1)] for line in lined], axis=1)
        for k, name in enumerate(names)
    }
    inner_bias[...] = jnp.concatenate([line[2:3, : ff // parts] for line in lined], axis=1)

    pltpu.make_async_copy(output_w, output_w, in_sems.at[0]).wait()
    branch = vec["outb"]
    for m in range(CHIPS):
        branch = branch + plain_product(context[m][...], output_w[head_rows(m), :])
    first, unit_one, inverse_one = normed(text[:tok, :].astype(f32) + branch, vec["g1"], vec["s1"])
    low = first.astype(bf16)

    pltpu.make_async_copy(inner_w, inner_w, in_sems.at[1]).wait()

    def forward(s, carry):
        at = pl.ds(pl.multiple_of(2 * slot_w * s, TILE), 2 * slot_w)
        inner = plain_product(low, inner_w[:, at]) + inner_bias[:, at]
        cdf = 0.5 + 0.5 * lax.erf(inner * (0.5**0.5))
        hidden[:, at] = (inner * cdf).astype(bf16)
        slope[:, at] = cdf + inner * (jnp.exp(-0.5 * inner * inner) * (0.5 / jnp.pi) ** 0.5)
        return carry

    lax.fori_loop(0, CHIPS, forward, 0)
    pltpu.make_async_copy(outer_w, outer_w, in_sems.at[2]).wait()
    ffn = plain_product(hidden[...], outer_w[...]) + vec["outerb"]
    second, unit_two, inverse_two = normed(first + ffn, vec["g2"], vec["s2"])
    result[...] = second.astype(bf16)
    grad_out = cotangent[...].astype(f32)
    grad_two = normed_back(grad_out, unit_two, inverse_two, vec["g2"])
    low_two = grad_two.astype(bf16)

    sums[...] = jnp.zeros_like(sums)

    def put(row, value):
        for v in range(2):
            for z in range(parts):
                sums[z, row + v : row + v + 1, :] = value[:, slot_w * v : slot_w * (v + 1)]

    put(6, summed_rows(low_two.astype(f32)))
    put(8, summed_rows(grad_out * unit_two))
    put(10, summed_rows(grad_out))
    low_turned = low.astype(f32).T.astype(bf16)

    def backward(s, carry):
        at = pl.ds(pl.multiple_of(2 * slot_w * s, TILE), 2 * slot_w)
        grad_hidden = lanes_product(low_two, outer_w[at, :])
        grad_inner = (grad_hidden * slope[:, at]).astype(bf16)
        outer_g[at, :] = rows_product(hidden[:, at], low_two).astype(bf16)
        hidden[:, at] = grad_inner
        inner_g[:, at] = plain_product(low_turned, grad_inner).astype(bf16)
        totals = summed_rows(grad_inner.astype(f32))
        sums[s, 12:13, :] = totals[:, :slot_w]
        sums[s, 13:14, :] = totals[:, slot_w:]
        return carry

    lax.fori_loop(0, CHIPS, backward, 0)

    def targets():
        spans = [(3, 0, 4, 0, 0), (1, 0, 2, 0, 4), (2, 2, 4, 0, 6), (0, 0, 4, 1, 0), (1, 2, 4, 1, 4), (2, 0, 2, 1, 6)]
        for m in range(CHIPS):
            yield kept.at[m], 0, parts, jnp.bitwise_xor(chip, m), core, 0
        for m, low_z, high_z, which, at in spans:
            target = (sent_first, sent_second)[which].at[pl.ds(at, high_z - low_z)]
            yield target, low_z, high_z - low_z, jnp.bitwise_xor(chip, m), 1 - core, 1 + which

    inner_view = inner_g.reshape(parts, rows, ff)
    outer_view = outer_g.reshape(parts, dmod, dmod)
    output_view = output_g.reshape(parts, rows, dmod)
    for target, z, count, g, side, sem in targets():
        s = 2 * g + side
        pltpu.make_async_copy(
            inner_view.at[pl.ds(z, count), :, pl.ds(pl.multiple_of(slot_w * s, TILE), slot_w)],
            target.at[:, pl.ds(0, rows), :],
            out_sems.at[sem],
        ).start()
        for v in range(2):
            pltpu.make_async_copy(
                outer_view.at[
                    pl.ds(z, count), pl.ds(pl.multiple_of(half * s, 16), half), pl.ds(slot_w * v, slot_w)
                ],
                target.at[:, pl.ds(rows + half * v, half), :],
                out_sems.at[sem],
            ).start()

    grad_first = grad_two + lanes_product(hidden[...], inner_w[...])
    put(2, summed_rows(grad_first * unit_one))
    put(4, summed_rows(grad_first))
    grad_one = normed_back(grad_first, unit_one, inverse_one, vec["g1"])
    grad_sum[...] = grad_one
    low_one = grad_one.astype(bf16)
    put(0, summed_rows(low_one.astype(f32)))
    small[0] = jnp.zeros_like(small[0])
    small[1] = sums[...].astype(bf16)
    for m in range(CHIPS):
        at = head_rows(m)
        output_g[at, :] = rows_product(context[m][...], low_one).astype(bf16)
        (grad0, grad1, grad2, grad3)[m][...] = lanes_product(low_one, output_w[at, :]).astype(bf16)
    for target, z, count, g, side, sem in targets():
        pltpu.make_async_copy(
            output_view.at[
                pl.ds(z, count),
                pl.ds(pl.multiple_of(quarter * g, 16), quarter),
                pl.ds(pl.multiple_of(slot_w * side, TILE), slot_w),
            ],
            target.at[:, pl.ds(2 * rows, quarter), :],
            out_sems.at[sem],
        ).start()
        filled = jnp.where(2 * g + side == 0, 1, 0)
        pltpu.make_async_copy(
            small.at[filled, pl.ds(z, count)],
            target.at[:, pl.ds(2 * rows + quarter, TAG_ROWS), :],
            out_sems.at[sem],
        ).start()
    for sem, target in enumerate((kept, sent_first, sent_second)):
        pltpu.make_async_copy(target, target, out_sems.at[sem]).wait()


def head_grads_kernel(place, tokens, dq, dkv, kept, sent, acc):
    tok = dq.shape[1]
    core = place[1]
    wide = dq.shape[2]
    parts, rows = kept.shape[0], kept.shape[1] - TAG_ROWS
    acc[...] = jnp.zeros_like(acc)

    def piece(m, carry):
        text = tokens[m, :tok]
        text_turned = text.astype(jnp.float32).T.astype(jnp.bfloat16)
        acc[:, :wide] += plain_product(text_turned, dq[m])
        acc[:, wide:] += plain_product(text_turned, dkv[m])
        return (
            carry[0] + summed_rows(dq[m].astype(jnp.float32)),
            carry[1] + summed_rows(dkv[m].astype(jnp.float32)),
        )

    start = (jnp.zeros((1, wide), jnp.float32), jnp.zeros((1, wide // 2), jnp.float32))
    sums = jnp.concatenate(lax.fori_loop(0, CHIPS, piece, start), axis=1)
    sums = jnp.broadcast_to(sums, (TAG_ROWS, sums.shape[1]))
    for z in range(parts):
        for target, side in ((kept, core), (sent, 1 - core)):
            at = pl.ds(pl.multiple_of(2 * rows * z + rows * side, 32), rows)
            target[z, :rows] = acc[at, :].astype(jnp.bfloat16)
            target[z, rows:] = jnp.where(side == 0, sums, 0.0).astype(jnp.bfloat16)


def token_grads_kernel(dq, dkv_own, dkv_other, weight, dkv, partial):
    wide = dq.shape[2]

    def piece(m, carry):
        both = dkv_own[m].astype(jnp.float32) + dkv_other[m].astype(jnp.float32)
        dkv[m] = both.astype(jnp.bfloat16)
        partial[m] = (
            lanes_product(dq[m], weight[:, :wide]) + lanes_product(dkv[m], weight[:, wide:])
        ).astype(jnp.bfloat16)
        return carry

    lax.fori_loop(0, CHIPS, piece, 0)


def picked_piece(place, own, other, g, side, rows):
    m = jnp.bitwise_xor(place[0], g)
    here = own[m, rows, :].astype(jnp.float32)
    there = other[m, rows, :].astype(jnp.float32)
    return jnp.where(place[1] == side, here, there)


def unpack_dense_kernel(place, own, other, inner, outer, output, small):
    rows = inner.shape[0]
    half, quarter = rows // 2, rows // CHIPS
    slot_w = own.shape[2]
    for g in range(CHIPS):
        for side in range(2):
            s = 2 * g + side
            at = slice(slot_w * s, slot_w * (s + 1))
            inner[:, at] = picked_piece(place, own, other, g, side, slice(0, rows))
            for v in range(2):
                outer[half * s : half * (s + 1), slot_w * v : slot_w * (v + 1)] = picked_piece(
                    place, own, other, g, side, slice(rows + half * v, rows + half * (v + 1))
                )
            output[quarter * g : quarter * (g + 1), slot_w * side : slot_w * (side + 1)] = picked_piece(
                place, own, other, g, side, slice(2 * rows, 2 * rows + quarter)
            )
    small[...] = picked_piece(place, own, other, 0, 0, slice(2 * rows + quarter, own.shape[1]))


def unpack_heads_kernel(
    place, own, other, ww, we, ew, ee, key, value, sum_ww, sum_we, sum_ew, sum_ee, sum_value
):
    rows = own.shape[1] - TAG_ROWS
    wide = 4 * 3 * HD
    for side in range(2):
        at = slice(rows * side, rows * (side + 1))
        pieces = [picked_piece(place, own, other, g, side, slice(0, rows)) for g in range(CHIPS)]
        for k, target in enumerate((ww, we, ew, ee)):
            target[at, :] = jnp.concatenate(
                [p[:, HD * (4 * h + k) : HD * (4 * h + k + 1)] for p in pieces for h in range(3)], axis=1
            )
        for k, target in enumerate((key, value)):
            target[at, :] = jnp.concatenate(
                [
                    p[:, wide + HD * (2 * h + k) : wide + HD * (2 * h + k + 1)]
                    for p in pieces
                    for h in range(3)
                ],
                axis=1,
            )
    sums = picked_piece(place, own, other, place[2], 0, slice(rows, rows + TAG_ROWS))[:1]
    for k, target in enumerate((sum_ww, sum_we, sum_ew, sum_ee)):
        line = [sums[:, HD * (4 * h + k) : HD * (4 * h + k + 1)] for h in range(3)]
        target[...] = jnp.concatenate(line, axis=1).reshape(target.shape[0])
    line = [sums[:, wide + HD * (2 * h + 1) : wide + HD * (2 * h + 2)] for h in range(3)]
    sum_value[...] = jnp.concatenate(line, axis=1).reshape(sum_value.shape[0])


def smem():
    return pl.BlockSpec(memory_space=pltpu.SMEM)


def vmem():
    return pl.BlockSpec(memory_space=pltpu.VMEM)


def hbm():
    return pl.BlockSpec(memory_space=pl.ANY)


def whole_call(kernel, operands, outs, scratch=(), micros=1, mebibytes=16):
    return pl.pallas_call(
        kernel,
        out_shape=[jax.ShapeDtypeStruct(shape, dtype) for shape, dtype, _ in outs],
        in_specs=[spec() for _, spec in operands],
        out_specs=[spec() for _, _, spec in outs],
        scratch_shapes=list(scratch),
        compiler_params=pltpu.CompilerParams(vmem_limit_bytes=mebibytes << 20),
        cost_estimate=pl.CostEstimate(
            flops=micros * FLOPS_PER_MICRO, bytes_accessed=micros << 20, transcendentals=0
        ),
    )(*(value for value, _ in operands))


def grouped_device(
    tokens,
    cotangent,
    segment_ids,
    token_types,
    query_wordword,
    query_wordentity,
    query_entityword,
    query_entityentity,
    bias_wordword,
    bias_wordentity,
    bias_entityword,
    bias_entityentity,
    key_weight,
    value_weight,
    value_bias,
    output_weight,
    output_bias,
    first_gain,
    first_bias,
    inner_weight,
    inner_bias,
    outer_weight,
    outer_bias,
    second_gain,
    second_bias,
):
    bf16, f32 = jnp.bfloat16, jnp.float32
    index = lax.axis_index("ctx")
    chip, core = index // 2, index % 2
    wa = lax.axis_index("wa")
    parts = lax.axis_size("wa")
    place = jnp.stack([chip, core, wa]).astype(jnp.int32)
    inputs = tokens[0]
    tok, dmod = inputs.shape
    length = 2 * CHIPS * tok
    rows = key_weight.shape[0]
    half, quarter = rows // 2, rows // CHIPS
    group = dmod // CHIPS
    ff = inner_weight.shape[1]
    slot_w = ff // (2 * CHIPS)

    lines = (
        bias_wordword,
        bias_wordentity,
        bias_entityword,
        bias_entityentity,
        value_bias,
        output_bias,
        first_gain,
        first_bias,
        outer_bias,
        second_gain,
        second_bias,
        inner_bias,
    )
    six = (query_wordword, query_wordentity, query_entityword, query_entityentity, key_weight, value_weight)
    mine, slot = whole_call(
        prepare_kernel,
        [(place, smem)]
        + [(a, vmem) for a in (*six, *lines)]
        + [(a, hbm) for a in (inner_weight, outer_weight, output_weight)],
        [((half + TAG_ROWS, 6 * group), bf16, vmem), ((2 * rows + quarter, slot_w), bf16, vmem)],
        [pltpu.SemaphoreType.DMA((4,))],
        micros=3,
        mebibytes=58,
    )
    inputs, mine, slot = ordered(inputs, mine, slot)
    tags = (segment_ids[0] * 2 + token_types[0]).astype(bf16)
    tag_rows = jnp.pad(tags[None], ((0, TAG_ROWS - 1), (0, dmod - tok)))
    text = jnp.concatenate([inputs, tag_rows], axis=0)
    cut = tok // 2
    text_x, text_y = swapped(text, 2), swapped(text, 4)

    one, three = turned(mine, 1), turned(mine, 3)
    text_x, text_y, one, three, slot = ordered(text_x, text_y, one, three, slot)
    text_far = swapped(text_x[:cut], 4), swapped(text_y[cut:], 2)

    right, left = turned(slot, 1), turned(slot, 3)
    *text_far, right, left = ordered(*text_far, right, left)
    near_slot = jnp.stack([right, left])
    split, wide = half // 2, 6 * group // slot_w
    middle = TAG_ROWS * (slot.shape[0] // TAG_ROWS // 2)
    right = jnp.concatenate([*narrowed(one[:split], slot_w), right[:middle]], axis=0)
    left = jnp.concatenate([*narrowed(three[split:], slot_w), left[middle:]], axis=0)
    mine3 = jnp.stack([mine, one, three])
    right, left, mine3 = ordered(right, left, mine3)
    right, left = turned(right, 1), turned(left, 3)
    theirs3 = swapped(mine3, 1)
    near_x, near_y = swapped(near_slot, 2), swapped(near_slot, 4)
    right, left, theirs3 = ordered(right, left, theirs3)
    cut_right, cut_left = split * wide, (half + TAG_ROWS - split) * wide
    two = jnp.concatenate([widened(right[:cut_right], wide), widened(left[:cut_left], wide)], axis=0)
    theirs_two = swapped(two, 1)
    far_slot = jnp.concatenate([right[cut_right:], left[cut_left:]], axis=0)
    lines = jnp.stack([mine3[0, half:], mine3[1, half:], two[half:], mine3[2, half:]])

    weight, all_text, q, kv = whole_call(
        project_kernel,
        [(place, smem)] + [(a, vmem) for a in (text, text_x, text_y, *text_far, mine3, two, theirs3, theirs_two)],
        [
            ((dmod, 6 * group), bf16, vmem),
            ((CHIPS, tok + TAG_ROWS, dmod), bf16, vmem),
            ((CHIPS, tok, 2 * group), bf16, vmem),
            ((CHIPS, tok + TAG_ROWS, 2 * group), bf16, vmem),
        ],
        [pltpu.VMEM((parts, half + TAG_ROWS, 6 * group), bf16)] * 2,
        micros=8,
        mebibytes=20,
    )
    kv, near_x, near_y, far_slot = ordered(kv, near_x, near_y, far_slot)
    kv_other = swapped(kv, 1)
    first_slots = jnp.concatenate([*near_slot, *near_x, *near_y, far_slot], axis=0)
    to_x = jnp.concatenate([far_slot, near_y[1]], axis=0)
    to_y = jnp.concatenate([far_slot, near_x[0]], axis=0)
    kv_other, to_x, to_y, first_slots = ordered(kv_other, to_x, to_y, first_slots)
    to_x, to_y, to_far = swapped(to_x, 2), swapped(to_y, 4), swapped(far_slot, 6)
    first_other = swapped(first_slots, 1)

    *context, turned_out, lse, bounds = whole_call(
        attend_kernel,
        [(place, smem), (q, vmem), (kv, vmem), (kv_other, vmem)],
        [
            *[((tok, group), bf16, vmem)] * CHIPS,
            ((CHIPS, group, tok), f32, vmem),
            ((CHIPS, 3, 1, tok), f32, vmem),
            ((2, CHIPS), jnp.int32, smem),
        ],
        [
            pltpu.VMEM((3, length, 2 * HD), bf16),
            pltpu.VMEM((3, HD, length), bf16),
            pltpu.VMEM((length, TILE), f32),
            pltpu.VMEM((2 * CHIPS, 8, tok), f32),
            pltpu.VMEM((3, HD, tok), f32),
            pltpu.VMEM((CHIPS, tok, group), bf16),
        ],
        micros=25,
        mebibytes=20,
    )
    *context, to_x, to_y, to_far, first_other = ordered(*context, to_x, to_y, to_far, first_other)

    def exchanged(value):
        return [value[0]] + [swapped(value[m], 2 * m) for m in range(1, CHIPS)]

    contexts = exchanged(context)
    second_slots = jnp.concatenate([to_x, to_y, to_far], axis=0)
    second_other = swapped(second_slots, 1)

    slot_rows = 2 * rows + quarter + TAG_ROWS
    result, grad_sum, *grad_context, kept, sent_first, sent_second = whole_call(
        dense_kernel,
        [(place, smem)]
        + [(a, vmem) for a in (*contexts, text, cotangent[0], lines)]
        + [
            (a, hbm)
            for a in (inner_weight, outer_weight, output_weight, first_slots, first_other, second_slots, second_other)
        ],
        [
            ((tok, dmod), bf16, vmem),
            ((tok, dmod), f32, vmem),
            *[((tok, group), bf16, vmem)] * CHIPS,
            ((CHIPS, parts, slot_rows, slot_w), bf16, hbm),
            ((2 * parts, slot_rows, slot_w), bf16, hbm),
            ((2 * parts, slot_rows, slot_w), bf16, hbm),
        ],
        [
            pltpu.VMEM((dmod, ff), bf16),
            pltpu.VMEM((ff, dmod), bf16),
            pltpu.VMEM((dmod, dmod), bf16),
            pltpu.VMEM((tok, ff), bf16),
            pltpu.VMEM((tok, ff), f32),
            pltpu.VMEM((dmod, ff), bf16),
            pltpu.VMEM((ff, dmod), bf16),
            pltpu.VMEM((dmod, dmod), bf16),
            pltpu.VMEM((2, parts, TAG_ROWS, slot_w), bf16),
            pltpu.VMEM((parts, TAG_ROWS, slot_w), f32),
            pltpu.VMEM((1, ff), f32),
            pltpu.SemaphoreType.DMA((3,)),
            pltpu.SemaphoreType.DMA((3,)),
        ],
        micros=26,
        mebibytes=50,
    )
    grad_pieces = exchanged(grad_context)

    def added(*values):
        total = values[0].astype(f32)
        for v in values[1:]:
            total = total + v.astype(f32)
        return total

    middle = parts // 2
    upper, lower = slice(0, middle), slice(middle, None)
    first, second = swapped(sent_first, 1), swapped(sent_second, 1)
    far_x = added(kept[3, upper], first[:2]).astype(bf16)
    far_y = added(kept[3, lower], first[2:4]).astype(bf16)
    near_x = added(kept[1, upper], first[4:6]).astype(bf16)
    near_y = added(kept[2, lower], first[6:]).astype(bf16)
    *grad_pieces, far_x, far_y, near_x, near_y = ordered(*grad_pieces, far_x, far_y, near_x, near_y)
    far_x, far_y = swapped(far_x, 2), swapped(far_y, 4)
    near_x, near_y = swapped(near_x, 2), swapped(near_y, 4)

    dq, dkv, dkv_sent = whole_call(
        attend_back_kernel,
        [(place, smem), (bounds, smem)]
        + [(a, vmem) for a in (q, kv, kv_other, turned_out, lse, *grad_pieces)],
        [
            ((CHIPS, tok, 4 * group), bf16, vmem),
            ((CHIPS, tok, 2 * group), bf16, vmem),
            ((CHIPS, tok, 2 * group), bf16, vmem),
        ],
        [
            pltpu.VMEM((3, length, 4 * HD), bf16),
            pltpu.VMEM((3, 2 * HD, length), bf16),
            pltpu.VMEM((3, length, 4 * HD), f32),
            pltpu.VMEM((length, TILE), f32),
            pltpu.VMEM((2 * CHIPS, 8, tok), f32),
            pltpu.VMEM((3, 2 * HD, tok), f32),
            pltpu.VMEM((CHIPS, tok, group), bf16),
            pltpu.VMEM((3, 2 * tok, 4 * HD), bf16),
            pltpu.VMEM((3, KEY_BLOCK, 2 * tok), bf16),
        ],
        micros=34,
        mebibytes=36,
    )
    dq, dkv, dkv_sent, far_x, far_y, near_x, near_y, second = ordered(
        dq, dkv, dkv_sent, far_x, far_y, near_x, near_y, second
    )
    dkv_received = swapped(dkv_sent, 1)
    last_x = added(kept[1, lower], second[4:6], far_y).astype(bf16)
    last_y = added(kept[2, upper], second[6:], far_x).astype(bf16)
    last_x, last_y = ordered(last_x, last_y)
    last_x, last_y = swapped(last_x, 2), swapped(last_y, 4)
    dkv, partial = whole_call(
        token_grads_kernel,
        [(a, vmem) for a in (dq, dkv, dkv_received, weight)],
        [((CHIPS, tok, 2 * group), bf16, vmem), ((CHIPS, tok, dmod), bf16, vmem)],
        micros=8,
        mebibytes=16,
    )
    head_kept, head_sent = whole_call(
        head_grads_kernel,
        [(place, smem)] + [(a, vmem) for a in (all_text, dq, dkv)],
        [
            ((parts, half + TAG_ROWS, 6 * group), bf16, vmem),
            ((parts, half + TAG_ROWS, 6 * group), bf16, vmem),
        ],
        [pltpu.VMEM((dmod, 6 * group), f32)],
        micros=10,
        mebibytes=20,
    )
    head_kept, head_sent, last_x, last_y = ordered(head_kept, head_sent, last_x, last_y)

    def parts_sent(*values):
        shards = [
            added(*(lax.dynamic_index_in_dim(v, (wa + k) % parts, 0, keepdims=False) for v in values))
            for k in range(parts)
        ]
        return [v.astype(bf16) for v in shards]

    def parts_moved(values):
        return [turned(v, k) for k, v in enumerate(values) if k]

    def chips_moved(value):
        return [swapped(value, 2 * m) for m in range(1, CHIPS)]

    low, high = slice(0, cut), slice(cut, None)
    summed = jnp.concatenate(
        [
            added(kept[0, upper], second[:2], near_x, last_y),
            added(kept[0, lower], second[2:4], last_x, near_y),
        ],
        axis=0,
    ).astype(bf16)
    dense_parts = parts_sent(summed)
    text_x = jnp.stack([partial[3, low], partial[1, low]])
    text_y = jnp.stack([partial[3, high], partial[2, high]])
    *dense_parts, text_x, text_y = ordered(*dense_parts, text_x, text_y)
    dense_moved = parts_moved(dense_parts)
    head_received = swapped(head_sent, 1)
    text_x, text_y = swapped(text_x, 2), swapped(text_y, 4)
    *dense_moved, text_x, text_y, head_received = ordered(*dense_moved, text_x, text_y, head_received)

    count = dmod // slot_w
    dense_summed = added(dense_parts[0], *dense_moved).astype(bf16)
    (far_x, near_x), (far_y, near_y) = text_x, text_y
    last_x = added(partial[1, high], far_y).astype(bf16)
    last_y = added(partial[2, low], far_x).astype(bf16)
    to_x = jnp.concatenate([dense_summed, *narrowed(last_x, slot_w)], axis=0)
    to_y = jnp.concatenate([dense_summed, *narrowed(last_y, slot_w)], axis=0)
    head_parts = parts_sent(head_kept, head_received)
    *head_parts, to_x, to_y, dense_summed = ordered(*head_parts, to_x, to_y, dense_summed)
    head_moved = parts_moved(head_parts)
    head_moved[0], dense_far = ordered(head_moved[0], dense_summed)
    to_x, to_y, dense_far = swapped(to_x, 2), swapped(to_y, 4), swapped(dense_far, 6)
    *head_moved, to_x, to_y, dense_far = ordered(*head_moved, to_x, to_y, dense_far)

    deep = dense_summed.shape[0]
    dense_all = jnp.stack([dense_summed, to_x[:deep], to_y[:deep], dense_far])
    head_summed = added(head_parts[0], *head_moved).astype(bf16)
    head_summed, dense_all = ordered(head_summed, dense_all)
    head_moved = chips_moved(head_summed)
    dense_other = swapped(dense_all, 1)
    out_inner, out_outer, out_output, small = whole_call(
        unpack_dense_kernel,
        [(place, smem), (dense_all, vmem), (dense_other, vmem)],
        [
            ((rows, ff), f32, vmem),
            (outer_weight.shape, f32, vmem),
            ((rows, dmod), f32, vmem),
            ((TAG_ROWS, slot_w), f32, vmem),
        ],
        micros=4,
    )
    last_x, last_y = widened(to_x[deep:], count), widened(to_y[deep:], count)
    input_grads = grad_sum + jnp.concatenate(
        [added(partial[0, low], near_x, last_y), added(partial[0, high], last_x, near_y)], axis=0
    )
    *head_moved, out_inner, out_outer, out_output, small, input_grads = ordered(
        *head_moved, out_inner, out_outer, out_output, small, input_grads
    )
    head_all = jnp.stack([head_summed, *head_moved])
    out_heads = whole_call(
        unpack_heads_kernel,
        [(place, smem), (head_all, vmem), (swapped(head_all, 1), vmem)],
        [((rows, dmod), f32, vmem)] * 6 + [((rows,), f32, vmem)] * 5,
        micros=4,
    )

    own_small = lax.dynamic_slice(small[:12].reshape(6, dmod), (0, wa * rows), (6, rows))
    return (
        result[None],
        input_grads[None],
        *out_heads[:4],
        *out_heads[6:10],
        *out_heads[4:6],
        out_heads[10],
        out_output,
        own_small[0],
        own_small[1],
        own_small[2],
        out_inner,
        small[12:14].reshape(ff // parts),
        out_outer,
        own_small[3],
        own_small[4],
        own_small[5],
    )


def solution(mesh):
    in_specs = (
        P("wa", "ctx", None),
        P("wa", "ctx", None),
        P("wa", "ctx"),
        P("wa", "ctx"),
        P("wa", None),
        P("wa", None),
        P("wa", None),
        P("wa", None),
        P("wa"),
        P("wa"),
        P("wa"),
        P("wa"),
        P("wa", None),
        P("wa", None),
        P("wa"),
        P("wa", None),
        P("wa"),
        P("wa"),
        P("wa"),
        P("wa", None),
        P("wa"),
        P("wa", None),
        P("wa"),
        P("wa"),
        P("wa"),
    )
    out_specs = (
        P("wa", "ctx", None),
        P("wa", "ctx", None),
        P("wa", None),
        P("wa", None),
        P("wa", None),
        P("wa", None),
        P("wa"),
        P("wa"),
        P("wa"),
        P("wa"),
        P("wa", None),
        P("wa", None),
        P("wa"),
        P("wa", None),
        P("wa"),
        P("wa"),
        P("wa"),
        P("wa", None),
        P("wa"),
        P("wa", None),
        P("wa"),
        P("wa"),
        P("wa"),
    )
    body = grouped_device if mesh.shape["ctx"] == 2 * CHIPS else windowed_device
    return jax.shard_map(
        body, mesh=mesh, in_specs=in_specs, out_specs=out_specs, check_vma=False
    )
```
